32 devices in a mesh: wide: 8 (over z, y), narrow: 4 (over x, core).
Axes of the slice: x: 2, y: 2, z: 4, core: 2. Of those that a mesh axis runs over, the one named last changes fastest.
Arguments:
- tokens: bfloat16 [32768, 768], P(('wide', 'narrow')), may hold values from -6 to 6
- bucket: int32 [256], P(('wide', 'narrow')), may hold values from 0 to 7, as said below
- lengths: int32 [832], P(('wide', 'narrow')), may hold values from 5 to 128, as said below
- pairing: int32 [32, 26], P(('wide', 'narrow')), may hold values from 0 to 25, as said below
- targets: float32 [416], P(('wide', 'narrow')), may hold values from 0 to 1
- w_qkv: bfloat16 [768, 2304], replicated, may hold values from -0.21875 to 0.21875
- bias_q: bfloat16 [768], replicated, may hold values from -3 to 3
- bias_v: bfloat16 [768], replicated, may hold values from -3 to 3
- w_out: bfloat16 [768, 768], replicated, may hold values from -0.4375 to 0.4375
- bias_out: bfloat16 [768], replicated, may hold values from -3 to 3
- gain_attn: bfloat16 [768], replicated, may hold values from 0.5 to 1.5
- shift_attn: bfloat16 [768], replicated, may hold values from -1.1953125 to 1.1953125
- w_up: bfloat16 [768, 3072], replicated, may hold values from -0.21875 to 0.21875
- bias_up: bfloat16 [3072], replicated, may hold values from -3 to 3
- w_down: bfloat16 [3072, 768], replicated, may hold values from -0.109375 to 0.109375
- bias_down: bfloat16 [768], replicated, may hold values from -3 to 3
- gain_ffn: bfloat16 [768], replicated, may hold values from 0.5 to 1.5
- shift_ffn: bfloat16 [768], replicated, may hold values from -1.1953125 to 1.1953125
Outputs:
- encoded: bfloat16 [32768, 768], P(('wide', 'narrow'))
- grad_tokens: bfloat16 [32768, 768], P(('wide', 'narrow'))
- grad_w_qkv: float32 [768, 2304], P('wide')
- grad_bias_q: float32 [768], P('wide')
- grad_bias_v: float32 [768], P('wide')
- grad_w_out: float32 [768, 768], P('wide')
- grad_bias_out: float32 [768], P('wide')
- grad_gain_attn: float32 [768], P('wide')
- grad_shift_attn: float32 [768], P('wide')
- grad_w_up: float32 [768, 3072], P('wide')
- grad_bias_up: float32 [3072], P('wide')
- grad_w_down: float32 [3072, 768], P('wide')
- grad_bias_down: float32 [768], P('wide')
- grad_gain_ffn: float32 [768], P('wide')
- grad_shift_ffn: float32 [768], P('wide')
The draws below stay inside these ranges and needn't reach their ends.
Inputs may be any that keep to these rules, and one draw needn't show every extreme that they name: `bucket`: A device's 8 batches go to different wide indices, one batch of each class c, to a wide index of c * 1 to (c + 1) * 1 - 1; in every group each wide index takes exactly 8 batches. A batch of class c holds max(1, 12 div 2^c) sentences of together at most 128 tokens; a device's lengths list its batches' sentences batch after batch; every device has a sentence of exactly 128 tokens. `pairing`: each row is a permutation of 0 to 25; entries 2p and 2p + 1 name pair p.
All inputs are finite; a program needn't handle non-finite values.
Results may differ from the reference program's by a relative error of at most 0.012.
Values may be sent and summed in bfloat16 or wider, within the bound.
No kernel may reach another device: no remote copies, remote signals or barrier semaphores. Data moves between devices by JAX's collectives and lax.ppermute only.
A program may use at most 192 MiB of HBM per device.

```python
import jax
import jax.numpy as jnp
import numpy as np
from jax import lax

D = 768
HEADS = 12
HDIM = 64
FF = 3072
LMAX = 128
MINLEN = 5
BATCHES = 8
KTOP = 12
SENT_DEV = 26
TOK_DEV = 1024
GROUP = 1
HOMES = 32
TOKENS = 32768
PAIRS = 416
N_WIDE = 8
N_NARROW = 4


def class_counts_drawn():
    return np.array([max(1, KTOP // 2 ** number) for number in range(BATCHES)], dtype=np.int32)


def class_layout(key):
    base = jax.random.fold_in(key, 303)

    def one_device(number):
        return jax.random.permutation(jax.random.fold_in(base, number), BATCHES).astype(jnp.int32)
    wide_count = GROUP * BATCHES
    narrow_count = HOMES // wide_count
    return jax.vmap(one_device)(jnp.arange(HOMES, dtype=jnp.int32)).reshape(wide_count, narrow_count, BATCHES)


def draw_bucket(key, part):
    classes = class_layout(key)
    wide_count = GROUP * BATCHES
    narrow_count = HOMES // wide_count
    base = jax.random.fold_in(key, 404)

    def offsets(number):
        order = jax.random.permutation(jax.random.fold_in(base, number), wide_count)
        return (order // BATCHES).astype(jnp.int32)
    table = jax.vmap(offsets)(jnp.arange(narrow_count * BATCHES, dtype=jnp.int32)).reshape(narrow_count, BATCHES, wide_count)
    group_ids = jnp.arange(narrow_count, dtype=jnp.int32)[None, :, None]
    source_ids = jnp.arange(wide_count, dtype=jnp.int32)[:, None, None]
    offset = table[group_ids, classes, source_ids]
    return (classes * GROUP + offset).astype(jnp.int32).reshape(HOMES * BATCHES)


def draw_lengths(key, part):
    classes = class_layout(key).reshape(HOMES, BATCHES)
    counts = jnp.array(class_counts_drawn(), dtype=jnp.int32)
    highs = (LMAX // counts).astype(jnp.int32)
    lows = jnp.maximum(MINLEN, highs // 2).astype(jnp.int32)
    low_of = lows[classes][:, :, None]
    high_of = highs[classes][:, :, None]
    drawn = jax.random.randint(jax.random.fold_in(key, 505), (HOMES, BATCHES, KTOP), low_of, high_of + 1)
    drawn = jnp.where(classes[:, :, None] == BATCHES - 1, LMAX, drawn).astype(jnp.int32)
    valid = (jnp.arange(KTOP, dtype=jnp.int32)[None, None, :] < counts[classes][:, :, None]).astype(jnp.int32)
    flat = drawn.reshape(HOMES, BATCHES * KTOP)
    valid = valid.reshape(HOMES, BATCHES * KTOP)
    position = jnp.where(valid > 0, jnp.cumsum(valid, axis=1) - valid, SENT_DEV).astype(jnp.int32)
    row_ids = jnp.broadcast_to(jnp.arange(HOMES, dtype=jnp.int32)[:, None], position.shape)
    result = jnp.zeros((HOMES, SENT_DEV), jnp.int32).at[row_ids, position].set(flat, mode='drop')
    return result.reshape(HOMES * SENT_DEV)


def pair_table(key):
    base = jax.random.fold_in(key, 606)

    def one_device(number):
        return jax.random.permutation(jax.random.fold_in(base, number), SENT_DEV).astype(jnp.int32)
    return jax.vmap(one_device)(jnp.arange(HOMES, dtype=jnp.int32))


def draw_pairing(key, part):
    return pair_table(key)


def partner_table(key):
    order = pair_table(key)
    evens = order[:, 0::2]
    odds = order[:, 1::2]
    row_ids = jnp.broadcast_to(jnp.arange(HOMES, dtype=jnp.int32)[:, None], evens.shape)
    table = jnp.zeros((HOMES, SENT_DEV), jnp.int32).at[row_ids, evens].set(odds)
    return table.at[row_ids, odds].set(evens)


def row_layout(classes_row, lengths_row):
    counts = jnp.array(class_counts_drawn(), dtype=jnp.int32)[classes_row]
    starts = (jnp.cumsum(counts) - counts).astype(jnp.int32)
    sentence = jnp.arange(SENT_DEV, dtype=jnp.int32)
    batch_ids = jnp.arange(BATCHES, dtype=jnp.int32)
    batch_of = (jnp.sum((sentence[:, None] >= starts[None, :]).astype(jnp.int32), axis=1) - 1).astype(jnp.int32)
    owner = batch_of[:, None] == batch_ids[None, :]
    earlier = jnp.sum(lengths_row[:, None] * (batch_of[:, None] < batch_ids[None, :]).astype(jnp.int32), axis=0)
    finish = (jnp.cumsum(lengths_row) - jnp.sum(owner.astype(jnp.int32) * earlier[None, :], axis=1)).astype(jnp.int32)
    begin = (finish - lengths_row).astype(jnp.int32)
    position = jnp.arange(LMAX, dtype=jnp.int32)
    inside = (owner.T[:, None, :] & (begin[None, None, :] <= position[None, :, None]) & (position[None, :, None] < finish[None, None, :])).astype(jnp.int32)
    live = jnp.sum(inside, axis=2).astype(jnp.int32)
    sent_row = jnp.sum(inside * sentence[None, None, :], axis=2).astype(jnp.int32)
    offset = (position[None, :] - jnp.sum(inside * begin[None, None, :], axis=2)).astype(jnp.int32)
    return (sent_row.reshape(TOK_DEV), live.reshape(TOK_DEV), offset.reshape(TOK_DEV))


def draw_tokens(key, part):
    classes = class_layout(key).reshape(HOMES, BATCHES)
    sizes = draw_lengths(key, part).reshape(HOMES, SENT_DEV)
    partners = partner_table(key)
    dir_key = jax.random.fold_in(key, 707)
    noise_key = jax.random.fold_in(key, 708)

    def one_device(item):
        number, classes_row, lengths_row, partner_row = item
        sent_row, live, offset = row_layout(classes_row, lengths_row)
        directions = jax.random.normal(jax.random.fold_in(dir_key, number), (SENT_DEV, D), jnp.float32)
        noise = jax.random.normal(jax.random.fold_in(noise_key, number), (TOK_DEV, D), jnp.float32)
        own = directions[sent_row]
        other = directions[partner_row[sent_row]]
        sign = (1 - 2 * (offset % 2)).astype(jnp.float32)[:, None]
        inside = (live > 0)[:, None]
        rows = jnp.where(inside, 0.6 * own + 0.65 * sign * other + 0.4 * noise, noise)
        return jnp.clip(rows, -6.0, 6.0)
    result = lax.map(one_device, (jnp.arange(HOMES, dtype=jnp.int32), classes, sizes, partners))
    return result.reshape(TOKENS, D).astype(jnp.bfloat16)


def block_levels(stream_key, extent, pieces, smallest, top_value):
    level = 1.0
    for dim, shards_of in pieces:
        steps = jax.random.uniform(jax.random.fold_in(jax.random.fold_in(stream_key, 6), dim), (shards_of,), jnp.float32, smallest / len(pieces), top_value / len(pieces))
        level = level * jnp.repeat(jnp.exp(steps), extent[dim] // shards_of).reshape((-1,) + (1,) * (len(extent) - 1 - dim))
    return level


def scatter_about(rng, extent, width, reach, held_as=jnp.bfloat16):
    values = jax.random.normal(rng, extent, jnp.float32) * width
    return jnp.minimum(jnp.maximum(values, -reach), reach).astype(held_as)


def setup_inputs(seed: int = 0) -> dict:
    key_list = jax.random.split(jax.random.key(seed), 19)
    tokens = draw_tokens(jax.random.fold_in(key_list[18], 71), 0)
    bucket = draw_bucket(jax.random.fold_in(key_list[18], 71), 0)
    lengths = draw_lengths(jax.random.fold_in(key_list[18], 71), 0)
    pairing = draw_pairing(jax.random.fold_in(key_list[18], 71), 0)
    targets = jnp.clip(1.0 * jax.random.uniform(key_list[4], (PAIRS,), jnp.float32) ** block_levels(key_list[4], (PAIRS,), ((0, 32),), -0.2, 0.2), 0.0, 1.0)
    w_qkv = scatter_about(key_list[5], (D, 3 * D), D ** -0.5, 0.21875)
    bias_q = scatter_about(key_list[6], (D,), 0.5, 3.0)
    bias_v = scatter_about(key_list[7], (D,), 0.5, 3.0)
    w_out = scatter_about(key_list[8], (D, D), (D // 4) ** -0.5, 0.4375)
    bias_out = scatter_about(key_list[9], (D,), 0.5, 3.0)
    gain_attn = jnp.clip(1.0 + 0.1 * jax.random.normal(key_list[10], (D,), jnp.float32), 0.5, 1.5).astype(jnp.bfloat16)
    shift_attn = scatter_about(key_list[11], (D,), 0.2, 1.1953125)
    w_up = scatter_about(key_list[12], (D, FF), D ** -0.5, 0.21875)
    bias_up = scatter_about(key_list[13], (FF,), 0.5, 3.0)
    w_down = scatter_about(key_list[14], (FF, D), FF ** -0.5, 0.109375)
    bias_down = scatter_about(key_list[15], (D,), 0.5, 3.0)
    gain_ffn = jnp.clip(1.0 + 0.1 * jax.random.normal(key_list[16], (D,), jnp.float32), 0.5, 1.5).astype(jnp.bfloat16)
    shift_ffn = scatter_about(key_list[17], (D,), 0.2, 1.1953125)
    return dict(tokens=tokens, bucket=bucket, lengths=lengths, pairing=pairing, targets=targets, w_qkv=w_qkv, bias_q=bias_q, bias_v=bias_v, w_out=w_out, bias_out=bias_out, gain_attn=gain_attn, shift_attn=shift_attn, w_up=w_up, bias_up=bias_up, w_down=w_down, bias_down=bias_down, gain_ffn=gain_ffn, shift_ffn=shift_ffn)


EXACT = lax.Precision.HIGHEST
NORM_EPS = 1e-12
COS_EPS = 1e-06
MASKED = -1000000000.0
LOSS_SCALE = 1024.0

@jax.custom_vjp
def low(v):
    return lax.optimization_barrier(v.astype(jnp.bfloat16)).astype(jnp.float32)

@jax.custom_vjp
def low_back(v):
    return v

def low_keep(v):
    return (low(v), None)

def low_pass(kept, grad):
    return (grad,)

def back_keep(v):
    return (v, None)

def back_low(kept, grad):
    return (low(grad),)
low.defvjp(low_keep, low_pass)
low_back.defvjp(back_keep, back_low)

def matmul(left, right):
    return jnp.dot(left, right, precision=EXACT, preferred_element_type=jnp.float32)

def layer_norm(values, gain, shift):
    center = values - lax.optimization_barrier(jnp.mean(values, axis=-1, keepdims=True))
    spread = lax.rsqrt(lax.optimization_barrier(jnp.mean(center * center, axis=-1, keepdims=True)) + NORM_EPS)
    return center * spread * gain + shift

def class_counts():
    return jnp.array([max(1, KTOP // 2 ** number) for number in range(BATCHES)], dtype=jnp.int32)

def source_layout(bucket_row, lengths_row, group_size):
    batch_ids = jnp.arange(BATCHES, dtype=jnp.int32)
    classes = (bucket_row // group_size).astype(jnp.int32)
    choose = (classes[:, None] == batch_ids[None, :]).astype(jnp.int32)
    counts = lax.optimization_barrier(jnp.sum(choose * class_counts()[None, :], axis=1)).astype(jnp.int32)
    starts = (jnp.cumsum(counts) - counts).astype(jnp.int32)
    sentence = jnp.arange(lengths_row.shape[0], dtype=jnp.int32)
    batch_of = (lax.optimization_barrier(jnp.sum((sentence[:, None] >= starts[None, :]).astype(jnp.int32), axis=1)) - 1).astype(jnp.int32)
    owner = (batch_of[:, None] == batch_ids[None, :]).astype(jnp.int32)
    within = (sentence - lax.optimization_barrier(jnp.sum(owner * starts[None, :], axis=1))).astype(jnp.int32)
    earlier = lax.optimization_barrier(jnp.sum(lengths_row[:, None] * (batch_of[:, None] < batch_ids[None, :]).astype(jnp.int32), axis=0))
    finish = (jnp.cumsum(lengths_row) - lax.optimization_barrier(jnp.sum(owner * earlier[None, :], axis=1))).astype(jnp.int32)
    position = jnp.arange(LMAX, dtype=jnp.int32)
    before = (owner.T[:, None, :] > 0) & (finish[None, None, :] <= position[None, :, None])
    passed = lax.optimization_barrier(jnp.sum(before.astype(jnp.int32), axis=2)).astype(jnp.int32)
    row_tags = jnp.where(passed < counts[:, None], passed + 1, 0).astype(jnp.int32)
    return (row_tags, batch_of, within)

def allowed_pairs(row_tags):
    span = row_tags.shape[1]
    same = (row_tags[:, :, None] == row_tags[:, None, :]) & (row_tags[:, :, None] > 0)
    return same | jnp.eye(span, dtype=jnp.bool_)[None]

def device_forward(rows, row_tags, params):
    w_qkv, bias_q, bias_v, w_out, bias_out, gain_attn, shift_attn, w_up, bias_up, w_down, bias_down, gain_ffn, shift_ffn = params
    batch_count, span = row_tags.shape
    rows_count = batch_count * span
    flat = rows.reshape(rows_count, D)
    mixed = matmul(flat, w_qkv)
    queries = low_back(low((mixed[:, :D] + bias_q) * 0.125)).reshape(batch_count, span, HEADS, HDIM)
    keys_all = low_back(low(mixed[:, D:2 * D])).reshape(batch_count, span, HEADS, HDIM)
    values_all = low_back(low(mixed[:, 2 * D:] + bias_v)).reshape(batch_count, span, HEADS, HDIM)
    affinity = low_back(jnp.einsum('bqhd,bkhd->bhqk', queries, keys_all, precision=EXACT))
    affinity = jnp.where(allowed_pairs(row_tags)[:, None], affinity, MASKED)
    probs = low(jax.nn.softmax(affinity, axis=-1))
    attended = jnp.einsum('bhqk,bkhd->bqhd', probs, values_all, precision=EXACT).reshape(rows_count, D)
    attended = low_back(low(attended))
    branch = low_back(matmul(attended, w_out) + bias_out)
    hidden = layer_norm(flat + branch, gain_attn, shift_attn)
    inner = low_back(matmul(low(hidden), w_up) + bias_up)
    activated = low(jax.nn.gelu(inner, approximate=False))
    second = low_back(matmul(activated, w_down) + bias_down)
    normed_out = layer_norm(hidden + second, gain_ffn, shift_ffn)
    member = (row_tags[:, None, :] == jnp.arange(1, KTOP + 1, dtype=jnp.int32)[None, :, None]).astype(jnp.float32)
    pooling = member / jnp.maximum(lax.optimization_barrier(jnp.sum(member, axis=2, keepdims=True)), 1.0)
    pooled = jnp.einsum('bjl,bld->bjd', pooling, normed_out.reshape(batch_count, span, D), precision=EXACT)
    valid = (row_tags > 0).reshape(rows_count, 1).astype(jnp.float32)
    return (normed_out * valid, pooled)

def reference(tokens, bucket, lengths, pairing, targets, w_qkv, bias_q, bias_v, w_out, bias_out, gain_attn, shift_attn, w_up, bias_up, w_down, bias_down, gain_ffn, shift_ffn):
    params = tuple((item.astype(jnp.float32) for item in (w_qkv, bias_q, bias_v, w_out, bias_out, gain_attn, shift_attn, w_up, bias_up, w_down, bias_down, gain_ffn, shift_ffn)))
    bucket_rows = bucket.reshape(N_WIDE, N_NARROW, BATCHES)
    length_rows = lengths.reshape(N_WIDE, N_NARROW, SENT_DEV)
    layout = jax.vmap(jax.vmap(lambda marks, sizes: source_layout(marks, sizes, GROUP)))
    source_tags, batch_of, within = layout(bucket_rows, length_rows)
    dest_ids = jnp.arange(N_WIDE, dtype=jnp.int32)
    onehot = (bucket_rows[:, :, :, None] == dest_ids[None, None, None, :]).astype(jnp.int32)
    sent_to = lax.optimization_barrier(jnp.sum(onehot, axis=2)).astype(jnp.int32)
    batch_to = lax.optimization_barrier(jnp.sum(onehot * jnp.arange(BATCHES, dtype=jnp.int32)[None, None, :, None], axis=2)).astype(jnp.int32)
    rank = (jnp.cumsum(sent_to, axis=0) - sent_to).astype(jnp.int32)
    source_ids = jnp.arange(N_WIDE, dtype=jnp.int32)[:, None, None]
    group_ids = jnp.arange(N_NARROW, dtype=jnp.int32)[None, :, None]
    batch_ids = ((source_ids * N_NARROW + group_ids) * BATCHES + batch_to).astype(jnp.int32)
    full_shape = (N_WIDE, N_NARROW, N_WIDE)
    dest_index = jnp.broadcast_to(dest_ids[None, None, :], full_shape)
    group_index = jnp.broadcast_to(group_ids, full_shape)
    place = jnp.where(sent_to > 0, rank, BATCHES).astype(jnp.int32)
    arrive_index = jnp.zeros((N_WIDE, N_NARROW, BATCHES), jnp.int32).at[dest_index, group_index, place].set(batch_ids, mode='drop').reshape(HOMES, BATCHES)
    arrive_tags = source_tags.reshape(HOMES * BATCHES, LMAX)[arrive_index]
    dest_of = jnp.take_along_axis(bucket_rows, batch_of, axis=2).astype(jnp.int32)
    slot_of = jnp.take_along_axis(rank, dest_of, axis=2).astype(jnp.int32)
    home_index = (((dest_of * N_NARROW + group_ids) * BATCHES + slot_of) * KTOP + within).astype(jnp.int32).reshape(HOMES, SENT_DEV)
    pair_rows = pairing.reshape(HOMES, SENT_DEV)
    target_rows = targets.reshape(HOMES, SENT_DEV // 2)

    def total(source, weights):
        arrived = source.reshape(HOMES * BATCHES, LMAX, D)[arrive_index]

        def one_device(item):
            return jax.checkpoint(device_forward)(item[0], item[1], weights)
        encoded_rows, pooled = lax.map(one_device, (arrived, arrive_tags))
        home = pooled.reshape(HOMES * BATCHES * KTOP, D)[home_index]
        first = jax.vmap(lambda rows, ids: rows[ids[0::2]])(home, pair_rows)
        partner = jax.vmap(lambda rows, ids: rows[ids[1::2]])(home, pair_rows)
        cross = lax.optimization_barrier(jnp.sum(first * partner, axis=-1))
        scale_first = lax.rsqrt(lax.optimization_barrier(jnp.sum(first * first, axis=-1)) + COS_EPS)
        scale_partner = lax.rsqrt(lax.optimization_barrier(jnp.sum(partner * partner, axis=-1)) + COS_EPS)
        cosine = cross * scale_first * scale_partner
        error = cosine - target_rows
        return (LOSS_SCALE * jnp.sum(error * error), encoded_rows)
    loss_value, back_fn, encoded_rows = jax.vjp(total, tokens.astype(jnp.float32), params, has_aux=True)
    grad_source, grads = back_fn(jnp.ones_like(loss_value))
    encoded = encoded_rows.reshape(TOKENS, D).astype(jnp.bfloat16)
    grad_tokens = grad_source.reshape(TOKENS, D).astype(jnp.bfloat16)
    return (encoded, grad_tokens, grads[0], grads[1], grads[2], grads[3], grads[4], grads[5], grads[6], grads[7], grads[8], grads[9], grads[10], grads[11], grads[12])
```

```python
from functools import partial

import jax
import jax.numpy as jnp
from jax import lax
from jax.sharding import PartitionSpec as P

HEADS = 12
HDIM = 64
KTOP = 12


EXACT = lax.Precision.HIGHEST
NORM_EPS = 1e-12
COS_EPS = 1e-06
MASKED = -1000000000.0
LOSS_SCALE = 1024.0


def contract_rows(left, right):
    return lax.dot_general(
        left, right, (((0,), (0,)), ((), ())), preferred_element_type=jnp.float32
    )


def times_transpose(left, right):
    return lax.dot_general(
        left, right, (((1,), (1,)), ((), ())), preferred_element_type=jnp.float32
    )


def norm_forward(values, gain, shift):
    center = values - jnp.mean(values, axis=-1, keepdims=True)
    spread = lax.rsqrt(jnp.mean(center * center, axis=-1, keepdims=True) + NORM_EPS)
    normed = center * spread
    return (normed * gain + shift, normed, spread)


def norm_backward(grad_out, normed, spread, gain):
    scaled = grad_out * gain
    grad_in = spread * (
        scaled
        - jnp.mean(scaled, axis=-1, keepdims=True)
        - normed * jnp.mean(scaled * normed, axis=-1, keepdims=True)
    )
    return (grad_in, jnp.sum(grad_out * normed, axis=0), jnp.sum(grad_out, axis=0))


def class_counts(batches):
    return jnp.array([max(1, KTOP // 2**number) for number in range(batches)], dtype=jnp.int32)


def source_layout(bucket_row, lengths_row, group_size, span):
    batches = bucket_row.shape[0]
    batch_ids = jnp.arange(batches, dtype=jnp.int32)
    classes = bucket_row // group_size
    choose = (classes[:, None] == batch_ids[None, :]).astype(jnp.int32)
    counts = jnp.sum(choose * class_counts(batches)[None, :], axis=1)
    starts = jnp.cumsum(counts) - counts
    sentence = jnp.arange(lengths_row.shape[0], dtype=jnp.int32)
    batch_of = jnp.sum((sentence[:, None] >= starts[None, :]).astype(jnp.int32), axis=1) - 1
    owner = (batch_of[:, None] == batch_ids[None, :]).astype(jnp.int32)
    within = sentence - jnp.sum(owner * starts[None, :], axis=1)
    earlier = jnp.sum(
        lengths_row[:, None] * (batch_of[:, None] < batch_ids[None, :]).astype(jnp.int32), axis=0
    )
    finish = jnp.cumsum(lengths_row) - jnp.sum(owner * earlier[None, :], axis=1)
    position = jnp.arange(span, dtype=jnp.int32)
    before = (owner.T[:, None, :] > 0) & (finish[None, None, :] <= position[None, :, None])
    passed = jnp.sum(before.astype(jnp.int32), axis=2)
    row_tags = jnp.where(passed < counts[:, None], passed + 1, 0)
    return (row_tags, batch_of, within)


def allowed_pairs(row_tags):
    span = row_tags.shape[1]
    same = (row_tags[:, :, None] == row_tags[:, None, :]) & (row_tags[:, :, None] > 0)
    return same | jnp.eye(span, dtype=jnp.bool_)[None]


def pack_rows(item, wide_count, narrow_count):
    blocks = item.reshape(wide_count, -1)
    extent = blocks.shape[1]
    padded_len = (extent + narrow_count - 1) // narrow_count * narrow_count
    blocks = jnp.pad(blocks, ((0, 0), (0, padded_len - extent)))
    return blocks.reshape(-1)


def unpack_rows(whole, item, wide_count):
    extent = item.size // wide_count
    return whole[:extent].reshape((item.shape[0] // wide_count,) + item.shape[1:])


def regroup_rows(rows, bucket, wide_count):
    batches, span, width = rows.shape
    send = jnp.zeros((wide_count, span, width), rows.dtype).at[bucket].set(rows)
    got = lax.all_to_all(send, "wide", split_axis=0, concat_axis=0, tiled=True)
    if wide_count == batches:
        return got.reshape(batches * span, width)
    marks = jnp.zeros((wide_count, 1), jnp.int32).at[bucket].set(1)
    filled = lax.all_to_all(marks, "wide", split_axis=0, concat_axis=0, tiled=True)[:, 0]
    place = jnp.where(filled > 0, jnp.cumsum(filled) - filled, batches)
    chosen = (
        jnp.zeros((batches,), jnp.int32)
        .at[place]
        .set(jnp.arange(wide_count, dtype=jnp.int32), mode="drop")
    )
    return got[chosen].reshape(batches * span, width)


def swap(item, axis, step):
    count = lax.axis_size(axis)
    return lax.ppermute(item, axis, [(index, index ^ step) for index in range(count)])


def bit(axis, step):
    return (lax.axis_index(axis) // step) % 2


def halves(item, dim, mine):
    keep = lax.dynamic_index_in_dim(item, mine, dim, keepdims=False)
    give = lax.dynamic_index_in_dim(item, 1 - mine, dim, keepdims=False)
    return keep, give


def fold(item, dim, axis, step):
    keep, give = halves(item, dim, bit(axis, step))
    got = swap(give.astype(jnp.bfloat16), axis, step)
    return (keep.astype(jnp.float32) + got.astype(jnp.float32)).astype(jnp.bfloat16)


def spread(item, axis, step):
    got = swap(item, axis, step)
    mine = bit(axis, step)
    return jnp.stack([jnp.where(mine == 0, item, got), jnp.where(mine == 0, got, item)])


def sum_matrix(grad):
    rows, cols = grad.shape
    part = rows // 32
    cut = grad.reshape(2, 2, 2, 2, 2, part, cols)
    cut = fold(cut, 3, "narrow", 1)
    first, second = cut[..., : cols // 2], cut[..., cols // 2 :]
    first = fold(first, 3, "narrow", 2)
    first = fold(first, 2, "wide", 1)
    second = fold(second, 2, "wide", 1)
    second = fold(second, 2, "narrow", 2)
    both = jnp.concatenate([first, second], axis=-1)
    both = fold(both, 1, "wide", 2)
    both = fold(both, 0, "wide", 4)
    both = spread(both, "narrow", 2)
    both = spread(both, "narrow", 1)
    return both.reshape(rows // 8, cols).astype(jnp.float32)


def sum_vectors(items, wide_count):
    flat = jnp.concatenate([item.reshape(wide_count, -1) for item in items], axis=1)
    for axis, step in (("narrow", 1), ("narrow", 2), ("wide", 1), ("wide", 2), ("wide", 4)):
        flat = flat + swap(flat, axis, step)
    mine = lax.dynamic_index_in_dim(flat, lax.axis_index("wide"), 0, keepdims=False)
    sizes = [item.size // wide_count for item in items]
    out, start = [], 0
    for size in sizes:
        out.append(mine[start : start + size])
        start += size
    return out


def sum_terms(grads, wide_count, narrow_count):
    if (wide_count, narrow_count) == (8, 4):
        vectors = iter(sum_vectors([item for item in grads if item.ndim == 1], wide_count))
        return [sum_matrix(item) if item.ndim == 2 else next(vectors) for item in grads]
    out = []
    for item in grads:
        share = lax.psum_scatter(
            pack_rows(item, wide_count, narrow_count),
            ("wide", "narrow"),
            scatter_dimension=0,
            tiled=True,
        )
        whole = lax.all_gather(share.astype(jnp.bfloat16), "narrow", axis=0, tiled=True)
        out.append(unpack_rows(whole.astype(jnp.float32), item, wide_count))
    return out


def body(
    tokens,
    bucket,
    lengths,
    pairing,
    targets,
    w_qkv,
    bias_q,
    bias_v,
    w_out,
    bias_out,
    gain_attn,
    shift_attn,
    w_up,
    bias_up,
    w_down,
    bias_down,
    gain_ffn,
    shift_ffn,
):
    wide_count = lax.axis_size("wide")
    narrow_count = lax.axis_size("narrow")
    batches = bucket.shape[0]
    span = tokens.shape[0] // batches
    width = w_out.shape[0]
    rows_count = batches * span
    source_tags, batch_of, within = source_layout(bucket, lengths, wide_count // batches, span)
    arrived = tokens
    row_tags = source_tags
    allowed = allowed_pairs(row_tags)
    mixed = jnp.dot(arrived, w_qkv, preferred_element_type=jnp.float32)
    queries = (
        ((mixed[:, :width] + bias_q) * 0.125)
        .astype(jnp.bfloat16)
        .reshape(batches, span, HEADS, HDIM)
    )
    keys_all = mixed[:, width : 2 * width].astype(jnp.bfloat16).reshape(batches, span, HEADS, HDIM)
    values_all = (
        (mixed[:, 2 * width :] + bias_v).astype(jnp.bfloat16).reshape(batches, span, HEADS, HDIM)
    )

    def scores():
        product = jnp.einsum(
            "bqhd,bkhd->bhqk", queries, keys_all, preferred_element_type=jnp.float32
        )
        return jnp.where(allowed[:, None], product, MASKED)

    logits = scores()
    peak = jnp.max(logits, axis=-1, keepdims=True)
    raised = jnp.exp(logits - peak)
    row_total = jnp.sum(raised, axis=-1, keepdims=True)
    log_total = peak + jnp.log(row_total)
    probs_low = (raised / row_total).astype(jnp.bfloat16)
    attended = jnp.einsum(
        "bhqk,bkhd->bqhd", probs_low, values_all, preferred_element_type=jnp.float32
    )
    attended = attended.reshape(rows_count, width).astype(jnp.bfloat16)
    branch = jnp.dot(attended, w_out, preferred_element_type=jnp.float32) + bias_out
    hidden, normed_attn, spread_attn = norm_forward(
        arrived.astype(jnp.float32) + branch, gain_attn, shift_attn
    )
    hidden_low = hidden.astype(jnp.bfloat16)
    inner = jnp.dot(hidden_low, w_up, preferred_element_type=jnp.float32) + bias_up
    activated, gelu_back = jax.vjp(partial(jax.nn.gelu, approximate=False), inner)
    activated_low = activated.astype(jnp.bfloat16)
    second = jnp.dot(activated_low, w_down, preferred_element_type=jnp.float32) + bias_down
    normed_out, normed_ffn, spread_ffn = norm_forward(hidden + second, gain_ffn, shift_ffn)
    valid = (row_tags > 0).reshape(rows_count, 1).astype(jnp.float32)
    encoded = (normed_out * valid).astype(jnp.bfloat16)
    member = (
        row_tags[:, None, :] == jnp.arange(1, KTOP + 1, dtype=jnp.int32)[None, :, None]
    ).astype(jnp.float32)
    pooling = member / jnp.maximum(jnp.sum(member, axis=2, keepdims=True), 1.0)
    pooled = jnp.einsum(
        "bjl,bld->bjd", pooling, normed_out.reshape(batches, span, width), precision=EXACT
    )
    encoded = regroup_rows(encoded.reshape(batches, span, width), bucket, wide_count)
    sent_index = batch_of * KTOP + within
    home = pooled.reshape(batches * KTOP, width)[sent_index]
    pair_ids = pairing[0]
    first_ids = pair_ids[0::2]
    partner_ids = pair_ids[1::2]
    first = home[first_ids]
    partner = home[partner_ids]
    cross = jnp.sum(first * partner, axis=-1)
    scale_first = lax.rsqrt(jnp.sum(first * first, axis=-1) + COS_EPS)
    scale_partner = lax.rsqrt(jnp.sum(partner * partner, axis=-1) + COS_EPS)
    cosine = cross * scale_first * scale_partner
    factor = 2.0 * LOSS_SCALE * (cosine - targets)
    both_scales = (factor * scale_first * scale_partner)[:, None]
    grad_first = (
        both_scales * partner - (factor * cosine * scale_first * scale_first)[:, None] * first
    )
    grad_partner = (
        both_scales * first - (factor * cosine * scale_partner * scale_partner)[:, None] * partner
    )
    grad_home = (
        jnp.zeros(home.shape, jnp.float32)
        .at[first_ids]
        .add(grad_first)
        .at[partner_ids]
        .add(grad_partner)
    )
    grad_pooled = (
        jnp.zeros((batches * KTOP, width), jnp.float32)
        .at[sent_index]
        .set(grad_home)
        .reshape(batches, KTOP, width)
    )
    grad_normed = jnp.einsum("bjl,bjd->bld", pooling, grad_pooled, precision=EXACT).reshape(
        rows_count, width
    )
    grad_resid_ffn, grad_gain_ffn, grad_shift_ffn = norm_backward(
        grad_normed, normed_ffn, spread_ffn, gain_ffn
    )
    grad_second_low = grad_resid_ffn.astype(jnp.bfloat16)
    grad_bias_down = jnp.sum(grad_second_low.astype(jnp.float32), axis=0)
    grad_w_down = contract_rows(activated_low, grad_second_low)
    grad_active = times_transpose(grad_second_low, w_down)
    grad_inner_low = gelu_back(grad_active)[0].astype(jnp.bfloat16)
    grad_bias_up = jnp.sum(grad_inner_low.astype(jnp.float32), axis=0)
    grad_w_up = contract_rows(hidden_low, grad_inner_low)
    grad_hidden = times_transpose(grad_inner_low, w_up) + grad_resid_ffn
    grad_resid_attn, grad_gain_attn, grad_shift_attn = norm_backward(
        grad_hidden, normed_attn, spread_attn, gain_attn
    )
    grad_branch_low = grad_resid_attn.astype(jnp.bfloat16)
    grad_bias_out = jnp.sum(grad_branch_low.astype(jnp.float32), axis=0)
    grad_w_out = contract_rows(attended, grad_branch_low)
    grad_attended = (
        times_transpose(grad_branch_low, w_out)
        .astype(jnp.bfloat16)
        .reshape(batches, span, HEADS, HDIM)
    )
    logits = scores()
    probs = jnp.exp(logits - log_total)
    probs_again = probs.astype(jnp.bfloat16)
    grad_probs = jnp.einsum(
        "bqhd,bkhd->bhqk", grad_attended, values_all, preferred_element_type=jnp.float32
    )
    balance = jnp.sum(probs * grad_probs, axis=-1, keepdims=True)
    grad_logits = (probs * (grad_probs - balance)).astype(jnp.bfloat16)
    grad_queries = jnp.einsum(
        "bhqk,bkhd->bqhd", grad_logits, keys_all, preferred_element_type=jnp.float32
    )
    grad_keys = jnp.einsum(
        "bhqk,bqhd->bkhd", grad_logits, queries, preferred_element_type=jnp.float32
    )
    grad_values = jnp.einsum(
        "bhqk,bqhd->bkhd", probs_again, grad_attended, preferred_element_type=jnp.float32
    )
    grad_queries_low = grad_queries.reshape(rows_count, width).astype(jnp.bfloat16)
    grad_values_low = grad_values.reshape(rows_count, width).astype(jnp.bfloat16)
    grad_mixed = jnp.concatenate(
        [
            grad_queries_low * jnp.bfloat16(0.125),
            grad_keys.reshape(rows_count, width).astype(jnp.bfloat16),
            grad_values_low,
        ],
        axis=1,
    )
    grad_bias_q = jnp.sum(grad_queries_low.astype(jnp.float32) * 0.125, axis=0)
    grad_bias_v = jnp.sum(grad_values_low.astype(jnp.float32), axis=0)
    grad_w_qkv = contract_rows(arrived, grad_mixed)
    grad_arrived = (times_transpose(grad_mixed, w_qkv) + grad_resid_attn).astype(jnp.bfloat16)
    grad_tokens = grad_arrived
    grads = (
        grad_w_qkv,
        grad_bias_q,
        grad_bias_v,
        grad_w_out,
        grad_bias_out,
        grad_gain_attn,
        grad_shift_attn,
        grad_w_up,
        grad_bias_up,
        grad_w_down,
        grad_bias_down,
        grad_gain_ffn,
        grad_shift_ffn,
    )
    summed = sum_terms(grads, wide_count, narrow_count)
    return (
        encoded,
        grad_tokens,
        summed[0],
        summed[1],
        summed[2],
        summed[3],
        summed[4],
        summed[5],
        summed[6],
        summed[7],
        summed[8],
        summed[9],
        summed[10],
        summed[11],
        summed[12],
    )


def solution(mesh):
    in_specs = (
        P(("wide", "narrow"), None),
        P(("wide", "narrow")),
        P(("wide", "narrow")),
        P(("wide", "narrow"), None),
        P(("wide", "narrow")),
        P(),
        P(),
        P(),
        P(),
        P(),
        P(),
        P(),
        P(),
        P(),
        P(),
        P(),
        P(),
        P(),
    )
    out_specs = (
        P(("wide", "narrow"), None),
        P(("wide", "narrow"), None),
        P("wide", None),
        P("wide"),
        P("wide"),
        P("wide", None),
        P("wide"),
        P("wide"),
        P("wide"),
        P("wide", None),
        P("wide"),
        P("wide", None),
        P("wide"),
        P("wide"),
        P("wide"),
    )
    return jax.shard_map(body, mesh=mesh, in_specs=in_specs, out_specs=out_specs, check_vma=False)
```

```python
from functools import partial

import jax
import jax.numpy as jnp
from jax import lax
from jax.experimental import pallas as pl
from jax.experimental.pallas import tpu as pltpu
from jax.sharding import PartitionSpec as P

HDIM = 64
KTOP = 12
NORM_EPS = 1e-12
COS_EPS = 1e-06
MASKED = -1000000000.0
LOSS_SCALE = 1024.0
F32 = jnp.float32
BF16 = jnp.bfloat16
LANES = 128
VMEM_LIMIT = 60 * 1024 * 1024
ERF_P = 0.3275911
ERF_A = (0.254829592, -0.284496736, 1.421413741, -1.453152027, 1.061405429)
HALF_ROOT = 0.7071067811865476
PEAK = 0.3989422804014327
ROW_BQ, ROW_BV, ROW_BO, ROW_GA, ROW_SA, ROW_BD, ROW_GF, ROW_SF = range(8)


def dot(left, right):
    return jnp.dot(left, right, preferred_element_type=F32)


def dot_t(left, right):
    return lax.dot_general(left, right, (((1,), (1,)), ((), ())), preferred_element_type=F32)


def t_dot(left, right):
    return lax.dot_general(left, right, (((0,), (0,)), ((), ())), preferred_element_type=F32)


def full(shape):
    return pl.BlockSpec(shape, lambda *_: (0,) * len(shape))


def once(shape):
    return pl.BlockSpec(shape, lambda *_: (0,) * len(shape), pipeline_mode=pl.Buffered(1))


def shaped(shape, dtype):
    return jax.ShapeDtypeStruct(shape, dtype)


def call(kernel, name, grid, prefetch, in_specs, out_specs, out_shape, scratch, flops, moved, args):
    return pl.pallas_call(
        kernel,
        grid_spec=pltpu.PrefetchScalarGridSpec(
            num_scalar_prefetch=len(prefetch),
            grid=grid,
            in_specs=in_specs,
            out_specs=out_specs,
            scratch_shapes=scratch,
        ),
        out_shape=out_shape,
        compiler_params=pltpu.CompilerParams(
            dimension_semantics=("arbitrary",) * len(grid), vmem_limit_bytes=VMEM_LIMIT
        ),
        cost_estimate=pl.CostEstimate(flops=int(flops), bytes_accessed=int(moved), transcendentals=0),
        name=name,
    )(*prefetch, *args)


def norm_forward(values):
    center = values - jnp.mean(values, axis=-1, keepdims=True)
    spread = lax.rsqrt(jnp.mean(center * center, axis=-1, keepdims=True) + NORM_EPS)
    return center * spread, spread


def norm_backward(grad_out, normed, spread, gain):
    scaled = grad_out * gain
    mean_scaled = jnp.mean(scaled, axis=-1, keepdims=True)
    mean_product = jnp.mean(scaled * normed, axis=-1, keepdims=True)
    return spread * (scaled - mean_scaled - normed * mean_product)


def column_sum(values):
    return jnp.sum(values, axis=0, keepdims=True)


def gelu_pair(v):
    t = 1.0 / (1.0 + (ERF_P * HALF_ROOT) * jnp.abs(v))
    bell = jnp.exp(-0.5 * (v * v))
    poly = 0.5 * ERF_A[4]
    for coef in ERF_A[3::-1]:
        poly = poly * t + 0.5 * coef
    tail = poly * t * bell
    phi = jnp.where(v > 0, 1.0 - tail, tail)
    return v * phi, phi + v * (PEAK * bell)


def head_masks():
    lane = lax.broadcasted_iota(jnp.int32, (1, LANES), 1)
    low = (lane < HDIM).astype(F32)
    return low.astype(BF16), (1.0 - low).astype(BF16), lane < HDIM


def sentence_count(bucket_s, number, group_size):
    kind = bucket_s[number]
    if group_size > 1:
        kind = kind // group_size
    return jnp.maximum(1, lax.shift_right_logical(jnp.int32(KTOP), kind))


def row_sentences(batch, bucket_s, lengths_s, group_size, batches, sent, span):
    start = jnp.int32(0)
    for other in range(batches):
        start += jnp.where(other < batch, sentence_count(bucket_s, other, group_size), 0)
    count = sentence_count(bucket_s, batch, group_size)
    lane = lax.broadcasted_iota(jnp.int32, (8, span), 1)
    row = lax.broadcasted_iota(jnp.int32, (span, span), 0)
    passed_lane = jnp.zeros((8, span), jnp.int32)
    passed_row = jnp.zeros((span, span), jnp.int32)
    finish = jnp.int32(0)
    for number in range(KTOP):
        finish += lengths_s[jnp.minimum(start + number, sent - 1)]
        bound = jnp.where(number < count, finish, span)
        passed_lane += (lane >= bound).astype(jnp.int32)
        passed_row += (row >= bound).astype(jnp.int32)
    sid_lane = jnp.where(passed_lane < count, start + passed_lane, -1)
    sid_row = jnp.where(passed_row < count, start + passed_row, -1)
    return sid_lane, sid_row


def attention_forward(x, w_qkv, w_out, table, bucket, lengths, group_size, span, rows_step):
    rows, width = x.shape
    batches = rows // span
    pairs = width // LANES
    sent = lengths.shape[0]
    per_step = rows_step // span

    def kernel(bucket_s, lengths_s, x_ref, wq_ref, wo_ref, tab_ref, qkv_ref, p_ref, att_ref, n_ref, s_ref, sid_ref):
        step = pl.program_id(0)
        low_b, high_b, low_m = head_masks()
        x_in = x_ref[...]
        mixed = dot(x_in, wq_ref[:, :width]) + tab_ref[ROW_BQ : ROW_BQ + 1, :]
        qkv_ref[:, :width] = (mixed * 0.125).astype(BF16)
        qkv_ref[:, width : 2 * width] = dot(x_in, wq_ref[:, width : 2 * width]).astype(BF16)
        mixed = dot(x_in, wq_ref[:, 2 * width :]) + tab_ref[ROW_BV : ROW_BV + 1, :]
        qkv_ref[:, 2 * width :] = mixed.astype(BF16)
        eye = lax.broadcasted_iota(jnp.int32, (span, span), 0) == lax.broadcasted_iota(
            jnp.int32, (span, span), 1
        )
        for inner in range(per_step):
            sid_lane, sid_row = row_sentences(
                step * per_step + inner, bucket_s, lengths_s, group_size, batches, sent, span
            )
            sid_ref[inner] = sid_lane
            same = (sid_row == sid_lane[0:1, :]) & (sid_row >= 0)
            bias = jnp.where(same | eye, 0.0, MASKED)
            bias = jnp.concatenate([bias, bias], axis=0)
            base = slice(inner * span, (inner + 1) * span)
            for pair in range(pairs):
                cols = slice(pair * LANES, (pair + 1) * LANES)
                q = qkv_ref[base, cols]
                k = qkv_ref[base, width + pair * LANES : width + (pair + 1) * LANES]
                v = qkv_ref[base, 2 * width + pair * LANES : 2 * width + (pair + 1) * LANES]
                both = jnp.concatenate([q * low_b, q * high_b], axis=0)
                logits = dot_t(both, k) + bias
                raised = jnp.exp(logits - jnp.max(logits, axis=-1, keepdims=True))
                total = jnp.sum(raised, axis=-1, keepdims=True)
                probs = (raised * (1.0 / total)).astype(BF16)
                p_ref[inner, pair] = probs
                mix = dot(probs, v)
                att_ref[base, cols] = jnp.where(low_m, mix[:span], mix[span:]).astype(BF16)
        branch = dot(att_ref[...], wo_ref[...]) + tab_ref[ROW_BO : ROW_BO + 1, :]
        normed, spread = norm_forward(x_in.astype(F32) + branch)
        n_ref[...] = normed
        s_ref[...] = jnp.broadcast_to(spread, (rows_step, LANES))

    return call(
        kernel,
        "attn_fwd",
        (rows // rows_step,),
        (bucket, lengths),
        [
            pl.BlockSpec((rows_step, width), lambda i, *_: (i, 0)),
            once((width, 3 * width)),
            once((width, width)),
            once((8, width)),
        ],
        [
            pl.BlockSpec((rows_step, 3 * width), lambda i, *_: (i, 0)),
            pl.BlockSpec((per_step, pairs, 2 * span, span), lambda i, *_: (i, 0, 0, 0)),
            pl.BlockSpec((rows_step, width), lambda i, *_: (i, 0)),
            pl.BlockSpec((rows_step, width), lambda i, *_: (i, 0)),
            pl.BlockSpec((rows_step, LANES), lambda i, *_: (i, 0)),
            pl.BlockSpec((per_step, 8, span), lambda i, *_: (i, 0, 0)),
        ],
        [
            shaped((rows, 3 * width), BF16),
            shaped((batches, pairs, 2 * span, span), BF16),
            shaped((rows, width), BF16),
            shaped((rows, width), F32),
            shaped((rows, LANES), F32),
            shaped((batches, 8, span), jnp.int32),
        ],
        [],
        8 * rows * width * width * 2,
        30e6,
        (x, w_qkv, w_out, table),
    )


def feed_forward(n_attn, w_up, w_down, bias_up, table, sid, slots, pairing, targets, slot_count, chunk, block):
    rows, width = n_attn.shape
    ff = w_up.shape[1]
    batches, _, span = sid.shape
    pair_count = targets.shape[0]
    side = -(-pair_count // 8) * 8
    steps = ff // chunk
    blocks = rows // block
    per_block = block // span

    def kernel(
        slots_s, pairing_s, targets_s, n_ref, wu_ref, wd_ref, bu_ref, tab_ref, sid_ref,
        act_ref, dg_ref, ht_ref, enc_ref, gres_ref, gsl_ref, vec_ref, low_scr, acc_scr, spread_scr,
    ):
        step = pl.program_id(0)
        gain = tab_ref[ROW_GA : ROW_GA + 1, :]
        shift = tab_ref[ROW_SA : ROW_SA + 1, :]

        @pl.when(step == 0)
        def _():
            hidden = (n_ref[...] * gain + shift).astype(BF16)
            low_scr[...] = hidden
            ht_ref[...] = hidden.T
            acc_scr[...] = jnp.zeros_like(acc_scr)

        for number in range(blocks):
            base = slice(number * block, (number + 1) * block)
            inner = dot(low_scr[base, :], wu_ref[...]) + bu_ref[...].astype(F32)
            active, slope = gelu_pair(inner)
            active = active.astype(BF16)
            act_ref[base, :] = active
            dg_ref[base, :] = slope.astype(BF16)
            acc_scr[base, :] += dot(active, wd_ref[...])

        @pl.when(step == steps - 1)
        def _():
            gain_out = tab_ref[ROW_GF : ROW_GF + 1, :]
            shift_out = tab_ref[ROW_SF : ROW_SF + 1, :]
            slot = lax.broadcasted_iota(jnp.int32, (2 * side, span), 0)
            wanted = jnp.full((2 * side, span), -2, jnp.int32)
            goal = jnp.zeros((side, LANES), F32)
            goal_slot = lax.broadcasted_iota(jnp.int32, (side, LANES), 0)
            for number in range(pair_count):
                wanted = jnp.where(slot == number, pairing_s[0, 2 * number], wanted)
                wanted = jnp.where(slot == side + number, pairing_s[0, 2 * number + 1], wanted)
                goal = jnp.where(goal_slot == number, targets_s[number], goal)
            members = [
                (sid_ref[number][0:1, :] == wanted).astype(F32) for number in range(batches)
            ]
            sizes = jnp.zeros((2 * side, 1), F32)
            for member in members:
                sizes += jnp.sum(member, axis=-1, keepdims=True)
            share = 1.0 / jnp.maximum(sizes, 1.0)
            picks = [
                jnp.concatenate(members[number * per_block : (number + 1) * per_block], axis=1).astype(BF16)
                for number in range(blocks)
            ]
            ones = jnp.ones((2 * side, LANES), BF16)
            pooled = jnp.zeros((2 * side, width), F32)
            for number in range(blocks):
                base = slice(number * block, (number + 1) * block)
                resid = (
                    n_ref[base, :] * gain + shift + acc_scr[base, :] + tab_ref[ROW_BD : ROW_BD + 1, :]
                )
                normed, spread = norm_forward(resid)
                acc_scr[base, :] = normed
                spread_scr[base, :] = jnp.broadcast_to(spread, (block, LANES))
                out = normed * gain_out + shift_out
                high = out.astype(BF16)
                rest = (out - high.astype(F32)).astype(BF16)
                pooled += dot(picks[number], high) + dot(picks[number], rest)
                valid = t_dot(picks[number], ones)
                for col in range(width // LANES):
                    cols = slice(col * LANES, (col + 1) * LANES)
                    kept = (out[:, cols] * valid).astype(BF16)
                    for inner in range(per_block):
                        enc_ref[slots_s[number * per_block + inner], :, cols] = kept[
                            inner * span : (inner + 1) * span
                        ]
            pooled = pooled * share
            first, partner = pooled[:side], pooled[side:]
            cross = jnp.sum(first * partner, axis=-1, keepdims=True)
            scale_first = lax.rsqrt(jnp.sum(first * first, axis=-1, keepdims=True) + COS_EPS)
            scale_partner = lax.rsqrt(jnp.sum(partner * partner, axis=-1, keepdims=True) + COS_EPS)
            cosine = cross * scale_first * scale_partner
            factor = 2.0 * LOSS_SCALE * (cosine - goal[:, :1])
            both_scales = factor * scale_first * scale_partner
            grad_first = both_scales * partner - (factor * cosine * scale_first * scale_first) * first
            grad_partner = (
                both_scales * first - (factor * cosine * scale_partner * scale_partner) * partner
            )
            grad_home = jnp.concatenate([grad_first, grad_partner], axis=0) * share
            high = grad_home.astype(BF16)
            rest = (grad_home - high.astype(F32)).astype(BF16)
            vec_ref[...] = jnp.zeros_like(vec_ref)
            for number in range(blocks):
                base = slice(number * block, (number + 1) * block)
                grad_out = t_dot(picks[number], high) + t_dot(picks[number], rest)
                normed = acc_scr[base, :]
                resid = norm_backward(grad_out, normed, spread_scr[base, :1], gain_out)
                gres_ref[base, :] = resid
                low = resid.astype(BF16)
                gsl_ref[base, :] = low
                vec_ref[0:1, :] += column_sum(grad_out * normed)
                vec_ref[1:2, :] += column_sum(grad_out)
                vec_ref[2:3, :] += column_sum(low.astype(F32))

    return call(
        kernel,
        "ffn_fwd",
        (steps,),
        (slots, pairing, targets),
        [
            once((rows, width)),
            pl.BlockSpec((width, chunk), lambda j, *_: (0, j)),
            pl.BlockSpec((chunk, width), lambda j, *_: (j, 0)),
            pl.BlockSpec((1, chunk), lambda j, *_: (0, j)),
            once((8, width)),
            once((batches, 8, span)),
        ],
        [
            pl.BlockSpec((rows, chunk), lambda j, *_: (0, j)),
            pl.BlockSpec((rows, chunk), lambda j, *_: (0, j)),
            once((width, rows)),
            once((slot_count, span, width)),
            once((rows, width)),
            once((rows, width)),
            once((8, width)),
        ],
        [
            shaped((rows, ff), BF16),
            shaped((rows, ff), BF16),
            shaped((width, rows), BF16),
            shaped((slot_count, span, width), BF16),
            shaped((rows, width), F32),
            shaped((rows, width), BF16),
            shaped((8, width), F32),
        ],
        [
            pltpu.VMEM((rows, width), BF16),
            pltpu.VMEM((rows, width), F32),
            pltpu.VMEM((rows, LANES), F32),
        ],
        8 * rows * width * ff,
        40e6,
        (n_attn, w_up, w_down, bias_up, table, sid),
    )


def deal(scratch, here_s, outs, z_count, pieces):
    send_a, keep_a, send_b, keep_b = outs
    x, y = here_s[2], here_s[3]
    for z in range(z_count):
        for other in range(2):
            at = pl.ds((z * 2 + other) * pieces, pieces)
            send_a[at] = scratch[z, other, 1 - x, 0].astype(BF16)
            keep_a[at] = scratch[z, other, x, 0].astype(BF16)
            send_b[at] = scratch[z, 1 - y, other, 1].astype(BF16)
            keep_b[at] = scratch[z, y, other, 1].astype(BF16)


def down_terms(active, grad_second, here, which, got=None):
    rows, ff = active.shape
    half = grad_second.shape[1] // 2
    steps = 4
    tall = ff // steps
    pieces = ff // 32 // 8

    def give(here_s, act_ref, gs_ref, out_ref):
        out_ref[...] = t_dot(act_ref[...], gs_ref[...]).astype(BF16)

    def own(here_s, act_ref, gs_ref, got_ref, *rest):
        outs, scratch = rest[:4], rest[4]
        term = t_dot(act_ref[...], gs_ref[...]) + got_ref[...].astype(F32)
        scratch[...] = term.reshape(scratch.shape)
        deal(scratch, here_s, outs, 1, pieces)

    in_specs = [
        pl.BlockSpec((rows, tall), lambda i, here_s: (0, i)),
        pl.BlockSpec((rows, half), lambda i, here_s: (0, here_s[which]), pipeline_mode=pl.Buffered(1)),
    ]
    flops = 2 * rows * ff * half
    if got is None:
        return call(
            give, "down_give", (steps,), (here,), in_specs,
            pl.BlockSpec((tall, half), lambda i, *_: (i, 0)),
            shaped((ff, half), BF16), [], flops, 9e6, (active, grad_second),
        )
    block = (2 * pieces, 8, half)
    return call(
        own, "down_own", (steps,), (here,),
        in_specs + [pl.BlockSpec((tall, half), lambda i, *_: (i, 0))],
        [pl.BlockSpec(block, lambda i, *_: (i, 0, 0))] * 4,
        [shaped((8 * pieces, 8, half), BF16)] * 4,
        [pltpu.VMEM((1, 2, 2, 2, pieces, 8, half), F32)],
        flops, 11e6, (active, grad_second, got),
    )


def up_terms(grad_second, slope, hidden_t, w_up, w_down, here, which, chunk, block, so_far=None, got=None):
    rows, width = grad_second.shape
    ff = w_up.shape[1]
    half = ff // 2
    steps = half // chunk
    blocks = rows // block
    pieces = width // 32 // 8
    more = so_far is not None

    def kernel(here_s, *refs):
        gs_ref, dg_ref, ht_ref, wu_ref, wd_ref = refs[:5]
        refs = refs[5:]
        if more:
            so_far_ref, refs = refs[0], refs[1:]
        if got is not None:
            got_ref, refs = refs[0], refs[1:]
            outs, refs = refs[:4], refs[4:]
        else:
            out_ref, refs = refs[0], refs[1:]
        gh_ref, bu_ref, gi_scr = refs[:3]
        step = pl.program_id(0)

        @pl.when(step == 0)
        def _():
            gh_ref[...] = so_far_ref[...] if more else jnp.zeros_like(gh_ref)

        sums = jnp.zeros((1, chunk), F32)
        for number in range(blocks):
            base = slice(number * block, (number + 1) * block)
            grad_active = dot_t(gs_ref[base, :], wd_ref[...])
            low = (grad_active * dg_ref[base, :].astype(F32)).astype(BF16)
            gi_scr[base, :] = low
            sums += column_sum(low.astype(F32))
            gh_ref[base, :] += dot_t(low, wu_ref[...])
        bu_ref[...] = sums
        term = dot(ht_ref[...], gi_scr[...])
        if got is None:
            out_ref[...] = term.astype(BF16)
        else:
            scratch = refs[3]
            term += got_ref[...].astype(F32)
            scratch[...] = term.reshape(scratch.shape)
            deal(scratch, here_s, outs, 4, pieces)

    def col(i, here_s):
        return here_s[which] * steps + i

    in_specs = [
        once((rows, width)),
        pl.BlockSpec((rows, chunk), lambda i, h: (0, col(i, h))),
        once((width, rows)),
        pl.BlockSpec((width, chunk), lambda i, h: (0, col(i, h))),
        pl.BlockSpec((chunk, width), lambda i, h: (col(i, h), 0)),
    ]
    args = [grad_second, slope, hidden_t, w_up, w_down]
    if more:
        in_specs.append(once((rows, width)))
        args.append(so_far)
    scratch = [pltpu.VMEM((rows, chunk), BF16)]
    if got is None:
        out_specs = [pl.BlockSpec((width, chunk), lambda i, *_: (0, i))]
        out_shape = [shaped((width, half), BF16)]
    else:
        in_specs.append(pl.BlockSpec((width, chunk), lambda i, *_: (0, i)))
        args.append(got)
        out_specs = [pl.BlockSpec((8 * pieces, 8, chunk), lambda i, *_: (0, 0, i))] * 4
        out_shape = [shaped((8 * pieces, 8, half), BF16)] * 4
        scratch.append(pltpu.VMEM((4, 2, 2, 2, pieces, 8, chunk), F32))
    return call(
        kernel, "up_give" if got is None else "up_own", (steps,), (here,), in_specs,
        out_specs + [once((rows, width)), pl.BlockSpec((1, chunk), lambda i, *_: (0, i))],
        out_shape + [shaped((rows, width), F32), shaped((1, half), F32)],
        scratch, 6 * rows * width * half, 20e6, args,
    )


def attention_backward(gh, gres, n_attn, spread, table, w_out, qkv, probs, span, rows_step):
    rows, width = gh.shape
    pairs = width // LANES
    per_step = rows_step // span

    def kernel(gh_ref, gres_ref, n_ref, s_ref, tab_ref, wo_ref, qkv_ref, p_ref, gr_ref, gb_ref, gm_ref, vec_ref, ga_scr):
        step = pl.program_id(0)
        low_b, high_b, low_m = head_masks()

        @pl.when(step == 0)
        def _():
            vec_ref[...] = jnp.zeros_like(vec_ref)

        normed = n_ref[...]
        grad_hidden = gh_ref[...] + gres_ref[...]
        resid = norm_backward(grad_hidden, normed, s_ref[:, :1], tab_ref[ROW_GA : ROW_GA + 1, :])
        gr_ref[...] = resid
        low = resid.astype(BF16)
        gb_ref[...] = low
        vec_ref[2:3, :] += column_sum(low.astype(F32))
        vec_ref[3:4, :] += column_sum(grad_hidden * normed)
        vec_ref[4:5, :] += column_sum(grad_hidden)
        ga_scr[...] = dot_t(low, wo_ref[...]).astype(BF16)
        for inner in range(per_step):
            base = slice(inner * span, (inner + 1) * span)
            for pair in range(pairs):
                cols = slice(pair * LANES, (pair + 1) * LANES)
                k_cols = slice(width + pair * LANES, width + (pair + 1) * LANES)
                v_cols = slice(2 * width + pair * LANES, 2 * width + (pair + 1) * LANES)
                q, k, v = qkv_ref[base, cols], qkv_ref[base, k_cols], qkv_ref[base, v_cols]
                grad = ga_scr[base, cols]
                grads = jnp.concatenate([grad * low_b, grad * high_b], axis=0)
                both = jnp.concatenate([q * low_b, q * high_b], axis=0)
                weights = p_ref[inner, pair]
                wide = weights.astype(F32)
                grad_probs = dot_t(grads, v)
                balance = jnp.sum(wide * grad_probs, axis=-1, keepdims=True)
                grad_logits = (wide * (grad_probs - balance)).astype(BF16)
                mix = dot(grad_logits, k)
                grad_q = jnp.where(low_m, mix[:span], mix[span:]).astype(BF16) * jnp.bfloat16(0.125)
                grad_v = t_dot(weights, grads).astype(BF16)
                gm_ref[base, cols] = grad_q
                gm_ref[base, k_cols] = t_dot(grad_logits, both).astype(BF16)
                gm_ref[base, v_cols] = grad_v
                vec_ref[0:1, cols] += column_sum(grad_q.astype(F32))
                vec_ref[1:2, cols] += column_sum(grad_v.astype(F32))

    def rows_of(cols):
        return pl.BlockSpec((rows_step, cols), lambda i: (i, 0))

    return call(
        kernel,
        "attn_bwd",
        (rows // rows_step,),
        (),
        [
            rows_of(width), rows_of(width), rows_of(width), rows_of(LANES),
            once((8, width)), once((width, width)), rows_of(3 * width),
            pl.BlockSpec((per_step, pairs, 2 * span, span), lambda i: (i, 0, 0, 0)),
        ],
        [rows_of(width), rows_of(width), rows_of(3 * width), full((8, width))],
        [
            shaped((rows, width), F32), shaped((rows, width), BF16),
            shaped((rows, 3 * width), BF16), shaped((8, width), F32),
        ],
        [pltpu.VMEM((rows_step, width), BF16)],
        8 * rows * width * width * 2,
        34e6,
        (gh, gres, n_attn, spread, table, w_out, qkv, probs),
    )


def projection_terms(x, grad_mixed, attended, grad_branch, vectors, here, which, got=None):
    rows, width = x.shape
    part = width // 2
    pieces = width // 32 // 8

    def product(refs):
        x_ref, gm_ref, att_ref, gb_ref, scr = refs
        step = pl.program_id(0)

        @pl.when(step < 3)
        def _():
            scr[...] = t_dot(x_ref[...], gm_ref[...])

        @pl.when(step == 3)
        def _():
            scr[...] = t_dot(att_ref[...], gb_ref[...])

    def give(here_s, x_ref, gm_ref, att_ref, gb_ref, vec_ref, out_ref, scr):
        product((x_ref, gm_ref, att_ref, gb_ref, scr))
        out_ref[:width, :] = scr[...].astype(BF16)
        out_ref[width:, :] = vec_ref[...].astype(BF16)

    def own(here_s, x_ref, gm_ref, att_ref, gb_ref, vec_ref, got_ref, send_a, keep_a, send_b, keep_b, scr, cut):
        product((x_ref, gm_ref, att_ref, gb_ref, scr))
        term = scr[...] + got_ref[:width, :].astype(F32)
        cut[...] = term.reshape(cut.shape)
        deal(cut, here_s, (send_a, keep_a, send_b, keep_b), 4, pieces)
        extra = (vec_ref[...] + got_ref[width:, :].astype(F32)).astype(BF16)
        send_a[8 * pieces] = extra
        keep_a[8 * pieces] = extra

    in_specs = [
        once((rows, width)),
        pl.BlockSpec((rows, part), lambda i, h: (0, h[which] * 3 + jnp.minimum(i, 2))),
        once((rows, width)),
        pl.BlockSpec((rows, part), lambda i, h: (0, h[which]), pipeline_mode=pl.Buffered(1)),
        pl.BlockSpec((8, part), lambda i, h: (0, i)),
    ]
    args = [x, grad_mixed, attended, grad_branch, vectors]
    flops = 4 * rows * width * width
    if got is None:
        return call(
            give, "proj_give", (4,), (here,), in_specs,
            pl.BlockSpec((width + 8, part), lambda i, *_: (0, i)),
            shaped((width + 8, 4 * part), BF16),
            [pltpu.VMEM((width, part), F32)], flops, 9e6, args,
        )
    return call(
        own, "proj_own", (4,), (here,),
        in_specs + [pl.BlockSpec((width + 8, part), lambda i, *_: (0, i))],
        [
            pl.BlockSpec((8 * pieces + extra, 8, part), lambda i, *_: (0, 0, i))
            for extra in (1, 1, 0, 0)
        ],
        [shaped((8 * pieces + extra, 8, 4 * part), BF16) for extra in (1, 1, 0, 0)],
        [pltpu.VMEM((width, part), F32), pltpu.VMEM((4, 2, 2, 2, pieces, 8, part), F32)],
        flops, 11e6, args + [got],
    )


def input_gradient(grad_mixed, w_qkv, grad_resid, rows_step):
    rows, width = grad_resid.shape

    def kernel(gm_ref, wq_ref, gr_ref, out_ref):
        out_ref[...] = (dot_t(gm_ref[...], wq_ref[...]) + gr_ref[...]).astype(BF16)

    return call(
        kernel, "input_grad", (rows // rows_step,), (),
        [
            pl.BlockSpec((rows_step, 3 * width), lambda i: (i, 0)),
            once((width, 3 * width)),
            pl.BlockSpec((rows_step, width), lambda i: (i, 0)),
        ],
        pl.BlockSpec((rows_step, width), lambda i: (i, 0)),
        shaped((rows, width), BF16), [], 6 * rows * width * width, 13e6,
        (grad_mixed, w_qkv, grad_resid),
    )


def add_call(kernel, name, here, args, outs):
    moved = sum(item.size * 2 for item in args) + sum(2 * a * b * c for a, b, c in outs)
    return call(
        kernel, name, (), (here,), [pl.BlockSpec(memory_space=pltpu.VMEM)] * len(args),
        [pl.BlockSpec(memory_space=pltpu.VMEM)] * len(outs),
        [shaped(shape, BF16) for shape in outs], [], moved // 4, moved, args,
    )


def add(left, right):
    return (left.astype(F32) + right.astype(F32)).astype(BF16)


def fold_second(keep_a, got_a, keep_b, got_b, here, pieces, extra):
    cols = keep_a.shape[2]

    def kernel(here_s, ka, ga, kb, gb, send_a, left_a, send_b, left_b):
        x, y = here_s[2], here_s[3]
        for z in range(4):
            at = pl.ds(z * pieces, pieces)

            def sum_of(keep, got, other):
                rows = pl.ds(z * 2 * pieces + other * pieces, pieces)
                return add(keep[rows], got[rows])

            send_a[at] = sum_of(ka, ga, 1 - y)
            left_a[at] = sum_of(ka, ga, y)
            send_b[at] = sum_of(kb, gb, 1 - x)
            left_b[at] = sum_of(kb, gb, x)
        if extra:
            total = add(ka[8 * pieces], ga[8 * pieces])
            send_a[4 * pieces] = total
            left_a[4 * pieces] = total

    a_shape, b_shape = (4 * pieces + extra, 8, cols), (4 * pieces, 8, cols)
    return add_call(
        kernel, "fold_second", here, (keep_a, got_a, keep_b, got_b), (a_shape, a_shape, b_shape, b_shape)
    )


def fold_third(keep_a, got_a, keep_b, got_b, here, pieces, extra):
    cols = keep_a.shape[2]

    def kernel(here_s, ka, ga, kb, gb, send, left):
        low = here_s[4]
        for high in range(2):
            for number, (keep, got) in enumerate(((ka, ga), (kb, gb))):
                at = pl.ds((high * 2 + number) * pieces, pieces)
                for out, pick in ((send, 1 - low), (left, low)):
                    rows = pl.ds((high * 2 + pick) * pieces, pieces)
                    out[at] = add(keep[rows], got[rows])
        if extra:
            total = add(ka[4 * pieces], ga[4 * pieces])
            send[4 * pieces] = total
            left[4 * pieces] = total

    shape = (4 * pieces + extra, 8, cols)
    return add_call(kernel, "fold_third", here, (keep_a, got_a, keep_b, got_b), (shape, shape))


def fold_fourth(keep, got, here, pieces, extra):
    cols = keep.shape[2]

    def kernel(here_s, keep_ref, got_ref, send, left):
        high = here_s[5]
        for out, pick in ((send, 1 - high), (left, high)):
            rows = pl.ds(pick * 2 * pieces, 2 * pieces)
            out[: 2 * pieces] = add(keep_ref[rows], got_ref[rows])
        if extra:
            total = add(keep_ref[4 * pieces], got_ref[4 * pieces])
            send[2 * pieces] = total
            left[2 * pieces] = total

    shape = (2 * pieces + extra, 8, cols)
    return add_call(kernel, "fold_fourth", here, (keep, got), (shape, shape))


def fold_last(keep, got, here, pieces, extra):
    cols = keep.shape[2]

    def kernel(here_s, keep_ref, got_ref, *outs):
        outs[0][...] = add(keep_ref[: 2 * pieces], got_ref[: 2 * pieces])
        if extra:
            outs[1][0] = add(keep_ref[2 * pieces], got_ref[2 * pieces])

    shapes = [(2 * pieces, 8, cols)] + [(1, 8, cols)] * extra
    return add_call(kernel, "fold_last", here, (keep, got), shapes)


def whole_block(mine, over_x, over_core, over_both, here, vectors=None):
    count, _, cols = mine.shape
    rows = 8 * count

    def pick(here_s, refs, core, side):
        me, gx, gc, gd = [item[...].astype(F32).reshape(rows, cols) for item in refs]
        same_core, same_side = here_s[0] == core, here_s[2] == side
        return jnp.where(
            same_core, jnp.where(same_side, me, gx), jnp.where(same_side, gc, gd)
        )

    def kernel(here_s, me, gx, gc, gd, *rest):
        outs = rest[1:] if vectors is not None else rest
        for core in range(2):
            for side in range(2):
                value = pick(here_s, (me, gx, gc, gd), core, side)
                at = slice(side * rows, (side + 1) * rows)
                if vectors is None:
                    outs[0][at, core * cols : (core + 1) * cols] = value
                else:
                    cut = cols // 4 * 3
                    outs[0][at, core * cut : (core + 1) * cut] = value[:, :cut]
                    outs[1][at, core * (cols - cut) : (core + 1) * (cols - cut)] = value[:, cut:]
        if vectors is not None:
            table = rest[0][0].astype(F32)
            wide = here_s[6]
            width = cols // 2
            small = width // 8
            left = pltpu.roll(table[:, :width], lax.rem(width - wide * small, width), 1)
            right = pltpu.roll(table[:, width:], lax.rem(width - wide * small, width), 1)
            for row in range(4):
                outs[2 + 2 * row][...] = left[row : row + 1, :small]
                outs[3 + 2 * row][...] = right[row : row + 1, :small]
            large = 2 * cols // 8
            turned = pltpu.roll(table, lax.rem(cols - lax.rem(wide, 4) * large, cols), 1)
            outs[10][...] = jnp.where(wide < 4, turned[4:5, :large], turned[5:6, :large])

    if vectors is None:
        shapes = [(2 * rows, 2 * cols)]
        args = (mine, over_x, over_core, over_both)
    else:
        cut = cols // 4 * 3
        shapes = [(2 * rows, 2 * cut), (2 * rows, 2 * (cols - cut))]
        shapes += [(1, cols // 16)] * 8 + [(1, cols // 4)]
        args = (mine, over_x, over_core, over_both, vectors)
    return call(
        kernel, "whole_block", (), (here,), [pl.BlockSpec(memory_space=pltpu.VMEM)] * len(args),
        [pl.BlockSpec(memory_space=pltpu.VMEM)] * len(shapes),
        [shaped(shape, F32) for shape in shapes], [], 1e6, 4e6, args,
    )


def swap(item, axis, step):
    count = lax.axis_size(axis)
    return lax.ppermute(item, axis, [(index, index ^ step) for index in range(count)])


def finish(dealt, here, pieces, extra):
    send_a, keep_a, send_b, keep_b = dealt
    got_a, got_b = swap(send_a, "narrow", 2), swap(send_b, "wide", 1)
    send_a, keep_a, send_b, keep_b = fold_second(keep_a, got_a, keep_b, got_b, here, pieces, extra)
    got_a, got_b = swap(send_a, "wide", 1), swap(send_b, "narrow", 2)
    send, keep = fold_third(keep_a, got_a, keep_b, got_b, here, pieces, extra)
    send, keep = fold_fourth(keep, swap(send, "wide", 2), here, pieces, extra)
    last = fold_last(keep, swap(send, "wide", 4), here, pieces, extra)
    mine = last[0]
    parts = (mine, swap(mine, "narrow", 2), swap(mine, "narrow", 1), swap(mine, "narrow", 3))
    return whole_block(*parts, here, *last[1:])


def regroup_rows(sent, bucket, wide_count, batches):
    span, width = sent.shape[1:]
    if wide_count == batches:
        got = lax.all_to_all(sent, "wide", split_axis=0, concat_axis=0, tiled=True)
        return got.reshape(batches * span, width)
    send = jnp.zeros((wide_count, span, width), sent.dtype).at[bucket].set(sent)
    got = lax.all_to_all(send, "wide", split_axis=0, concat_axis=0, tiled=True)
    marks = jnp.zeros((wide_count, 1), jnp.int32).at[bucket].set(1)
    filled = lax.all_to_all(marks, "wide", split_axis=0, concat_axis=0, tiled=True)[:, 0]
    place = jnp.where(filled > 0, jnp.cumsum(filled) - filled, batches)
    chosen = (
        jnp.zeros((batches,), jnp.int32)
        .at[place]
        .set(jnp.arange(wide_count, dtype=jnp.int32), mode="drop")
    )
    return got[chosen].reshape(batches * span, width)


def sum_anywhere(item, wide_count, narrow_count):
    blocks = item.astype(F32).reshape(wide_count, -1)
    extent = blocks.shape[1]
    padded = (extent + narrow_count - 1) // narrow_count * narrow_count
    blocks = jnp.pad(blocks, ((0, 0), (0, padded - extent))).reshape(-1)
    share = lax.psum_scatter(blocks, ("wide", "narrow"), scatter_dimension=0, tiled=True)
    whole = lax.all_gather(share.astype(BF16), "narrow", axis=0, tiled=True).astype(F32)
    return whole[:extent].reshape((item.shape[0] // wide_count,) + item.shape[1:])


def body(
    tokens, bucket, lengths, pairing, targets, w_qkv, bias_q, bias_v, w_out, bias_out,
    gain_attn, shift_attn, w_up, bias_up, w_down, bias_down, gain_ffn, shift_ffn,
):
    wide_count, narrow_count = lax.axis_size("wide"), lax.axis_size("narrow")
    batches = bucket.shape[0]
    rows, width = tokens.shape
    span = rows // batches
    paired = (wide_count, narrow_count) == (8, 4)
    wide, narrow = lax.axis_index("wide"), lax.axis_index("narrow")
    if paired:
        core = narrow % 2
        here = jnp.stack(
            [core, 1 - core, narrow // 2, wide % 2, wide // 2 % 2, wide // 4, wide, narrow]
        ).astype(jnp.int32)
    else:
        here = jnp.arange(8, dtype=jnp.int32)
    table = jnp.stack(
        [bias_q, bias_v, bias_out, gain_attn, shift_attn, bias_down, gain_ffn, shift_ffn]
    ).astype(F32)
    ordered = wide_count == batches
    slots = bucket if ordered else jnp.arange(batches, dtype=jnp.int32)

    qkv, probs, attended, n_attn, spread, sid = attention_forward(
        tokens, w_qkv, w_out, table, bucket, lengths, wide_count // batches, span, 2 * span
    )
    active, slope, hidden_t, sent, gres, grad_second, vec_ffn = feed_forward(
        n_attn, w_up, w_down, bias_up.reshape(1, -1), table, sid, slots, pairing, targets,
        batches, 512, 256,
    )
    encoded = regroup_rows(sent, bucket, wide_count, batches)
    ups = (grad_second, slope, hidden_t, w_up, w_down, here)
    down_sent = down_terms(active, grad_second, here, 1)
    up_sent, gh, bup_sent = up_terms(*ups, 1, 512, 256)
    if paired:
        down_dealt = down_terms(active, grad_second, here, 0, swap(down_sent, "narrow", 1))
        *up_dealt, gh, bup_kept = up_terms(*ups, 0, 512, 256, gh, swap(up_sent, "narrow", 1))
    else:
        down_kept = down_terms(active, grad_second, here, 0)
        up_kept, gh, bup_kept = up_terms(*ups, 0, 512, 256, gh)
    gr, gb, gm, vec_attn = attention_backward(
        gh, gres, n_attn, spread, table, w_out, qkv, probs, span, 2 * span
    )
    if paired:
        first_up = jnp.where(here[0] == 0, bup_kept, bup_sent)
        second_up = jnp.where(here[0] == 0, bup_sent, bup_kept)
    else:
        first_up, second_up = bup_kept, bup_sent
    vectors = jnp.concatenate(
        [
            vec_ffn[:2].reshape(1, -1),
            jnp.concatenate([vec_ffn[2:3], vec_attn[0:1]], axis=1),
            vec_attn[1:5].reshape(2, -1),
            first_up,
            second_up,
            jnp.zeros((2, 2 * width), F32),
        ],
        axis=0,
    )
    projections = (tokens, gm, attended, gb, vectors, here)
    proj_sent = projection_terms(*projections, 1)
    grad_tokens = input_gradient(gm, w_qkv, gr, 2 * span)
    if paired:
        proj_dealt = projection_terms(*projections, 0, swap(proj_sent, "narrow", 1))
        (grad_w_down,) = finish(down_dealt, here, 12, 0)
        (grad_w_up,) = finish(up_dealt, here, 3, 0)
        grad_w_qkv, grad_w_out, *small = finish(proj_dealt, here, 3, 1)
        small = [item.reshape(-1) for item in small]
    else:
        proj_kept = projection_terms(*projections, 0)
        total = partial(sum_anywhere, wide_count=wide_count, narrow_count=narrow_count)
        cut = width // 2 * 3
        grad_w_down = total(jnp.concatenate([down_kept, down_sent], axis=1))
        grad_w_up = total(jnp.concatenate([up_kept, up_sent], axis=1))
        grad_w_qkv = total(jnp.concatenate([proj_kept[:width, :cut], proj_sent[:width, :cut]], axis=1))
        grad_w_out = total(jnp.concatenate([proj_kept[:width, cut:], proj_sent[:width, cut:]], axis=1))
        small = [total(item) for item in vectors[:4].reshape(8, width)]
        small.append(total(vectors[4:6].reshape(-1)))
    gain_out, shift_out, b_down, b_q, b_v, b_out, g_attn, s_attn, b_up = small
    return (
        encoded, grad_tokens, grad_w_qkv, b_q, b_v, grad_w_out, b_out, g_attn, s_attn,
        grad_w_up, b_up, grad_w_down, b_down, gain_out, shift_out,
    )


def solution(mesh):
    split = P(("wide", "narrow"))
    in_specs = (
        P(("wide", "narrow"), None), split, split, P(("wide", "narrow"), None), split,
    ) + (P(),) * 13
    out_specs = (
        P(("wide", "narrow"), None), P(("wide", "narrow"), None),
        P("wide", None), P("wide"), P("wide"), P("wide", None), P("wide"), P("wide"), P("wide"),
        P("wide", None), P("wide"), P("wide", None), P("wide"), P("wide"), P("wide"),
    )
    return jax.shard_map(body, mesh=mesh, in_specs=in_specs, out_specs=out_specs, check_vma=False)
```

```python
from functools import partial

import jax
import jax.numpy as jnp
from jax import lax
from jax.experimental import pallas as pl
from jax.experimental.pallas import tpu as pltpu
from jax.sharding import PartitionSpec as P

HDIM = 64
KTOP = 12
NORM_EPS = 1e-12
COS_EPS = 1e-06
MASKED = -1000000000.0
LOSS_SCALE = 1024.0
F32 = jnp.float32
BF16 = jnp.bfloat16
LANES = 128
MIB = 1024 * 1024
LARGE = 100000
COST = 0.05
ERF_P = 0.3275911
ERF_A = (0.254829592, -0.284496736, 1.421413741, -1.453152027, 1.061405429)
HALF_ROOT = 0.7071067811865476
PEAK = 0.3989422804014327
ROW_BQ, ROW_BV, ROW_BO, ROW_GA, ROW_SA, ROW_BD, ROW_GF, ROW_SF, ROW_BU = range(9)


def dot(left, right):
    return jnp.dot(left, right, preferred_element_type=F32)


def dot_t(left, right):
    return lax.dot_general(left, right, (((1,), (1,)), ((), ())), preferred_element_type=F32)


def t_dot(left, right):
    return lax.dot_general(left, right, (((0,), (0,)), ((), ())), preferred_element_type=F32)


def full(shape):
    return pl.BlockSpec(shape, lambda *_: (0,) * len(shape))


def once(shape):
    return pl.BlockSpec(shape, lambda *_: (0,) * len(shape), pipeline_mode=pl.Buffered(1))


def large(item):
    return item.size >= LARGE


def shaped(shape, dtype):
    return jax.ShapeDtypeStruct(shape, dtype)


def call(
    kernel, name, grid, prefetch, in_specs, out_specs, out_shape, scratch, flops, moved, args, vmem=24, free=0, loose=0
):
    single = not isinstance(out_shape, list)
    shapes = [out_shape] if single else out_shape
    shapes = [
        pltpu.HBM(item.shape, item.dtype) if large(item) and number >= loose else item
        for number, item in enumerate(shapes)
    ]
    out_shape = shapes[0] if single else shapes
    args = [
        pltpu.with_memory_space_constraint(item, pltpu.HBM) if large(item) and number < len(args) - free else item
        for number, item in enumerate(args)
    ]
    return pl.pallas_call(
        kernel,
        grid_spec=pltpu.PrefetchScalarGridSpec(
            num_scalar_prefetch=len(prefetch),
            grid=grid,
            in_specs=in_specs,
            out_specs=out_specs,
            scratch_shapes=scratch,
        ),
        out_shape=out_shape,
        compiler_params=pltpu.CompilerParams(
            dimension_semantics=("arbitrary",) * len(grid), vmem_limit_bytes=vmem * MIB
        ),
        cost_estimate=pl.CostEstimate(flops=int(flops * COST), bytes_accessed=int(moved * COST), transcendentals=0),
        name=name,
    )(*[pltpu.with_memory_space_constraint(item, pltpu.HBM) for item in prefetch], *args)


def norm_forward(values):
    center = values - jnp.mean(values, axis=-1, keepdims=True)
    spread = lax.rsqrt(jnp.mean(center * center, axis=-1, keepdims=True) + NORM_EPS)
    return center * spread, spread


def norm_backward(grad_out, normed, spread, gain):
    scaled = grad_out * gain
    mean_scaled = jnp.mean(scaled, axis=-1, keepdims=True)
    mean_product = jnp.mean(scaled * normed, axis=-1, keepdims=True)
    return spread * (scaled - mean_scaled - normed * mean_product)


def column_sum(values):
    return jnp.sum(values, axis=0, keepdims=True)


def gelu_pair(v):
    t = 1.0 / (1.0 + (ERF_P * HALF_ROOT) * jnp.abs(v))
    bell = jnp.exp(-0.5 * (v * v))
    poly = 0.5 * ERF_A[4]
    for coef in ERF_A[3::-1]:
        poly = poly * t + 0.5 * coef
    tail = poly * t * bell
    phi = jnp.where(v > 0, 1.0 - tail, tail)
    return v * phi, phi + v * (PEAK * bell)


def head_masks():
    lane = lax.broadcasted_iota(jnp.int32, (1, LANES), 1)
    low = (lane < HDIM).astype(F32)
    return low.astype(BF16), (1.0 - low).astype(BF16), lane < HDIM


def sentence_count(bucket_s, number, group_size):
    kind = bucket_s[number]
    if group_size > 1:
        kind = kind // group_size
    return jnp.maximum(1, lax.shift_right_logical(jnp.int32(KTOP), kind))


def row_sentences(batch, bucket_s, lengths_s, group_size, batches, sent, span):
    start = jnp.int32(0)
    for other in range(batches):
        start += jnp.where(other < batch, sentence_count(bucket_s, other, group_size), 0)
    count = sentence_count(bucket_s, batch, group_size)
    lane = lax.broadcasted_iota(jnp.int32, (8, span), 1)
    row = lax.broadcasted_iota(jnp.int32, (span, span), 0)
    passed_lane = jnp.zeros((8, span), jnp.int32)
    passed_row = jnp.zeros((span, span), jnp.int32)
    finish = jnp.int32(0)
    for number in range(KTOP):
        finish += lengths_s[jnp.minimum(start + number, sent - 1)]
        bound = jnp.where(number < count, finish, span)
        passed_lane += (lane >= bound).astype(jnp.int32)
        passed_row += (row >= bound).astype(jnp.int32)
    sid_lane = jnp.where(passed_lane < count, start + passed_lane, -1)
    sid_row = jnp.where(passed_row < count, start + passed_row, -1)
    return sid_lane, sid_row


def vector_table(vectors, width):
    def kernel(*refs):
        out_ref = refs[-1]
        at = 0
        for ref in refs[:-1]:
            for part in range(ref.shape[0] // width):
                out_ref[at : at + 1, :] = ref[part * width : (part + 1) * width].astype(F32).reshape(1, width)
                at += 1

    rows = sum(item.shape[0] for item in vectors) // width
    return pl.pallas_call(
        kernel,
        grid=(1,),
        in_specs=[full(item.shape) for item in vectors],
        out_specs=full((rows, width)),
        out_shape=shaped((rows, width), F32),
        compiler_params=pltpu.CompilerParams(vmem_limit_bytes=4 * MIB),
        name="vector_table",
    )(*[pltpu.with_memory_space_constraint(item, pltpu.HBM) for item in vectors])


def attention_forward(x, w_qkv, w_out, table, bucket, lengths, group_size, span, rows_step):
    rows, width = x.shape
    batches = rows // span
    pairs = width // LANES
    sent = lengths.shape[0]
    per_step = rows_step // span

    def kernel(bucket_s, lengths_s, x_ref, wq_ref, wo_ref, tab_ref, qkv_ref, p_ref, att_ref, n_ref, s_ref, sid_ref):
        step = pl.program_id(0)
        low_b, high_b, low_m = head_masks()
        x_in = x_ref[...]
        mixed = dot(x_in, wq_ref[:, :width]) + tab_ref[ROW_BQ : ROW_BQ + 1, :]
        qkv_ref[:, :width] = (mixed * 0.125).astype(BF16)
        qkv_ref[:, width : 2 * width] = dot(x_in, wq_ref[:, width : 2 * width]).astype(BF16)
        mixed = dot(x_in, wq_ref[:, 2 * width :]) + tab_ref[ROW_BV : ROW_BV + 1, :]
        qkv_ref[:, 2 * width :] = mixed.astype(BF16)
        eye = lax.broadcasted_iota(jnp.int32, (span, span), 0) == lax.broadcasted_iota(
            jnp.int32, (span, span), 1
        )
        for inner in range(per_step):
            sid_lane, sid_row = row_sentences(
                step * per_step + inner, bucket_s, lengths_s, group_size, batches, sent, span
            )
            sid_ref[inner] = sid_lane
            same = (sid_row == sid_lane[0:1, :]) & (sid_row >= 0)
            bias = jnp.where(same | eye, 0.0, MASKED)
            bias = jnp.concatenate([bias, bias], axis=0)
            base = slice(inner * span, (inner + 1) * span)
            for pair in range(pairs):
                cols = slice(pair * LANES, (pair + 1) * LANES)
                q = qkv_ref[base, cols]
                k = qkv_ref[base, width + pair * LANES : width + (pair + 1) * LANES]
                v = qkv_ref[base, 2 * width + pair * LANES : 2 * width + (pair + 1) * LANES]
                both = jnp.concatenate([q * low_b, q * high_b], axis=0)
                logits = dot_t(both, k) + bias
                raised = jnp.exp(logits - jnp.max(logits, axis=-1, keepdims=True))
                total = jnp.sum(raised, axis=-1, keepdims=True)
                probs = (raised * (1.0 / total)).astype(BF16)
                p_ref[inner, pair] = probs
                mix = dot(probs, v)
                att_ref[base, cols] = jnp.where(low_m, mix[:span], mix[span:]).astype(BF16)
        branch = dot(att_ref[...], wo_ref[...]) + tab_ref[ROW_BO : ROW_BO + 1, :]
        normed, spread = norm_forward(x_in.astype(F32) + branch)
        n_ref[...] = normed
        s_ref[...] = jnp.broadcast_to(spread, (rows_step, LANES))

    return call(
        kernel,
        "attn_fwd",
        (rows // rows_step,),
        (bucket, lengths),
        [
            pl.BlockSpec((rows_step, width), lambda i, *_: (i, 0)),
            once((width, 3 * width)),
            once((width, width)),
            once(table.shape),
        ],
        [
            pl.BlockSpec((rows_step, 3 * width), lambda i, *_: (i, 0)),
            pl.BlockSpec((per_step, pairs, 2 * span, span), lambda i, *_: (i, 0, 0, 0)),
            pl.BlockSpec((rows_step, width), lambda i, *_: (i, 0)),
            pl.BlockSpec((rows_step, width), lambda i, *_: (i, 0)),
            pl.BlockSpec((rows_step, LANES), lambda i, *_: (i, 0)),
            pl.BlockSpec((per_step, 8, span), lambda i, *_: (i, 0, 0)),
        ],
        [
            shaped((rows, 3 * width), BF16),
            shaped((batches, pairs, 2 * span, span), BF16),
            shaped((rows, width), BF16),
            shaped((rows, width), F32),
            shaped((rows, LANES), F32),
            shaped((batches, 8, span), jnp.int32),
        ],
        [],
        8 * rows * width * width * 2,
        30e6,
        (x, w_qkv, w_out, table),
        26,
    )


def feed_forward(n_attn, w_up, w_down, table, sid, slots, pairing, targets, slot_count, block):
    rows, width = n_attn.shape
    ff = w_up.shape[1]
    batches, _, span = sid.shape
    pair_count = targets.shape[0]
    side = -(-pair_count // 8) * 8
    chunk = width
    steps = ff // chunk
    blocks = rows // block
    per_block = block // span

    def kernel(
        slots_s, pairing_s, targets_s, n_ref, wu_ref, wd_ref, tab_ref, sid_ref,
        act_ref, dg_ref, ht_ref, enc_ref, gres_ref, gsl_ref, vec_ref, low_scr, acc_scr, spread_scr,
    ):
        step = pl.program_id(0)
        gain = tab_ref[ROW_GA : ROW_GA + 1, :]
        shift = tab_ref[ROW_SA : ROW_SA + 1, :]

        @pl.when(step == 0)
        def _():
            hidden = (n_ref[...] * gain + shift).astype(BF16)
            low_scr[...] = hidden
            ht_ref[...] = hidden.T
            acc_scr[...] = jnp.zeros_like(acc_scr)

        for number in range(blocks):
            base = slice(number * block, (number + 1) * block)
            inner = dot(low_scr[base, :], wu_ref[...]) + tab_ref[pl.ds(ROW_BU + step, 1), :]
            active, slope = gelu_pair(inner)
            active = active.astype(BF16)
            act_ref[base, :] = active
            dg_ref[base, :] = slope.astype(BF16)
            acc_scr[base, :] += dot(active, wd_ref[...])

        @pl.when(step == steps - 1)
        def _():
            gain_out = tab_ref[ROW_GF : ROW_GF + 1, :]
            shift_out = tab_ref[ROW_SF : ROW_SF + 1, :]
            slot = lax.broadcasted_iota(jnp.int32, (2 * side, span), 0)
            wanted = jnp.full((2 * side, span), -2, jnp.int32)
            goal = jnp.zeros((side, LANES), F32)
            goal_slot = lax.broadcasted_iota(jnp.int32, (side, LANES), 0)
            for number in range(pair_count):
                wanted = jnp.where(slot == number, pairing_s[0, 2 * number], wanted)
                wanted = jnp.where(slot == side + number, pairing_s[0, 2 * number + 1], wanted)
                goal = jnp.where(goal_slot == number, targets_s[number], goal)
            members = [
                (sid_ref[number][0:1, :] == wanted).astype(F32) for number in range(batches)
            ]
            sizes = jnp.zeros((2 * side, 1), F32)
            for member in members:
                sizes += jnp.sum(member, axis=-1, keepdims=True)
            share = 1.0 / jnp.maximum(sizes, 1.0)
            picks = [
                jnp.concatenate(members[number * per_block : (number + 1) * per_block], axis=1).astype(BF16)
                for number in range(blocks)
            ]
            ones = jnp.ones((2 * side, LANES), BF16)
            pooled = jnp.zeros((2 * side, width), F32)
            for number in range(blocks):
                base = slice(number * block, (number + 1) * block)
                resid = (
                    n_ref[base, :] * gain + shift + acc_scr[base, :] + tab_ref[ROW_BD : ROW_BD + 1, :]
                )
                normed, spread = norm_forward(resid)
                acc_scr[base, :] = normed
                spread_scr[base, :] = jnp.broadcast_to(spread, (block, LANES))
                out = normed * gain_out + shift_out
                high = out.astype(BF16)
                rest = (out - high.astype(F32)).astype(BF16)
                pooled += dot(picks[number], high) + dot(picks[number], rest)
                valid = t_dot(picks[number], ones)
                for col in range(width // LANES):
                    cols = slice(col * LANES, (col + 1) * LANES)
                    kept = (out[:, cols] * valid).astype(BF16)
                    for inner in range(per_block):
                        enc_ref[slots_s[number * per_block + inner], :, cols] = kept[
                            inner * span : (inner + 1) * span
                        ]
            pooled = pooled * share
            first, partner = pooled[:side], pooled[side:]
            cross = jnp.sum(first * partner, axis=-1, keepdims=True)
            scale_first = lax.rsqrt(jnp.sum(first * first, axis=-1, keepdims=True) + COS_EPS)
            scale_partner = lax.rsqrt(jnp.sum(partner * partner, axis=-1, keepdims=True) + COS_EPS)
            cosine = cross * scale_first * scale_partner
            factor = 2.0 * LOSS_SCALE * (cosine - goal[:, :1])
            both_scales = factor * scale_first * scale_partner
            grad_first = both_scales * partner - (factor * cosine * scale_first * scale_first) * first
            grad_partner = (
                both_scales * first - (factor * cosine * scale_partner * scale_partner) * partner
            )
            grad_home = jnp.concatenate([grad_first, grad_partner], axis=0) * share
            high = grad_home.astype(BF16)
            rest = (grad_home - high.astype(F32)).astype(BF16)
            vec_ref[...] = jnp.zeros_like(vec_ref)
            for number in range(blocks):
                base = slice(number * block, (number + 1) * block)
                grad_out = t_dot(picks[number], high) + t_dot(picks[number], rest)
                normed = acc_scr[base, :]
                resid = norm_backward(grad_out, normed, spread_scr[base, :1], gain_out)
                gres_ref[base, :] = resid
                low = resid.astype(BF16)
                gsl_ref[base, :] = low
                vec_ref[0:1, :] += column_sum(grad_out * normed)
                vec_ref[1:2, :] += column_sum(grad_out)
                vec_ref[2:3, :] += column_sum(low.astype(F32))

    return call(
        kernel,
        "ffn_fwd",
        (steps,),
        (slots, pairing, targets),
        [
            once((rows, width)),
            pl.BlockSpec((width, chunk), lambda j, *_: (0, j)),
            pl.BlockSpec((chunk, width), lambda j, *_: (j, 0)),
            once(table.shape),
            once((batches, 8, span)),
        ],
        [
            pl.BlockSpec((rows, chunk), lambda j, *_: (0, j)),
            pl.BlockSpec((rows, chunk), lambda j, *_: (0, j)),
            once((width, rows)),
            once((slot_count, span, width)),
            once((rows, width)),
            once((rows, width)),
            once((8, width)),
        ],
        [
            shaped((rows, ff), BF16),
            shaped((rows, ff), BF16),
            shaped((width, rows), BF16),
            shaped((slot_count, span, width), BF16),
            shaped((rows, width), F32),
            shaped((rows, width), BF16),
            shaped((8, width), F32),
        ],
        [
            pltpu.VMEM((rows, width), BF16),
            pltpu.VMEM((rows, width), F32),
            pltpu.VMEM((rows, LANES), F32),
        ],
        8 * rows * width * ff,
        40e6,
        (n_attn, w_up, w_down, table, sid),
        44,
    )


def deal(scratch, here_s, outs, z_count, pieces, folds=1):
    send_a, keep_a, send_b, keep_b = outs
    x, y = here_s[2], here_s[3]
    cols = scratch.shape[-1]
    for z in range(z_count):
        for other in range(2):
            at = pl.ds((z * 2 + other) * pieces, pieces)
            for fold in range(folds):
                part = pl.ds(fold * pieces, pieces)
                to = slice(fold * cols, (fold + 1) * cols)
                send_a[at, :, to] = scratch[z, other, 1 - x, 0, part].astype(BF16)
                keep_a[at, :, to] = scratch[z, other, x, 0, part].astype(BF16)
                send_b[at, :, to] = scratch[z, 1 - y, other, 1, part].astype(BF16)
                keep_b[at, :, to] = scratch[z, y, other, 1, part].astype(BF16)


def down_terms(active, grad_second, here, which, got=None):
    rows, ff = active.shape
    width = grad_second.shape[1]
    half = width // 2
    steps = 4
    tall = ff // steps
    pieces = width // 32 // 8
    folds = ff // width

    def give(here_s, act_ref, gs_ref, out_ref):
        out_ref[...] = t_dot(act_ref[...], gs_ref[...]).astype(BF16)

    def own(here_s, act_ref, gs_ref, got_ref, *rest):
        outs, scratch = rest[:4], rest[4]
        term = t_dot(act_ref[...], gs_ref[...]) + got_ref[...].astype(F32)
        scratch[...] = term.reshape(scratch.shape)
        deal(scratch, here_s, outs, 1, pieces, folds)

    in_specs = [
        pl.BlockSpec((rows, tall), lambda i, here_s: (0, i)),
        pl.BlockSpec((rows, half), lambda i, here_s: (0, here_s[which]), pipeline_mode=pl.Buffered(1)),
    ]
    flops = 2 * rows * ff * half
    if got is None:
        return call(
            give, "down_give", (steps,), (here,), in_specs,
            pl.BlockSpec((tall, half), lambda i, *_: (i, 0)),
            shaped((ff, half), BF16), [], flops, 9e6, (active, grad_second), 20, 0, 1,
        )
    block = (2 * pieces, 8, folds * half)
    return call(
        own, "down_own", (steps,), (here,),
        in_specs + [pl.BlockSpec((tall, half), lambda i, *_: (i, 0))],
        [pl.BlockSpec(block, lambda i, *_: (i, 0, 0))] * 4,
        [shaped((8 * pieces, 8, folds * half), BF16)] * 4,
        [pltpu.VMEM((1, 2, 2, 2, folds * pieces, 8, half), F32)],
        flops, 11e6, (active, grad_second, got), 24, 1, 4,
    )


def up_terms(grad_second, slope, hidden_t, w_down, here, which, got=None):
    rows, width = grad_second.shape
    ff = w_down.shape[0]
    half = ff // 2
    chunk = width
    steps = half // chunk
    block = rows // 4
    pieces = width // 32 // 8

    def kernel(here_s, gs_ref, dg_ref, ht_ref, wd_ref, *refs):
        if got is not None:
            got_ref, refs = refs[0], refs[1:]
            outs, refs = refs[:4], refs[4:]
        else:
            out_ref, refs = refs[0], refs[1:]
        gi_ref, bu_ref = refs[:2]
        sums = jnp.zeros((1, chunk), F32)
        for number in range(rows // block):
            base = slice(number * block, (number + 1) * block)
            grad_active = dot_t(gs_ref[base, :], wd_ref[...])
            low = (grad_active * dg_ref[base, :].astype(F32)).astype(BF16)
            gi_ref[base, :] = low
            sums += column_sum(low.astype(F32))
        bu_ref[...] = sums
        term = dot(ht_ref[...], gi_ref[...])
        if got is None:
            out_ref[...] = term.astype(BF16)
        else:
            scratch = refs[2]
            term += got_ref[...].astype(F32)
            scratch[...] = term.reshape(scratch.shape)
            deal(scratch, here_s, outs, 4, pieces)

    def col(i, here_s):
        return here_s[which] * steps + i

    in_specs = [
        once((rows, width)),
        pl.BlockSpec((rows, chunk), lambda i, h: (0, col(i, h))),
        once((width, rows)),
        pl.BlockSpec((chunk, width), lambda i, h: (col(i, h), 0)),
    ]
    args = [grad_second, slope, hidden_t, w_down]
    scratch = []
    if got is None:
        out_specs = [pl.BlockSpec((width, chunk), lambda i, *_: (0, i))]
        out_shape = [shaped((width, half), BF16)]
    else:
        in_specs.append(pl.BlockSpec((width, chunk), lambda i, *_: (0, i)))
        args.append(got)
        out_specs = [pl.BlockSpec((8 * pieces, 8, chunk), lambda i, *_: (0, 0, i))] * 4
        out_shape = [shaped((8 * pieces, 8, half), BF16)] * 4
        scratch.append(pltpu.VMEM((4, 2, 2, 2, pieces, 8, chunk), F32))
    return call(
        kernel, "up_give" if got is None else "up_own", (steps,), (here,), in_specs,
        out_specs
        + [
            pl.BlockSpec((rows, chunk), lambda i, *_: (0, i)),
            pl.BlockSpec((1, chunk), lambda i, *_: (0, i)),
        ],
        out_shape + [shaped((rows, half), BF16), shaped((1, half), F32)],
        scratch, 4 * rows * width * half, 16e6, args, 34, 0 if got is None else 1, 1 if got is None else 4,
    )


def hidden_gradient(grad_inner, w_up, here, which):
    rows, half = grad_inner.shape
    width = w_up.shape[0]
    block = rows // 2

    def kernel(here_s, gi_ref, wu_ref, out_ref):
        out_ref[...] = dot_t(gi_ref[...], wu_ref[...])

    return call(
        kernel, "hidden_grad", (rows // block,), (here,),
        [
            pl.BlockSpec((block, half), lambda i, h: (i, 0)),
            pl.BlockSpec((width, half), lambda i, h: (0, h[which]), pipeline_mode=pl.Buffered(1)),
        ],
        pl.BlockSpec((block, width), lambda i, h: (i, 0)),
        shaped((rows, width), F32), [], 2 * rows * width * half, 9e6, (grad_inner, w_up), 16,
    )


def attention_backward(gh, gres, grad_inner, w_up, n_attn, spread, table, w_out, qkv, probs, here, which, span, rows_step):
    rows, width = gh.shape
    half = grad_inner.shape[1]
    pairs = width // LANES
    per_step = rows_step // span

    def kernel(here_s, gh_ref, gres_ref, gi_ref, wu_ref, n_ref, s_ref, tab_ref, wo_ref, qkv_ref, p_ref, gr_ref, gb_ref, gm_ref, vec_ref, ga_scr):
        step = pl.program_id(0)
        low_b, high_b, low_m = head_masks()

        @pl.when(step == 0)
        def _():
            vec_ref[...] = jnp.zeros_like(vec_ref)

        normed = n_ref[...]
        grad_hidden = dot_t(gi_ref[...], wu_ref[...]) + gh_ref[...] + gres_ref[...]
        resid = norm_backward(grad_hidden, normed, s_ref[:, :1], tab_ref[ROW_GA : ROW_GA + 1, :])
        gr_ref[...] = resid
        low = resid.astype(BF16)
        gb_ref[...] = low
        vec_ref[2:3, :] += column_sum(low.astype(F32))
        vec_ref[3:4, :] += column_sum(grad_hidden * normed)
        vec_ref[4:5, :] += column_sum(grad_hidden)
        ga_scr[...] = dot_t(low, wo_ref[...]).astype(BF16)
        for inner in range(per_step):
            base = slice(inner * span, (inner + 1) * span)
            for pair in range(pairs):
                cols = slice(pair * LANES, (pair + 1) * LANES)
                k_cols = slice(width + pair * LANES, width + (pair + 1) * LANES)
                v_cols = slice(2 * width + pair * LANES, 2 * width + (pair + 1) * LANES)
                q, k, v = qkv_ref[base, cols], qkv_ref[base, k_cols], qkv_ref[base, v_cols]
                grad = ga_scr[base, cols]
                grads = jnp.concatenate([grad * low_b, grad * high_b], axis=0)
                both = jnp.concatenate([q * low_b, q * high_b], axis=0)
                weights = p_ref[inner, pair]
                wide = weights.astype(F32)
                grad_probs = dot_t(grads, v)
                balance = jnp.sum(wide * grad_probs, axis=-1, keepdims=True)
                grad_logits = (wide * (grad_probs - balance)).astype(BF16)
                mix = dot(grad_logits, k)
                grad_q = jnp.where(low_m, mix[:span], mix[span:]).astype(BF16) * jnp.bfloat16(0.125)
                grad_v = t_dot(weights, grads).astype(BF16)
                gm_ref[base, cols] = grad_q
                gm_ref[base, k_cols] = t_dot(grad_logits, both).astype(BF16)
                gm_ref[base, v_cols] = grad_v
                vec_ref[0:1, cols] += column_sum(grad_q.astype(F32))
                vec_ref[1:2, cols] += column_sum(grad_v.astype(F32))

    def rows_of(cols):
        return pl.BlockSpec((rows_step, cols), lambda i, h: (i, 0))

    return call(
        kernel,
        "attn_bwd",
        (rows // rows_step,),
        (here,),
        [
            rows_of(width), rows_of(width), rows_of(half),
            pl.BlockSpec((width, half), lambda i, h: (0, h[which]), pipeline_mode=pl.Buffered(1)),
            rows_of(width), rows_of(LANES),
            once(table.shape), once((width, width)), rows_of(3 * width),
            pl.BlockSpec((per_step, pairs, 2 * span, span), lambda i, h: (i, 0, 0, 0)),
        ],
        [rows_of(width), rows_of(width), rows_of(3 * width), full((8, width))],
        [
            shaped((rows, width), F32), shaped((rows, width), BF16),
            shaped((rows, 3 * width), BF16), shaped((8, width), F32),
        ],
        [pltpu.VMEM((rows_step, width), BF16)],
        8 * rows * width * width * 2,
        40e6,
        (gh, gres, grad_inner, w_up, n_attn, spread, table, w_out, qkv, probs),
        34,
    )


def projection_terms(x, grad_mixed, attended, grad_branch, vectors, here, which, got=None):
    rows, width = x.shape
    part = width // 2
    pieces = width // 32 // 8

    def product(x_ref, gm_ref, att_ref, gb_ref, scr):
        step = pl.program_id(0)

        @pl.when(step < 3)
        def _():
            scr[...] = t_dot(x_ref[...], gm_ref[...])

        @pl.when(step == 3)
        def _():
            scr[...] = t_dot(att_ref[...], gb_ref[...])

    def small(here_s, ffn_ref, attn_ref, sent_ref, kept_ref, store):
        first = here_s[0] == 0
        for step in range(4):

            @pl.when(pl.program_id(0) == step)
            def _():
                side, at = step // 2, slice(step % 2 * part, (step % 2 + 1) * part)
                wide = slice(step * part, (step + 1) * part)
                rows_of = (
                    (ffn_ref[0:1, at], ffn_ref[2:3, at], attn_ref[1:2, at], attn_ref[3:4, at]),
                    (ffn_ref[1:2, at], attn_ref[0:1, at], attn_ref[2:3, at], attn_ref[4:5, at]),
                )[side]
                sent, kept = sent_ref[:, wide], kept_ref[:, wide]
                ups = (jnp.where(first, kept, sent), jnp.where(first, sent, kept))
                store(jnp.concatenate(rows_of + ups + (jnp.zeros((2, part), F32),), axis=0))

    def give(here_s, x_ref, gm_ref, att_ref, gb_ref, ffn_ref, attn_ref, sent_ref, kept_ref, out_ref, scr):
        product(x_ref, gm_ref, att_ref, gb_ref, scr)
        out_ref[:width, :] = scr[...].astype(BF16)

        def store(value):
            out_ref[width:, :] = value.astype(BF16)

        small(here_s, ffn_ref, attn_ref, sent_ref, kept_ref, store)

    def own(
        here_s, x_ref, gm_ref, att_ref, gb_ref, ffn_ref, attn_ref, sent_ref, kept_ref, got_ref,
        send_a, keep_a, send_b, keep_b, scr, cut,
    ):
        product(x_ref, gm_ref, att_ref, gb_ref, scr)
        term = scr[...] + got_ref[:width, :].astype(F32)
        cut[...] = term.reshape(cut.shape)
        deal(cut, here_s, (send_a, keep_a, send_b, keep_b), 4, pieces)

        def store(value):
            extra = (value + got_ref[width:, :].astype(F32)).astype(BF16)
            send_a[8 * pieces] = extra
            keep_a[8 * pieces] = extra

        small(here_s, ffn_ref, attn_ref, sent_ref, kept_ref, store)

    in_specs = [
        once((rows, width)),
        pl.BlockSpec((rows, part), lambda i, h: (0, h[which] * 3 + jnp.minimum(i, 2))),
        once((rows, width)),
        pl.BlockSpec((rows, part), lambda i, h: (0, h[which]), pipeline_mode=pl.Buffered(1)),
    ] + [once(item.shape) for item in vectors]
    args = [x, grad_mixed, attended, grad_branch, *vectors]
    flops = 4 * rows * width * width
    if got is None:
        return call(
            give, "proj_give", (4,), (here,), in_specs,
            pl.BlockSpec((width + 8, part), lambda i, *_: (0, i)),
            shaped((width + 8, 4 * part), BF16),
            [pltpu.VMEM((width, part), F32)], flops, 9e6, args, 20, 0, 1,
        )
    return call(
        own, "proj_own", (4,), (here,),
        in_specs + [pl.BlockSpec((width + 8, part), lambda i, *_: (0, i))],
        [
            pl.BlockSpec((8 * pieces + extra, 8, part), lambda i, *_: (0, 0, i))
            for extra in (1, 1, 0, 0)
        ],
        [shaped((8 * pieces + extra, 8, 4 * part), BF16) for extra in (1, 1, 0, 0)],
        [pltpu.VMEM((width, part), F32), pltpu.VMEM((4, 2, 2, 2, pieces, 8, part), F32)],
        flops, 11e6, args + [got], 24, 1, 4,
    )


def input_gradient(grad_mixed, w_qkv, grad_resid, rows_step):
    rows, width = grad_resid.shape

    def kernel(gm_ref, wq_ref, gr_ref, out_ref):
        out_ref[...] = (dot_t(gm_ref[...], wq_ref[...]) + gr_ref[...]).astype(BF16)

    return call(
        kernel, "input_grad", (rows // rows_step,), (),
        [
            pl.BlockSpec((rows_step, 3 * width), lambda i: (i, 0)),
            once((width, 3 * width)),
            pl.BlockSpec((rows_step, width), lambda i: (i, 0)),
        ],
        pl.BlockSpec((rows_step, width), lambda i: (i, 0)),
        shaped((rows, width), BF16), [], 6 * rows * width * width, 13e6,
        (grad_mixed, w_qkv, grad_resid), 20,
    )


def copied(item, here, block):
    rows, width = item.shape

    def kernel(here_s, in_ref, out_ref):
        out_ref[...] = in_ref[...]

    spec = pl.BlockSpec((block, width), lambda i, *_: (i, 0))
    return call(
        kernel, "copied", (rows // block,), (here,), [spec], spec,
        shaped((rows, width), item.dtype), [], 1, 3e6, (item,), 4,
    )


def small_call(kernel, name, here, args, outs, vmem=12):
    return pl.pallas_call(
        kernel,
        in_specs=[pl.BlockSpec(memory_space=pltpu.SMEM)]
        + [pl.BlockSpec(memory_space=pltpu.VMEM)] * len(args),
        out_specs=[pl.BlockSpec(memory_space=pltpu.VMEM)] * len(outs),
        out_shape=outs,
        compiler_params=pltpu.CompilerParams(vmem_limit_bytes=vmem * MIB),
        cost_estimate=pl.CostEstimate(flops=int(1e6 * COST), bytes_accessed=int(4e6 * COST), transcendentals=0),
        name=name,
    )(here, *args)


def add(left, right):
    return (left.astype(F32) + right.astype(F32)).astype(BF16)


def fold_second(keep_a, got_a, keep_b, got_b, here, pieces, extra):
    cols = keep_a.shape[2]

    def kernel(here_s, ka, ga, kb, gb, send_a, left_a, send_b, left_b):
        x, y = here_s[2], here_s[3]
        for z in range(4):
            at = pl.ds(z * pieces, pieces)

            def sum_of(keep, got, other):
                rows = pl.ds(z * 2 * pieces + other * pieces, pieces)
                return add(keep[rows], got[rows])

            send_a[at] = sum_of(ka, ga, 1 - y)
            left_a[at] = sum_of(ka, ga, y)
            send_b[at] = sum_of(kb, gb, 1 - x)
            left_b[at] = sum_of(kb, gb, x)
        if extra:
            total = add(ka[8 * pieces], ga[8 * pieces])
            send_a[4 * pieces] = total
            left_a[4 * pieces] = total

    a_out = shaped((4 * pieces + extra, 8, cols), BF16)
    b_out = shaped((4 * pieces, 8, cols), BF16)
    return small_call(
        kernel, "fold_second", here, (keep_a, got_a, keep_b, got_b), [a_out, a_out, b_out, b_out]
    )


def fold_third(terms, here, pieces, extra):
    cols = terms[0][0].shape[2]
    count = len(terms)

    def kernel(here_s, *refs):
        ins, (send, left) = refs[:-2], refs[-2:]
        low = here_s[4]
        for high in range(2):
            for number in range(2 * count):
                keep, got = ins[2 * number : 2 * number + 2]
                at = pl.ds((high * 2 * count + number) * pieces, pieces)
                for out, pick in ((send, 1 - low), (left, low)):
                    rows = pl.ds((high * 2 + pick) * pieces, pieces)
                    out[at] = add(keep[rows], got[rows])
        if extra:
            total = add(ins[0][4 * pieces], ins[1][4 * pieces])
            send[4 * count * pieces] = total
            left[4 * count * pieces] = total

    out = shaped((4 * count * pieces + extra, 8, cols), BF16)
    args = [item for term in terms for item in term]
    return small_call(kernel, "fold_third", here, args, [out, out])


def fold_fourth(keep, got, here, extra):
    cols = keep.shape[2]
    count = (keep.shape[0] - extra) // 2

    def kernel(here_s, keep_ref, got_ref, send, left):
        high = here_s[5]
        for out, pick in ((send, 1 - high), (left, high)):
            rows = pl.ds(pick * count, count)
            out[:count] = add(keep_ref[rows], got_ref[rows])
        if extra:
            total = add(keep_ref[2 * count], got_ref[2 * count])
            send[count] = total
            left[count] = total

    out = shaped((count + extra, 8, cols), BF16)
    return small_call(kernel, "fold_fourth", here, (keep, got), [out, out])


def fold_last(keep, got, here, extra):
    cols = keep.shape[2]
    count = keep.shape[0] - extra

    def kernel(here_s, keep_ref, got_ref, *outs):
        outs[0][...] = add(keep_ref[:count], got_ref[:count])
        if extra:
            outs[1][0] = add(keep_ref[count], got_ref[count])

    outs = [shaped((count, 8, cols), BF16)] + [shaped((1, 8, cols), BF16)] * extra
    return small_call(kernel, "fold_last", here, (keep, got), outs)


def chosen_part(here_s, refs, core, side, at):
    me, gx, gc, gd = [item[at].astype(F32) for item in refs]
    same_core, same_side = here_s[0] == core, here_s[2] == side
    return jnp.where(same_core, jnp.where(same_side, me, gx), jnp.where(same_side, gc, gd))


def feed_blocks(parts, here, pieces, width):
    cols = parts[0].shape[2]
    half = width // 2
    folds = cols // half
    rows = 2 * pieces * 8

    def kernel(here_s, me, gx, gc, gd, down_ref, up_ref):
        refs = (me, gx, gc, gd)
        for core in range(2):
            for side in range(2):
                tall = side * folds * rows
                for ab in range(2):
                    at = pl.ds(ab * pieces, pieces)
                    value = chosen_part(here_s, refs, core, side, at).reshape(rows // 2, cols)
                    for fold in range(folds):
                        start = tall + (ab * folds + fold) * (rows // 2)
                        down_ref[start : start + rows // 2, core * half : (core + 1) * half] = value[
                            :, fold * half : (fold + 1) * half
                        ]
                at = pl.ds(2 * pieces, 2 * pieces)
                value = chosen_part(here_s, refs, core, side, at).reshape(rows, cols)
                up_ref[side * rows : (side + 1) * rows, core * cols : (core + 1) * cols] = value

    outs = [shaped((2 * folds * rows, width), F32), shaped((2 * rows, 2 * cols), F32)]
    return small_call(kernel, "feed_blocks", here, parts, outs, 16)


def projection_blocks(parts, vectors, here, pieces):
    cols = parts[0].shape[2]
    rows = 2 * pieces * 8
    cut = cols // 4 * 3
    width = cols // 2
    small = width // 8
    large = cols // 4

    def kernel(here_s, me, gx, gc, gd, vec_ref, qkv_ref, out_ref, *outs):
        refs = (me, gx, gc, gd)
        for core in range(2):
            for side in range(2):
                value = chosen_part(here_s, refs, core, side, slice(None)).reshape(rows, cols)
                at = slice(side * rows, (side + 1) * rows)
                qkv_ref[at, core * cut : (core + 1) * cut] = value[:, :cut]
                out_ref[at, core * (cols - cut) : (core + 1) * (cols - cut)] = value[:, cut:]
        table = vec_ref[0].astype(F32)
        wide = here_s[6]
        shift = lax.rem(width - wide * small, width)
        left, right = pltpu.roll(table[:, :width], shift, 1), pltpu.roll(table[:, width:], shift, 1)
        for row in range(4):
            outs[2 * row][...] = left[row : row + 1, :small]
            outs[2 * row + 1][...] = right[row : row + 1, :small]
        turned = pltpu.roll(table, lax.rem(cols - lax.rem(wide, 4) * large, cols), 1)
        outs[8][...] = jnp.where(wide < 4, turned[4:5, :large], turned[5:6, :large])

    outs = [shaped((2 * rows, 2 * cut), F32), shaped((2 * rows, 2 * (cols - cut)), F32)]
    outs += [shaped((1, small), F32)] * 8 + [shaped((1, large), F32)]
    return small_call(kernel, "projection_blocks", here, (*parts, vectors), outs, 16)


def after(item, *earlier):
    return lax.optimization_barrier((item, *earlier))[0]


def swap(item, axis, step):
    count = lax.axis_size(axis)
    return lax.ppermute(item, axis, [(index, index ^ step) for index in range(count)])


def quarters(mine):
    return mine, swap(mine, "narrow", 2), swap(mine, "narrow", 1), swap(mine, "narrow", 3)


def regroup_rows(sent, bucket, wide_count, batches):
    span, width = sent.shape[1:]
    if wide_count == batches:
        got = lax.all_to_all(sent, "wide", split_axis=0, concat_axis=0, tiled=True)
        return got.reshape(batches * span, width)
    send = jnp.zeros((wide_count, span, width), sent.dtype).at[bucket].set(sent)
    got = lax.all_to_all(send, "wide", split_axis=0, concat_axis=0, tiled=True)
    marks = jnp.zeros((wide_count, 1), jnp.int32).at[bucket].set(1)
    filled = lax.all_to_all(marks, "wide", split_axis=0, concat_axis=0, tiled=True)[:, 0]
    place = jnp.where(filled > 0, jnp.cumsum(filled) - filled, batches)
    chosen = (
        jnp.zeros((batches,), jnp.int32)
        .at[place]
        .set(jnp.arange(wide_count, dtype=jnp.int32), mode="drop")
    )
    return got[chosen].reshape(batches * span, width)


def sum_anywhere(item, wide_count, narrow_count):
    blocks = item.astype(F32).reshape(wide_count, -1)
    extent = blocks.shape[1]
    padded = (extent + narrow_count - 1) // narrow_count * narrow_count
    blocks = jnp.pad(blocks, ((0, 0), (0, padded - extent))).reshape(-1)
    share = lax.psum_scatter(blocks, ("wide", "narrow"), scatter_dimension=0, tiled=True)
    whole = lax.all_gather(share.astype(BF16), "narrow", axis=0, tiled=True).astype(F32)
    return whole[:extent].reshape((item.shape[0] // wide_count,) + item.shape[1:])


def body(
    tokens, bucket, lengths, pairing, targets, w_qkv, bias_q, bias_v, w_out, bias_out,
    gain_attn, shift_attn, w_up, bias_up, w_down, bias_down, gain_ffn, shift_ffn,
):
    wide_count, narrow_count = lax.axis_size("wide"), lax.axis_size("narrow")
    batches = bucket.shape[0]
    rows, width = tokens.shape
    span = rows // batches
    paired = (wide_count, narrow_count) == (8, 4)
    wide, narrow = lax.axis_index("wide"), lax.axis_index("narrow")
    if paired:
        core = narrow % 2
        here = jnp.stack(
            [core, 1 - core, narrow // 2, wide % 2, wide // 2 % 2, wide // 4, wide, narrow]
        ).astype(jnp.int32)
    else:
        here = jnp.arange(8, dtype=jnp.int32)
    table = vector_table(
        [bias_q, bias_v, bias_out, gain_attn, shift_attn, bias_down, gain_ffn, shift_ffn, bias_up], width
    )
    ordered = wide_count == batches
    slots = bucket if ordered else jnp.arange(batches, dtype=jnp.int32)
    pieces = width // 32 // 8

    qkv, probs, attended, n_attn, spread, sid = attention_forward(
        tokens, w_qkv, w_out, table, bucket, lengths, wide_count // batches, span, 2 * span
    )
    active, slope, hidden_t, sent, gres, grad_second, vec_ffn = feed_forward(
        n_attn, w_up, w_down, table, sid, slots, pairing, targets, batches, 2 * span
    )
    ups = (grad_second, slope, hidden_t, w_down)
    heads = (n_attn, spread, table, w_out, qkv, probs)
    down_sent = down_terms(active, grad_second, here, 1)
    encoded = regroup_rows(after(sent, down_sent), bucket, wide_count, batches)
    if paired:
        down_dealt = down_terms(active, grad_second, here, 0, swap(down_sent, "narrow", 1))
        down_a, down_b = swap(down_dealt[0], "narrow", 2), swap(down_dealt[2], "wide", 1)
        up_sent, gi_sent, bup_sent = up_terms(*ups, after(here, down_dealt[1]), 1)
        gh = hidden_gradient(gi_sent, w_up, here, 1)
        *up_dealt, gi_kept, bup_kept = up_terms(
            *ups, after(here, gh), 0, swap(up_sent, "narrow", 1)
        )
        up_a, up_b = swap(up_dealt[0], "narrow", 2), swap(up_dealt[2], "wide", 1)
        down_dealt = fold_second(
            down_dealt[1], down_a, down_dealt[3], down_b, after(here, bup_kept), pieces, 0
        )
        down_a, down_b = swap(down_dealt[0], "wide", 1), swap(down_dealt[2], "narrow", 2)
        gr, gb, gm, vec_attn = attention_backward(
            gh, gres, gi_kept, w_up, *heads, after(here, down_dealt[1]), 0, span, 2 * span
        )
        up_dealt = fold_second(
            up_dealt[1], up_a, up_dealt[3], up_b, after(here, vec_attn, encoded), pieces, 0
        )
        up_a, up_b = swap(up_dealt[0], "wide", 1), swap(up_dealt[2], "narrow", 2)
        projections = (tokens, gm, attended, gb, (vec_ffn, vec_attn, bup_sent, bup_kept))
        proj_sent = projection_terms(*projections, after(here, up_dealt[1]), 1)
        grad_tokens = input_gradient(after(gm, proj_sent), w_qkv, gr, 2 * span)
        send, feed = fold_third(
            [(down_dealt[1], down_a, down_dealt[3], down_b), (up_dealt[1], up_a, up_dealt[3], up_b)],
            after(here, grad_tokens), pieces, 0,
        )
        feed_got = swap(send, "wide", 2)
        proj_dealt = projection_terms(
            *projections, after(here, feed), 0, swap(proj_sent, "narrow", 1)
        )
        proj_a, proj_b = swap(proj_dealt[0], "narrow", 2), swap(proj_dealt[2], "wide", 1)
        encoded = copied(encoded, after(here, proj_dealt[1]), span)
        send, feed = fold_fourth(feed, feed_got, after(here, encoded), 0)
        feed_got = swap(send, "wide", 4)
        proj_dealt = fold_second(
            proj_dealt[1], proj_a, proj_dealt[3], proj_b, after(here, feed), pieces, 1
        )
        proj_a, proj_b = swap(proj_dealt[0], "wide", 1), swap(proj_dealt[2], "narrow", 2)
        (feed,) = fold_last(feed, feed_got, after(here, proj_dealt[1]), 0)
        feed = quarters(feed)
        send, proj = fold_third(
            [(proj_dealt[1], proj_a, proj_dealt[3], proj_b)], after(here, feed[0]), pieces, 1
        )
        proj_got = swap(send, "wide", 2)
        grad_w_down, grad_w_up = feed_blocks(feed, after(here, proj), pieces, width)
        send, proj = fold_fourth(proj, proj_got, after(here, grad_w_down), 1)
        proj_got = swap(send, "wide", 4)
        proj, vectors = fold_last(proj, proj_got, here, 1)
        proj = quarters(proj)
        grad_w_qkv, grad_w_out, *small = projection_blocks(proj, vectors, here, pieces)
        small = [item.reshape(-1) for item in small]
    else:
        down_kept = down_terms(active, grad_second, here, 0)
        up_sent, gi_sent, bup_sent = up_terms(*ups, here, 1)
        up_kept, gi_kept, bup_kept = up_terms(*ups, here, 0)
        gh = hidden_gradient(gi_sent, w_up, here, 1)
        gr, gb, gm, vec_attn = attention_backward(
            gh, gres, gi_kept, w_up, *heads, here, 0, span, 2 * span
        )
        projections = (tokens, gm, attended, gb, (vec_ffn, vec_attn, bup_sent, bup_kept), here)
        grad_tokens = input_gradient(gm, w_qkv, gr, 2 * span)
        proj_sent, proj_kept = projection_terms(*projections, 1), projection_terms(*projections, 0)
        total = partial(sum_anywhere, wide_count=wide_count, narrow_count=narrow_count)
        cut = width // 2 * 3
        grad_w_down = total(jnp.concatenate([down_kept, down_sent], axis=1))
        grad_w_up = total(jnp.concatenate([up_kept, up_sent], axis=1))
        grad_w_qkv = total(jnp.concatenate([proj_kept[:width, :cut], proj_sent[:width, :cut]], axis=1))
        grad_w_out = total(jnp.concatenate([proj_kept[:width, cut:], proj_sent[:width, cut:]], axis=1))
        small = [
            total(item)
            for item in (*vec_ffn[:3], *vec_attn[:5], jnp.concatenate([bup_kept[0], bup_sent[0]]))
        ]
    gain_out, shift_out, b_down, b_q, b_v, b_out, g_attn, s_attn, b_up = small
    return (
        encoded, grad_tokens, grad_w_qkv, b_q, b_v, grad_w_out, b_out, g_attn, s_attn,
        grad_w_up, b_up, grad_w_down, b_down, gain_out, shift_out,
    )


def solution(mesh):
    split = P(("wide", "narrow"))
    in_specs = (
        P(("wide", "narrow"), None), split, split, P(("wide", "narrow"), None), split,
    ) + (P(),) * 13
    out_specs = (
        P(("wide", "narrow"), None), P(("wide", "narrow"), None),
        P("wide", None), P("wide"), P("wide"), P("wide", None), P("wide"), P("wide"), P("wide"),
        P("wide", None), P("wide"), P("wide", None), P("wide"), P("wide"), P("wide"),
    )
    return jax.shard_map(body, mesh=mesh, in_specs=in_specs, out_specs=out_specs, check_vma=False)
```

```python
from functools import partial

import jax
import jax.numpy as jnp
from jax import lax
from jax.experimental import pallas as pl
from jax.experimental.pallas import tpu as pltpu
from jax.sharding import PartitionSpec as P

HDIM = 64
KTOP = 12
NORM_EPS = 1e-12
COS_EPS = 1e-06
MASKED = -1000000000.0
LOSS_SCALE = 1024.0
F32 = jnp.float32
BF16 = jnp.bfloat16
LANES = 128
MIB = 1024 * 1024
LARGE = 100000
COST = 0.05
ERF_P = 0.3275911
ERF_A = (0.254829592, -0.284496736, 1.421413741, -1.453152027, 1.061405429)
HALF_ROOT = 0.7071067811865476
PEAK = 0.3989422804014327
ROW_BQ, ROW_BV, ROW_BO, ROW_GA, ROW_SA, ROW_BD, ROW_GF, ROW_SF, ROW_BU = range(9)


def dot(left, right):
    return jnp.dot(left, right, preferred_element_type=F32)


def dot_t(left, right):
    return lax.dot_general(left, right, (((1,), (1,)), ((), ())), preferred_element_type=F32)


def t_dot(left, right):
    return lax.dot_general(left, right, (((0,), (0,)), ((), ())), preferred_element_type=F32)


def full(shape):
    return pl.BlockSpec(shape, lambda *_: (0,) * len(shape))


def once(shape):
    return pl.BlockSpec(shape, lambda *_: (0,) * len(shape), pipeline_mode=pl.Buffered(1))


def large(item):
    return item.size >= LARGE


def shaped(shape, dtype):
    return jax.ShapeDtypeStruct(shape, dtype)


def call(
    kernel, name, grid, prefetch, in_specs, out_specs, out_shape, scratch, flops, moved, args, vmem=24, free=0, loose=()
):
    single = not isinstance(out_shape, list)
    shapes = [out_shape] if single else out_shape
    shapes = [
        pltpu.HBM(item.shape, item.dtype) if large(item) and number not in loose else item
        for number, item in enumerate(shapes)
    ]
    out_shape = shapes[0] if single else shapes
    args = [
        pltpu.with_memory_space_constraint(item, pltpu.HBM) if large(item) and number < len(args) - free else item
        for number, item in enumerate(args)
    ]
    return pl.pallas_call(
        kernel,
        grid_spec=pltpu.PrefetchScalarGridSpec(
            num_scalar_prefetch=len(prefetch),
            grid=grid,
            in_specs=in_specs,
            out_specs=out_specs,
            scratch_shapes=scratch,
        ),
        out_shape=out_shape,
        compiler_params=pltpu.CompilerParams(
            dimension_semantics=("arbitrary",) * len(grid), vmem_limit_bytes=vmem * MIB
        ),
        cost_estimate=pl.CostEstimate(flops=int(flops * COST), bytes_accessed=int(moved * COST), transcendentals=0),
        name=name,
    )(*[pltpu.with_memory_space_constraint(item, pltpu.HBM) for item in prefetch], *args)


def norm_forward(values):
    center = values - jnp.mean(values, axis=-1, keepdims=True)
    spread = lax.rsqrt(jnp.mean(center * center, axis=-1, keepdims=True) + NORM_EPS)
    return center * spread, spread


def norm_backward(grad_out, normed, spread, gain):
    scaled = grad_out * gain
    mean_scaled = jnp.mean(scaled, axis=-1, keepdims=True)
    mean_product = jnp.mean(scaled * normed, axis=-1, keepdims=True)
    return spread * (scaled - mean_scaled - normed * mean_product)


def column_sum(values):
    return jnp.sum(values, axis=0, keepdims=True)


def gelu_pair(v):
    t = 1.0 / (1.0 + (ERF_P * HALF_ROOT) * jnp.abs(v))
    bell = jnp.exp(-0.5 * (v * v))
    poly = 0.5 * ERF_A[4]
    for coef in ERF_A[3::-1]:
        poly = poly * t + 0.5 * coef
    tail = poly * t * bell
    phi = jnp.where(v > 0, 1.0 - tail, tail)
    return v * phi, phi + v * (PEAK * bell)


def head_masks():
    lane = lax.broadcasted_iota(jnp.int32, (1, LANES), 1)
    low = (lane < HDIM).astype(F32)
    return low.astype(BF16), (1.0 - low).astype(BF16), lane < HDIM


def sentence_count(bucket_s, number, group_size):
    kind = bucket_s[number]
    if group_size > 1:
        kind = kind // group_size
    return jnp.maximum(1, lax.shift_right_logical(jnp.int32(KTOP), kind))


def row_sentences(batch, bucket_s, lengths_s, group_size, batches, sent, span):
    start = jnp.int32(0)
    for other in range(batches):
        start += jnp.where(other < batch, sentence_count(bucket_s, other, group_size), 0)
    count = sentence_count(bucket_s, batch, group_size)
    lane = lax.broadcasted_iota(jnp.int32, (8, span), 1)
    row = lax.broadcasted_iota(jnp.int32, (span, span), 0)
    passed_lane = jnp.zeros((8, span), jnp.int32)
    passed_row = jnp.zeros((span, span), jnp.int32)
    finish = jnp.int32(0)
    for number in range(KTOP):
        finish += lengths_s[jnp.minimum(start + number, sent - 1)]
        bound = jnp.where(number < count, finish, span)
        passed_lane += (lane >= bound).astype(jnp.int32)
        passed_row += (row >= bound).astype(jnp.int32)
    sid_lane = jnp.where(passed_lane < count, start + passed_lane, -1)
    sid_row = jnp.where(passed_row < count, start + passed_row, -1)
    return sid_lane, sid_row


def vector_table(vectors, width):
    def kernel(*refs):
        out_ref = refs[-1]
        at = 0
        for ref in refs[:-1]:
            for part in range(ref.shape[0] // width):
                out_ref[at : at + 1, :] = ref[part * width : (part + 1) * width].astype(F32).reshape(1, width)
                at += 1

    rows = sum(item.shape[0] for item in vectors) // width
    return pl.pallas_call(
        kernel,
        grid=(1,),
        in_specs=[full(item.shape) for item in vectors],
        out_specs=full((rows, width)),
        out_shape=shaped((rows, width), F32),
        compiler_params=pltpu.CompilerParams(vmem_limit_bytes=4 * MIB),
        name="vector_table",
    )(*[pltpu.with_memory_space_constraint(item, pltpu.HBM) for item in vectors])


def attention_forward(x, w_qkv, w_out, table, bucket, lengths, group_size, span, rows_step):
    rows, width = x.shape
    batches = rows // span
    pairs = width // LANES
    sent = lengths.shape[0]
    per_step = rows_step // span

    def kernel(bucket_s, lengths_s, x_ref, wq_ref, wo_ref, tab_ref, qkv_ref, p_ref, att_ref, n_ref, s_ref, sid_ref):
        step = pl.program_id(0)
        low_b, high_b, low_m = head_masks()
        x_in = x_ref[...]
        mixed = dot(x_in, wq_ref[:, :width]) + tab_ref[ROW_BQ : ROW_BQ + 1, :]
        qkv_ref[:, :width] = (mixed * 0.125).astype(BF16)
        qkv_ref[:, width : 2 * width] = dot(x_in, wq_ref[:, width : 2 * width]).astype(BF16)
        mixed = dot(x_in, wq_ref[:, 2 * width :]) + tab_ref[ROW_BV : ROW_BV + 1, :]
        qkv_ref[:, 2 * width :] = mixed.astype(BF16)
        eye = lax.broadcasted_iota(jnp.int32, (span, span), 0) == lax.broadcasted_iota(
            jnp.int32, (span, span), 1
        )
        for inner in range(per_step):
            sid_lane, sid_row = row_sentences(
                step * per_step + inner, bucket_s, lengths_s, group_size, batches, sent, span
            )
            sid_ref[inner] = sid_lane
            same = (sid_row == sid_lane[0:1, :]) & (sid_row >= 0)
            bias = jnp.where(same | eye, 0.0, MASKED)
            bias = jnp.concatenate([bias, bias], axis=0)
            base = slice(inner * span, (inner + 1) * span)
            for pair in range(pairs):
                cols = slice(pair * LANES, (pair + 1) * LANES)
                q = qkv_ref[base, cols]
                k = qkv_ref[base, width + pair * LANES : width + (pair + 1) * LANES]
                v = qkv_ref[base, 2 * width + pair * LANES : 2 * width + (pair + 1) * LANES]
                both = jnp.concatenate([q * low_b, q * high_b], axis=0)
                logits = dot_t(both, k) + bias
                raised = jnp.exp(logits - jnp.max(logits, axis=-1, keepdims=True))
                total = jnp.sum(raised, axis=-1, keepdims=True)
                probs = (raised * (1.0 / total)).astype(BF16)
                p_ref[inner, pair] = probs
                mix = dot(probs, v)
                att_ref[base, cols] = jnp.where(low_m, mix[:span], mix[span:]).astype(BF16)
        branch = dot(att_ref[...], wo_ref[...]) + tab_ref[ROW_BO : ROW_BO + 1, :]
        normed, spread = norm_forward(x_in.astype(F32) + branch)
        n_ref[...] = normed
        s_ref[...] = jnp.broadcast_to(spread, (rows_step, LANES))

    return call(
        kernel,
        "attn_fwd",
        (rows // rows_step,),
        (bucket, lengths),
        [
            pl.BlockSpec((rows_step, width), lambda i, *_: (i, 0)),
            once((width, 3 * width)),
            once((width, width)),
            once(table.shape),
        ],
        [
            pl.BlockSpec((rows_step, 3 * width), lambda i, *_: (i, 0)),
            pl.BlockSpec((per_step, pairs, 2 * span, span), lambda i, *_: (i, 0, 0, 0)),
            pl.BlockSpec((rows_step, width), lambda i, *_: (i, 0)),
            pl.BlockSpec((rows_step, width), lambda i, *_: (i, 0)),
            pl.BlockSpec((rows_step, LANES), lambda i, *_: (i, 0)),
            pl.BlockSpec((per_step, 8, span), lambda i, *_: (i, 0, 0)),
        ],
        [
            shaped((rows, 3 * width), BF16),
            shaped((batches, pairs, 2 * span, span), BF16),
            shaped((rows, width), BF16),
            shaped((rows, width), F32),
            shaped((rows, LANES), F32),
            shaped((batches, 8, span), jnp.int32),
        ],
        [],
        8 * rows * width * width * 2,
        30e6,
        (x, w_qkv, w_out, table),
        26,
    )


def feed_forward(n_attn, w_up, w_down, table, sid, slots, pairing, targets, slot_count, block):
    rows, width = n_attn.shape
    ff = w_up.shape[1]
    batches, _, span = sid.shape
    pair_count = targets.shape[0]
    side = -(-pair_count // 8) * 8
    chunk = width
    steps = ff // chunk
    blocks = rows // block
    per_block = block // span

    def kernel(
        slots_s, pairing_s, targets_s, n_ref, wu_ref, wd_ref, tab_ref, sid_ref,
        act_ref, dg_ref, ht_ref, enc_ref, gres_ref, gsl_ref, vec_ref, low_scr, acc_scr, spread_scr,
    ):
        step = pl.program_id(0)
        gain = tab_ref[ROW_GA : ROW_GA + 1, :]
        shift = tab_ref[ROW_SA : ROW_SA + 1, :]

        @pl.when(step == 0)
        def _():
            hidden = (n_ref[...] * gain + shift).astype(BF16)
            low_scr[...] = hidden
            ht_ref[...] = hidden.T
            acc_scr[...] = jnp.zeros_like(acc_scr)

        for number in range(blocks):
            base = slice(number * block, (number + 1) * block)
            inner = dot(low_scr[base, :], wu_ref[...]) + tab_ref[pl.ds(ROW_BU + step, 1), :]
            active, slope = gelu_pair(inner)
            active = active.astype(BF16)
            act_ref[base, :] = active
            dg_ref[base, :] = slope.astype(BF16)
            acc_scr[base, :] += dot(active, wd_ref[...])

        @pl.when(step == steps - 1)
        def _():
            gain_out = tab_ref[ROW_GF : ROW_GF + 1, :]
            shift_out = tab_ref[ROW_SF : ROW_SF + 1, :]
            slot = lax.broadcasted_iota(jnp.int32, (2 * side, span), 0)
            wanted = jnp.full((2 * side, span), -2, jnp.int32)
            goal = jnp.zeros((side, LANES), F32)
            goal_slot = lax.broadcasted_iota(jnp.int32, (side, LANES), 0)
            for number in range(pair_count):
                wanted = jnp.where(slot == number, pairing_s[0, 2 * number], wanted)
                wanted = jnp.where(slot == side + number, pairing_s[0, 2 * number + 1], wanted)
                goal = jnp.where(goal_slot == number, targets_s[number], goal)
            members = [
                (sid_ref[number][0:1, :] == wanted).astype(F32) for number in range(batches)
            ]
            sizes = jnp.zeros((2 * side, 1), F32)
            for member in members:
                sizes += jnp.sum(member, axis=-1, keepdims=True)
            share = 1.0 / jnp.maximum(sizes, 1.0)
            picks = [
                jnp.concatenate(members[number * per_block : (number + 1) * per_block], axis=1).astype(BF16)
                for number in range(blocks)
            ]
            ones = jnp.ones((2 * side, LANES), BF16)
            pooled = jnp.zeros((2 * side, width), F32)
            for number in range(blocks):
                base = slice(number * block, (number + 1) * block)
                resid = (
                    n_ref[base, :] * gain + shift + acc_scr[base, :] + tab_ref[ROW_BD : ROW_BD + 1, :]
                )
                normed, spread = norm_forward(resid)
                acc_scr[base, :] = normed
                spread_scr[base, :] = jnp.broadcast_to(spread, (block, LANES))
                out = normed * gain_out + shift_out
                high = out.astype(BF16)
                rest = (out - high.astype(F32)).astype(BF16)
                pooled += dot(picks[number], high) + dot(picks[number], rest)
                valid = t_dot(picks[number], ones)
                for col in range(width // LANES):
                    cols = slice(col * LANES, (col + 1) * LANES)
                    kept = (out[:, cols] * valid).astype(BF16)
                    for inner in range(per_block):
                        enc_ref[slots_s[number * per_block + inner], :, cols] = kept[
                            inner * span : (inner + 1) * span
                        ]
            pooled = pooled * share
            first, partner = pooled[:side], pooled[side:]
            cross = jnp.sum(first * partner, axis=-1, keepdims=True)
            scale_first = lax.rsqrt(jnp.sum(first * first, axis=-1, keepdims=True) + COS_EPS)
            scale_partner = lax.rsqrt(jnp.sum(partner * partner, axis=-1, keepdims=True) + COS_EPS)
            cosine = cross * scale_first * scale_partner
            factor = 2.0 * LOSS_SCALE * (cosine - goal[:, :1])
            both_scales = factor * scale_first * scale_partner
            grad_first = both_scales * partner - (factor * cosine * scale_first * scale_first) * first
            grad_partner = (
                both_scales * first - (factor * cosine * scale_partner * scale_partner) * partner
            )
            grad_home = jnp.concatenate([grad_first, grad_partner], axis=0) * share
            high = grad_home.astype(BF16)
            rest = (grad_home - high.astype(F32)).astype(BF16)
            vec_ref[...] = jnp.zeros_like(vec_ref)
            for number in range(blocks):
                base = slice(number * block, (number + 1) * block)
                grad_out = t_dot(picks[number], high) + t_dot(picks[number], rest)
                normed = acc_scr[base, :]
                resid = norm_backward(grad_out, normed, spread_scr[base, :1], gain_out)
                gres_ref[base, :] = resid
                low = resid.astype(BF16)
                gsl_ref[base, :] = low
                vec_ref[0:1, :] += column_sum(grad_out * normed)
                vec_ref[1:2, :] += column_sum(grad_out)
                vec_ref[2:3, :] += column_sum(low.astype(F32))

    return call(
        kernel,
        "ffn_fwd",
        (steps,),
        (slots, pairing, targets),
        [
            once((rows, width)),
            pl.BlockSpec((width, chunk), lambda j, *_: (0, j)),
            pl.BlockSpec((chunk, width), lambda j, *_: (j, 0)),
            once(table.shape),
            once((batches, 8, span)),
        ],
        [
            pl.BlockSpec((rows, chunk), lambda j, *_: (0, j)),
            pl.BlockSpec((rows, chunk), lambda j, *_: (0, j)),
            once((width, rows)),
            once((slot_count, span, width)),
            once((rows, width)),
            once((rows, width)),
            once((8, width)),
        ],
        [
            shaped((rows, ff), BF16),
            shaped((rows, ff), BF16),
            shaped((width, rows), BF16),
            shaped((slot_count, span, width), BF16),
            shaped((rows, width), F32),
            shaped((rows, width), BF16),
            shaped((8, width), F32),
        ],
        [
            pltpu.VMEM((rows, width), BF16),
            pltpu.VMEM((rows, width), F32),
            pltpu.VMEM((rows, LANES), F32),
        ],
        8 * rows * width * ff,
        40e6,
        (n_attn, w_up, w_down, table, sid),
        44,
    )


def deal(scratch, here_s, outs, z_count, pieces, folds=1):
    send_a, keep_a, send_b, keep_b = outs
    x, y = here_s[2], here_s[3]
    cols = scratch.shape[-1]
    for z in range(z_count):
        for other in range(2):
            at = pl.ds((z * 2 + other) * pieces, pieces)
            for fold in range(folds):
                part = pl.ds(fold * pieces, pieces)
                to = slice(fold * cols, (fold + 1) * cols)
                send_a[at, :, to] = scratch[z, other, 1 - x, 0, part].astype(BF16)
                keep_a[at, :, to] = scratch[z, other, x, 0, part].astype(BF16)
                send_b[at, :, to] = scratch[z, 1 - y, other, 1, part].astype(BF16)
                keep_b[at, :, to] = scratch[z, y, other, 1, part].astype(BF16)


def down_terms(active, grad_second, here, which, got=None):
    rows, ff = active.shape
    width = grad_second.shape[1]
    half = width // 2
    steps = 4
    tall = ff // steps
    pieces = width // 32 // 8
    folds = ff // width

    def give(here_s, act_ref, gs_ref, out_ref):
        out_ref[...] = t_dot(act_ref[...], gs_ref[...]).astype(BF16)

    def own(here_s, act_ref, gs_ref, got_ref, *rest):
        outs, scratch = rest[:4], rest[4]
        term = t_dot(act_ref[...], gs_ref[...]) + got_ref[...].astype(F32)
        scratch[...] = term.reshape(scratch.shape)
        deal(scratch, here_s, outs, 1, pieces, folds)

    in_specs = [
        pl.BlockSpec((rows, tall), lambda i, here_s: (0, i)),
        pl.BlockSpec((rows, half), lambda i, here_s: (0, here_s[which]), pipeline_mode=pl.Buffered(1)),
    ]
    flops = 2 * rows * ff * half
    if got is None:
        return call(
            give, "down_give", (steps,), (here,), in_specs,
            pl.BlockSpec((tall, half), lambda i, *_: (i, 0)),
            shaped((ff, half), BF16), [], flops, 9e6, (active, grad_second), 20, 0, (0,),
        )
    block = (2 * pieces, 8, folds * half)
    return call(
        own, "down_own", (steps,), (here,),
        in_specs + [pl.BlockSpec((tall, half), lambda i, *_: (i, 0))],
        [pl.BlockSpec(block, lambda i, *_: (i, 0, 0))] * 4,
        [shaped((8 * pieces, 8, folds * half), BF16)] * 4,
        [pltpu.VMEM((1, 2, 2, 2, folds * pieces, 8, half), F32)],
        flops, 11e6, (active, grad_second, got), 24, 1, (0, 2),
    )


def up_terms(grad_second, slope, hidden_t, w_down, here, which, got=None):
    rows, width = grad_second.shape
    ff = w_down.shape[0]
    half = ff // 2
    chunk = width
    steps = half // chunk
    block = rows // 4
    pieces = width // 32 // 8

    def kernel(here_s, gs_ref, dg_ref, ht_ref, wd_ref, *refs):
        if got is not None:
            got_ref, refs = refs[0], refs[1:]
            outs, refs = refs[:4], refs[4:]
        else:
            out_ref, refs = refs[0], refs[1:]
        gi_ref, bu_ref = refs[:2]
        sums = jnp.zeros((1, chunk), F32)
        for number in range(rows // block):
            base = slice(number * block, (number + 1) * block)
            grad_active = dot_t(gs_ref[base, :], wd_ref[...])
            low = (grad_active * dg_ref[base, :].astype(F32)).astype(BF16)
            gi_ref[base, :] = low
            sums += column_sum(low.astype(F32))
        bu_ref[...] = sums
        term = dot(ht_ref[...], gi_ref[...])
        if got is None:
            out_ref[...] = term.astype(BF16)
        else:
            scratch = refs[2]
            term += got_ref[...].astype(F32)
            scratch[...] = term.reshape(scratch.shape)
            deal(scratch, here_s, outs, 4, pieces)

    def col(i, here_s):
        return here_s[which] * steps + i

    in_specs = [
        once((rows, width)),
        pl.BlockSpec((rows, chunk), lambda i, h: (0, col(i, h))),
        once((width, rows)),
        pl.BlockSpec((chunk, width), lambda i, h: (col(i, h), 0)),
    ]
    args = [grad_second, slope, hidden_t, w_down]
    scratch = []
    if got is None:
        out_specs = [pl.BlockSpec((width, chunk), lambda i, *_: (0, i))]
        out_shape = [shaped((width, half), BF16)]
    else:
        in_specs.append(pl.BlockSpec((width, chunk), lambda i, *_: (0, i)))
        args.append(got)
        out_specs = [pl.BlockSpec((8 * pieces, 8, chunk), lambda i, *_: (0, 0, i))] * 4
        out_shape = [shaped((8 * pieces, 8, half), BF16)] * 4
        scratch.append(pltpu.VMEM((4, 2, 2, 2, pieces, 8, chunk), F32))
    return call(
        kernel, "up_give" if got is None else "up_own", (steps,), (here,), in_specs,
        out_specs
        + [
            pl.BlockSpec((rows, chunk), lambda i, *_: (0, i)),
            pl.BlockSpec((1, chunk), lambda i, *_: (0, i)),
        ],
        out_shape + [shaped((rows, half), BF16), shaped((1, half), F32)],
        scratch, 4 * rows * width * half, 16e6, args, 34, 0 if got is None else 1, (0,) if got is None else (0, 2),
    )


def hidden_gradient(grad_inner, w_up, here, which):
    rows, half = grad_inner.shape
    width = w_up.shape[0]
    block = rows // 2

    def kernel(here_s, gi_ref, wu_ref, out_ref):
        out_ref[...] = dot_t(gi_ref[...], wu_ref[...])

    return call(
        kernel, "hidden_grad", (rows // block,), (here,),
        [
            pl.BlockSpec((block, half), lambda i, h: (i, 0)),
            pl.BlockSpec((width, half), lambda i, h: (0, h[which]), pipeline_mode=pl.Buffered(1)),
        ],
        pl.BlockSpec((block, width), lambda i, h: (i, 0)),
        shaped((rows, width), F32), [], 2 * rows * width * half, 9e6, (grad_inner, w_up), 16,
    )


def attention_backward(gh, gres, grad_inner, w_up, n_attn, spread, table, w_out, qkv, probs, here, which, span, rows_step):
    rows, width = gh.shape
    half = grad_inner.shape[1]
    pairs = width // LANES
    per_step = rows_step // span

    def kernel(here_s, gh_ref, gres_ref, gi_ref, wu_ref, n_ref, s_ref, tab_ref, wo_ref, qkv_ref, p_ref, gr_ref, gb_ref, gm_ref, vec_ref, ga_scr):
        step = pl.program_id(0)
        low_b, high_b, low_m = head_masks()

        @pl.when(step == 0)
        def _():
            vec_ref[...] = jnp.zeros_like(vec_ref)

        normed = n_ref[...]
        grad_hidden = dot_t(gi_ref[...], wu_ref[...]) + gh_ref[...] + gres_ref[...]
        resid = norm_backward(grad_hidden, normed, s_ref[:, :1], tab_ref[ROW_GA : ROW_GA + 1, :])
        gr_ref[...] = resid
        low = resid.astype(BF16)
        gb_ref[...] = low
        vec_ref[2:3, :] += column_sum(low.astype(F32))
        vec_ref[3:4, :] += column_sum(grad_hidden * normed)
        vec_ref[4:5, :] += column_sum(grad_hidden)
        ga_scr[...] = dot_t(low, wo_ref[...]).astype(BF16)
        for inner in range(per_step):
            base = slice(inner * span, (inner + 1) * span)
            for pair in range(pairs):
                cols = slice(pair * LANES, (pair + 1) * LANES)
                k_cols = slice(width + pair * LANES, width + (pair + 1) * LANES)
                v_cols = slice(2 * width + pair * LANES, 2 * width + (pair + 1) * LANES)
                q, k, v = qkv_ref[base, cols], qkv_ref[base, k_cols], qkv_ref[base, v_cols]
                grad = ga_scr[base, cols]
                grads = jnp.concatenate([grad * low_b, grad * high_b], axis=0)
                both = jnp.concatenate([q * low_b, q * high_b], axis=0)
                weights = p_ref[inner, pair]
                wide = weights.astype(F32)
                grad_probs = dot_t(grads, v)
                balance = jnp.sum(wide * grad_probs, axis=-1, keepdims=True)
                grad_logits = (wide * (grad_probs - balance)).astype(BF16)
                mix = dot(grad_logits, k)
                grad_q = jnp.where(low_m, mix[:span], mix[span:]).astype(BF16) * jnp.bfloat16(0.125)
                grad_v = t_dot(weights, grads).astype(BF16)
                gm_ref[base, cols] = grad_q
                gm_ref[base, k_cols] = t_dot(grad_logits, both).astype(BF16)
                gm_ref[base, v_cols] = grad_v
                vec_ref[0:1, cols] += column_sum(grad_q.astype(F32))
                vec_ref[1:2, cols] += column_sum(grad_v.astype(F32))

    def rows_of(cols):
        return pl.BlockSpec((rows_step, cols), lambda i, h: (i, 0))

    return call(
        kernel,
        "attn_bwd",
        (rows // rows_step,),
        (here,),
        [
            rows_of(width), rows_of(width), rows_of(half),
            pl.BlockSpec((width, half), lambda i, h: (0, h[which]), pipeline_mode=pl.Buffered(1)),
            rows_of(width), rows_of(LANES),
            once(table.shape), once((width, width)), rows_of(3 * width),
            pl.BlockSpec((per_step, pairs, 2 * span, span), lambda i, h: (i, 0, 0, 0)),
        ],
        [rows_of(width), rows_of(width), rows_of(3 * width), full((8, width))],
        [
            shaped((rows, width), F32), shaped((rows, width), BF16),
            shaped((rows, 3 * width), BF16), shaped((8, width), F32),
        ],
        [pltpu.VMEM((rows_step, width), BF16)],
        8 * rows * width * width * 2,
        40e6,
        (gh, gres, grad_inner, w_up, n_attn, spread, table, w_out, qkv, probs),
        34,
    )


def projection_terms(x, grad_mixed, attended, grad_branch, vectors, here, which, got=None):
    rows, width = x.shape
    part = width // 2
    pieces = width // 32 // 8

    def product(x_ref, gm_ref, att_ref, gb_ref, scr):
        step = pl.program_id(0)

        @pl.when(step < 3)
        def _():
            scr[...] = t_dot(x_ref[...], gm_ref[...])

        @pl.when(step == 3)
        def _():
            scr[...] = t_dot(att_ref[...], gb_ref[...])

    def small(here_s, ffn_ref, attn_ref, sent_ref, kept_ref, store):
        first = here_s[0] == 0
        for step in range(4):

            @pl.when(pl.program_id(0) == step)
            def _():
                side, at = step // 2, slice(step % 2 * part, (step % 2 + 1) * part)
                wide = slice(step * part, (step + 1) * part)
                rows_of = (
                    (ffn_ref[0:1, at], ffn_ref[2:3, at], attn_ref[1:2, at], attn_ref[3:4, at]),
                    (ffn_ref[1:2, at], attn_ref[0:1, at], attn_ref[2:3, at], attn_ref[4:5, at]),
                )[side]
                sent, kept = sent_ref[:, wide], kept_ref[:, wide]
                ups = (jnp.where(first, kept, sent), jnp.where(first, sent, kept))
                store(jnp.concatenate(rows_of + ups + (jnp.zeros((2, part), F32),), axis=0))

    def give(here_s, x_ref, gm_ref, att_ref, gb_ref, ffn_ref, attn_ref, sent_ref, kept_ref, out_ref, scr):
        product(x_ref, gm_ref, att_ref, gb_ref, scr)
        out_ref[:width, :] = scr[...].astype(BF16)

        def store(value):
            out_ref[width:, :] = value.astype(BF16)

        small(here_s, ffn_ref, attn_ref, sent_ref, kept_ref, store)

    def own(
        here_s, x_ref, gm_ref, att_ref, gb_ref, ffn_ref, attn_ref, sent_ref, kept_ref, got_ref,
        send_a, keep_a, send_b, keep_b, scr, cut,
    ):
        product(x_ref, gm_ref, att_ref, gb_ref, scr)
        term = scr[...] + got_ref[:width, :].astype(F32)
        cut[...] = term.reshape(cut.shape)
        deal(cut, here_s, (send_a, keep_a, send_b, keep_b), 4, pieces)

        def store(value):
            extra = (value + got_ref[width:, :].astype(F32)).astype(BF16)
            send_a[8 * pieces] = extra
            keep_a[8 * pieces] = extra

        small(here_s, ffn_ref, attn_ref, sent_ref, kept_ref, store)

    in_specs = [
        once((rows, width)),
        pl.BlockSpec((rows, part), lambda i, h: (0, h[which] * 3 + jnp.minimum(i, 2))),
        once((rows, width)),
        pl.BlockSpec((rows, part), lambda i, h: (0, h[which]), pipeline_mode=pl.Buffered(1)),
    ] + [once(item.shape) for item in vectors]
    args = [x, grad_mixed, attended, grad_branch, *vectors]
    flops = 4 * rows * width * width
    if got is None:
        return call(
            give, "proj_give", (4,), (here,), in_specs,
            pl.BlockSpec((width + 8, part), lambda i, *_: (0, i)),
            shaped((width + 8, 4 * part), BF16),
            [pltpu.VMEM((width, part), F32)], flops, 9e6, args, 20, 0, (0,),
        )
    return call(
        own, "proj_own", (4,), (here,),
        in_specs + [pl.BlockSpec((width + 8, part), lambda i, *_: (0, i))],
        [
            pl.BlockSpec((8 * pieces + extra, 8, part), lambda i, *_: (0, 0, i))
            for extra in (1, 1, 0, 0)
        ],
        [shaped((8 * pieces + extra, 8, 4 * part), BF16) for extra in (1, 1, 0, 0)],
        [pltpu.VMEM((width, part), F32), pltpu.VMEM((4, 2, 2, 2, pieces, 8, part), F32)],
        flops, 11e6, args + [got], 24, 1, (0, 1, 2, 3),
    )


def input_gradient(grad_mixed, w_qkv, grad_resid, rows_step):
    rows, width = grad_resid.shape

    def kernel(gm_ref, wq_ref, gr_ref, out_ref):
        out_ref[...] = (dot_t(gm_ref[...], wq_ref[...]) + gr_ref[...]).astype(BF16)

    return call(
        kernel, "input_grad", (rows // rows_step,), (),
        [
            pl.BlockSpec((rows_step, 3 * width), lambda i: (i, 0)),
            once((width, 3 * width)),
            pl.BlockSpec((rows_step, width), lambda i: (i, 0)),
        ],
        pl.BlockSpec((rows_step, width), lambda i: (i, 0)),
        shaped((rows, width), BF16), [], 6 * rows * width * width, 13e6,
        (grad_mixed, w_qkv, grad_resid), 20,
    )


def copied(item, here, block):
    rows, width = item.shape

    def kernel(here_s, in_ref, out_ref):
        out_ref[...] = in_ref[...]

    spec = pl.BlockSpec((block, width), lambda i, *_: (i, 0))
    return call(
        kernel, "copied", (rows // block,), (here,), [spec], spec,
        shaped((rows, width), item.dtype), [], 1, 3e6, (item,), 4,
    )


def small_call(kernel, name, here, args, outs, vmem=12):
    return pl.pallas_call(
        kernel,
        in_specs=[pl.BlockSpec(memory_space=pltpu.SMEM)]
        + [pl.BlockSpec(memory_space=pltpu.VMEM)] * len(args),
        out_specs=[pl.BlockSpec(memory_space=pltpu.VMEM)] * len(outs),
        out_shape=outs,
        compiler_params=pltpu.CompilerParams(vmem_limit_bytes=vmem * MIB),
        cost_estimate=pl.CostEstimate(flops=int(1e6 * COST), bytes_accessed=int(4e6 * COST), transcendentals=0),
        name=name,
    )(here, *args)


def add(left, right):
    return (left.astype(F32) + right.astype(F32)).astype(BF16)


def fold_second(keep_a, got_a, keep_b, got_b, here, pieces, extra):
    cols = keep_a.shape[2]

    def kernel(here_s, ka, ga, kb, gb, send_a, left_a, send_b, left_b):
        x, y = here_s[2], here_s[3]
        for z in range(4):
            at = pl.ds(z * pieces, pieces)

            def sum_of(keep, got, other):
                rows = pl.ds(z * 2 * pieces + other * pieces, pieces)
                return add(keep[rows], got[rows])

            send_a[at] = sum_of(ka, ga, 1 - y)
            left_a[at] = sum_of(ka, ga, y)
            send_b[at] = sum_of(kb, gb, 1 - x)
            left_b[at] = sum_of(kb, gb, x)
        if extra:
            total = add(ka[8 * pieces], ga[8 * pieces])
            send_a[4 * pieces] = total
            left_a[4 * pieces] = total

    a_out = shaped((4 * pieces + extra, 8, cols), BF16)
    b_out = shaped((4 * pieces, 8, cols), BF16)
    return small_call(
        kernel, "fold_second", here, (keep_a, got_a, keep_b, got_b), [a_out, a_out, b_out, b_out]
    )


def fold_third(terms, here, pieces, extra):
    cols = terms[0][0].shape[2]
    count = len(terms)

    def kernel(here_s, *refs):
        ins, (send, left) = refs[:-2], refs[-2:]
        low = here_s[4]
        for high in range(2):
            for number in range(2 * count):
                keep, got = ins[2 * number : 2 * number + 2]
                at = pl.ds((high * 2 * count + number) * pieces, pieces)
                for out, pick in ((send, 1 - low), (left, low)):
                    rows = pl.ds((high * 2 + pick) * pieces, pieces)
                    out[at] = add(keep[rows], got[rows])
        if extra:
            total = add(ins[0][4 * pieces], ins[1][4 * pieces])
            send[4 * count * pieces] = total
            left[4 * count * pieces] = total

    out = shaped((4 * count * pieces + extra, 8, cols), BF16)
    args = [item for term in terms for item in term]
    return small_call(kernel, "fold_third", here, args, [out, out])


def fold_fourth(keep, got, here, extra):
    cols = keep.shape[2]
    count = (keep.shape[0] - extra) // 2

    def kernel(here_s, keep_ref, got_ref, send, left):
        high = here_s[5]
        for out, pick in ((send, 1 - high), (left, high)):
            rows = pl.ds(pick * count, count)
            out[:count] = add(keep_ref[rows], got_ref[rows])
        if extra:
            total = add(keep_ref[2 * count], got_ref[2 * count])
            send[count] = total
            left[count] = total

    out = shaped((count + extra, 8, cols), BF16)
    return small_call(kernel, "fold_fourth", here, (keep, got), [out, out])


def fold_last(keep, got, here, extra):
    cols = keep.shape[2]
    count = keep.shape[0] - extra

    def kernel(here_s, keep_ref, got_ref, *outs):
        outs[0][...] = add(keep_ref[:count], got_ref[:count])
        if extra:
            outs[1][0] = add(keep_ref[count], got_ref[count])

    outs = [shaped((count, 8, cols), BF16)] + [shaped((1, 8, cols), BF16)] * extra
    return small_call(kernel, "fold_last", here, (keep, got), outs)


def chosen_part(here_s, refs, core, side, at):
    me, gx, gc, gd = [item[at].astype(F32) for item in refs]
    same_core, same_side = here_s[0] == core, here_s[2] == side
    return jnp.where(same_core, jnp.where(same_side, me, gx), jnp.where(same_side, gc, gd))


def feed_blocks(parts, here, pieces, width):
    cols = parts[0].shape[2]
    half = width // 2
    folds = cols // half
    rows = 2 * pieces * 8

    def kernel(here_s, me, gx, gc, gd, down_ref, up_ref):
        refs = (me, gx, gc, gd)
        for core in range(2):
            for side in range(2):
                tall = side * folds * rows
                for ab in range(2):
                    at = pl.ds(ab * pieces, pieces)
                    value = chosen_part(here_s, refs, core, side, at).reshape(rows // 2, cols)
                    for fold in range(folds):
                        start = tall + (ab * folds + fold) * (rows // 2)
                        down_ref[start : start + rows // 2, core * half : (core + 1) * half] = value[
                            :, fold * half : (fold + 1) * half
                        ]
                at = pl.ds(2 * pieces, 2 * pieces)
                value = chosen_part(here_s, refs, core, side, at).reshape(rows, cols)
                up_ref[side * rows : (side + 1) * rows, core * cols : (core + 1) * cols] = value

    outs = [shaped((2 * folds * rows, width), F32), shaped((2 * rows, 2 * cols), F32)]
    return small_call(kernel, "feed_blocks", here, parts, outs, 16)


def projection_blocks(parts, vectors, here, pieces):
    cols = parts[0].shape[2]
    rows = 2 * pieces * 8
    cut = cols // 4 * 3
    width = cols // 2
    small = width // 8
    large = cols // 4

    def kernel(here_s, me, gx, gc, gd, vec_ref, qkv_ref, out_ref, *outs):
        refs = (me, gx, gc, gd)
        for core in range(2):
            for side in range(2):
                value = chosen_part(here_s, refs, core, side, slice(None)).reshape(rows, cols)
                at = slice(side * rows, (side + 1) * rows)
                qkv_ref[at, core * cut : (core + 1) * cut] = value[:, :cut]
                out_ref[at, core * (cols - cut) : (core + 1) * (cols - cut)] = value[:, cut:]
        table = vec_ref[0].astype(F32)
        wide = here_s[6]
        shift = lax.rem(width - wide * small, width)
        left, right = pltpu.roll(table[:, :width], shift, 1), pltpu.roll(table[:, width:], shift, 1)
        for row in range(4):
            outs[2 * row][...] = left[row : row + 1, :small]
            outs[2 * row + 1][...] = right[row : row + 1, :small]
        turned = pltpu.roll(table, lax.rem(cols - lax.rem(wide, 4) * large, cols), 1)
        outs[8][...] = jnp.where(wide < 4, turned[4:5, :large], turned[5:6, :large])

    outs = [shaped((2 * rows, 2 * cut), F32), shaped((2 * rows, 2 * (cols - cut)), F32)]
    outs += [shaped((1, small), F32)] * 8 + [shaped((1, large), F32)]
    return small_call(kernel, "projection_blocks", here, (*parts, vectors), outs, 16)


def after(item, *earlier):
    return lax.optimization_barrier((item, *earlier))[0]


def swap(item, axis, step):
    count = lax.axis_size(axis)
    return lax.ppermute(item, axis, [(index, index ^ step) for index in range(count)])


def quarters(mine):
    across = swap(mine, "narrow", 2)
    return mine, across, swap(mine, "narrow", 1), swap(across, "narrow", 1)


def regroup_rows(sent, bucket, wide_count, batches):
    span, width = sent.shape[1:]
    if wide_count == batches:
        got = lax.all_to_all(sent, "wide", split_axis=0, concat_axis=0, tiled=True)
        return got.reshape(batches * span, width)
    send = jnp.zeros((wide_count, span, width), sent.dtype).at[bucket].set(sent)
    got = lax.all_to_all(send, "wide", split_axis=0, concat_axis=0, tiled=True)
    marks = jnp.zeros((wide_count, 1), jnp.int32).at[bucket].set(1)
    filled = lax.all_to_all(marks, "wide", split_axis=0, concat_axis=0, tiled=True)[:, 0]
    place = jnp.where(filled > 0, jnp.cumsum(filled) - filled, batches)
    chosen = (
        jnp.zeros((batches,), jnp.int32)
        .at[place]
        .set(jnp.arange(wide_count, dtype=jnp.int32), mode="drop")
    )
    return got[chosen].reshape(batches * span, width)


def sum_anywhere(item, wide_count, narrow_count):
    blocks = item.astype(F32).reshape(wide_count, -1)
    extent = blocks.shape[1]
    padded = (extent + narrow_count - 1) // narrow_count * narrow_count
    blocks = jnp.pad(blocks, ((0, 0), (0, padded - extent))).reshape(-1)
    share = lax.psum_scatter(blocks, ("wide", "narrow"), scatter_dimension=0, tiled=True)
    whole = lax.all_gather(share.astype(BF16), "narrow", axis=0, tiled=True).astype(F32)
    return whole[:extent].reshape((item.shape[0] // wide_count,) + item.shape[1:])


def body(
    tokens, bucket, lengths, pairing, targets, w_qkv, bias_q, bias_v, w_out, bias_out,
    gain_attn, shift_attn, w_up, bias_up, w_down, bias_down, gain_ffn, shift_ffn,
):
    wide_count, narrow_count = lax.axis_size("wide"), lax.axis_size("narrow")
    batches = bucket.shape[0]
    rows, width = tokens.shape
    span = rows // batches
    paired = (wide_count, narrow_count) == (8, 4)
    wide, narrow = lax.axis_index("wide"), lax.axis_index("narrow")
    if paired:
        core = narrow % 2
        here = jnp.stack(
            [core, 1 - core, narrow // 2, wide % 2, wide // 2 % 2, wide // 4, wide, narrow]
        ).astype(jnp.int32)
    else:
        here = jnp.arange(8, dtype=jnp.int32)
    table = vector_table(
        [bias_q, bias_v, bias_out, gain_attn, shift_attn, bias_down, gain_ffn, shift_ffn, bias_up], width
    )
    ordered = wide_count == batches
    slots = bucket if ordered else jnp.arange(batches, dtype=jnp.int32)
    pieces = width // 32 // 8

    qkv, probs, attended, n_attn, spread, sid = attention_forward(
        tokens, w_qkv, w_out, table, bucket, lengths, wide_count // batches, span, 2 * span
    )
    active, slope, hidden_t, sent, gres, grad_second, vec_ffn = feed_forward(
        n_attn, w_up, w_down, table, sid, slots, pairing, targets, batches, 2 * span
    )
    ups = (grad_second, slope, hidden_t, w_down)
    heads = (n_attn, spread, table, w_out, qkv, probs)
    down_sent = down_terms(active, grad_second, here, 1)
    if paired:
        up_sent, gi_sent, bup_sent = up_terms(*ups, after(here, down_sent), 1)
        down_dealt = down_terms(active, grad_second, after(here, bup_sent), 0, swap(down_sent, "narrow", 1))
        down_a, down_b = swap(down_dealt[0], "narrow", 2), swap(down_dealt[2], "wide", 1)
        encoded = regroup_rows(after(sent, down_dealt[1]), bucket, wide_count, batches)
        gh = hidden_gradient(gi_sent, w_up, after(here, down_dealt[1]), 1)
        *up_dealt, gi_kept, bup_kept = up_terms(
            *ups, after(here, gh), 0, swap(up_sent, "narrow", 1)
        )
        up_a, up_b = swap(up_dealt[0], "narrow", 2), swap(up_dealt[2], "wide", 1)
        down_dealt = fold_second(
            down_dealt[1], down_a, down_dealt[3], down_b, after(here, bup_kept), pieces, 0
        )
        down_a, down_b = swap(down_dealt[0], "wide", 1), swap(down_dealt[2], "narrow", 2)
        gr, gb, gm, vec_attn = attention_backward(
            gh, gres, gi_kept, w_up, *heads, after(here, down_dealt[1]), 0, span, 2 * span
        )
        up_dealt = fold_second(
            up_dealt[1], up_a, up_dealt[3], up_b, after(here, vec_attn, encoded), pieces, 0
        )
        up_a, up_b = swap(up_dealt[0], "wide", 1), swap(up_dealt[2], "narrow", 2)
        projections = (tokens, gm, attended, gb, (vec_ffn, vec_attn, bup_sent, bup_kept))
        proj_sent = projection_terms(*projections, after(here, up_dealt[1]), 1)
        grad_tokens = input_gradient(after(gm, proj_sent), w_qkv, gr, 2 * span)
        send, feed = fold_third(
            [(down_dealt[1], down_a, down_dealt[3], down_b), (up_dealt[1], up_a, up_dealt[3], up_b)],
            after(here, grad_tokens), pieces, 0,
        )
        feed_got = swap(send, "wide", 2)
        proj_dealt = projection_terms(
            *projections, after(here, feed), 0, swap(proj_sent, "narrow", 1)
        )
        proj_a, proj_b = swap(proj_dealt[0], "narrow", 2), swap(proj_dealt[2], "wide", 1)
        send, feed = fold_fourth(feed, feed_got, after(here, proj_dealt[1]), 0)
        feed_got = swap(send, "wide", 4)
        encoded = copied(encoded, after(here, feed), span)
        (feed,) = fold_last(feed, feed_got, after(here, encoded), 0)
        proj_dealt = fold_second(
            proj_dealt[1], proj_a, proj_dealt[3], proj_b, after(here, feed), pieces, 1
        )
        proj_a, proj_b = swap(proj_dealt[0], "wide", 1), swap(proj_dealt[2], "narrow", 2)
        feed = quarters(after(feed, proj_dealt[1]))
        send, proj = fold_third(
            [(proj_dealt[1], proj_a, proj_dealt[3], proj_b)], here, pieces, 1
        )
        proj_got = swap(send, "wide", 2)
        grad_w_down, grad_w_up = feed_blocks(feed, after(here, proj), pieces, width)
        send, proj = fold_fourth(proj, proj_got, after(here, grad_w_down), 1)
        proj_got = swap(send, "wide", 4)
        proj, vectors = fold_last(proj, proj_got, here, 1)
        proj = quarters(proj)
        grad_w_qkv, grad_w_out, *small = projection_blocks(proj, vectors, here, pieces)
        small = [item.reshape(-1) for item in small]
    else:
        encoded = regroup_rows(sent, bucket, wide_count, batches)
        down_kept = down_terms(active, grad_second, here, 0)
        up_sent, gi_sent, bup_sent = up_terms(*ups, here, 1)
        up_kept, gi_kept, bup_kept = up_terms(*ups, here, 0)
        gh = hidden_gradient(gi_sent, w_up, here, 1)
        gr, gb, gm, vec_attn = attention_backward(
            gh, gres, gi_kept, w_up, *heads, here, 0, span, 2 * span
        )
        projections = (tokens, gm, attended, gb, (vec_ffn, vec_attn, bup_sent, bup_kept), here)
        grad_tokens = input_gradient(gm, w_qkv, gr, 2 * span)
        proj_sent, proj_kept = projection_terms(*projections, 1), projection_terms(*projections, 0)
        total = partial(sum_anywhere, wide_count=wide_count, narrow_count=narrow_count)
        cut = width // 2 * 3
        grad_w_down = total(jnp.concatenate([down_kept, down_sent], axis=1))
        grad_w_up = total(jnp.concatenate([up_kept, up_sent], axis=1))
        grad_w_qkv = total(jnp.concatenate([proj_kept[:width, :cut], proj_sent[:width, :cut]], axis=1))
        grad_w_out = total(jnp.concatenate([proj_kept[:width, cut:], proj_sent[:width, cut:]], axis=1))
        small = [
            total(item)
            for item in (*vec_ffn[:3], *vec_attn[:5], jnp.concatenate([bup_kept[0], bup_sent[0]]))
        ]
    gain_out, shift_out, b_down, b_q, b_v, b_out, g_attn, s_attn, b_up = small
    return (
        encoded, grad_tokens, grad_w_qkv, b_q, b_v, grad_w_out, b_out, g_attn, s_attn,
        grad_w_up, b_up, grad_w_down, b_down, gain_out, shift_out,
    )


def solution(mesh):
    split = P(("wide", "narrow"))
    in_specs = (
        P(("wide", "narrow"), None), split, split, P(("wide", "narrow"), None), split,
    ) + (P(),) * 13
    out_specs = (
        P(("wide", "narrow"), None), P(("wide", "narrow"), None),
        P("wide", None), P("wide"), P("wide"), P("wide", None), P("wide"), P("wide"), P("wide"),
        P("wide", None), P("wide"), P("wide", None), P("wide"), P("wide"), P("wide"),
    )
    return jax.shard_map(body, mesh=mesh, in_specs=in_specs, out_specs=out_specs, check_vma=False)
```

```python
from functools import partial

import jax
import jax.numpy as jnp
from jax import lax
from jax.experimental import pallas as pl
from jax.experimental.pallas import tpu as pltpu
from jax.sharding import PartitionSpec as P

HDIM = 64
KTOP = 12
NORM_EPS = 1e-12
COS_EPS = 1e-06
MASKED = -1000000000.0
LOSS_SCALE = 1024.0
F32 = jnp.float32
BF16 = jnp.bfloat16
LANES = 128
MIB = 1024 * 1024
LARGE = 100000
COST = 0.05
HALF_ROOT = 0.7071067811865476
BELL_RATE = -0.7213475204444817
BELL_PEAK = -1.3257480647361595
ROW_BQ, ROW_BV, ROW_BO, ROW_GA, ROW_SA, ROW_BD, ROW_GF, ROW_SF, ROW_BU = range(9)


def dot(left, right):
    return jnp.dot(left, right, preferred_element_type=F32)


def dot_t(left, right):
    return lax.dot_general(left, right, (((1,), (1,)), ((), ())), preferred_element_type=F32)


def t_dot(left, right):
    return lax.dot_general(left, right, (((0,), (0,)), ((), ())), preferred_element_type=F32)


def full(shape):
    return pl.BlockSpec(shape, lambda *_: (0,) * len(shape))


def once(shape):
    return pl.BlockSpec(shape, lambda *_: (0,) * len(shape), pipeline_mode=pl.Buffered(1))


def large(item):
    return item.size >= LARGE


def shaped(shape, dtype):
    return jax.ShapeDtypeStruct(shape, dtype)


def call(
    kernel, name, grid, prefetch, in_specs, out_specs, out_shape, scratch, flops, moved, args, vmem=24, free=0, loose=()
):
    single = not isinstance(out_shape, list)
    shapes = [out_shape] if single else out_shape
    shapes = [
        pltpu.HBM(item.shape, item.dtype) if large(item) and number not in loose else item
        for number, item in enumerate(shapes)
    ]
    out_shape = shapes[0] if single else shapes
    args = [
        pltpu.with_memory_space_constraint(item, pltpu.HBM) if large(item) and number < len(args) - free else item
        for number, item in enumerate(args)
    ]
    return pl.pallas_call(
        kernel,
        grid_spec=pltpu.PrefetchScalarGridSpec(
            num_scalar_prefetch=len(prefetch),
            grid=grid,
            in_specs=in_specs,
            out_specs=out_specs,
            scratch_shapes=scratch,
        ),
        out_shape=out_shape,
        compiler_params=pltpu.CompilerParams(
            dimension_semantics=("arbitrary",) * len(grid), vmem_limit_bytes=vmem * MIB
        ),
        cost_estimate=pl.CostEstimate(flops=int(flops * COST), bytes_accessed=int(moved * COST), transcendentals=0),
        name=name,
    )(*[pltpu.with_memory_space_constraint(item, pltpu.HBM) for item in prefetch], *args)


def norm_forward(values):
    center = values - jnp.mean(values, axis=-1, keepdims=True)
    spread = lax.rsqrt(jnp.mean(center * center, axis=-1, keepdims=True) + NORM_EPS)
    return center * spread, spread


def norm_backward(grad_out, normed, spread, gain):
    scaled = grad_out * gain
    mean_scaled = jnp.mean(scaled, axis=-1, keepdims=True)
    mean_product = jnp.mean(scaled * normed, axis=-1, keepdims=True)
    return spread * (scaled - mean_scaled - normed * mean_product)


def column_sum(values):
    return jnp.sum(values, axis=0, keepdims=True)


def gelu_pair(v):
    phi = 0.5 + 0.5 * lax.erf(v * HALF_ROOT)
    bell = jnp.exp2((v * v) * BELL_RATE + BELL_PEAK)
    return v * phi, phi + v * bell


def head_masks():
    lane = lax.broadcasted_iota(jnp.int32, (1, LANES), 1)
    low = (lane < HDIM).astype(F32)
    return low.astype(BF16), (1.0 - low).astype(BF16), lane < HDIM


def sentence_count(bucket_s, number, group_size):
    kind = bucket_s[number]
    if group_size > 1:
        kind = kind // group_size
    return jnp.maximum(1, lax.shift_right_logical(jnp.int32(KTOP), kind))


def row_sentences(batch, bucket_s, lengths_s, group_size, batches, sent, span):
    start = jnp.int32(0)
    for other in range(batches):
        start += jnp.where(other < batch, sentence_count(bucket_s, other, group_size), 0)
    count = sentence_count(bucket_s, batch, group_size)
    lane = lax.broadcasted_iota(jnp.int32, (8, span), 1)
    row = lax.broadcasted_iota(jnp.int32, (span, span), 0)
    passed_lane = jnp.zeros((8, span), jnp.int32)
    passed_row = jnp.zeros((span, span), jnp.int32)
    finish = jnp.int32(0)
    for number in range(KTOP):
        finish += lengths_s[jnp.minimum(start + number, sent - 1)]
        bound = jnp.where(number < count, finish, span)
        passed_lane += (lane >= bound).astype(jnp.int32)
        passed_row += (row >= bound).astype(jnp.int32)
    sid_lane = jnp.where(passed_lane < count, start + passed_lane, -1)
    sid_row = jnp.where(passed_row < count, start + passed_row, -1)
    return sid_lane, sid_row


def vector_table(vectors, width):
    def kernel(*refs):
        out_ref = refs[-1]
        at = 0
        for ref in refs[:-1]:
            for part in range(ref.shape[0] // width):
                out_ref[at : at + 1, :] = ref[part * width : (part + 1) * width].astype(F32).reshape(1, width)
                at += 1

    rows = sum(item.shape[0] for item in vectors) // width
    return pl.pallas_call(
        kernel,
        grid=(1,),
        in_specs=[full(item.shape) for item in vectors],
        out_specs=full((rows, width)),
        out_shape=shaped((rows, width), F32),
        compiler_params=pltpu.CompilerParams(vmem_limit_bytes=4 * MIB),
        name="vector_table",
    )(*[pltpu.with_memory_space_constraint(item, pltpu.HBM) for item in vectors])


def attention_forward(x, w_qkv, w_out, table, bucket, lengths, group_size, span, rows_step):
    rows, width = x.shape
    batches = rows // span
    pairs = width // LANES
    sent = lengths.shape[0]
    per_step = rows_step // span

    def kernel(bucket_s, lengths_s, x_ref, wq_ref, wo_ref, tab_ref, qkv_ref, p_ref, att_ref, n_ref, s_ref, sid_ref):
        step = pl.program_id(0)
        low_b, high_b, low_m = head_masks()
        x_in = x_ref[...]
        mixed = dot(x_in, wq_ref[:, :width]) + tab_ref[ROW_BQ : ROW_BQ + 1, :]
        qkv_ref[:, :width] = (mixed * 0.125).astype(BF16)
        qkv_ref[:, width : 2 * width] = dot(x_in, wq_ref[:, width : 2 * width]).astype(BF16)
        mixed = dot(x_in, wq_ref[:, 2 * width :]) + tab_ref[ROW_BV : ROW_BV + 1, :]
        qkv_ref[:, 2 * width :] = mixed.astype(BF16)
        eye = lax.broadcasted_iota(jnp.int32, (span, span), 0) == lax.broadcasted_iota(
            jnp.int32, (span, span), 1
        )
        for inner in range(per_step):
            sid_lane, sid_row = row_sentences(
                step * per_step + inner, bucket_s, lengths_s, group_size, batches, sent, span
            )
            sid_ref[inner] = sid_lane
            same = (sid_row == sid_lane[0:1, :]) & (sid_row >= 0)
            bias = jnp.where(same | eye, 0.0, MASKED)
            bias = jnp.concatenate([bias, bias], axis=0)
            base = slice(inner * span, (inner + 1) * span)
            for pair in range(pairs):
                cols = slice(pair * LANES, (pair + 1) * LANES)
                q = qkv_ref[base, cols]
                k = qkv_ref[base, width + pair * LANES : width + (pair + 1) * LANES]
                v = qkv_ref[base, 2 * width + pair * LANES : 2 * width + (pair + 1) * LANES]
                both = jnp.concatenate([q * low_b, q * high_b], axis=0)
                logits = dot_t(both, k) + bias
                raised = jnp.exp(logits - jnp.max(logits, axis=-1, keepdims=True))
                total = jnp.sum(raised, axis=-1, keepdims=True)
                probs = (raised * (1.0 / total)).astype(BF16)
                p_ref[inner, pair] = probs
                mix = dot(probs, v)
                att_ref[base, cols] = jnp.where(low_m, mix[:span], mix[span:]).astype(BF16)
        branch = dot(att_ref[...], wo_ref[...]) + tab_ref[ROW_BO : ROW_BO + 1, :]
        normed, spread = norm_forward(x_in.astype(F32) + branch)
        n_ref[...] = normed
        s_ref[...] = jnp.broadcast_to(spread, (rows_step, LANES))

    return call(
        kernel,
        "attn_fwd",
        (rows // rows_step,),
        (bucket, lengths),
        [
            pl.BlockSpec((rows_step, width), lambda i, *_: (i, 0)),
            once((width, 3 * width)),
            once((width, width)),
            once(table.shape),
        ],
        [
            pl.BlockSpec((rows_step, 3 * width), lambda i, *_: (i, 0)),
            pl.BlockSpec((per_step, pairs, 2 * span, span), lambda i, *_: (i, 0, 0, 0)),
            pl.BlockSpec((rows_step, width), lambda i, *_: (i, 0)),
            pl.BlockSpec((rows_step, width), lambda i, *_: (i, 0)),
            pl.BlockSpec((rows_step, LANES), lambda i, *_: (i, 0)),
            pl.BlockSpec((per_step, 8, span), lambda i, *_: (i, 0, 0)),
        ],
        [
            shaped((rows, 3 * width), BF16),
            shaped((batches, pairs, 2 * span, span), BF16),
            shaped((rows, width), BF16),
            shaped((rows, width), F32),
            shaped((rows, LANES), F32),
            shaped((batches, 8, span), jnp.int32),
        ],
        [],
        8 * rows * width * width * 2,
        30e6,
        (x, w_qkv, w_out, table),
        26,
    )


def feed_forward(n_attn, w_up, w_down, table, sid, slots, pairing, targets, slot_count, block):
    rows, width = n_attn.shape
    ff = w_up.shape[1]
    batches, _, span = sid.shape
    pair_count = targets.shape[0]
    side = -(-pair_count // 8) * 8
    chunk = width
    steps = ff // chunk
    blocks = rows // block
    per_block = block // span

    def kernel(
        slots_s, pairing_s, targets_s, n_ref, wu_ref, wd_ref, tab_ref, sid_ref,
        act_ref, dg_ref, ht_ref, enc_ref, gres_ref, gsl_ref, vec_ref, low_scr, acc_scr, spread_scr,
    ):
        step = pl.program_id(0)
        gain = tab_ref[ROW_GA : ROW_GA + 1, :]
        shift = tab_ref[ROW_SA : ROW_SA + 1, :]

        @pl.when(step == 0)
        def _():
            hidden = (n_ref[...] * gain + shift).astype(BF16)
            low_scr[...] = hidden
            ht_ref[...] = hidden.T
            acc_scr[...] = jnp.zeros_like(acc_scr)

        for number in range(blocks):
            base = slice(number * block, (number + 1) * block)
            inner = dot(low_scr[base, :], wu_ref[...]) + tab_ref[pl.ds(ROW_BU + step, 1), :]
            active, slope = gelu_pair(inner)
            active = active.astype(BF16)
            act_ref[base, :] = active
            dg_ref[base, :] = slope.astype(BF16)
            acc_scr[base, :] += dot(active, wd_ref[...])

        @pl.when(step == steps - 1)
        def _():
            gain_out = tab_ref[ROW_GF : ROW_GF + 1, :]
            shift_out = tab_ref[ROW_SF : ROW_SF + 1, :]
            slot = lax.broadcasted_iota(jnp.int32, (2 * side, span), 0)
            wanted = jnp.full((2 * side, span), -2, jnp.int32)
            goal = jnp.zeros((side, LANES), F32)
            goal_slot = lax.broadcasted_iota(jnp.int32, (side, LANES), 0)
            for number in range(pair_count):
                wanted = jnp.where(slot == number, pairing_s[0, 2 * number], wanted)
                wanted = jnp.where(slot == side + number, pairing_s[0, 2 * number + 1], wanted)
                goal = jnp.where(goal_slot == number, targets_s[number], goal)
            members = [
                (sid_ref[number][0:1, :] == wanted).astype(F32) for number in range(batches)
            ]
            sizes = jnp.zeros((2 * side, 1), F32)
            for member in members:
                sizes += jnp.sum(member, axis=-1, keepdims=True)
            share = 1.0 / jnp.maximum(sizes, 1.0)
            picks = [
                jnp.concatenate(members[number * per_block : (number + 1) * per_block], axis=1).astype(BF16)
                for number in range(blocks)
            ]
            ones = jnp.ones((2 * side, LANES), BF16)
            pooled = jnp.zeros((2 * side, width), F32)
            for number in range(blocks):
                base = slice(number * block, (number + 1) * block)
                resid = (
                    n_ref[base, :] * gain + shift + acc_scr[base, :] + tab_ref[ROW_BD : ROW_BD + 1, :]
                )
                normed, spread = norm_forward(resid)
                acc_scr[base, :] = normed
                spread_scr[base, :] = jnp.broadcast_to(spread, (block, LANES))
                out = normed * gain_out + shift_out
                high = out.astype(BF16)
                rest = (out - high.astype(F32)).astype(BF16)
                pooled += dot(picks[number], high) + dot(picks[number], rest)
                valid = t_dot(picks[number], ones)
                for col in range(width // LANES):
                    cols = slice(col * LANES, (col + 1) * LANES)
                    kept = (out[:, cols] * valid).astype(BF16)
                    for inner in range(per_block):
                        enc_ref[slots_s[number * per_block + inner], :, cols] = kept[
                            inner * span : (inner + 1) * span
                        ]
            pooled = pooled * share
            first, partner = pooled[:side], pooled[side:]
            cross = jnp.sum(first * partner, axis=-1, keepdims=True)
            scale_first = lax.rsqrt(jnp.sum(first * first, axis=-1, keepdims=True) + COS_EPS)
            scale_partner = lax.rsqrt(jnp.sum(partner * partner, axis=-1, keepdims=True) + COS_EPS)
            cosine = cross * scale_first * scale_partner
            factor = 2.0 * LOSS_SCALE * (cosine - goal[:, :1])
            both_scales = factor * scale_first * scale_partner
            grad_first = both_scales * partner - (factor * cosine * scale_first * scale_first) * first
            grad_partner = (
                both_scales * first - (factor * cosine * scale_partner * scale_partner) * partner
            )
            grad_home = jnp.concatenate([grad_first, grad_partner], axis=0) * share
            high = grad_home.astype(BF16)
            rest = (grad_home - high.astype(F32)).astype(BF16)
            vec_ref[...] = jnp.zeros_like(vec_ref)
            for number in range(blocks):
                base = slice(number * block, (number + 1) * block)
                grad_out = t_dot(picks[number], high) + t_dot(picks[number], rest)
                normed = acc_scr[base, :]
                resid = norm_backward(grad_out, normed, spread_scr[base, :1], gain_out)
                gres_ref[base, :] = resid
                low = resid.astype(BF16)
                gsl_ref[base, :] = low
                vec_ref[0:1, :] += column_sum(grad_out * normed)
                vec_ref[1:2, :] += column_sum(grad_out)
                vec_ref[2:3, :] += column_sum(low.astype(F32))

    return call(
        kernel,
        "ffn_fwd",
        (steps,),
        (slots, pairing, targets),
        [
            once((rows, width)),
            pl.BlockSpec((width, chunk), lambda j, *_: (0, j)),
            pl.BlockSpec((chunk, width), lambda j, *_: (j, 0)),
            once(table.shape),
            once((batches, 8, span)),
        ],
        [
            pl.BlockSpec((rows, chunk), lambda j, *_: (0, j)),
            pl.BlockSpec((rows, chunk), lambda j, *_: (0, j)),
            once((width, rows)),
            once((slot_count, span, width)),
            once((rows, width)),
            once((rows, width)),
            once((8, width)),
        ],
        [
            shaped((rows, ff), BF16),
            shaped((rows, ff), BF16),
            shaped((width, rows), BF16),
            shaped((slot_count, span, width), BF16),
            shaped((rows, width), F32),
            shaped((rows, width), BF16),
            shaped((8, width), F32),
        ],
        [
            pltpu.VMEM((rows, width), BF16),
            pltpu.VMEM((rows, width), F32),
            pltpu.VMEM((rows, LANES), F32),
        ],
        8 * rows * width * ff,
        40e6,
        (n_attn, w_up, w_down, table, sid),
        44,
    )


def deal(scratch, here_s, outs, z_count, pieces, folds=1):
    send_a, keep_a, send_b, keep_b = outs
    x, y = here_s[2], here_s[3]
    cols = scratch.shape[-1]
    for z in range(z_count):
        for other in range(2):
            at = pl.ds((z * 2 + other) * pieces, pieces)
            for fold in range(folds):
                part = pl.ds(fold * pieces, pieces)
                to = slice(fold * cols, (fold + 1) * cols)
                send_a[at, :, to] = scratch[z, other, 1 - x, 0, part].astype(BF16)
                keep_a[at, :, to] = scratch[z, other, x, 0, part].astype(BF16)
                send_b[at, :, to] = scratch[z, 1 - y, other, 1, part].astype(BF16)
                keep_b[at, :, to] = scratch[z, y, other, 1, part].astype(BF16)


def down_terms(active, grad_second, here, which, got=None):
    rows, ff = active.shape
    width = grad_second.shape[1]
    half = width // 2
    steps = 4
    tall = ff // steps
    pieces = width // 32 // 8
    folds = ff // width

    def give(here_s, act_ref, gs_ref, out_ref):
        out_ref[...] = t_dot(act_ref[...], gs_ref[...]).astype(BF16)

    def own(here_s, act_ref, gs_ref, got_ref, *rest):
        outs, scratch = rest[:4], rest[4]
        term = t_dot(act_ref[...], gs_ref[...]) + got_ref[...].astype(F32)
        scratch[...] = term.reshape(scratch.shape)
        deal(scratch, here_s, outs, 1, pieces, folds)

    in_specs = [
        pl.BlockSpec((rows, tall), lambda i, here_s: (0, i)),
        pl.BlockSpec((rows, half), lambda i, here_s: (0, here_s[which]), pipeline_mode=pl.Buffered(1)),
    ]
    flops = 2 * rows * ff * half
    if got is None:
        return call(
            give, "down_give", (steps,), (here,), in_specs,
            pl.BlockSpec((tall, half), lambda i, *_: (i, 0)),
            shaped((ff, half), BF16), [], flops, 9e6, (active, grad_second), 20, 0, (0,),
        )
    block = (2 * pieces, 8, folds * half)
    return call(
        own, "down_own", (steps,), (here,),
        in_specs + [pl.BlockSpec((tall, half), lambda i, *_: (i, 0))],
        [pl.BlockSpec(block, lambda i, *_: (i, 0, 0))] * 4,
        [shaped((8 * pieces, 8, folds * half), BF16)] * 4,
        [pltpu.VMEM((1, 2, 2, 2, folds * pieces, 8, half), F32)],
        flops, 11e6, (active, grad_second, got), 24, 1, (0, 2),
    )


def up_terms(grad_second, slope, hidden_t, w_down, here, which, got=None):
    rows, width = grad_second.shape
    ff = w_down.shape[0]
    half = ff // 2
    chunk = width
    steps = half // chunk
    block = rows // 4
    pieces = width // 32 // 8

    def kernel(here_s, gs_ref, dg_ref, ht_ref, wd_ref, *refs):
        if got is not None:
            got_ref, refs = refs[0], refs[1:]
            outs, refs = refs[:4], refs[4:]
        else:
            out_ref, refs = refs[0], refs[1:]
        gi_ref, bu_ref = refs[:2]
        sums = jnp.zeros((1, chunk), F32)
        for number in range(rows // block):
            base = slice(number * block, (number + 1) * block)
            grad_active = dot_t(gs_ref[base, :], wd_ref[...])
            low = (grad_active * dg_ref[base, :].astype(F32)).astype(BF16)
            gi_ref[base, :] = low
            sums += column_sum(low.astype(F32))
        bu_ref[...] = sums
        term = dot(ht_ref[...], gi_ref[...])
        if got is None:
            out_ref[...] = term.astype(BF16)
        else:
            scratch = refs[2]
            term += got_ref[...].astype(F32)
            scratch[...] = term.reshape(scratch.shape)
            deal(scratch, here_s, outs, 4, pieces)

    def col(i, here_s):
        return here_s[which] * steps + i

    in_specs = [
        once((rows, width)),
        pl.BlockSpec((rows, chunk), lambda i, h: (0, col(i, h))),
        once((width, rows)),
        pl.BlockSpec((chunk, width), lambda i, h: (col(i, h), 0)),
    ]
    args = [grad_second, slope, hidden_t, w_down]
    scratch = []
    if got is None:
        out_specs = [pl.BlockSpec((width, chunk), lambda i, *_: (0, i))]
        out_shape = [shaped((width, half), BF16)]
    else:
        in_specs.append(pl.BlockSpec((width, chunk), lambda i, *_: (0, i)))
        args.append(got)
        out_specs = [pl.BlockSpec((8 * pieces, 8, chunk), lambda i, *_: (0, 0, i))] * 4
        out_shape = [shaped((8 * pieces, 8, half), BF16)] * 4
        scratch.append(pltpu.VMEM((4, 2, 2, 2, pieces, 8, chunk), F32))
    return call(
        kernel, "up_give" if got is None else "up_own", (steps,), (here,), in_specs,
        out_specs
        + [
            pl.BlockSpec((rows, chunk), lambda i, *_: (0, i)),
            pl.BlockSpec((1, chunk), lambda i, *_: (0, i)),
        ],
        out_shape + [shaped((rows, half), BF16), shaped((1, half), F32)],
        scratch, 4 * rows * width * half, 16e6, args, 34, 0 if got is None else 1, (0,) if got is None else (0, 2),
    )


def hidden_gradient(grad_inner, w_up, here, which):
    rows, half = grad_inner.shape
    width = w_up.shape[0]
    block = rows // 2

    def kernel(here_s, gi_ref, wu_ref, out_ref):
        out_ref[...] = dot_t(gi_ref[...], wu_ref[...])

    return call(
        kernel, "hidden_grad", (rows // block,), (here,),
        [
            pl.BlockSpec((block, half), lambda i, h: (i, 0)),
            pl.BlockSpec((width, half), lambda i, h: (0, h[which]), pipeline_mode=pl.Buffered(1)),
        ],
        pl.BlockSpec((block, width), lambda i, h: (i, 0)),
        shaped((rows, width), F32), [], 2 * rows * width * half, 9e6, (grad_inner, w_up), 16,
    )


def attention_backward(gh, gres, grad_inner, w_up, n_attn, spread, table, w_out, qkv, probs, here, which, span, rows_step):
    rows, width = gh.shape
    half = grad_inner.shape[1]
    pairs = width // LANES
    per_step = rows_step // span

    def kernel(here_s, gh_ref, gres_ref, gi_ref, wu_ref, n_ref, s_ref, tab_ref, wo_ref, qkv_ref, p_ref, gr_ref, gb_ref, gm_ref, vec_ref, ga_scr):
        step = pl.program_id(0)
        low_b, high_b, low_m = head_masks()

        @pl.when(step == 0)
        def _():
            vec_ref[...] = jnp.zeros_like(vec_ref)

        normed = n_ref[...]
        grad_hidden = dot_t(gi_ref[...], wu_ref[...]) + gh_ref[...] + gres_ref[...]
        resid = norm_backward(grad_hidden, normed, s_ref[:, :1], tab_ref[ROW_GA : ROW_GA + 1, :])
        gr_ref[...] = resid
        low = resid.astype(BF16)
        gb_ref[...] = low
        vec_ref[2:3, :] += column_sum(low.astype(F32))
        vec_ref[3:4, :] += column_sum(grad_hidden * normed)
        vec_ref[4:5, :] += column_sum(grad_hidden)
        ga_scr[...] = dot_t(low, wo_ref[...]).astype(BF16)
        for inner in range(per_step):
            base = slice(inner * span, (inner + 1) * span)
            for pair in range(pairs):
                cols = slice(pair * LANES, (pair + 1) * LANES)
                k_cols = slice(width + pair * LANES, width + (pair + 1) * LANES)
                v_cols = slice(2 * width + pair * LANES, 2 * width + (pair + 1) * LANES)
                q, k, v = qkv_ref[base, cols], qkv_ref[base, k_cols], qkv_ref[base, v_cols]
                grad = ga_scr[base, cols]
                grads = jnp.concatenate([grad * low_b, grad * high_b], axis=0)
                both = jnp.concatenate([q * low_b, q * high_b], axis=0)
                weights = p_ref[inner, pair]
                wide = weights.astype(F32)
                grad_probs = dot_t(grads, v)
                balance = jnp.sum(wide * grad_probs, axis=-1, keepdims=True)
                grad_logits = (wide * (grad_probs - balance)).astype(BF16)
                mix = dot(grad_logits, k)
                grad_q = jnp.where(low_m, mix[:span], mix[span:]).astype(BF16) * jnp.bfloat16(0.125)
                grad_v = t_dot(weights, grads).astype(BF16)
                gm_ref[base, cols] = grad_q
                gm_ref[base, k_cols] = t_dot(grad_logits, both).astype(BF16)
                gm_ref[base, v_cols] = grad_v
                vec_ref[0:1, cols] += column_sum(grad_q.astype(F32))
                vec_ref[1:2, cols] += column_sum(grad_v.astype(F32))

    def rows_of(cols):
        return pl.BlockSpec((rows_step, cols), lambda i, h: (i, 0))

    return call(
        kernel,
        "attn_bwd",
        (rows // rows_step,),
        (here,),
        [
            rows_of(width), rows_of(width), rows_of(half),
            pl.BlockSpec((width, half), lambda i, h: (0, h[which]), pipeline_mode=pl.Buffered(1)),
            rows_of(width), rows_of(LANES),
            once(table.shape), once((width, width)), rows_of(3 * width),
            pl.BlockSpec((per_step, pairs, 2 * span, span), lambda i, h: (i, 0, 0, 0)),
        ],
        [rows_of(width), rows_of(width), rows_of(3 * width), full((8, width))],
        [
            shaped((rows, width), F32), shaped((rows, width), BF16),
            shaped((rows, 3 * width), BF16), shaped((8, width), F32),
        ],
        [pltpu.VMEM((rows_step, width), BF16)],
        8 * rows * width * width * 2,
        40e6,
        (gh, gres, grad_inner, w_up, n_attn, spread, table, w_out, qkv, probs),
        34,
    )


def projection_terms(x, grad_mixed, attended, grad_branch, vectors, here, which, got=None):
    rows, width = x.shape
    part = width // 2
    pieces = width // 32 // 8

    def product(x_ref, gm_ref, att_ref, gb_ref, scr):
        step = pl.program_id(0)

        @pl.when(step < 3)
        def _():
            scr[...] = t_dot(x_ref[...], gm_ref[...])

        @pl.when(step == 3)
        def _():
            scr[...] = t_dot(att_ref[...], gb_ref[...])

    def small(here_s, ffn_ref, attn_ref, sent_ref, kept_ref, store):
        first = here_s[0] == 0
        for step in range(4):

            @pl.when(pl.program_id(0) == step)
            def _():
                side, at = step // 2, slice(step % 2 * part, (step % 2 + 1) * part)
                wide = slice(step * part, (step + 1) * part)
                rows_of = (
                    (ffn_ref[0:1, at], ffn_ref[2:3, at], attn_ref[1:2, at], attn_ref[3:4, at]),
                    (ffn_ref[1:2, at], attn_ref[0:1, at], attn_ref[2:3, at], attn_ref[4:5, at]),
                )[side]
                sent, kept = sent_ref[:, wide], kept_ref[:, wide]
                ups = (jnp.where(first, kept, sent), jnp.where(first, sent, kept))
                store(jnp.concatenate(rows_of + ups + (jnp.zeros((2, part), F32),), axis=0))

    def give(here_s, x_ref, gm_ref, att_ref, gb_ref, ffn_ref, attn_ref, sent_ref, kept_ref, out_ref, scr):
        product(x_ref, gm_ref, att_ref, gb_ref, scr)
        out_ref[:width, :] = scr[...].astype(BF16)

        def store(value):
            out_ref[width:, :] = value.astype(BF16)

        small(here_s, ffn_ref, attn_ref, sent_ref, kept_ref, store)

    def own(
        here_s, x_ref, gm_ref, att_ref, gb_ref, ffn_ref, attn_ref, sent_ref, kept_ref, got_ref,
        send_a, keep_a, send_b, keep_b, scr, cut,
    ):
        product(x_ref, gm_ref, att_ref, gb_ref, scr)
        term = scr[...] + got_ref[:width, :].astype(F32)
        cut[...] = term.reshape(cut.shape)
        deal(cut, here_s, (send_a, keep_a, send_b, keep_b), 4, pieces)

        def store(value):
            extra = (value + got_ref[width:, :].astype(F32)).astype(BF16)
            send_a[8 * pieces] = extra
            keep_a[8 * pieces] = extra

        small(here_s, ffn_ref, attn_ref, sent_ref, kept_ref, store)

    in_specs = [
        once((rows, width)),
        pl.BlockSpec((rows, part), lambda i, h: (0, h[which] * 3 + jnp.minimum(i, 2))),
        once((rows, width)),
        pl.BlockSpec((rows, part), lambda i, h: (0, h[which]), pipeline_mode=pl.Buffered(1)),
    ] + [once(item.shape) for item in vectors]
    args = [x, grad_mixed, attended, grad_branch, *vectors]
    flops = 4 * rows * width * width
    if got is None:
        return call(
            give, "proj_give", (4,), (here,), in_specs,
            pl.BlockSpec((width + 8, part), lambda i, *_: (0, i)),
            shaped((width + 8, 4 * part), BF16),
            [pltpu.VMEM((width, part), F32)], flops, 9e6, args, 20, 0, (0,),
        )
    return call(
        own, "proj_own", (4,), (here,),
        in_specs + [pl.BlockSpec((width + 8, part), lambda i, *_: (0, i))],
        [
            pl.BlockSpec((8 * pieces + extra, 8, part), lambda i, *_: (0, 0, i))
            for extra in (1, 1, 0, 0)
        ],
        [shaped((8 * pieces + extra, 8, 4 * part), BF16) for extra in (1, 1, 0, 0)],
        [pltpu.VMEM((width, part), F32), pltpu.VMEM((4, 2, 2, 2, pieces, 8, part), F32)],
        flops, 11e6, args + [got], 24, 1, (0, 1, 2, 3),
    )


def input_gradient(grad_mixed, w_qkv, grad_resid, rows_step):
    rows, width = grad_resid.shape

    def kernel(gm_ref, wq_ref, gr_ref, out_ref):
        out_ref[...] = (dot_t(gm_ref[...], wq_ref[...]) + gr_ref[...]).astype(BF16)

    return call(
        kernel, "input_grad", (rows // rows_step,), (),
        [
            pl.BlockSpec((rows_step, 3 * width), lambda i: (i, 0)),
            once((width, 3 * width)),
            pl.BlockSpec((rows_step, width), lambda i: (i, 0)),
        ],
        pl.BlockSpec((rows_step, width), lambda i: (i, 0)),
        shaped((rows, width), BF16), [], 6 * rows * width * width, 13e6,
        (grad_mixed, w_qkv, grad_resid), 20,
    )


def copied(item, here, block):
    rows, width = item.shape

    def kernel(here_s, in_ref, out_ref):
        out_ref[...] = in_ref[...]

    spec = pl.BlockSpec((block, width), lambda i, *_: (i, 0))
    return call(
        kernel, "copied", (rows // block,), (here,), [spec], spec,
        shaped((rows, width), item.dtype), [], 1, 3e6, (item,), 4,
    )


def small_call(kernel, name, here, args, outs, vmem=12):
    return pl.pallas_call(
        kernel,
        in_specs=[pl.BlockSpec(memory_space=pltpu.SMEM)]
        + [pl.BlockSpec(memory_space=pltpu.VMEM)] * len(args),
        out_specs=[pl.BlockSpec(memory_space=pltpu.VMEM)] * len(outs),
        out_shape=outs,
        compiler_params=pltpu.CompilerParams(vmem_limit_bytes=vmem * MIB),
        cost_estimate=pl.CostEstimate(flops=int(1e6 * COST), bytes_accessed=int(4e6 * COST), transcendentals=0),
        name=name,
    )(here, *args)


def add(left, right):
    return (left.astype(F32) + right.astype(F32)).astype(BF16)


def fold_second(keep_a, got_a, keep_b, got_b, here, pieces, extra):
    cols = keep_a.shape[2]

    def kernel(here_s, ka, ga, kb, gb, send_a, left_a, send_b, left_b):
        x, y = here_s[2], here_s[3]
        for z in range(4):
            at = pl.ds(z * pieces, pieces)

            def sum_of(keep, got, other):
                rows = pl.ds(z * 2 * pieces + other * pieces, pieces)
                return add(keep[rows], got[rows])

            send_a[at] = sum_of(ka, ga, 1 - y)
            left_a[at] = sum_of(ka, ga, y)
            send_b[at] = sum_of(kb, gb, 1 - x)
            left_b[at] = sum_of(kb, gb, x)
        if extra:
            total = add(ka[8 * pieces], ga[8 * pieces])
            send_a[4 * pieces] = total
            left_a[4 * pieces] = total

    a_out = shaped((4 * pieces + extra, 8, cols), BF16)
    b_out = shaped((4 * pieces, 8, cols), BF16)
    return small_call(
        kernel, "fold_second", here, (keep_a, got_a, keep_b, got_b), [a_out, a_out, b_out, b_out]
    )


def fold_third(terms, here, pieces, extra):
    cols = terms[0][0].shape[2]
    count = len(terms)

    def kernel(here_s, *refs):
        ins, (send, left) = refs[:-2], refs[-2:]
        low = here_s[4]
        for high in range(2):
            for number in range(2 * count):
                keep, got = ins[2 * number : 2 * number + 2]
                at = pl.ds((high * 2 * count + number) * pieces, pieces)
                for out, pick in ((send, 1 - low), (left, low)):
                    rows = pl.ds((high * 2 + pick) * pieces, pieces)
                    out[at] = add(keep[rows], got[rows])
        if extra:
            total = add(ins[0][4 * pieces], ins[1][4 * pieces])
            send[4 * count * pieces] = total
            left[4 * count * pieces] = total

    out = shaped((4 * count * pieces + extra, 8, cols), BF16)
    args = [item for term in terms for item in term]
    return small_call(kernel, "fold_third", here, args, [out, out])


def fold_fourth(keep, got, here, extra):
    cols = keep.shape[2]
    count = (keep.shape[0] - extra) // 2

    def kernel(here_s, keep_ref, got_ref, send, left):
        high = here_s[5]
        for out, pick in ((send, 1 - high), (left, high)):
            rows = pl.ds(pick * count, count)
            out[:count] = add(keep_ref[rows], got_ref[rows])
        if extra:
            total = add(keep_ref[2 * count], got_ref[2 * count])
            send[count] = total
            left[count] = total

    out = shaped((count + extra, 8, cols), BF16)
    return small_call(kernel, "fold_fourth", here, (keep, got), [out, out])


def fold_last(keep, got, here, extra):
    cols = keep.shape[2]
    count = keep.shape[0] - extra

    def kernel(here_s, keep_ref, got_ref, *outs):
        outs[0][...] = add(keep_ref[:count], got_ref[:count])
        if extra:
            outs[1][0] = add(keep_ref[count], got_ref[count])

    outs = [shaped((count, 8, cols), BF16)] + [shaped((1, 8, cols), BF16)] * extra
    return small_call(kernel, "fold_last", here, (keep, got), outs)


def chosen_part(here_s, refs, core, side, at):
    me, gx, gc, gd = [item[at].astype(F32) for item in refs]
    same_core, same_side = here_s[0] == core, here_s[2] == side
    return jnp.where(same_core, jnp.where(same_side, me, gx), jnp.where(same_side, gc, gd))


def feed_blocks(parts, here, pieces, width):
    cols = parts[0].shape[2]
    half = width // 2
    folds = cols // half
    rows = 2 * pieces * 8

    def kernel(here_s, me, gx, gc, gd, down_ref, up_ref):
        refs = (me, gx, gc, gd)
        for core in range(2):
            for side in range(2):
                tall = side * folds * rows
                for ab in range(2):
                    at = pl.ds(ab * pieces, pieces)
                    value = chosen_part(here_s, refs, core, side, at).reshape(rows // 2, cols)
                    for fold in range(folds):
                        start = tall + (ab * folds + fold) * (rows // 2)
                        down_ref[start : start + rows // 2, core * half : (core + 1) * half] = value[
                            :, fold * half : (fold + 1) * half
                        ]
                at = pl.ds(2 * pieces, 2 * pieces)
                value = chosen_part(here_s, refs, core, side, at).reshape(rows, cols)
                up_ref[side * rows : (side + 1) * rows, core * cols : (core + 1) * cols] = value

    outs = [shaped((2 * folds * rows, width), F32), shaped((2 * rows, 2 * cols), F32)]
    return small_call(kernel, "feed_blocks", here, parts, outs, 16)


def projection_blocks(parts, vectors, here, pieces):
    cols = parts[0].shape[2]
    rows = 2 * pieces * 8
    cut = cols // 4 * 3
    width = cols // 2
    small = width // 8
    large = cols // 4

    def kernel(here_s, me, gx, gc, gd, vec_ref, qkv_ref, out_ref, *outs):
        refs = (me, gx, gc, gd)
        for core in range(2):
            for side in range(2):
                value = chosen_part(here_s, refs, core, side, slice(None)).reshape(rows, cols)
                at = slice(side * rows, (side + 1) * rows)
                qkv_ref[at, core * cut : (core + 1) * cut] = value[:, :cut]
                out_ref[at, core * (cols - cut) : (core + 1) * (cols - cut)] = value[:, cut:]
        table = vec_ref[0].astype(F32)
        wide = here_s[6]
        shift = lax.rem(width - wide * small, width)
        left, right = pltpu.roll(table[:, :width], shift, 1), pltpu.roll(table[:, width:], shift, 1)
        for row in range(4):
            outs[2 * row][...] = left[row : row + 1, :small]
            outs[2 * row + 1][...] = right[row : row + 1, :small]
        turned = pltpu.roll(table, lax.rem(cols - lax.rem(wide, 4) * large, cols), 1)
        outs[8][...] = jnp.where(wide < 4, turned[4:5, :large], turned[5:6, :large])

    outs = [shaped((2 * rows, 2 * cut), F32), shaped((2 * rows, 2 * (cols - cut)), F32)]
    outs += [shaped((1, small), F32)] * 8 + [shaped((1, large), F32)]
    return small_call(kernel, "projection_blocks", here, (*parts, vectors), outs, 16)


def after(item, *earlier):
    return lax.optimization_barrier((item, *earlier))[0]


def swap(item, axis, step):
    count = lax.axis_size(axis)
    return lax.ppermute(item, axis, [(index, index ^ step) for index in range(count)])


def quarters(mine):
    across = swap(mine, "narrow", 2)
    return mine, across, swap(mine, "narrow", 1), swap(across, "narrow", 1)


def regroup_rows(sent, bucket, wide_count, batches):
    span, width = sent.shape[1:]
    if wide_count == batches:
        got = lax.all_to_all(sent, "wide", split_axis=0, concat_axis=0, tiled=True)
        return got.reshape(batches * span, width)
    send = jnp.zeros((wide_count, span, width), sent.dtype).at[bucket].set(sent)
    got = lax.all_to_all(send, "wide", split_axis=0, concat_axis=0, tiled=True)
    marks = jnp.zeros((wide_count, 1), jnp.int32).at[bucket].set(1)
    filled = lax.all_to_all(marks, "wide", split_axis=0, concat_axis=0, tiled=True)[:, 0]
    place = jnp.where(filled > 0, jnp.cumsum(filled) - filled, batches)
    chosen = (
        jnp.zeros((batches,), jnp.int32)
        .at[place]
        .set(jnp.arange(wide_count, dtype=jnp.int32), mode="drop")
    )
    return got[chosen].reshape(batches * span, width)


def sum_anywhere(item, wide_count, narrow_count):
    blocks = item.astype(F32).reshape(wide_count, -1)
    extent = blocks.shape[1]
    padded = (extent + narrow_count - 1) // narrow_count * narrow_count
    blocks = jnp.pad(blocks, ((0, 0), (0, padded - extent))).reshape(-1)
    share = lax.psum_scatter(blocks, ("wide", "narrow"), scatter_dimension=0, tiled=True)
    whole = lax.all_gather(share.astype(BF16), "narrow", axis=0, tiled=True).astype(F32)
    return whole[:extent].reshape((item.shape[0] // wide_count,) + item.shape[1:])


def body(
    tokens, bucket, lengths, pairing, targets, w_qkv, bias_q, bias_v, w_out, bias_out,
    gain_attn, shift_attn, w_up, bias_up, w_down, bias_down, gain_ffn, shift_ffn,
):
    wide_count, narrow_count = lax.axis_size("wide"), lax.axis_size("narrow")
    batches = bucket.shape[0]
    rows, width = tokens.shape
    span = rows // batches
    paired = (wide_count, narrow_count) == (8, 4)
    wide, narrow = lax.axis_index("wide"), lax.axis_index("narrow")
    if paired:
        core = narrow % 2
        here = jnp.stack(
            [core, 1 - core, narrow // 2, wide % 2, wide // 2 % 2, wide // 4, wide, narrow]
        ).astype(jnp.int32)
    else:
        here = jnp.arange(8, dtype=jnp.int32)
    table = vector_table(
        [bias_q, bias_v, bias_out, gain_attn, shift_attn, bias_down, gain_ffn, shift_ffn, bias_up], width
    )
    ordered = wide_count == batches
    slots = bucket if ordered else jnp.arange(batches, dtype=jnp.int32)
    pieces = width // 32 // 8

    qkv, probs, attended, n_attn, spread, sid = attention_forward(
        tokens, w_qkv, w_out, table, bucket, lengths, wide_count // batches, span, 2 * span
    )
    active, slope, hidden_t, sent, gres, grad_second, vec_ffn = feed_forward(
        n_attn, w_up, w_down, table, sid, slots, pairing, targets, batches, 2 * span
    )
    ups = (grad_second, slope, hidden_t, w_down)
    heads = (n_attn, spread, table, w_out, qkv, probs)
    down_sent = down_terms(active, grad_second, here, 1)
    if paired:
        encoded = regroup_rows(after(sent, down_sent), bucket, wide_count, batches)
        up_sent, gi_sent, bup_sent = up_terms(*ups, after(here, down_sent), 1)
        down_dealt = down_terms(active, grad_second, after(here, bup_sent), 0, swap(down_sent, "narrow", 1))
        down_a, down_b = swap(down_dealt[0], "narrow", 2), swap(down_dealt[2], "wide", 1)
        gh = hidden_gradient(gi_sent, w_up, after(here, down_dealt[1]), 1)
        *up_dealt, gi_kept, bup_kept = up_terms(
            *ups, after(here, gh), 0, swap(up_sent, "narrow", 1)
        )
        up_a, up_b = swap(up_dealt[0], "narrow", 2), swap(up_dealt[2], "wide", 1)
        down_dealt = fold_second(
            down_dealt[1], down_a, down_dealt[3], down_b, after(here, bup_kept), pieces, 0
        )
        down_a, down_b = swap(down_dealt[0], "wide", 1), swap(down_dealt[2], "narrow", 2)
        gr, gb, gm, vec_attn = attention_backward(
            gh, gres, gi_kept, w_up, *heads, after(here, down_dealt[1]), 0, span, 2 * span
        )
        up_dealt = fold_second(
            up_dealt[1], up_a, up_dealt[3], up_b, after(here, vec_attn, encoded), pieces, 0
        )
        up_a, up_b = swap(up_dealt[0], "wide", 1), swap(up_dealt[2], "narrow", 2)
        projections = (tokens, gm, attended, gb, (vec_ffn, vec_attn, bup_sent, bup_kept))
        proj_sent = projection_terms(*projections, after(here, up_dealt[1]), 1)
        send, feed = fold_third(
            [(down_dealt[1], down_a, down_dealt[3], down_b), (up_dealt[1], up_a, up_dealt[3], up_b)],
            after(here, proj_sent), pieces, 0,
        )
        feed_got = swap(send, "wide", 2)
        grad_tokens = input_gradient(after(gm, feed), w_qkv, gr, 2 * span)
        proj_dealt = projection_terms(
            *projections, after(here, grad_tokens), 0, swap(proj_sent, "narrow", 1)
        )
        proj_a, proj_b = swap(proj_dealt[0], "narrow", 2), swap(proj_dealt[2], "wide", 1)
        send, feed = fold_fourth(feed, feed_got, after(here, proj_dealt[1]), 0)
        feed_got = swap(send, "wide", 4)
        encoded = copied(encoded, after(here, feed), span)
        proj_dealt = fold_second(
            proj_dealt[1], proj_a, proj_dealt[3], proj_b, after(here, encoded), pieces, 1
        )
        proj_a, proj_b = swap(proj_dealt[0], "wide", 1), swap(proj_dealt[2], "narrow", 2)
        (feed,) = fold_last(feed, feed_got, after(here, proj_dealt[1]), 0)
        feed = quarters(feed)
        send, proj = fold_third(
            [(proj_dealt[1], proj_a, proj_dealt[3], proj_b)], here, pieces, 1
        )
        proj_got = swap(send, "wide", 2)
        grad_w_down, grad_w_up = feed_blocks(feed, after(here, proj), pieces, width)
        send, proj = fold_fourth(proj, proj_got, after(here, grad_w_down), 1)
        proj_got = swap(send, "wide", 4)
        proj, vectors = fold_last(proj, proj_got, here, 1)
        proj = quarters(proj)
        grad_w_qkv, grad_w_out, *small = projection_blocks(proj, vectors, here, pieces)
        small = [item.reshape(-1) for item in small]
    else:
        encoded = regroup_rows(sent, bucket, wide_count, batches)
        down_kept = down_terms(active, grad_second, here, 0)
        up_sent, gi_sent, bup_sent = up_terms(*ups, here, 1)
        up_kept, gi_kept, bup_kept = up_terms(*ups, here, 0)
        gh = hidden_gradient(gi_sent, w_up, here, 1)
        gr, gb, gm, vec_attn = attention_backward(
            gh, gres, gi_kept, w_up, *heads, here, 0, span, 2 * span
        )
        projections = (tokens, gm, attended, gb, (vec_ffn, vec_attn, bup_sent, bup_kept), here)
        grad_tokens = input_gradient(gm, w_qkv, gr, 2 * span)
        proj_sent, proj_kept = projection_terms(*projections, 1), projection_terms(*projections, 0)
        total = partial(sum_anywhere, wide_count=wide_count, narrow_count=narrow_count)
        cut = width // 2 * 3
        grad_w_down = total(jnp.concatenate([down_kept, down_sent], axis=1))
        grad_w_up = total(jnp.concatenate([up_kept, up_sent], axis=1))
        grad_w_qkv = total(jnp.concatenate([proj_kept[:width, :cut], proj_sent[:width, :cut]], axis=1))
        grad_w_out = total(jnp.concatenate([proj_kept[:width, cut:], proj_sent[:width, cut:]], axis=1))
        small = [
            total(item)
            for item in (*vec_ffn[:3], *vec_attn[:5], jnp.concatenate([bup_kept[0], bup_sent[0]]))
        ]
    gain_out, shift_out, b_down, b_q, b_v, b_out, g_attn, s_attn, b_up = small
    return (
        encoded, grad_tokens, grad_w_qkv, b_q, b_v, grad_w_out, b_out, g_attn, s_attn,
        grad_w_up, b_up, grad_w_down, b_down, gain_out, shift_out,
    )


def solution(mesh):
    split = P(("wide", "narrow"))
    in_specs = (
        P(("wide", "narrow"), None), split, split, P(("wide", "narrow"), None), split,
    ) + (P(),) * 13
    out_specs = (
        P(("wide", "narrow"), None), P(("wide", "narrow"), None),
        P("wide", None), P("wide"), P("wide"), P("wide", None), P("wide"), P("wide"), P("wide"),
        P("wide", None), P("wide"), P("wide", None), P("wide"), P("wide"), P("wide"),
    )
    return jax.shard_map(body, mesh=mesh, in_specs=in_specs, out_specs=out_specs, check_vma=False)
```

```python
from functools import partial

import jax
import jax.numpy as jnp
from jax import lax
from jax.experimental import pallas as pl
from jax.experimental.pallas import tpu as pltpu
from jax.sharding import PartitionSpec as P

HDIM = 64
KTOP = 12
NORM_EPS = 1e-12
COS_EPS = 1e-06
MASKED = -1000000000.0
LOSS_SCALE = 1024.0
F32 = jnp.float32
BF16 = jnp.bfloat16
LANES = 128
MIB = 1024 * 1024
LARGE = 100000
COST = 0.05
HALF_ROOT = 0.7071067811865476
BELL_RATE = -0.7213475204444817
BELL_PEAK = -1.3257480647361595
ROW_BQ, ROW_BV, ROW_BO, ROW_GA, ROW_SA, ROW_BD, ROW_GF, ROW_SF, ROW_BU = range(9)


def dot(left, right):
    return jnp.dot(left, right, preferred_element_type=F32)


def dot_t(left, right):
    return lax.dot_general(left, right, (((1,), (1,)), ((), ())), preferred_element_type=F32)


def t_dot(left, right):
    return lax.dot_general(left, right, (((0,), (0,)), ((), ())), preferred_element_type=F32)


def full(shape):
    return pl.BlockSpec(shape, lambda *_: (0,) * len(shape))


def once(shape):
    return pl.BlockSpec(shape, lambda *_: (0,) * len(shape), pipeline_mode=pl.Buffered(1))


def large(item):
    return item.size >= LARGE


def shaped(shape, dtype):
    return jax.ShapeDtypeStruct(shape, dtype)


def call(
    kernel, name, grid, prefetch, in_specs, out_specs, out_shape, scratch, flops, moved, args, vmem=24, free=0, loose=(), near=()
):
    single = not isinstance(out_shape, list)
    shapes = [out_shape] if single else out_shape
    shapes = [
        pltpu.HBM(item.shape, item.dtype) if large(item) and number not in loose else item
        for number, item in enumerate(shapes)
    ]
    out_shape = shapes[0] if single else shapes
    args = [
        pltpu.with_memory_space_constraint(item, pltpu.HBM)
        if large(item) and number < len(args) - free and number not in near
        else item
        for number, item in enumerate(args)
    ]
    return pl.pallas_call(
        kernel,
        grid_spec=pltpu.PrefetchScalarGridSpec(
            num_scalar_prefetch=len(prefetch),
            grid=grid,
            in_specs=in_specs,
            out_specs=out_specs,
            scratch_shapes=scratch,
        ),
        out_shape=out_shape,
        compiler_params=pltpu.CompilerParams(
            dimension_semantics=("arbitrary",) * len(grid), vmem_limit_bytes=vmem * MIB
        ),
        cost_estimate=pl.CostEstimate(flops=int(flops * COST), bytes_accessed=int(moved * COST), transcendentals=0),
        name=name,
    )(*[pltpu.with_memory_space_constraint(item, pltpu.HBM) for item in prefetch], *args)


def norm_forward(values):
    center = values - jnp.mean(values, axis=-1, keepdims=True)
    spread = lax.rsqrt(jnp.mean(center * center, axis=-1, keepdims=True) + NORM_EPS)
    return center * spread, spread


def norm_backward(grad_out, normed, spread, gain):
    scaled = grad_out * gain
    mean_scaled = jnp.mean(scaled, axis=-1, keepdims=True)
    mean_product = jnp.mean(scaled * normed, axis=-1, keepdims=True)
    return spread * (scaled - mean_scaled - normed * mean_product)


def column_sum(values):
    return jnp.sum(values, axis=0, keepdims=True)


def gelu_pair(v):
    phi = 0.5 + 0.5 * lax.erf(v * HALF_ROOT)
    bell = jnp.exp2((v * v) * BELL_RATE + BELL_PEAK)
    return v * phi, phi + v * bell


def head_masks():
    lane = lax.broadcasted_iota(jnp.int32, (1, LANES), 1)
    low = (lane < HDIM).astype(F32)
    return low.astype(BF16), (1.0 - low).astype(BF16), lane < HDIM


def sentence_count(bucket_s, number, group_size):
    kind = bucket_s[number]
    if group_size > 1:
        kind = kind // group_size
    return jnp.maximum(1, lax.shift_right_logical(jnp.int32(KTOP), kind))


def row_sentences(batch, bucket_s, lengths_s, group_size, batches, sent, span):
    start = jnp.int32(0)
    for other in range(batches):
        start += jnp.where(other < batch, sentence_count(bucket_s, other, group_size), 0)
    count = sentence_count(bucket_s, batch, group_size)
    lane = lax.broadcasted_iota(jnp.int32, (8, span), 1)
    row = lax.broadcasted_iota(jnp.int32, (span, span), 0)
    passed_lane = jnp.zeros((8, span), jnp.int32)
    passed_row = jnp.zeros((span, span), jnp.int32)
    finish = jnp.int32(0)
    for number in range(KTOP):
        finish += lengths_s[jnp.minimum(start + number, sent - 1)]
        bound = jnp.where(number < count, finish, span)
        passed_lane += (lane >= bound).astype(jnp.int32)
        passed_row += (row >= bound).astype(jnp.int32)
    sid_lane = jnp.where(passed_lane < count, start + passed_lane, -1)
    sid_row = jnp.where(passed_row < count, start + passed_row, -1)
    return sid_lane, sid_row


def vector_table(vectors, width):
    def kernel(*refs):
        out_ref = refs[-1]
        at = 0
        for ref in refs[:-1]:
            for part in range(ref.shape[0] // width):
                out_ref[at : at + 1, :] = ref[part * width : (part + 1) * width].astype(F32).reshape(1, width)
                at += 1

    rows = sum(item.shape[0] for item in vectors) // width
    return pl.pallas_call(
        kernel,
        grid=(1,),
        in_specs=[full(item.shape) for item in vectors],
        out_specs=full((rows, width)),
        out_shape=shaped((rows, width), F32),
        compiler_params=pltpu.CompilerParams(vmem_limit_bytes=4 * MIB),
        name="vector_table",
    )(*[pltpu.with_memory_space_constraint(item, pltpu.HBM) for item in vectors])


def attention_forward(x, w_qkv, w_out, table, bucket, lengths, group_size, span, rows_step):
    rows, width = x.shape
    batches = rows // span
    pairs = width // LANES
    sent = lengths.shape[0]
    per_step = rows_step // span

    def kernel(bucket_s, lengths_s, x_ref, wq_ref, wo_ref, tab_ref, qkv_ref, p_ref, att_ref, n_ref, s_ref, sid_ref):
        step = pl.program_id(0)
        low_b, high_b, low_m = head_masks()
        x_in = x_ref[...]
        mixed = dot(x_in, wq_ref[:, :width]) + tab_ref[ROW_BQ : ROW_BQ + 1, :]
        qkv_ref[:, :width] = (mixed * 0.125).astype(BF16)
        qkv_ref[:, width : 2 * width] = dot(x_in, wq_ref[:, width : 2 * width]).astype(BF16)
        mixed = dot(x_in, wq_ref[:, 2 * width :]) + tab_ref[ROW_BV : ROW_BV + 1, :]
        qkv_ref[:, 2 * width :] = mixed.astype(BF16)
        eye = lax.broadcasted_iota(jnp.int32, (span, span), 0) == lax.broadcasted_iota(
            jnp.int32, (span, span), 1
        )
        for inner in range(per_step):
            sid_lane, sid_row = row_sentences(
                step * per_step + inner, bucket_s, lengths_s, group_size, batches, sent, span
            )
            sid_ref[inner] = sid_lane
            same = (sid_row == sid_lane[0:1, :]) & (sid_row >= 0)
            bias = jnp.where(same | eye, 0.0, MASKED)
            bias = jnp.concatenate([bias, bias], axis=0)
            base = slice(inner * span, (inner + 1) * span)
            for pair in range(pairs):
                cols = slice(pair * LANES, (pair + 1) * LANES)
                q = qkv_ref[base, cols]
                k = qkv_ref[base, width + pair * LANES : width + (pair + 1) * LANES]
                v = qkv_ref[base, 2 * width + pair * LANES : 2 * width + (pair + 1) * LANES]
                both = jnp.concatenate([q * low_b, q * high_b], axis=0)
                logits = dot_t(both, k) + bias
                raised = jnp.exp(logits - jnp.max(logits, axis=-1, keepdims=True))
                total = jnp.sum(raised, axis=-1, keepdims=True)
                probs = (raised * (1.0 / total)).astype(BF16)
                p_ref[inner, pair] = probs
                mix = dot(probs, v)
                att_ref[base, cols] = jnp.where(low_m, mix[:span], mix[span:]).astype(BF16)
        branch = dot(att_ref[...], wo_ref[...]) + tab_ref[ROW_BO : ROW_BO + 1, :]
        normed, spread = norm_forward(x_in.astype(F32) + branch)
        n_ref[...] = normed
        s_ref[...] = jnp.broadcast_to(spread, (rows_step, LANES))

    return call(
        kernel,
        "attn_fwd",
        (rows // rows_step,),
        (bucket, lengths),
        [
            pl.BlockSpec((rows_step, width), lambda i, *_: (i, 0)),
            once((width, 3 * width)),
            once((width, width)),
            once(table.shape),
        ],
        [
            pl.BlockSpec((rows_step, 3 * width), lambda i, *_: (i, 0)),
            pl.BlockSpec((per_step, pairs, 2 * span, span), lambda i, *_: (i, 0, 0, 0)),
            pl.BlockSpec((rows_step, width), lambda i, *_: (i, 0)),
            pl.BlockSpec((rows_step, width), lambda i, *_: (i, 0)),
            pl.BlockSpec((rows_step, LANES), lambda i, *_: (i, 0)),
            pl.BlockSpec((per_step, 8, span), lambda i, *_: (i, 0, 0)),
        ],
        [
            shaped((rows, 3 * width), BF16),
            shaped((batches, pairs, 2 * span, span), BF16),
            shaped((rows, width), BF16),
            shaped((rows, width), F32),
            shaped((rows, LANES), F32),
            shaped((batches, 8, span), jnp.int32),
        ],
        [],
        8 * rows * width * width * 2,
        30e6,
        (x, w_qkv, w_out, table),
        26,
    )


def feed_forward(n_attn, w_up, w_down, table, sid, slots, pairing, targets, slot_count, block):
    rows, width = n_attn.shape
    ff = w_up.shape[1]
    batches, _, span = sid.shape
    pair_count = targets.shape[0]
    side = -(-pair_count // 8) * 8
    chunk = width
    steps = ff // chunk
    blocks = rows // block
    per_block = block // span

    def kernel(
        slots_s, pairing_s, targets_s, n_ref, wu_ref, wd_ref, tab_ref, sid_ref,
        act_ref, dg_ref, ht_ref, enc_ref, gres_ref, gsl_ref, vec_ref, low_scr, acc_scr, spread_scr,
    ):
        step = pl.program_id(0)
        gain = tab_ref[ROW_GA : ROW_GA + 1, :]
        shift = tab_ref[ROW_SA : ROW_SA + 1, :]

        @pl.when(step == 0)
        def _():
            hidden = (n_ref[...] * gain + shift).astype(BF16)
            low_scr[...] = hidden
            ht_ref[...] = hidden.T
            acc_scr[...] = jnp.zeros_like(acc_scr)

        for number in range(blocks):
            base = slice(number * block, (number + 1) * block)
            inner = dot(low_scr[base, :], wu_ref[...]) + tab_ref[pl.ds(ROW_BU + step, 1), :]
            active, slope = gelu_pair(inner)
            active = active.astype(BF16)
            act_ref[base, :] = active
            dg_ref[base, :] = slope.astype(BF16)
            acc_scr[base, :] += dot(active, wd_ref[...])

        @pl.when(step == steps - 1)
        def _():
            gain_out = tab_ref[ROW_GF : ROW_GF + 1, :]
            shift_out = tab_ref[ROW_SF : ROW_SF + 1, :]
            slot = lax.broadcasted_iota(jnp.int32, (2 * side, span), 0)
            wanted = jnp.full((2 * side, span), -2, jnp.int32)
            goal = jnp.zeros((side, LANES), F32)
            goal_slot = lax.broadcasted_iota(jnp.int32, (side, LANES), 0)
            for number in range(pair_count):
                wanted = jnp.where(slot == number, pairing_s[0, 2 * number], wanted)
                wanted = jnp.where(slot == side + number, pairing_s[0, 2 * number + 1], wanted)
                goal = jnp.where(goal_slot == number, targets_s[number], goal)
            members = [
                (sid_ref[number][0:1, :] == wanted).astype(F32) for number in range(batches)
            ]
            sizes = jnp.zeros((2 * side, 1), F32)
            for member in members:
                sizes += jnp.sum(member, axis=-1, keepdims=True)
            share = 1.0 / jnp.maximum(sizes, 1.0)
            picks = [
                jnp.concatenate(members[number * per_block : (number + 1) * per_block], axis=1).astype(BF16)
                for number in range(blocks)
            ]
            ones = jnp.ones((2 * side, LANES), BF16)
            pooled = jnp.zeros((2 * side, width), F32)
            for number in range(blocks):
                base = slice(number * block, (number + 1) * block)
                resid = (
                    n_ref[base, :] * gain + shift + acc_scr[base, :] + tab_ref[ROW_BD : ROW_BD + 1, :]
                )
                normed, spread = norm_forward(resid)
                acc_scr[base, :] = normed
                spread_scr[base, :] = jnp.broadcast_to(spread, (block, LANES))
                out = normed * gain_out + shift_out
                high = out.astype(BF16)
                rest = (out - high.astype(F32)).astype(BF16)
                pooled += dot(picks[number], high) + dot(picks[number], rest)
                valid = t_dot(picks[number], ones)
                for col in range(width // LANES):
                    cols = slice(col * LANES, (col + 1) * LANES)
                    kept = (out[:, cols] * valid).astype(BF16)
                    for inner in range(per_block):
                        enc_ref[slots_s[number * per_block + inner], :, cols] = kept[
                            inner * span : (inner + 1) * span
                        ]
            pooled = pooled * share
            first, partner = pooled[:side], pooled[side:]
            cross = jnp.sum(first * partner, axis=-1, keepdims=True)
            scale_first = lax.rsqrt(jnp.sum(first * first, axis=-1, keepdims=True) + COS_EPS)
            scale_partner = lax.rsqrt(jnp.sum(partner * partner, axis=-1, keepdims=True) + COS_EPS)
            cosine = cross * scale_first * scale_partner
            factor = 2.0 * LOSS_SCALE * (cosine - goal[:, :1])
            both_scales = factor * scale_first * scale_partner
            grad_first = both_scales * partner - (factor * cosine * scale_first * scale_first) * first
            grad_partner = (
                both_scales * first - (factor * cosine * scale_partner * scale_partner) * partner
            )
            grad_home = jnp.concatenate([grad_first, grad_partner], axis=0) * share
            high = grad_home.astype(BF16)
            rest = (grad_home - high.astype(F32)).astype(BF16)
            vec_ref[...] = jnp.zeros_like(vec_ref)
            for number in range(blocks):
                base = slice(number * block, (number + 1) * block)
                grad_out = t_dot(picks[number], high) + t_dot(picks[number], rest)
                normed = acc_scr[base, :]
                resid = norm_backward(grad_out, normed, spread_scr[base, :1], gain_out)
                gres_ref[base, :] = resid
                low = resid.astype(BF16)
                gsl_ref[base, :] = low
                vec_ref[0:1, :] += column_sum(grad_out * normed)
                vec_ref[1:2, :] += column_sum(grad_out)
                vec_ref[2:3, :] += column_sum(low.astype(F32))

    return call(
        kernel,
        "ffn_fwd",
        (steps,),
        (slots, pairing, targets),
        [
            once((rows, width)),
            pl.BlockSpec((width, chunk), lambda j, *_: (0, j)),
            pl.BlockSpec((chunk, width), lambda j, *_: (j, 0)),
            once(table.shape),
            once((batches, 8, span)),
        ],
        [
            pl.BlockSpec((rows, chunk), lambda j, *_: (0, j)),
            pl.BlockSpec((rows, chunk), lambda j, *_: (0, j)),
            once((width, rows)),
            once((slot_count, span, width)),
            once((rows, width)),
            once((rows, width)),
            once((8, width)),
        ],
        [
            shaped((rows, ff), BF16),
            shaped((rows, ff), BF16),
            shaped((width, rows), BF16),
            shaped((slot_count, span, width), BF16),
            shaped((rows, width), F32),
            shaped((rows, width), BF16),
            shaped((8, width), F32),
        ],
        [
            pltpu.VMEM((rows, width), BF16),
            pltpu.VMEM((rows, width), F32),
            pltpu.VMEM((rows, LANES), F32),
        ],
        8 * rows * width * ff,
        40e6,
        (n_attn, w_up, w_down, table, sid),
        38, 0, (2, 5),
    )


def deal(scratch, here_s, outs, z_count, pieces, folds=1):
    send_a, keep_a, send_b, keep_b = outs
    x, y = here_s[2], here_s[3]
    cols = scratch.shape[-1]
    for z in range(z_count):
        for other in range(2):
            at = pl.ds((z * 2 + other) * pieces, pieces)
            for fold in range(folds):
                part = pl.ds(fold * pieces, pieces)
                to = slice(fold * cols, (fold + 1) * cols)
                send_a[at, :, to] = scratch[z, other, 1 - x, 0, part].astype(BF16)
                keep_a[at, :, to] = scratch[z, other, x, 0, part].astype(BF16)
                send_b[at, :, to] = scratch[z, 1 - y, other, 1, part].astype(BF16)
                keep_b[at, :, to] = scratch[z, y, other, 1, part].astype(BF16)


def down_terms(active, grad_second, here, which, got=None):
    rows, ff = active.shape
    width = grad_second.shape[1]
    half = width // 2
    steps = 4
    tall = ff // steps
    pieces = width // 32 // 8
    folds = ff // width

    def give(here_s, act_ref, gs_ref, out_ref):
        out_ref[...] = t_dot(act_ref[...], gs_ref[...]).astype(BF16)

    def own(here_s, act_ref, gs_ref, got_ref, *rest):
        outs, scratch = rest[:4], rest[4]
        term = t_dot(act_ref[...], gs_ref[...]) + got_ref[...].astype(F32)
        scratch[...] = term.reshape(scratch.shape)
        deal(scratch, here_s, outs, 1, pieces, folds)

    in_specs = [
        pl.BlockSpec((rows, tall), lambda i, here_s: (0, i)),
        pl.BlockSpec((rows, half), lambda i, here_s: (0, here_s[which]), pipeline_mode=pl.Buffered(1)),
    ]
    flops = 2 * rows * ff * half
    if got is None:
        return call(
            give, "down_give", (steps,), (here,), in_specs,
            pl.BlockSpec((tall, half), lambda i, *_: (i, 0)),
            shaped((ff, half), BF16), [], flops, 9e6, (active, grad_second), 20, 0, (0,), (1,),
        )
    block = (2 * pieces, 8, folds * half)
    return call(
        own, "down_own", (steps,), (here,),
        in_specs + [pl.BlockSpec((tall, half), lambda i, *_: (i, 0))],
        [pl.BlockSpec(block, lambda i, *_: (i, 0, 0))] * 4,
        [shaped((8 * pieces, 8, folds * half), BF16)] * 4,
        [pltpu.VMEM((1, 2, 2, 2, folds * pieces, 8, half), F32)],
        flops, 11e6, (active, grad_second, got), 24, 1, (0, 2), (1,),
    )


def up_terms(grad_second, slope, hidden_t, w_down, here, which, got=None):
    rows, width = grad_second.shape
    ff = w_down.shape[0]
    half = ff // 2
    chunk = width
    steps = half // chunk
    block = rows // 4
    pieces = width // 32 // 8

    def kernel(here_s, gs_ref, dg_ref, ht_ref, wd_ref, *refs):
        if got is not None:
            got_ref, refs = refs[0], refs[1:]
            outs, refs = refs[:4], refs[4:]
        else:
            out_ref, refs = refs[0], refs[1:]
        gi_ref, bu_ref = refs[:2]
        sums = jnp.zeros((1, chunk), F32)
        for number in range(rows // block):
            base = slice(number * block, (number + 1) * block)
            grad_active = dot_t(gs_ref[base, :], wd_ref[...])
            low = (grad_active * dg_ref[base, :].astype(F32)).astype(BF16)
            gi_ref[base, :] = low
            sums += column_sum(low.astype(F32))
        bu_ref[...] = sums
        term = dot(ht_ref[...], gi_ref[...])
        if got is None:
            out_ref[...] = term.astype(BF16)
        else:
            scratch = refs[2]
            term += got_ref[...].astype(F32)
            scratch[...] = term.reshape(scratch.shape)
            deal(scratch, here_s, outs, 4, pieces)

    def col(i, here_s):
        return here_s[which] * steps + i

    in_specs = [
        once((rows, width)),
        pl.BlockSpec((rows, chunk), lambda i, h: (0, col(i, h))),
        once((width, rows)),
        pl.BlockSpec((chunk, width), lambda i, h: (col(i, h), 0)),
    ]
    args = [grad_second, slope, hidden_t, w_down]
    scratch = []
    if got is None:
        out_specs = [pl.BlockSpec((width, chunk), lambda i, *_: (0, i))]
        out_shape = [shaped((width, half), BF16)]
    else:
        in_specs.append(pl.BlockSpec((width, chunk), lambda i, *_: (0, i)))
        args.append(got)
        out_specs = [pl.BlockSpec((8 * pieces, 8, chunk), lambda i, *_: (0, 0, i))] * 4
        out_shape = [shaped((8 * pieces, 8, half), BF16)] * 4
        scratch.append(pltpu.VMEM((4, 2, 2, 2, pieces, 8, chunk), F32))
    return call(
        kernel, "up_give" if got is None else "up_own", (steps,), (here,), in_specs,
        out_specs
        + [
            pl.BlockSpec((rows, chunk), lambda i, *_: (0, i)),
            pl.BlockSpec((1, chunk), lambda i, *_: (0, i)),
        ],
        out_shape + [shaped((rows, half), BF16), shaped((1, half), F32)],
        scratch, 4 * rows * width * half, 16e6, args, 26, 0 if got is None else 1, (0,) if got is None else (0, 2, 4), (0, 2),
    )


def hidden_gradient(grad_inner, w_up, here, which):
    rows, half = grad_inner.shape
    width = w_up.shape[0]
    block = rows // 2

    def kernel(here_s, gi_ref, wu_ref, out_ref):
        out_ref[...] = dot_t(gi_ref[...], wu_ref[...])

    return call(
        kernel, "hidden_grad", (rows // block,), (here,),
        [
            pl.BlockSpec((block, half), lambda i, h: (i, 0)),
            pl.BlockSpec((width, half), lambda i, h: (0, h[which]), pipeline_mode=pl.Buffered(1)),
        ],
        pl.BlockSpec((block, width), lambda i, h: (i, 0)),
        shaped((rows, width), F32), [], 2 * rows * width * half, 9e6, (grad_inner, w_up), 16, 0, (0,),
    )


def attention_backward(gh, gres, grad_inner, w_up, n_attn, spread, table, w_out, qkv, probs, here, which, span, rows_step):
    rows, width = gh.shape
    half = grad_inner.shape[1]
    pairs = width // LANES
    per_step = rows_step // span

    def kernel(here_s, gh_ref, gres_ref, gi_ref, wu_ref, n_ref, s_ref, tab_ref, wo_ref, qkv_ref, p_ref, gr_ref, gb_ref, gm_ref, vec_ref, ga_scr):
        step = pl.program_id(0)
        low_b, high_b, low_m = head_masks()

        @pl.when(step == 0)
        def _():
            vec_ref[...] = jnp.zeros_like(vec_ref)

        normed = n_ref[...]
        grad_hidden = dot_t(gi_ref[...], wu_ref[...]) + gh_ref[...] + gres_ref[...]
        resid = norm_backward(grad_hidden, normed, s_ref[:, :1], tab_ref[ROW_GA : ROW_GA + 1, :])
        gr_ref[...] = resid
        low = resid.astype(BF16)
        gb_ref[...] = low
        vec_ref[2:3, :] += column_sum(low.astype(F32))
        vec_ref[3:4, :] += column_sum(grad_hidden * normed)
        vec_ref[4:5, :] += column_sum(grad_hidden)
        ga_scr[...] = dot_t(low, wo_ref[...]).astype(BF16)
        for inner in range(per_step):
            base = slice(inner * span, (inner + 1) * span)
            for pair in range(pairs):
                cols = slice(pair * LANES, (pair + 1) * LANES)
                k_cols = slice(width + pair * LANES, width + (pair + 1) * LANES)
                v_cols = slice(2 * width + pair * LANES, 2 * width + (pair + 1) * LANES)
                q, k, v = qkv_ref[base, cols], qkv_ref[base, k_cols], qkv_ref[base, v_cols]
                grad = ga_scr[base, cols]
                grads = jnp.concatenate([grad * low_b, grad * high_b], axis=0)
                both = jnp.concatenate([q * low_b, q * high_b], axis=0)
                weights = p_ref[inner, pair]
                wide = weights.astype(F32)
                grad_probs = dot_t(grads, v)
                balance = jnp.sum(wide * grad_probs, axis=-1, keepdims=True)
                grad_logits = (wide * (grad_probs - balance)).astype(BF16)
                mix = dot(grad_logits, k)
                grad_q = jnp.where(low_m, mix[:span], mix[span:]).astype(BF16) * jnp.bfloat16(0.125)
                grad_v = t_dot(weights, grads).astype(BF16)
                gm_ref[base, cols] = grad_q
                gm_ref[base, k_cols] = t_dot(grad_logits, both).astype(BF16)
                gm_ref[base, v_cols] = grad_v
                vec_ref[0:1, cols] += column_sum(grad_q.astype(F32))
                vec_ref[1:2, cols] += column_sum(grad_v.astype(F32))

    def rows_of(cols):
        return pl.BlockSpec((rows_step, cols), lambda i, h: (i, 0))

    return call(
        kernel,
        "attn_bwd",
        (rows // rows_step,),
        (here,),
        [
            rows_of(width), rows_of(width), rows_of(half),
            pl.BlockSpec((width, half), lambda i, h: (0, h[which]), pipeline_mode=pl.Buffered(1)),
            rows_of(width), rows_of(LANES),
            once(table.shape), once((width, width)), rows_of(3 * width),
            pl.BlockSpec((per_step, pairs, 2 * span, span), lambda i, h: (i, 0, 0, 0)),
        ],
        [rows_of(width), rows_of(width), rows_of(3 * width), full((8, width))],
        [
            shaped((rows, width), F32), shaped((rows, width), BF16),
            shaped((rows, 3 * width), BF16), shaped((8, width), F32),
        ],
        [pltpu.VMEM((rows_step, width), BF16)],
        8 * rows * width * width * 2,
        40e6,
        (gh, gres, grad_inner, w_up, n_attn, spread, table, w_out, qkv, probs),
        24, 0, (1,), (0, 2),
    )


def projection_terms(x, grad_mixed, attended, grad_branch, vectors, here, which, got=None):
    rows, width = x.shape
    part = width // 2
    pieces = width // 32 // 8

    def product(x_ref, gm_ref, att_ref, gb_ref, scr):
        step = pl.program_id(0)

        @pl.when(step < 3)
        def _():
            scr[...] = t_dot(x_ref[...], gm_ref[...])

        @pl.when(step == 3)
        def _():
            scr[...] = t_dot(att_ref[...], gb_ref[...])

    def small(here_s, ffn_ref, attn_ref, sent_ref, kept_ref, store):
        first = here_s[0] == 0
        for step in range(4):

            @pl.when(pl.program_id(0) == step)
            def _():
                side, at = step // 2, slice(step % 2 * part, (step % 2 + 1) * part)
                wide = slice(step * part, (step + 1) * part)
                rows_of = (
                    (ffn_ref[0:1, at], ffn_ref[2:3, at], attn_ref[1:2, at], attn_ref[3:4, at]),
                    (ffn_ref[1:2, at], attn_ref[0:1, at], attn_ref[2:3, at], attn_ref[4:5, at]),
                )[side]
                sent, kept = sent_ref[:, wide], kept_ref[:, wide]
                ups = (jnp.where(first, kept, sent), jnp.where(first, sent, kept))
                store(jnp.concatenate(rows_of + ups + (jnp.zeros((2, part), F32),), axis=0))

    def give(here_s, x_ref, gm_ref, att_ref, gb_ref, ffn_ref, attn_ref, sent_ref, kept_ref, out_ref, scr):
        product(x_ref, gm_ref, att_ref, gb_ref, scr)
        out_ref[:width, :] = scr[...].astype(BF16)

        def store(value):
            out_ref[width:, :] = value.astype(BF16)

        small(here_s, ffn_ref, attn_ref, sent_ref, kept_ref, store)

    def own(
        here_s, x_ref, gm_ref, att_ref, gb_ref, ffn_ref, attn_ref, sent_ref, kept_ref, got_ref,
        send_a, keep_a, send_b, keep_b, scr, cut,
    ):
        product(x_ref, gm_ref, att_ref, gb_ref, scr)
        term = scr[...] + got_ref[:width, :].astype(F32)
        cut[...] = term.reshape(cut.shape)
        deal(cut, here_s, (send_a, keep_a, send_b, keep_b), 4, pieces)

        def store(value):
            extra = (value + got_ref[width:, :].astype(F32)).astype(BF16)
            send_a[8 * pieces] = extra
            keep_a[8 * pieces] = extra

        small(here_s, ffn_ref, attn_ref, sent_ref, kept_ref, store)

    in_specs = [
        once((rows, width)),
        pl.BlockSpec((rows, part), lambda i, h: (0, h[which] * 3 + jnp.minimum(i, 2))),
        once((rows, width)),
        pl.BlockSpec((rows, part), lambda i, h: (0, h[which]), pipeline_mode=pl.Buffered(1)),
    ] + [once(item.shape) for item in vectors]
    args = [x, grad_mixed, attended, grad_branch, *vectors]
    flops = 4 * rows * width * width
    if got is None:
        return call(
            give, "proj_give", (4,), (here,), in_specs,
            pl.BlockSpec((width + 8, part), lambda i, *_: (0, i)),
            shaped((width + 8, 4 * part), BF16),
            [pltpu.VMEM((width, part), F32)], flops, 9e6, args, 20, 0, (0,), (3,),
        )
    return call(
        own, "proj_own", (4,), (here,),
        in_specs + [pl.BlockSpec((width + 8, part), lambda i, *_: (0, i))],
        [
            pl.BlockSpec((8 * pieces + extra, 8, part), lambda i, *_: (0, 0, i))
            for extra in (1, 1, 0, 0)
        ],
        [shaped((8 * pieces + extra, 8, 4 * part), BF16) for extra in (1, 1, 0, 0)],
        [pltpu.VMEM((width, part), F32), pltpu.VMEM((4, 2, 2, 2, pieces, 8, part), F32)],
        flops, 11e6, args + [got], 24, 1, (0, 1, 2, 3), (3,),
    )


def input_gradient(grad_mixed, w_qkv, grad_resid, rows_step):
    rows, width = grad_resid.shape

    def kernel(gm_ref, wq_ref, gr_ref, out_ref):
        out_ref[...] = (dot_t(gm_ref[...], wq_ref[...]) + gr_ref[...]).astype(BF16)

    return call(
        kernel, "input_grad", (rows // rows_step,), (),
        [
            pl.BlockSpec((rows_step, 3 * width), lambda i: (i, 0)),
            once((width, 3 * width)),
            pl.BlockSpec((rows_step, width), lambda i: (i, 0)),
        ],
        pl.BlockSpec((rows_step, width), lambda i: (i, 0)),
        shaped((rows, width), BF16), [], 6 * rows * width * width, 13e6,
        (grad_mixed, w_qkv, grad_resid), 20,
    )


def copied(item, here, block):
    rows, width = item.shape

    def kernel(here_s, in_ref, out_ref):
        out_ref[...] = in_ref[...]

    spec = pl.BlockSpec((block, width), lambda i, *_: (i, 0))
    return call(
        kernel, "copied", (rows // block,), (here,), [spec], spec,
        shaped((rows, width), item.dtype), [], 1, 3e6, (item,), 4,
    )


def small_call(kernel, name, here, args, outs, vmem=12):
    return pl.pallas_call(
        kernel,
        in_specs=[pl.BlockSpec(memory_space=pltpu.SMEM)]
        + [pl.BlockSpec(memory_space=pltpu.VMEM)] * len(args),
        out_specs=[pl.BlockSpec(memory_space=pltpu.VMEM)] * len(outs),
        out_shape=outs,
        compiler_params=pltpu.CompilerParams(vmem_limit_bytes=vmem * MIB),
        cost_estimate=pl.CostEstimate(flops=int(1e6 * COST), bytes_accessed=int(4e6 * COST), transcendentals=0),
        name=name,
    )(here, *args)


def add(left, right):
    return (left.astype(F32) + right.astype(F32)).astype(BF16)


def fold_second(keep_a, got_a, keep_b, got_b, here, pieces, extra, far=False):
    cols = keep_a.shape[2]

    def kernel(here_s, ka, ga, kb, gb, send_a, left_a, send_b, left_b):
        x, y = here_s[2], here_s[3]
        for z in range(4):
            at = pl.ds(z * pieces, pieces)

            def sum_of(keep, got, other):
                rows = pl.ds(z * 2 * pieces + other * pieces, pieces)
                return add(keep[rows], got[rows])

            send_a[at] = sum_of(ka, ga, 1 - y)
            left_a[at] = sum_of(ka, ga, y)
            send_b[at] = sum_of(kb, gb, 1 - x)
            left_b[at] = sum_of(kb, gb, x)
        if extra:
            total = add(ka[8 * pieces], ga[8 * pieces])
            send_a[4 * pieces] = total
            left_a[4 * pieces] = total

    a_out = shaped((4 * pieces + extra, 8, cols), BF16)
    b_out = shaped((4 * pieces, 8, cols), BF16)
    a_left, b_left = a_out, b_out
    if far:
        a_left, b_left = pltpu.HBM(a_out.shape, BF16), pltpu.HBM(b_out.shape, BF16)
    return small_call(
        kernel, "fold_second", here, (keep_a, got_a, keep_b, got_b), [a_out, a_left, b_out, b_left]
    )


def fold_third(terms, here, pieces, extra):
    cols = terms[0][0].shape[2]
    count = len(terms)

    def kernel(here_s, *refs):
        ins, (send, left) = refs[:-2], refs[-2:]
        low = here_s[4]
        for high in range(2):
            for number in range(2 * count):
                keep, got = ins[2 * number : 2 * number + 2]
                at = pl.ds((high * 2 * count + number) * pieces, pieces)
                for out, pick in ((send, 1 - low), (left, low)):
                    rows = pl.ds((high * 2 + pick) * pieces, pieces)
                    out[at] = add(keep[rows], got[rows])
        if extra:
            total = add(ins[0][4 * pieces], ins[1][4 * pieces])
            send[4 * count * pieces] = total
            left[4 * count * pieces] = total

    out = shaped((4 * count * pieces + extra, 8, cols), BF16)
    args = [item for term in terms for item in term]
    return small_call(kernel, "fold_third", here, args, [out, out])


def fold_fourth(keep, got, here, extra):
    cols = keep.shape[2]
    count = (keep.shape[0] - extra) // 2

    def kernel(here_s, keep_ref, got_ref, send, left):
        high = here_s[5]
        for out, pick in ((send, 1 - high), (left, high)):
            rows = pl.ds(pick * count, count)
            out[:count] = add(keep_ref[rows], got_ref[rows])
        if extra:
            total = add(keep_ref[2 * count], got_ref[2 * count])
            send[count] = total
            left[count] = total

    out = shaped((count + extra, 8, cols), BF16)
    return small_call(kernel, "fold_fourth", here, (keep, got), [out, out])


def fold_last(keep, got, here, extra):
    cols = keep.shape[2]
    count = keep.shape[0] - extra

    def kernel(here_s, keep_ref, got_ref, *outs):
        outs[0][...] = add(keep_ref[:count], got_ref[:count])
        if extra:
            outs[1][0] = add(keep_ref[count], got_ref[count])

    outs = [shaped((count, 8, cols), BF16)] + [shaped((1, 8, cols), BF16)] * extra
    return small_call(kernel, "fold_last", here, (keep, got), outs)


def chosen_part(here_s, refs, core, side, at):
    me, gx, gc, gd = [item[at].astype(F32) for item in refs]
    same_core, same_side = here_s[0] == core, here_s[2] == side
    return jnp.where(same_core, jnp.where(same_side, me, gx), jnp.where(same_side, gc, gd))


def feed_blocks(parts, here, pieces, width):
    cols = parts[0].shape[2]
    half = width // 2
    folds = cols // half
    rows = 2 * pieces * 8

    def kernel(here_s, me, gx, gc, gd, down_ref, up_ref):
        refs = (me, gx, gc, gd)
        for core in range(2):
            for side in range(2):
                tall = side * folds * rows
                for ab in range(2):
                    at = pl.ds(ab * pieces, pieces)
                    value = chosen_part(here_s, refs, core, side, at).reshape(rows // 2, cols)
                    for fold in range(folds):
                        start = tall + (ab * folds + fold) * (rows // 2)
                        down_ref[start : start + rows // 2, core * half : (core + 1) * half] = value[
                            :, fold * half : (fold + 1) * half
                        ]
                at = pl.ds(2 * pieces, 2 * pieces)
                value = chosen_part(here_s, refs, core, side, at).reshape(rows, cols)
                up_ref[side * rows : (side + 1) * rows, core * cols : (core + 1) * cols] = value

    outs = [shaped((2 * folds * rows, width), F32), shaped((2 * rows, 2 * cols), F32)]
    return small_call(kernel, "feed_blocks", here, parts, outs, 16)


def projection_blocks(parts, vectors, here, pieces):
    cols = parts[0].shape[2]
    rows = 2 * pieces * 8
    cut = cols // 4 * 3
    width = cols // 2
    small = width // 8
    large = cols // 4

    def kernel(here_s, me, gx, gc, gd, vec_ref, qkv_ref, out_ref, *outs):
        refs = (me, gx, gc, gd)
        for core in range(2):
            for side in range(2):
                value = chosen_part(here_s, refs, core, side, slice(None)).reshape(rows, cols)
                at = slice(side * rows, (side + 1) * rows)
                qkv_ref[at, core * cut : (core + 1) * cut] = value[:, :cut]
                out_ref[at, core * (cols - cut) : (core + 1) * (cols - cut)] = value[:, cut:]
        table = vec_ref[0].astype(F32)
        wide = here_s[6]
        shift = lax.rem(width - wide * small, width)
        left, right = pltpu.roll(table[:, :width], shift, 1), pltpu.roll(table[:, width:], shift, 1)
        for row in range(4):
            outs[2 * row][...] = left[row : row + 1, :small]
            outs[2 * row + 1][...] = right[row : row + 1, :small]
        turned = pltpu.roll(table, lax.rem(cols - lax.rem(wide, 4) * large, cols), 1)
        outs[8][...] = jnp.where(wide < 4, turned[4:5, :large], turned[5:6, :large])

    outs = [shaped((2 * rows, 2 * cut), F32), shaped((2 * rows, 2 * (cols - cut)), F32)]
    outs += [shaped((1, small), F32)] * 8 + [shaped((1, large), F32)]
    return small_call(kernel, "projection_blocks", here, (*parts, vectors), outs, 16)


def after(item, *earlier):
    return lax.optimization_barrier((item, *earlier))[0]


def swap(item, axis, step):
    count = lax.axis_size(axis)
    return lax.ppermute(item, axis, [(index, index ^ step) for index in range(count)])


def quarters(mine):
    across = swap(mine, "narrow", 2)
    return mine, across, swap(mine, "narrow", 1), swap(across, "narrow", 1)


def regroup_rows(sent, bucket, wide_count, batches):
    span, width = sent.shape[1:]
    if wide_count == batches:
        got = lax.all_to_all(sent, "wide", split_axis=0, concat_axis=0, tiled=True)
        return got.reshape(batches * span, width)
    send = jnp.zeros((wide_count, span, width), sent.dtype).at[bucket].set(sent)
    got = lax.all_to_all(send, "wide", split_axis=0, concat_axis=0, tiled=True)
    marks = jnp.zeros((wide_count, 1), jnp.int32).at[bucket].set(1)
    filled = lax.all_to_all(marks, "wide", split_axis=0, concat_axis=0, tiled=True)[:, 0]
    place = jnp.where(filled > 0, jnp.cumsum(filled) - filled, batches)
    chosen = (
        jnp.zeros((batches,), jnp.int32)
        .at[place]
        .set(jnp.arange(wide_count, dtype=jnp.int32), mode="drop")
    )
    return got[chosen].reshape(batches * span, width)


def sum_anywhere(item, wide_count, narrow_count):
    blocks = item.astype(F32).reshape(wide_count, -1)
    extent = blocks.shape[1]
    padded = (extent + narrow_count - 1) // narrow_count * narrow_count
    blocks = jnp.pad(blocks, ((0, 0), (0, padded - extent))).reshape(-1)
    share = lax.psum_scatter(blocks, ("wide", "narrow"), scatter_dimension=0, tiled=True)
    whole = lax.all_gather(share.astype(BF16), "narrow", axis=0, tiled=True).astype(F32)
    return whole[:extent].reshape((item.shape[0] // wide_count,) + item.shape[1:])


def body(
    tokens, bucket, lengths, pairing, targets, w_qkv, bias_q, bias_v, w_out, bias_out,
    gain_attn, shift_attn, w_up, bias_up, w_down, bias_down, gain_ffn, shift_ffn,
):
    wide_count, narrow_count = lax.axis_size("wide"), lax.axis_size("narrow")
    batches = bucket.shape[0]
    rows, width = tokens.shape
    span = rows // batches
    paired = (wide_count, narrow_count) == (8, 4)
    wide, narrow = lax.axis_index("wide"), lax.axis_index("narrow")
    if paired:
        core = narrow % 2
        here = jnp.stack(
            [core, 1 - core, narrow // 2, wide % 2, wide // 2 % 2, wide // 4, wide, narrow]
        ).astype(jnp.int32)
    else:
        here = jnp.arange(8, dtype=jnp.int32)
    table = vector_table(
        [bias_q, bias_v, bias_out, gain_attn, shift_attn, bias_down, gain_ffn, shift_ffn, bias_up], width
    )
    ordered = wide_count == batches
    slots = bucket if ordered else jnp.arange(batches, dtype=jnp.int32)
    pieces = width // 32 // 8

    qkv, probs, attended, n_attn, spread, sid = attention_forward(
        tokens, w_qkv, w_out, table, bucket, lengths, wide_count // batches, span, 2 * span
    )
    active, slope, hidden_t, sent, gres, grad_second, vec_ffn = feed_forward(
        n_attn, w_up, w_down, table, sid, slots, pairing, targets, batches, 2 * span
    )
    ups = (grad_second, slope, hidden_t, w_down)
    heads = (n_attn, spread, table, w_out, qkv, probs)
    down_sent = down_terms(active, grad_second, here, 1)
    if paired:
        encoded = regroup_rows(after(sent, down_sent), bucket, wide_count, batches)
        up_sent, gi_sent, bup_sent = up_terms(*ups, after(here, down_sent), 1)
        down_dealt = down_terms(active, grad_second, after(here, bup_sent), 0, swap(down_sent, "narrow", 1))
        down_a, down_b = swap(down_dealt[0], "narrow", 2), swap(down_dealt[2], "wide", 1)
        gh = hidden_gradient(gi_sent, w_up, after(here, down_dealt[1]), 1)
        *up_dealt, gi_kept, bup_kept = up_terms(
            *ups, after(here, gh), 0, swap(up_sent, "narrow", 1)
        )
        up_a, up_b = swap(up_dealt[0], "narrow", 2), swap(up_dealt[2], "wide", 1)
        down_dealt = fold_second(
            down_dealt[1], down_a, down_dealt[3], down_b, after(here, bup_kept), pieces, 0, True
        )
        down_a, down_b = swap(down_dealt[0], "wide", 1), swap(down_dealt[2], "narrow", 2)
        gr, gb, gm, vec_attn = attention_backward(
            gh, gres, gi_kept, w_up, *heads, after(here, down_dealt[1]), 0, span, 2 * span
        )
        up_dealt = fold_second(
            up_dealt[1], up_a, up_dealt[3], up_b, after(here, vec_attn, encoded), pieces, 0
        )
        up_a, up_b = swap(up_dealt[0], "wide", 1), swap(up_dealt[2], "narrow", 2)
        projections = (tokens, gm, attended, gb, (vec_ffn, vec_attn, bup_sent, bup_kept))
        proj_sent = projection_terms(*projections, after(here, up_dealt[1]), 1)
        proj_dealt = projection_terms(
            *projections, after(here, proj_sent), 0, swap(proj_sent, "narrow", 1)
        )
        proj_a, proj_b = swap(proj_dealt[0], "narrow", 2), swap(proj_dealt[2], "wide", 1)
        send, feed = fold_third(
            [(down_dealt[1], down_a, down_dealt[3], down_b), (up_dealt[1], up_a, up_dealt[3], up_b)],
            after(here, proj_dealt[1]), pieces, 0,
        )
        feed_got = swap(send, "wide", 2)
        grad_tokens = input_gradient(after(gm, feed), w_qkv, gr, 2 * span)
        encoded = copied(encoded, after(here, grad_tokens), span)
        send, feed = fold_fourth(feed, feed_got, after(here, encoded), 0)
        feed_got = swap(send, "wide", 4)
        proj_dealt = fold_second(
            proj_dealt[1], proj_a, proj_dealt[3], proj_b, after(here, feed), pieces, 1
        )
        proj_a, proj_b = swap(proj_dealt[0], "wide", 1), swap(proj_dealt[2], "narrow", 2)
        (feed,) = fold_last(feed, feed_got, after(here, proj_dealt[1]), 0)
        feed = quarters(feed)
        send, proj = fold_third(
            [(proj_dealt[1], proj_a, proj_dealt[3], proj_b)], here, pieces, 1
        )
        proj_got = swap(send, "wide", 2)
        grad_w_down, grad_w_up = feed_blocks(feed, after(here, proj), pieces, width)
        send, proj = fold_fourth(proj, proj_got, after(here, grad_w_down), 1)
        proj_got = swap(send, "wide", 4)
        proj, vectors = fold_last(proj, proj_got, here, 1)
        proj = quarters(proj)
        grad_w_qkv, grad_w_out, *small = projection_blocks(proj, vectors, here, pieces)
        small = [item.reshape(-1) for item in small]
    else:
        encoded = regroup_rows(sent, bucket, wide_count, batches)
        down_kept = down_terms(active, grad_second, here, 0)
        up_sent, gi_sent, bup_sent = up_terms(*ups, here, 1)
        up_kept, gi_kept, bup_kept = up_terms(*ups, here, 0)
        gh = hidden_gradient(gi_sent, w_up, here, 1)
        gr, gb, gm, vec_attn = attention_backward(
            gh, gres, gi_kept, w_up, *heads, here, 0, span, 2 * span
        )
        projections = (tokens, gm, attended, gb, (vec_ffn, vec_attn, bup_sent, bup_kept), here)
        grad_tokens = input_gradient(gm, w_qkv, gr, 2 * span)
        proj_sent, proj_kept = projection_terms(*projections, 1), projection_terms(*projections, 0)
        total = partial(sum_anywhere, wide_count=wide_count, narrow_count=narrow_count)
        cut = width // 2 * 3
        grad_w_down = total(jnp.concatenate([down_kept, down_sent], axis=1))
        grad_w_up = total(jnp.concatenate([up_kept, up_sent], axis=1))
        grad_w_qkv = total(jnp.concatenate([proj_kept[:width, :cut], proj_sent[:width, :cut]], axis=1))
        grad_w_out = total(jnp.concatenate([proj_kept[:width, cut:], proj_sent[:width, cut:]], axis=1))
        small = [
            total(item)
            for item in (*vec_ffn[:3], *vec_attn[:5], jnp.concatenate([bup_kept[0], bup_sent[0]]))
        ]
    gain_out, shift_out, b_down, b_q, b_v, b_out, g_attn, s_attn, b_up = small
    return (
        encoded, grad_tokens, grad_w_qkv, b_q, b_v, grad_w_out, b_out, g_attn, s_attn,
        grad_w_up, b_up, grad_w_down, b_down, gain_out, shift_out,
    )


def solution(mesh):
    split = P(("wide", "narrow"))
    in_specs = (
        P(("wide", "narrow"), None), split, split, P(("wide", "narrow"), None), split,
    ) + (P(),) * 13
    out_specs = (
        P(("wide", "narrow"), None), P(("wide", "narrow"), None),
        P("wide", None), P("wide"), P("wide"), P("wide", None), P("wide"), P("wide"), P("wide"),
        P("wide", None), P("wide"), P("wide", None), P("wide"), P("wide"), P("wide"),
    )
    return jax.shard_map(body, mesh=mesh, in_specs=in_specs, out_specs=out_specs, check_vma=False)
```

```python
from functools import partial

import jax
import jax.numpy as jnp
from jax import lax
from jax.experimental import pallas as pl
from jax.experimental.pallas import tpu as pltpu
from jax.sharding import PartitionSpec as P

HDIM = 64
KTOP = 12
NORM_EPS = 1e-12
COS_EPS = 1e-06
MASKED = -1000000000.0
LOSS_SCALE = 1024.0
F32 = jnp.float32
BF16 = jnp.bfloat16
LANES = 128
MIB = 1024 * 1024
LARGE = 100000
COST = 0.05
HALF_ROOT = 0.7071067811865476
BELL_RATE = -0.7213475204444817
BELL_PEAK = -1.3257480647361595
ROW_BQ, ROW_BV, ROW_BO, ROW_GA, ROW_SA, ROW_BD, ROW_GF, ROW_SF, ROW_BU = range(9)


def dot(left, right):
    return jnp.dot(left, right, preferred_element_type=F32)


def dot_t(left, right):
    return lax.dot_general(left, right, (((1,), (1,)), ((), ())), preferred_element_type=F32)


def t_dot(left, right):
    return lax.dot_general(left, right, (((0,), (0,)), ((), ())), preferred_element_type=F32)


def full(shape):
    return pl.BlockSpec(shape, lambda *_: (0,) * len(shape))


def once(shape):
    return pl.BlockSpec(shape, lambda *_: (0,) * len(shape), pipeline_mode=pl.Buffered(1))


def large(item):
    return item.size >= LARGE


def shaped(shape, dtype):
    return jax.ShapeDtypeStruct(shape, dtype)


def call(
    kernel, name, grid, prefetch, in_specs, out_specs, out_shape, scratch, flops, moved, args, vmem=24, free=0, loose=(), near=()
):
    single = not isinstance(out_shape, list)
    shapes = [out_shape] if single else out_shape
    shapes = [
        pltpu.HBM(item.shape, item.dtype) if large(item) and number not in loose else item
        for number, item in enumerate(shapes)
    ]
    out_shape = shapes[0] if single else shapes
    args = [
        pltpu.with_memory_space_constraint(item, pltpu.HBM)
        if large(item) and number < len(args) - free and number not in near
        else item
        for number, item in enumerate(args)
    ]
    return pl.pallas_call(
        kernel,
        grid_spec=pltpu.PrefetchScalarGridSpec(
            num_scalar_prefetch=len(prefetch),
            grid=grid,
            in_specs=in_specs,
            out_specs=out_specs,
            scratch_shapes=scratch,
        ),
        out_shape=out_shape,
        compiler_params=pltpu.CompilerParams(
            dimension_semantics=("arbitrary",) * len(grid), vmem_limit_bytes=vmem * MIB
        ),
        cost_estimate=pl.CostEstimate(flops=int(flops * COST), bytes_accessed=int(moved * COST), transcendentals=0),
        name=name,
    )(*[pltpu.with_memory_space_constraint(item, pltpu.HBM) for item in prefetch], *args)


def norm_forward(values):
    center = values - jnp.mean(values, axis=-1, keepdims=True)
    spread = lax.rsqrt(jnp.mean(center * center, axis=-1, keepdims=True) + NORM_EPS)
    return center * spread, spread


def norm_backward(grad_out, normed, spread, gain):
    scaled = grad_out * gain
    mean_scaled = jnp.mean(scaled, axis=-1, keepdims=True)
    mean_product = jnp.mean(scaled * normed, axis=-1, keepdims=True)
    return spread * (scaled - mean_scaled - normed * mean_product)


def column_sum(values):
    return jnp.sum(values, axis=0, keepdims=True)


def gelu_pair(v):
    phi = 0.5 + 0.5 * lax.erf(v * HALF_ROOT)
    bell = jnp.exp2((v * v) * BELL_RATE + BELL_PEAK)
    return v * phi, phi + v * bell


def head_masks():
    lane = lax.broadcasted_iota(jnp.int32, (1, LANES), 1)
    low = (lane < HDIM).astype(F32)
    return low.astype(BF16), (1.0 - low).astype(BF16), lane < HDIM


def sentence_count(bucket_s, number, group_size):
    kind = bucket_s[number]
    if group_size > 1:
        kind = kind // group_size
    return jnp.maximum(1, lax.shift_right_logical(jnp.int32(KTOP), kind))


def row_sentences(batch, bucket_s, lengths_s, group_size, batches, sent, span):
    start = jnp.int32(0)
    for other in range(batches):
        start += jnp.where(other < batch, sentence_count(bucket_s, other, group_size), 0)
    count = sentence_count(bucket_s, batch, group_size)
    lane = lax.broadcasted_iota(jnp.int32, (8, span), 1)
    row = lax.broadcasted_iota(jnp.int32, (span, span), 0)
    passed_lane = jnp.zeros((8, span), jnp.int32)
    passed_row = jnp.zeros((span, span), jnp.int32)
    finish = jnp.int32(0)
    for number in range(KTOP):
        finish += lengths_s[jnp.minimum(start + number, sent - 1)]
        bound = jnp.where(number < count, finish, span)
        passed_lane += (lane >= bound).astype(jnp.int32)
        passed_row += (row >= bound).astype(jnp.int32)
    sid_lane = jnp.where(passed_lane < count, start + passed_lane, -1)
    sid_row = jnp.where(passed_row < count, start + passed_row, -1)
    return sid_lane, sid_row


def vector_table(vectors, width):
    def kernel(*refs):
        out_ref = refs[-1]
        at = 0
        for ref in refs[:-1]:
            for part in range(ref.shape[0] // width):
                out_ref[at : at + 1, :] = ref[part * width : (part + 1) * width].astype(F32).reshape(1, width)
                at += 1

    rows = sum(item.shape[0] for item in vectors) // width
    return pl.pallas_call(
        kernel,
        grid=(1,),
        in_specs=[full(item.shape) for item in vectors],
        out_specs=full((rows, width)),
        out_shape=shaped((rows, width), F32),
        compiler_params=pltpu.CompilerParams(vmem_limit_bytes=4 * MIB),
        name="vector_table",
    )(*[pltpu.with_memory_space_constraint(item, pltpu.HBM) for item in vectors])


def attention_forward(x, w_qkv, w_out, table, bucket, lengths, group_size, span, rows_step):
    rows, width = x.shape
    batches = rows // span
    pairs = width // LANES
    sent = lengths.shape[0]
    per_step = rows_step // span

    def kernel(bucket_s, lengths_s, x_ref, wq_ref, wo_ref, tab_ref, qkv_ref, p_ref, att_ref, n_ref, s_ref, sid_ref):
        step = pl.program_id(0)
        low_b, high_b, low_m = head_masks()
        x_in = x_ref[...]
        mixed = dot(x_in, wq_ref[:, :width]) + tab_ref[ROW_BQ : ROW_BQ + 1, :]
        qkv_ref[:, :width] = (mixed * 0.125).astype(BF16)
        qkv_ref[:, width : 2 * width] = dot(x_in, wq_ref[:, width : 2 * width]).astype(BF16)
        mixed = dot(x_in, wq_ref[:, 2 * width :]) + tab_ref[ROW_BV : ROW_BV + 1, :]
        qkv_ref[:, 2 * width :] = mixed.astype(BF16)
        eye = lax.broadcasted_iota(jnp.int32, (span, span), 0) == lax.broadcasted_iota(
            jnp.int32, (span, span), 1
        )
        for inner in range(per_step):
            sid_lane, sid_row = row_sentences(
                step * per_step + inner, bucket_s, lengths_s, group_size, batches, sent, span
            )
            sid_ref[inner] = sid_lane
            same = (sid_row == sid_lane[0:1, :]) & (sid_row >= 0)
            bias = jnp.where(same | eye, 0.0, MASKED)
            bias = jnp.concatenate([bias, bias], axis=0)
            base = slice(inner * span, (inner + 1) * span)
            for pair in range(pairs):
                cols = slice(pair * LANES, (pair + 1) * LANES)
                q = qkv_ref[base, cols]
                k = qkv_ref[base, width + pair * LANES : width + (pair + 1) * LANES]
                v = qkv_ref[base, 2 * width + pair * LANES : 2 * width + (pair + 1) * LANES]
                both = jnp.concatenate([q * low_b, q * high_b], axis=0)
                logits = dot_t(both, k) + bias
                raised = jnp.exp(logits - jnp.max(logits, axis=-1, keepdims=True))
                total = jnp.sum(raised, axis=-1, keepdims=True)
                probs = (raised * (1.0 / total)).astype(BF16)
                p_ref[inner, pair] = probs
                mix = dot(probs, v)
                att_ref[base, cols] = jnp.where(low_m, mix[:span], mix[span:]).astype(BF16)
        branch = dot(att_ref[...], wo_ref[...]) + tab_ref[ROW_BO : ROW_BO + 1, :]
        normed, spread = norm_forward(x_in.astype(F32) + branch)
        n_ref[...] = normed
        s_ref[...] = jnp.broadcast_to(spread, (rows_step, LANES))

    return call(
        kernel,
        "attn_fwd",
        (rows // rows_step,),
        (bucket, lengths),
        [
            pl.BlockSpec((rows_step, width), lambda i, *_: (i, 0)),
            once((width, 3 * width)),
            once((width, width)),
            once(table.shape),
        ],
        [
            pl.BlockSpec((rows_step, 3 * width), lambda i, *_: (i, 0)),
            pl.BlockSpec((per_step, pairs, 2 * span, span), lambda i, *_: (i, 0, 0, 0)),
            pl.BlockSpec((rows_step, width), lambda i, *_: (i, 0)),
            pl.BlockSpec((rows_step, width), lambda i, *_: (i, 0)),
            pl.BlockSpec((rows_step, LANES), lambda i, *_: (i, 0)),
            pl.BlockSpec((per_step, 8, span), lambda i, *_: (i, 0, 0)),
        ],
        [
            shaped((rows, 3 * width), BF16),
            shaped((batches, pairs, 2 * span, span), BF16),
            shaped((rows, width), BF16),
            shaped((rows, width), F32),
            shaped((rows, LANES), F32),
            shaped((batches, 8, span), jnp.int32),
        ],
        [],
        8 * rows * width * width * 2,
        30e6,
        (x, w_qkv, w_out, table),
        26,
    )


def feed_forward(n_attn, w_up, w_down, table, sid, slots, pairing, targets, slot_count, block):
    rows, width = n_attn.shape
    ff = w_up.shape[1]
    batches, _, span = sid.shape
    pair_count = targets.shape[0]
    side = -(-pair_count // 8) * 8
    chunk = width
    steps = ff // chunk
    blocks = rows // block
    per_block = block // span

    def kernel(
        slots_s, pairing_s, targets_s, n_ref, wu_ref, wd_ref, tab_ref, sid_ref,
        act_ref, dg_ref, ht_ref, enc_ref, gres_ref, gsl_ref, vec_ref, low_scr, acc_scr, spread_scr,
    ):
        step = pl.program_id(0)
        gain = tab_ref[ROW_GA : ROW_GA + 1, :]
        shift = tab_ref[ROW_SA : ROW_SA + 1, :]

        @pl.when(step == 0)
        def _():
            hidden = (n_ref[...] * gain + shift).astype(BF16)
            low_scr[...] = hidden
            ht_ref[...] = hidden.T
            acc_scr[...] = jnp.zeros_like(acc_scr)

        for number in range(blocks):
            base = slice(number * block, (number + 1) * block)
            inner = dot(low_scr[base, :], wu_ref[...]) + tab_ref[pl.ds(ROW_BU + step, 1), :]
            active, slope = gelu_pair(inner)
            active = active.astype(BF16)
            act_ref[base, :] = active
            dg_ref[base, :] = slope.astype(BF16)
            acc_scr[base, :] += dot(active, wd_ref[...])

        @pl.when(step == steps - 1)
        def _():
            gain_out = tab_ref[ROW_GF : ROW_GF + 1, :]
            shift_out = tab_ref[ROW_SF : ROW_SF + 1, :]
            slot = lax.broadcasted_iota(jnp.int32, (2 * side, span), 0)
            wanted = jnp.full((2 * side, span), -2, jnp.int32)
            goal = jnp.zeros((side, LANES), F32)
            goal_slot = lax.broadcasted_iota(jnp.int32, (side, LANES), 0)
            for number in range(pair_count):
                wanted = jnp.where(slot == number, pairing_s[0, 2 * number], wanted)
                wanted = jnp.where(slot == side + number, pairing_s[0, 2 * number + 1], wanted)
                goal = jnp.where(goal_slot == number, targets_s[number], goal)
            members = [
                (sid_ref[number][0:1, :] == wanted).astype(F32) for number in range(batches)
            ]
            sizes = jnp.zeros((2 * side, 1), F32)
            for member in members:
                sizes += jnp.sum(member, axis=-1, keepdims=True)
            share = 1.0 / jnp.maximum(sizes, 1.0)
            picks = [
                jnp.concatenate(members[number * per_block : (number + 1) * per_block], axis=1).astype(BF16)
                for number in range(blocks)
            ]
            ones = jnp.ones((2 * side, LANES), BF16)
            pooled = jnp.zeros((2 * side, width), F32)
            for number in range(blocks):
                base = slice(number * block, (number + 1) * block)
                resid = (
                    n_ref[base, :] * gain + shift + acc_scr[base, :] + tab_ref[ROW_BD : ROW_BD + 1, :]
                )
                normed, spread = norm_forward(resid)
                acc_scr[base, :] = normed
                spread_scr[base, :] = jnp.broadcast_to(spread, (block, LANES))
                out = normed * gain_out + shift_out
                high = out.astype(BF16)
                rest = (out - high.astype(F32)).astype(BF16)
                pooled += dot(picks[number], high) + dot(picks[number], rest)
                valid = t_dot(picks[number], ones)
                for col in range(width // LANES):
                    cols = slice(col * LANES, (col + 1) * LANES)
                    kept = (out[:, cols] * valid).astype(BF16)
                    for inner in range(per_block):
                        enc_ref[slots_s[number * per_block + inner], :, cols] = kept[
                            inner * span : (inner + 1) * span
                        ]
            pooled = pooled * share
            first, partner = pooled[:side], pooled[side:]
            cross = jnp.sum(first * partner, axis=-1, keepdims=True)
            scale_first = lax.rsqrt(jnp.sum(first * first, axis=-1, keepdims=True) + COS_EPS)
            scale_partner = lax.rsqrt(jnp.sum(partner * partner, axis=-1, keepdims=True) + COS_EPS)
            cosine = cross * scale_first * scale_partner
            factor = 2.0 * LOSS_SCALE * (cosine - goal[:, :1])
            both_scales = factor * scale_first * scale_partner
            grad_first = both_scales * partner - (factor * cosine * scale_first * scale_first) * first
            grad_partner = (
                both_scales * first - (factor * cosine * scale_partner * scale_partner) * partner
            )
            grad_home = jnp.concatenate([grad_first, grad_partner], axis=0) * share
            high = grad_home.astype(BF16)
            rest = (grad_home - high.astype(F32)).astype(BF16)
            vec_ref[...] = jnp.zeros_like(vec_ref)
            for number in range(blocks):
                base = slice(number * block, (number + 1) * block)
                grad_out = t_dot(picks[number], high) + t_dot(picks[number], rest)
                normed = acc_scr[base, :]
                resid = norm_backward(grad_out, normed, spread_scr[base, :1], gain_out)
                gres_ref[base, :] = resid
                low = resid.astype(BF16)
                gsl_ref[base, :] = low
                vec_ref[0:1, :] += column_sum(grad_out * normed)
                vec_ref[1:2, :] += column_sum(grad_out)
                vec_ref[2:3, :] += column_sum(low.astype(F32))

    return call(
        kernel,
        "ffn_fwd",
        (steps,),
        (slots, pairing, targets),
        [
            once((rows, width)),
            pl.BlockSpec((width, chunk), lambda j, *_: (0, j)),
            pl.BlockSpec((chunk, width), lambda j, *_: (j, 0)),
            once(table.shape),
            once((batches, 8, span)),
        ],
        [
            pl.BlockSpec((rows, chunk), lambda j, *_: (0, j)),
            pl.BlockSpec((rows, chunk), lambda j, *_: (0, j)),
            once((width, rows)),
            once((slot_count, span, width)),
            once((rows, width)),
            once((rows, width)),
            once((8, width)),
        ],
        [
            shaped((rows, ff), BF16),
            shaped((rows, ff), BF16),
            shaped((width, rows), BF16),
            shaped((slot_count, span, width), BF16),
            shaped((rows, width), F32),
            shaped((rows, width), BF16),
            shaped((8, width), F32),
        ],
        [
            pltpu.VMEM((rows, width), BF16),
            pltpu.VMEM((rows, width), F32),
            pltpu.VMEM((rows, LANES), F32),
        ],
        8 * rows * width * ff,
        40e6,
        (n_attn, w_up, w_down, table, sid),
        38, 0, (2, 5),
    )


def deal(scratch, here_s, outs, z_count, pieces, folds=1):
    send_a, keep_a, send_b, keep_b = outs
    x, y = here_s[2], here_s[3]
    cols = scratch.shape[-1]
    for z in range(z_count):
        for other in range(2):
            at = pl.ds((z * 2 + other) * pieces, pieces)
            for fold in range(folds):
                part = pl.ds(fold * pieces, pieces)
                to = slice(fold * cols, (fold + 1) * cols)
                send_a[at, :, to] = scratch[z, other, 1 - x, 0, part].astype(BF16)
                keep_a[at, :, to] = scratch[z, other, x, 0, part].astype(BF16)
                send_b[at, :, to] = scratch[z, 1 - y, other, 1, part].astype(BF16)
                keep_b[at, :, to] = scratch[z, y, other, 1, part].astype(BF16)


def down_terms(active, grad_second, here, which, got=None):
    rows, ff = active.shape
    width = grad_second.shape[1]
    half = width // 2
    steps = 4
    tall = ff // steps
    pieces = width // 32 // 8
    folds = ff // width

    def give(here_s, act_ref, gs_ref, out_ref):
        out_ref[...] = t_dot(act_ref[...], gs_ref[...]).astype(BF16)

    def own(here_s, act_ref, gs_ref, got_ref, *rest):
        outs, scratch = rest[:4], rest[4]
        term = t_dot(act_ref[...], gs_ref[...]) + got_ref[...].astype(F32)
        scratch[...] = term.reshape(scratch.shape)
        deal(scratch, here_s, outs, 1, pieces, folds)

    in_specs = [
        pl.BlockSpec((rows, tall), lambda i, here_s: (0, i)),
        pl.BlockSpec((rows, half), lambda i, here_s: (0, here_s[which]), pipeline_mode=pl.Buffered(1)),
    ]
    flops = 2 * rows * ff * half
    if got is None:
        return call(
            give, "down_give", (steps,), (here,), in_specs,
            pl.BlockSpec((tall, half), lambda i, *_: (i, 0)),
            shaped((ff, half), BF16), [], flops, 9e6, (active, grad_second), 20, 0, (0,), (1,),
        )
    block = (2 * pieces, 8, folds * half)
    return call(
        own, "down_own", (steps,), (here,),
        in_specs + [pl.BlockSpec((tall, half), lambda i, *_: (i, 0))],
        [pl.BlockSpec(block, lambda i, *_: (i, 0, 0))] * 4,
        [shaped((8 * pieces, 8, folds * half), BF16)] * 4,
        [pltpu.VMEM((1, 2, 2, 2, folds * pieces, 8, half), F32)],
        flops, 11e6, (active, grad_second, got), 24, 1, (0, 2), (1,),
    )


def up_terms(grad_second, slope, hidden_t, w_down, here, which, got=None):
    rows, width = grad_second.shape
    ff = w_down.shape[0]
    half = ff // 2
    chunk = width
    steps = half // chunk
    block = rows // 4
    pieces = width // 32 // 8

    def kernel(here_s, gs_ref, dg_ref, ht_ref, wd_ref, *refs):
        if got is not None:
            got_ref, refs = refs[0], refs[1:]
            outs, refs = refs[:4], refs[4:]
        else:
            out_ref, refs = refs[0], refs[1:]
        gi_ref, bu_ref = refs[:2]
        sums = jnp.zeros((1, chunk), F32)
        for number in range(rows // block):
            base = slice(number * block, (number + 1) * block)
            grad_active = dot_t(gs_ref[base, :], wd_ref[...])
            low = (grad_active * dg_ref[base, :].astype(F32)).astype(BF16)
            gi_ref[base, :] = low
            sums += column_sum(low.astype(F32))
        bu_ref[...] = sums
        term = dot(ht_ref[...], gi_ref[...])
        if got is None:
            out_ref[...] = term.astype(BF16)
        else:
            scratch = refs[2]
            term += got_ref[...].astype(F32)
            scratch[...] = term.reshape(scratch.shape)
            deal(scratch, here_s, outs, 4, pieces)

    def col(i, here_s):
        return here_s[which] * steps + i

    in_specs = [
        once((rows, width)),
        pl.BlockSpec((rows, chunk), lambda i, h: (0, col(i, h))),
        once((width, rows)),
        pl.BlockSpec((chunk, width), lambda i, h: (col(i, h), 0)),
    ]
    args = [grad_second, slope, hidden_t, w_down]
    scratch = []
    if got is None:
        out_specs = [pl.BlockSpec((width, chunk), lambda i, *_: (0, i))]
        out_shape = [shaped((width, half), BF16)]
    else:
        in_specs.append(pl.BlockSpec((width, chunk), lambda i, *_: (0, i)))
        args.append(got)
        out_specs = [pl.BlockSpec((8 * pieces, 8, chunk), lambda i, *_: (0, 0, i))] * 4
        out_shape = [shaped((8 * pieces, 8, half), BF16)] * 4
        scratch.append(pltpu.VMEM((4, 2, 2, 2, pieces, 8, chunk), F32))
    return call(
        kernel, "up_give" if got is None else "up_own", (steps,), (here,), in_specs,
        out_specs
        + [
            pl.BlockSpec((rows, chunk), lambda i, *_: (0, i)),
            pl.BlockSpec((1, chunk), lambda i, *_: (0, i)),
        ],
        out_shape + [shaped((rows, half), BF16), shaped((1, half), F32)],
        scratch, 4 * rows * width * half, 16e6, args, 26, 0 if got is None else 1, (0,) if got is None else (0, 2, 4), (0, 2),
    )


def hidden_gradient(grad_inner, w_up, here, which):
    rows, half = grad_inner.shape
    width = w_up.shape[0]
    block = rows // 2

    def kernel(here_s, gi_ref, wu_ref, out_ref):
        out_ref[...] = dot_t(gi_ref[...], wu_ref[...])

    return call(
        kernel, "hidden_grad", (rows // block,), (here,),
        [
            pl.BlockSpec((block, half), lambda i, h: (i, 0)),
            pl.BlockSpec((width, half), lambda i, h: (0, h[which]), pipeline_mode=pl.Buffered(1)),
        ],
        pl.BlockSpec((block, width), lambda i, h: (i, 0)),
        shaped((rows, width), F32), [], 2 * rows * width * half, 9e6, (grad_inner, w_up), 16, 0, (0,),
    )


def attention_backward(gh, gres, grad_inner, w_up, n_attn, spread, table, w_out, qkv, probs, here, which, span, rows_step):
    rows, width = gh.shape
    half = grad_inner.shape[1]
    pairs = width // LANES
    per_step = rows_step // span

    def kernel(here_s, gh_ref, gres_ref, gi_ref, wu_ref, n_ref, s_ref, tab_ref, wo_ref, qkv_ref, p_ref, gr_ref, gb_ref, gm_ref, vec_ref, ga_scr):
        step = pl.program_id(0)
        low_b, high_b, low_m = head_masks()

        @pl.when(step == 0)
        def _():
            vec_ref[...] = jnp.zeros_like(vec_ref)

        normed = n_ref[...]
        grad_hidden = dot_t(gi_ref[...], wu_ref[...]) + gh_ref[...] + gres_ref[...]
        resid = norm_backward(grad_hidden, normed, s_ref[:, :1], tab_ref[ROW_GA : ROW_GA + 1, :])
        gr_ref[...] = resid
        low = resid.astype(BF16)
        gb_ref[...] = low
        vec_ref[2:3, :] += column_sum(low.astype(F32))
        vec_ref[3:4, :] += column_sum(grad_hidden * normed)
        vec_ref[4:5, :] += column_sum(grad_hidden)
        ga_scr[...] = dot_t(low, wo_ref[...]).astype(BF16)
        for inner in range(per_step):
            base = slice(inner * span, (inner + 1) * span)
            for pair in range(pairs):
                cols = slice(pair * LANES, (pair + 1) * LANES)
                k_cols = slice(width + pair * LANES, width + (pair + 1) * LANES)
                v_cols = slice(2 * width + pair * LANES, 2 * width + (pair + 1) * LANES)
                q, k, v = qkv_ref[base, cols], qkv_ref[base, k_cols], qkv_ref[base, v_cols]
                grad = ga_scr[base, cols]
                grads = jnp.concatenate([grad * low_b, grad * high_b], axis=0)
                both = jnp.concatenate([q * low_b, q * high_b], axis=0)
                weights = p_ref[inner, pair]
                wide = weights.astype(F32)
                grad_probs = dot_t(grads, v)
                balance = jnp.sum(wide * grad_probs, axis=-1, keepdims=True)
                grad_logits = (wide * (grad_probs - balance)).astype(BF16)
                mix = dot(grad_logits, k)
                grad_q = jnp.where(low_m, mix[:span], mix[span:]).astype(BF16) * jnp.bfloat16(0.125)
                grad_v = t_dot(weights, grads).astype(BF16)
                gm_ref[base, cols] = grad_q
                gm_ref[base, k_cols] = t_dot(grad_logits, both).astype(BF16)
                gm_ref[base, v_cols] = grad_v
                vec_ref[0:1, cols] += column_sum(grad_q.astype(F32))
                vec_ref[1:2, cols] += column_sum(grad_v.astype(F32))

    def rows_of(cols):
        return pl.BlockSpec((rows_step, cols), lambda i, h: (i, 0))

    return call(
        kernel,
        "attn_bwd",
        (rows // rows_step,),
        (here,),
        [
            rows_of(width), rows_of(width), rows_of(half),
            pl.BlockSpec((width, half), lambda i, h: (0, h[which]), pipeline_mode=pl.Buffered(1)),
            rows_of(width), rows_of(LANES),
            once(table.shape), once((width, width)), rows_of(3 * width),
            pl.BlockSpec((per_step, pairs, 2 * span, span), lambda i, h: (i, 0, 0, 0)),
        ],
        [rows_of(width), rows_of(width), rows_of(3 * width), full((8, width))],
        [
            shaped((rows, width), F32), shaped((rows, width), BF16),
            shaped((rows, 3 * width), BF16), shaped((8, width), F32),
        ],
        [pltpu.VMEM((rows_step, width), BF16)],
        8 * rows * width * width * 2,
        40e6,
        (gh, gres, grad_inner, w_up, n_attn, spread, table, w_out, qkv, probs),
        24, 0, (1,), (0, 2),
    )


def projection_terms(x, grad_mixed, attended, grad_branch, vectors, here, which, got=None):
    rows, width = x.shape
    part = width // 2
    pieces = width // 32 // 8

    def product(x_ref, gm_ref, att_ref, gb_ref, scr):
        step = pl.program_id(0)

        @pl.when(step < 3)
        def _():
            scr[...] = t_dot(x_ref[...], gm_ref[...])

        @pl.when(step == 3)
        def _():
            scr[...] = t_dot(att_ref[...], gb_ref[...])

    def small(here_s, ffn_ref, attn_ref, sent_ref, kept_ref, store):
        first = here_s[0] == 0
        for step in range(4):

            @pl.when(pl.program_id(0) == step)
            def _():
                side, at = step // 2, slice(step % 2 * part, (step % 2 + 1) * part)
                wide = slice(step * part, (step + 1) * part)
                rows_of = (
                    (ffn_ref[0:1, at], ffn_ref[2:3, at], attn_ref[1:2, at], attn_ref[3:4, at]),
                    (ffn_ref[1:2, at], attn_ref[0:1, at], attn_ref[2:3, at], attn_ref[4:5, at]),
                )[side]
                sent, kept = sent_ref[:, wide], kept_ref[:, wide]
                ups = (jnp.where(first, kept, sent), jnp.where(first, sent, kept))
                store(jnp.concatenate(rows_of + ups + (jnp.zeros((2, part), F32),), axis=0))

    def give(here_s, x_ref, gm_ref, att_ref, gb_ref, ffn_ref, attn_ref, sent_ref, kept_ref, out_ref, scr):
        product(x_ref, gm_ref, att_ref, gb_ref, scr)
        out_ref[:width, :] = scr[...].astype(BF16)

        def store(value):
            out_ref[width:, :] = value.astype(BF16)

        small(here_s, ffn_ref, attn_ref, sent_ref, kept_ref, store)

    def own(
        here_s, x_ref, gm_ref, att_ref, gb_ref, ffn_ref, attn_ref, sent_ref, kept_ref, got_ref,
        send_a, keep_a, send_b, keep_b, scr, cut,
    ):
        product(x_ref, gm_ref, att_ref, gb_ref, scr)
        term = scr[...] + got_ref[:width, :].astype(F32)
        cut[...] = term.reshape(cut.shape)
        deal(cut, here_s, (send_a, keep_a, send_b, keep_b), 4, pieces)

        def store(value):
            extra = (value + got_ref[width:, :].astype(F32)).astype(BF16)
            send_a[8 * pieces] = extra
            keep_a[8 * pieces] = extra

        small(here_s, ffn_ref, attn_ref, sent_ref, kept_ref, store)

    in_specs = [
        once((rows, width)),
        pl.BlockSpec((rows, part), lambda i, h: (0, h[which] * 3 + jnp.minimum(i, 2))),
        once((rows, width)),
        pl.BlockSpec((rows, part), lambda i, h: (0, h[which]), pipeline_mode=pl.Buffered(1)),
    ] + [once(item.shape) for item in vectors]
    args = [x, grad_mixed, attended, grad_branch, *vectors]
    flops = 4 * rows * width * width
    if got is None:
        return call(
            give, "proj_give", (4,), (here,), in_specs,
            pl.BlockSpec((width + 8, part), lambda i, *_: (0, i)),
            shaped((width + 8, 4 * part), BF16),
            [pltpu.VMEM((width, part), F32)], flops, 9e6, args, 20, 0, (0,), (3,),
        )
    return call(
        own, "proj_own", (4,), (here,),
        in_specs + [pl.BlockSpec((width + 8, part), lambda i, *_: (0, i))],
        [
            pl.BlockSpec((8 * pieces + extra, 8, part), lambda i, *_: (0, 0, i))
            for extra in (1, 1, 0, 0)
        ],
        [shaped((8 * pieces + extra, 8, 4 * part), BF16) for extra in (1, 1, 0, 0)],
        [pltpu.VMEM((width, part), F32), pltpu.VMEM((4, 2, 2, 2, pieces, 8, part), F32)],
        flops, 11e6, args + [got], 24, 1, (0, 1, 2, 3), (3,),
    )


def input_gradient(grad_mixed, w_qkv, grad_resid, rows_step):
    rows, width = grad_resid.shape

    def kernel(gm_ref, wq_ref, gr_ref, out_ref):
        out_ref[...] = (dot_t(gm_ref[...], wq_ref[...]) + gr_ref[...]).astype(BF16)

    return call(
        kernel, "input_grad", (rows // rows_step,), (),
        [
            pl.BlockSpec((rows_step, 3 * width), lambda i: (i, 0)),
            once((width, 3 * width)),
            pl.BlockSpec((rows_step, width), lambda i: (i, 0)),
        ],
        pl.BlockSpec((rows_step, width), lambda i: (i, 0)),
        shaped((rows, width), BF16), [], 6 * rows * width * width, 13e6,
        (grad_mixed, w_qkv, grad_resid), 20,
    )


def copied(item, here, block):
    rows, width = item.shape

    def kernel(here_s, in_ref, out_ref):
        out_ref[...] = in_ref[...]

    spec = pl.BlockSpec((block, width), lambda i, *_: (i, 0))
    return call(
        kernel, "copied", (rows // block,), (here,), [spec], spec,
        shaped((rows, width), item.dtype), [], 1, 3e6, (item,), 4,
    )


def small_call(kernel, name, here, args, outs, vmem=12):
    return pl.pallas_call(
        kernel,
        in_specs=[pl.BlockSpec(memory_space=pltpu.SMEM)]
        + [pl.BlockSpec(memory_space=pltpu.VMEM)] * len(args),
        out_specs=[pl.BlockSpec(memory_space=pltpu.VMEM)] * len(outs),
        out_shape=outs,
        compiler_params=pltpu.CompilerParams(vmem_limit_bytes=vmem * MIB),
        cost_estimate=pl.CostEstimate(flops=int(1e6 * COST), bytes_accessed=int(4e6 * COST), transcendentals=0),
        name=name,
    )(here, *args)


def add(left, right):
    return (left.astype(F32) + right.astype(F32)).astype(BF16)


def fold_second(terms, here, pieces, extra):
    cols = terms[0][0].shape[2]
    count = len(terms)

    def kernel(here_s, *refs):
        send_a, left_a, send_b, left_b = refs[4 * count :]
        x, y = here_s[2], here_s[3]
        for term in range(count):
            ka, ga, kb, gb = refs[4 * term : 4 * term + 4]
            for z in range(4):
                at = pl.ds((term * 4 + z) * pieces, pieces)

                def sum_of(keep, got, other):
                    rows = pl.ds(z * 2 * pieces + other * pieces, pieces)
                    return add(keep[rows], got[rows])

                send_a[at] = sum_of(ka, ga, 1 - y)
                left_a[at] = sum_of(ka, ga, y)
                send_b[at] = sum_of(kb, gb, 1 - x)
                left_b[at] = sum_of(kb, gb, x)
        if extra:
            total = add(refs[0][8 * pieces], refs[1][8 * pieces])
            send_a[4 * count * pieces] = total
            left_a[4 * count * pieces] = total

    a_out = shaped((4 * count * pieces + extra, 8, cols), BF16)
    b_out = shaped((4 * count * pieces, 8, cols), BF16)
    args = [item for term in terms for item in term]
    return small_call(kernel, "fold_second", here, args, [a_out, a_out, b_out, b_out])


def fold_third(pairs, here, pieces, extra):
    cols = pairs[0].shape[2]
    count = pairs[2].shape[0] // (4 * pieces)

    def kernel(here_s, *refs):
        ins, (send, left) = refs[:-2], refs[-2:]
        low = here_s[4]
        for high in range(2):
            for term in range(count):
                for ab in range(2):
                    keep, got = ins[2 * ab : 2 * ab + 2]
                    at = pl.ds(((high * count + term) * 2 + ab) * pieces, pieces)
                    for out, pick in ((send, 1 - low), (left, low)):
                        rows = pl.ds((term * 4 + high * 2 + pick) * pieces, pieces)
                        out[at] = add(keep[rows], got[rows])
        if extra:
            total = add(ins[0][4 * count * pieces], ins[1][4 * count * pieces])
            send[4 * count * pieces] = total
            left[4 * count * pieces] = total

    out = shaped((4 * count * pieces + extra, 8, cols), BF16)
    return small_call(kernel, "fold_third", here, pairs, [out, out])


def fold_fourth(keep, got, here, extra):
    cols = keep.shape[2]
    count = (keep.shape[0] - extra) // 2

    def kernel(here_s, keep_ref, got_ref, send, left):
        high = here_s[5]
        for out, pick in ((send, 1 - high), (left, high)):
            rows = pl.ds(pick * count, count)
            out[:count] = add(keep_ref[rows], got_ref[rows])
        if extra:
            total = add(keep_ref[2 * count], got_ref[2 * count])
            send[count] = total
            left[count] = total

    out = shaped((count + extra, 8, cols), BF16)
    return small_call(kernel, "fold_fourth", here, (keep, got), [out, out])


def fold_last(keep, got, here, extra):
    cols = keep.shape[2]
    count = keep.shape[0] - extra

    def kernel(here_s, keep_ref, got_ref, *outs):
        outs[0][...] = add(keep_ref[:count], got_ref[:count])
        if extra:
            outs[1][0] = add(keep_ref[count], got_ref[count])

    outs = [shaped((count, 8, cols), BF16)] + [shaped((1, 8, cols), BF16)] * extra
    return small_call(kernel, "fold_last", here, (keep, got), outs)


def chosen_part(here_s, refs, core, side, at):
    me, gx, gc, gd = [item[at].astype(F32) for item in refs]
    same_core, same_side = here_s[0] == core, here_s[2] == side
    return jnp.where(same_core, jnp.where(same_side, me, gx), jnp.where(same_side, gc, gd))


def feed_blocks(parts, here, pieces, width):
    cols = parts[0].shape[2]
    half = width // 2
    folds = cols // half
    rows = 2 * pieces * 8

    def kernel(here_s, me, gx, gc, gd, down_ref, up_ref):
        refs = (me, gx, gc, gd)
        for core in range(2):
            for side in range(2):
                tall = side * folds * rows
                for ab in range(2):
                    at = pl.ds(ab * pieces, pieces)
                    value = chosen_part(here_s, refs, core, side, at).reshape(rows // 2, cols)
                    for fold in range(folds):
                        start = tall + (ab * folds + fold) * (rows // 2)
                        down_ref[start : start + rows // 2, core * half : (core + 1) * half] = value[
                            :, fold * half : (fold + 1) * half
                        ]
                at = pl.ds(2 * pieces, 2 * pieces)
                value = chosen_part(here_s, refs, core, side, at).reshape(rows, cols)
                up_ref[side * rows : (side + 1) * rows, core * cols : (core + 1) * cols] = value

    outs = [shaped((2 * folds * rows, width), F32), shaped((2 * rows, 2 * cols), F32)]
    return small_call(kernel, "feed_blocks", here, parts, outs, 16)


def projection_blocks(parts, vectors, here, pieces):
    cols = parts[0].shape[2]
    rows = 2 * pieces * 8
    cut = cols // 4 * 3
    width = cols // 2
    small = width // 8
    large = cols // 4

    def kernel(here_s, me, gx, gc, gd, vec_ref, qkv_ref, out_ref, *outs):
        refs = (me, gx, gc, gd)
        for core in range(2):
            for side in range(2):
                value = chosen_part(here_s, refs, core, side, slice(None)).reshape(rows, cols)
                at = slice(side * rows, (side + 1) * rows)
                qkv_ref[at, core * cut : (core + 1) * cut] = value[:, :cut]
                out_ref[at, core * (cols - cut) : (core + 1) * (cols - cut)] = value[:, cut:]
        table = vec_ref[0].astype(F32)
        wide = here_s[6]
        shift = lax.rem(width - wide * small, width)
        left, right = pltpu.roll(table[:, :width], shift, 1), pltpu.roll(table[:, width:], shift, 1)
        for row in range(4):
            outs[2 * row][...] = left[row : row + 1, :small]
            outs[2 * row + 1][...] = right[row : row + 1, :small]
        turned = pltpu.roll(table, lax.rem(cols - lax.rem(wide, 4) * large, cols), 1)
        outs[8][...] = jnp.where(wide < 4, turned[4:5, :large], turned[5:6, :large])

    outs = [shaped((2 * rows, 2 * cut), F32), shaped((2 * rows, 2 * (cols - cut)), F32)]
    outs += [shaped((1, small), F32)] * 8 + [shaped((1, large), F32)]
    return small_call(kernel, "projection_blocks", here, (*parts, vectors), outs, 16)


def after(item, *earlier):
    return lax.optimization_barrier((item, *earlier))[0]


def swap(item, axis, step):
    count = lax.axis_size(axis)
    return lax.ppermute(item, axis, [(index, index ^ step) for index in range(count)])


def quarters(mine):
    across = swap(mine, "narrow", 2)
    return mine, across, swap(mine, "narrow", 1), swap(across, "narrow", 1)


def regroup_rows(sent, bucket, wide_count, batches):
    span, width = sent.shape[1:]
    if wide_count == batches:
        got = lax.all_to_all(sent, "wide", split_axis=0, concat_axis=0, tiled=True)
        return got.reshape(batches * span, width)
    send = jnp.zeros((wide_count, span, width), sent.dtype).at[bucket].set(sent)
    got = lax.all_to_all(send, "wide", split_axis=0, concat_axis=0, tiled=True)
    marks = jnp.zeros((wide_count, 1), jnp.int32).at[bucket].set(1)
    filled = lax.all_to_all(marks, "wide", split_axis=0, concat_axis=0, tiled=True)[:, 0]
    place = jnp.where(filled > 0, jnp.cumsum(filled) - filled, batches)
    chosen = (
        jnp.zeros((batches,), jnp.int32)
        .at[place]
        .set(jnp.arange(wide_count, dtype=jnp.int32), mode="drop")
    )
    return got[chosen].reshape(batches * span, width)


def sum_anywhere(item, wide_count, narrow_count):
    blocks = item.astype(F32).reshape(wide_count, -1)
    extent = blocks.shape[1]
    padded = (extent + narrow_count - 1) // narrow_count * narrow_count
    blocks = jnp.pad(blocks, ((0, 0), (0, padded - extent))).reshape(-1)
    share = lax.psum_scatter(blocks, ("wide", "narrow"), scatter_dimension=0, tiled=True)
    whole = lax.all_gather(share.astype(BF16), "narrow", axis=0, tiled=True).astype(F32)
    return whole[:extent].reshape((item.shape[0] // wide_count,) + item.shape[1:])


def body(
    tokens, bucket, lengths, pairing, targets, w_qkv, bias_q, bias_v, w_out, bias_out,
    gain_attn, shift_attn, w_up, bias_up, w_down, bias_down, gain_ffn, shift_ffn,
):
    wide_count, narrow_count = lax.axis_size("wide"), lax.axis_size("narrow")
    batches = bucket.shape[0]
    rows, width = tokens.shape
    span = rows // batches
    paired = (wide_count, narrow_count) == (8, 4)
    wide, narrow = lax.axis_index("wide"), lax.axis_index("narrow")
    if paired:
        core = narrow % 2
        here = jnp.stack(
            [core, 1 - core, narrow // 2, wide % 2, wide // 2 % 2, wide // 4, wide, narrow]
        ).astype(jnp.int32)
    else:
        here = jnp.arange(8, dtype=jnp.int32)
    table = vector_table(
        [bias_q, bias_v, bias_out, gain_attn, shift_attn, bias_down, gain_ffn, shift_ffn, bias_up], width
    )
    ordered = wide_count == batches
    slots = bucket if ordered else jnp.arange(batches, dtype=jnp.int32)
    pieces = width // 32 // 8

    qkv, probs, attended, n_attn, spread, sid = attention_forward(
        tokens, w_qkv, w_out, table, bucket, lengths, wide_count // batches, span, 2 * span
    )
    active, slope, hidden_t, sent, gres, grad_second, vec_ffn = feed_forward(
        n_attn, w_up, w_down, table, sid, slots, pairing, targets, batches, 2 * span
    )
    ups = (grad_second, slope, hidden_t, w_down)
    heads = (n_attn, spread, table, w_out, qkv, probs)
    down_sent = down_terms(active, grad_second, here, 1)
    if paired:
        encoded = regroup_rows(after(sent, down_sent), bucket, wide_count, batches)
        up_sent, gi_sent, bup_sent = up_terms(*ups, after(here, down_sent), 1)
        down_dealt = down_terms(active, grad_second, after(here, bup_sent), 0, swap(down_sent, "narrow", 1))
        down_a, down_b = swap(down_dealt[0], "narrow", 2), swap(down_dealt[2], "wide", 1)
        gh = hidden_gradient(gi_sent, w_up, after(here, down_dealt[1]), 1)
        *up_dealt, gi_kept, bup_kept = up_terms(
            *ups, after(here, gh), 0, swap(up_sent, "narrow", 1)
        )
        up_a, up_b = swap(up_dealt[0], "narrow", 2), swap(up_dealt[2], "wide", 1)
        gr, gb, gm, vec_attn = attention_backward(
            gh, gres, gi_kept, w_up, *heads, after(here, up_dealt[1]), 0, span, 2 * span
        )
        feed = fold_second(
            [
                (down_dealt[1], down_a, down_dealt[3], down_b),
                (up_dealt[1], up_a, up_dealt[3], up_b),
            ],
            after(here, vec_attn, encoded), pieces, 0,
        )
        feed_a, feed_b = swap(feed[0], "wide", 1), swap(feed[2], "narrow", 2)
        projections = (tokens, gm, attended, gb, (vec_ffn, vec_attn, bup_sent, bup_kept))
        proj_sent = projection_terms(*projections, after(here, feed[1]), 1)
        proj_dealt = projection_terms(
            *projections, after(here, proj_sent), 0, swap(proj_sent, "narrow", 1)
        )
        proj_a, proj_b = swap(proj_dealt[0], "narrow", 2), swap(proj_dealt[2], "wide", 1)
        send, feed = fold_third(
            [feed[1], feed_a, feed[3], feed_b], after(here, proj_dealt[1]), pieces, 0
        )
        feed_got = swap(send, "wide", 2)
        grad_tokens = input_gradient(after(gm, feed), w_qkv, gr, 2 * span)
        send, feed = fold_fourth(feed, feed_got, after(here, grad_tokens), 0)
        feed_got = swap(send, "wide", 4)
        proj_dealt = fold_second(
            [(proj_dealt[1], proj_a, proj_dealt[3], proj_b)], after(here, feed), pieces, 1
        )
        proj_a, proj_b = swap(proj_dealt[0], "wide", 1), swap(proj_dealt[2], "narrow", 2)
        encoded = copied(encoded, after(here, proj_dealt[1]), span)
        send, proj = fold_third(
            [proj_dealt[1], proj_a, proj_dealt[3], proj_b], after(here, encoded), pieces, 1
        )
        proj_got = swap(send, "wide", 2)
        (feed,) = fold_last(feed, feed_got, after(here, proj), 0)
        feed = quarters(feed)
        send, proj = fold_fourth(proj, proj_got, after(here, feed[0]), 1)
        grad_w_down, grad_w_up = feed_blocks(feed, after(here, proj), pieces, width)
        proj_got = swap(send, "wide", 4)
        proj, vectors = fold_last(proj, proj_got, after(here, grad_w_down), 1)
        proj = quarters(proj)
        grad_w_qkv, grad_w_out, *small = projection_blocks(proj, vectors, here, pieces)
        small = [item.reshape(-1) for item in small]
    else:
        encoded = regroup_rows(sent, bucket, wide_count, batches)
        down_kept = down_terms(active, grad_second, here, 0)
        up_sent, gi_sent, bup_sent = up_terms(*ups, here, 1)
        up_kept, gi_kept, bup_kept = up_terms(*ups, here, 0)
        gh = hidden_gradient(gi_sent, w_up, here, 1)
        gr, gb, gm, vec_attn = attention_backward(
            gh, gres, gi_kept, w_up, *heads, here, 0, span, 2 * span
        )
        projections = (tokens, gm, attended, gb, (vec_ffn, vec_attn, bup_sent, bup_kept), here)
        grad_tokens = input_gradient(gm, w_qkv, gr, 2 * span)
        proj_sent, proj_kept = projection_terms(*projections, 1), projection_terms(*projections, 0)
        total = partial(sum_anywhere, wide_count=wide_count, narrow_count=narrow_count)
        cut = width // 2 * 3
        grad_w_down = total(jnp.concatenate([down_kept, down_sent], axis=1))
        grad_w_up = total(jnp.concatenate([up_kept, up_sent], axis=1))
        grad_w_qkv = total(jnp.concatenate([proj_kept[:width, :cut], proj_sent[:width, :cut]], axis=1))
        grad_w_out = total(jnp.concatenate([proj_kept[:width, cut:], proj_sent[:width, cut:]], axis=1))
        small = [
            total(item)
            for item in (*vec_ffn[:3], *vec_attn[:5], jnp.concatenate([bup_kept[0], bup_sent[0]]))
        ]
    gain_out, shift_out, b_down, b_q, b_v, b_out, g_attn, s_attn, b_up = small
    return (
        encoded, grad_tokens, grad_w_qkv, b_q, b_v, grad_w_out, b_out, g_attn, s_attn,
        grad_w_up, b_up, grad_w_down, b_down, gain_out, shift_out,
    )


def solution(mesh):
    split = P(("wide", "narrow"))
    in_specs = (
        P(("wide", "narrow"), None), split, split, P(("wide", "narrow"), None), split,
    ) + (P(),) * 13
    out_specs = (
        P(("wide", "narrow"), None), P(("wide", "narrow"), None),
        P("wide", None), P("wide"), P("wide"), P("wide", None), P("wide"), P("wide"), P("wide"),
        P("wide", None), P("wide"), P("wide", None), P("wide"), P("wide"), P("wide"),
    )
    return jax.shard_map(body, mesh=mesh, in_specs=in_specs, out_specs=out_specs, check_vma=False)
```

```python
from functools import partial

import jax
import jax.numpy as jnp
from jax import lax
from jax.experimental import pallas as pl
from jax.experimental.pallas import tpu as pltpu
from jax.sharding import PartitionSpec as P

HDIM = 64
KTOP = 12
NORM_EPS = 1e-12
COS_EPS = 1e-06
MASKED = -1000000000.0
LOSS_SCALE = 1024.0
F32 = jnp.float32
BF16 = jnp.bfloat16
LANES = 128
MIB = 1024 * 1024
LARGE = 100000
COST = 0.05
HALF_ROOT = 0.7071067811865476
BELL_RATE = -0.7213475204444817
BELL_PEAK = -1.3257480647361595
ROW_BQ, ROW_BV, ROW_BO, ROW_GA, ROW_SA, ROW_BD, ROW_GF, ROW_SF, ROW_BU = range(9)


def dot(left, right):
    return jnp.dot(left, right, preferred_element_type=F32)


def dot_t(left, right):
    return lax.dot_general(left, right, (((1,), (1,)), ((), ())), preferred_element_type=F32)


def t_dot(left, right):
    return lax.dot_general(left, right, (((0,), (0,)), ((), ())), preferred_element_type=F32)


def full(shape):
    return pl.BlockSpec(shape, lambda *_: (0,) * len(shape))


def once(shape):
    return pl.BlockSpec(shape, lambda *_: (0,) * len(shape), pipeline_mode=pl.Buffered(1))


def large(item):
    return item.size >= LARGE


def shaped(shape, dtype):
    return jax.ShapeDtypeStruct(shape, dtype)


def call(
    kernel, name, grid, prefetch, in_specs, out_specs, out_shape, scratch, flops, moved, args, vmem=24, free=0, loose=(), near=()
):
    single = not isinstance(out_shape, list)
    shapes = [out_shape] if single else out_shape
    shapes = [
        pltpu.HBM(item.shape, item.dtype) if large(item) and number not in loose else item
        for number, item in enumerate(shapes)
    ]
    out_shape = shapes[0] if single else shapes
    args = [
        pltpu.with_memory_space_constraint(item, pltpu.HBM)
        if large(item) and number < len(args) - free and number not in near
        else item
        for number, item in enumerate(args)
    ]
    return pl.pallas_call(
        kernel,
        grid_spec=pltpu.PrefetchScalarGridSpec(
            num_scalar_prefetch=len(prefetch),
            grid=grid,
            in_specs=in_specs,
            out_specs=out_specs,
            scratch_shapes=scratch,
        ),
        out_shape=out_shape,
        compiler_params=pltpu.CompilerParams(
            dimension_semantics=("arbitrary",) * len(grid), vmem_limit_bytes=vmem * MIB
        ),
        cost_estimate=pl.CostEstimate(flops=int(flops * COST), bytes_accessed=int(moved * COST), transcendentals=0),
        name=name,
    )(*[pltpu.with_memory_space_constraint(item, pltpu.HBM) for item in prefetch], *args)


def norm_forward(values):
    center = values - jnp.mean(values, axis=-1, keepdims=True)
    spread = lax.rsqrt(jnp.mean(center * center, axis=-1, keepdims=True) + NORM_EPS)
    return center * spread, spread


def norm_backward(grad_out, normed, spread, gain):
    scaled = grad_out * gain
    mean_scaled = jnp.mean(scaled, axis=-1, keepdims=True)
    mean_product = jnp.mean(scaled * normed, axis=-1, keepdims=True)
    return spread * (scaled - mean_scaled - normed * mean_product)


def column_sum(values):
    return jnp.sum(values, axis=0, keepdims=True)


def gelu_pair(v):
    phi = 0.5 + 0.5 * lax.erf(v * HALF_ROOT)
    bell = jnp.exp2((v * v) * BELL_RATE + BELL_PEAK)
    return v * phi, phi + v * bell


def head_masks():
    lane = lax.broadcasted_iota(jnp.int32, (1, LANES), 1)
    low = (lane < HDIM).astype(F32)
    return low.astype(BF16), (1.0 - low).astype(BF16), lane < HDIM


def sentence_count(bucket_s, number, group_size):
    kind = bucket_s[number]
    if group_size > 1:
        kind = kind // group_size
    return jnp.maximum(1, lax.shift_right_logical(jnp.int32(KTOP), kind))


def row_sentences(batch, bucket_s, lengths_s, group_size, batches, sent, span):
    start = jnp.int32(0)
    for other in range(batches):
        start += jnp.where(other < batch, sentence_count(bucket_s, other, group_size), 0)
    count = sentence_count(bucket_s, batch, group_size)
    lane = lax.broadcasted_iota(jnp.int32, (8, span), 1)
    row = lax.broadcasted_iota(jnp.int32, (span, span), 0)
    passed_lane = jnp.zeros((8, span), jnp.int32)
    passed_row = jnp.zeros((span, span), jnp.int32)
    finish = jnp.int32(0)
    for number in range(KTOP):
        finish += lengths_s[jnp.minimum(start + number, sent - 1)]
        bound = jnp.where(number < count, finish, span)
        passed_lane += (lane >= bound).astype(jnp.int32)
        passed_row += (row >= bound).astype(jnp.int32)
    sid_lane = jnp.where(passed_lane < count, start + passed_lane, -1)
    sid_row = jnp.where(passed_row < count, start + passed_row, -1)
    return sid_lane, sid_row


def vector_table(vectors, width):
    def kernel(*refs):
        out_ref = refs[-1]
        at = 0
        for ref in refs[:-1]:
            for part in range(ref.shape[0] // width):
                out_ref[at : at + 1, :] = ref[part * width : (part + 1) * width].astype(F32).reshape(1, width)
                at += 1

    rows = sum(item.shape[0] for item in vectors) // width
    return pl.pallas_call(
        kernel,
        grid=(1,),
        in_specs=[full(item.shape) for item in vectors],
        out_specs=full((rows, width)),
        out_shape=shaped((rows, width), F32),
        compiler_params=pltpu.CompilerParams(vmem_limit_bytes=4 * MIB),
        name="vector_table",
    )(*[pltpu.with_memory_space_constraint(item, pltpu.HBM) for item in vectors])


def attention_forward(x, w_qkv, w_out, table, bucket, lengths, group_size, span, rows_step):
    rows, width = x.shape
    batches = rows // span
    pairs = width // LANES
    sent = lengths.shape[0]
    per_step = rows_step // span

    def kernel(bucket_s, lengths_s, x_ref, wq_ref, wo_ref, tab_ref, qkv_ref, p_ref, att_ref, n_ref, s_ref, sid_ref):
        step = pl.program_id(0)
        low_b, high_b, low_m = head_masks()
        x_in = x_ref[...]
        mixed = dot(x_in, wq_ref[:, :width]) + tab_ref[ROW_BQ : ROW_BQ + 1, :]
        qkv_ref[:, :width] = (mixed * 0.125).astype(BF16)
        qkv_ref[:, width : 2 * width] = dot(x_in, wq_ref[:, width : 2 * width]).astype(BF16)
        mixed = dot(x_in, wq_ref[:, 2 * width :]) + tab_ref[ROW_BV : ROW_BV + 1, :]
        qkv_ref[:, 2 * width :] = mixed.astype(BF16)
        eye = lax.broadcasted_iota(jnp.int32, (span, span), 0) == lax.broadcasted_iota(
            jnp.int32, (span, span), 1
        )
        for inner in range(per_step):
            sid_lane, sid_row = row_sentences(
                step * per_step + inner, bucket_s, lengths_s, group_size, batches, sent, span
            )
            sid_ref[inner] = sid_lane
            same = (sid_row == sid_lane[0:1, :]) & (sid_row >= 0)
            bias = jnp.where(same | eye, 0.0, MASKED)
            bias = jnp.concatenate([bias, bias], axis=0)
            base = slice(inner * span, (inner + 1) * span)
            for pair in range(pairs):
                cols = slice(pair * LANES, (pair + 1) * LANES)
                q = qkv_ref[base, cols]
                k = qkv_ref[base, width + pair * LANES : width + (pair + 1) * LANES]
                v = qkv_ref[base, 2 * width + pair * LANES : 2 * width + (pair + 1) * LANES]
                both = jnp.concatenate([q * low_b, q * high_b], axis=0)
                logits = dot_t(both, k) + bias
                raised = jnp.exp(logits - jnp.max(logits, axis=-1, keepdims=True))
                total = jnp.sum(raised, axis=-1, keepdims=True)
                probs = (raised * (1.0 / total)).astype(BF16)
                p_ref[inner, pair] = probs
                mix = dot(probs, v)
                att_ref[base, cols] = jnp.where(low_m, mix[:span], mix[span:]).astype(BF16)
        branch = dot(att_ref[...], wo_ref[...]) + tab_ref[ROW_BO : ROW_BO + 1, :]
        normed, spread = norm_forward(x_in.astype(F32) + branch)
        n_ref[...] = normed
        s_ref[...] = jnp.broadcast_to(spread, (rows_step, LANES))

    return call(
        kernel,
        "attn_fwd",
        (rows // rows_step,),
        (bucket, lengths),
        [
            pl.BlockSpec((rows_step, width), lambda i, *_: (i, 0)),
            once((width, 3 * width)),
            once((width, width)),
            once(table.shape),
        ],
        [
            pl.BlockSpec((rows_step, 3 * width), lambda i, *_: (i, 0)),
            pl.BlockSpec((per_step, pairs, 2 * span, span), lambda i, *_: (i, 0, 0, 0)),
            pl.BlockSpec((rows_step, width), lambda i, *_: (i, 0)),
            pl.BlockSpec((rows_step, width), lambda i, *_: (i, 0)),
            pl.BlockSpec((rows_step, LANES), lambda i, *_: (i, 0)),
            pl.BlockSpec((per_step, 8, span), lambda i, *_: (i, 0, 0)),
        ],
        [
            shaped((rows, 3 * width), BF16),
            shaped((batches, pairs, 2 * span, span), BF16),
            shaped((rows, width), BF16),
            shaped((rows, width), F32),
            shaped((rows, LANES), F32),
            shaped((batches, 8, span), jnp.int32),
        ],
        [],
        8 * rows * width * width * 2,
        30e6,
        (x, w_qkv, w_out, table),
        26,
    )


def feed_forward(n_attn, w_up, w_down, table, sid, slots, pairing, targets, slot_count, block):
    rows, width = n_attn.shape
    ff = w_up.shape[1]
    batches, _, span = sid.shape
    pair_count = targets.shape[0]
    side = -(-pair_count // 8) * 8
    chunk = width
    steps = ff // chunk
    blocks = rows // block
    per_block = block // span

    def kernel(
        slots_s, pairing_s, targets_s, n_ref, wu_ref, wd_ref, tab_ref, sid_ref,
        act_ref, dg_ref, ht_ref, enc_ref, gres_ref, gsl_ref, vec_ref, low_scr, acc_scr, spread_scr,
    ):
        step = pl.program_id(0)
        gain = tab_ref[ROW_GA : ROW_GA + 1, :]
        shift = tab_ref[ROW_SA : ROW_SA + 1, :]

        @pl.when(step == 0)
        def _():
            hidden = (n_ref[...] * gain + shift).astype(BF16)
            low_scr[...] = hidden
            ht_ref[...] = hidden.T
            acc_scr[...] = jnp.zeros_like(acc_scr)

        for number in range(blocks):
            base = slice(number * block, (number + 1) * block)
            inner = dot(low_scr[base, :], wu_ref[...]) + tab_ref[pl.ds(ROW_BU + step, 1), :]
            active, slope = gelu_pair(inner)
            active = active.astype(BF16)
            act_ref[base, :] = active
            dg_ref[base, :] = slope.astype(BF16)
            acc_scr[base, :] += dot(active, wd_ref[...])

        @pl.when(step == steps - 1)
        def _():
            gain_out = tab_ref[ROW_GF : ROW_GF + 1, :]
            shift_out = tab_ref[ROW_SF : ROW_SF + 1, :]
            slot = lax.broadcasted_iota(jnp.int32, (2 * side, span), 0)
            wanted = jnp.full((2 * side, span), -2, jnp.int32)
            goal = jnp.zeros((side, LANES), F32)
            goal_slot = lax.broadcasted_iota(jnp.int32, (side, LANES), 0)
            for number in range(pair_count):
                wanted = jnp.where(slot == number, pairing_s[0, 2 * number], wanted)
                wanted = jnp.where(slot == side + number, pairing_s[0, 2 * number + 1], wanted)
                goal = jnp.where(goal_slot == number, targets_s[number], goal)
            members = [
                (sid_ref[number][0:1, :] == wanted).astype(F32) for number in range(batches)
            ]
            sizes = jnp.zeros((2 * side, 1), F32)
            for member in members:
                sizes += jnp.sum(member, axis=-1, keepdims=True)
            share = 1.0 / jnp.maximum(sizes, 1.0)
            picks = [
                jnp.concatenate(members[number * per_block : (number + 1) * per_block], axis=1).astype(BF16)
                for number in range(blocks)
            ]
            ones = jnp.ones((2 * side, LANES), BF16)
            pooled = jnp.zeros((2 * side, width), F32)
            for number in range(blocks):
                base = slice(number * block, (number + 1) * block)
                resid = (
                    n_ref[base, :] * gain + shift + acc_scr[base, :] + tab_ref[ROW_BD : ROW_BD + 1, :]
                )
                normed, spread = norm_forward(resid)
                acc_scr[base, :] = normed
                spread_scr[base, :] = jnp.broadcast_to(spread, (block, LANES))
                out = normed * gain_out + shift_out
                high = out.astype(BF16)
                rest = (out - high.astype(F32)).astype(BF16)
                pooled += dot(picks[number], high) + dot(picks[number], rest)
                valid = t_dot(picks[number], ones)
                for col in range(width // LANES):
                    cols = slice(col * LANES, (col + 1) * LANES)
                    kept = (out[:, cols] * valid).astype(BF16)
                    for inner in range(per_block):
                        enc_ref[slots_s[number * per_block + inner], :, cols] = kept[
                            inner * span : (inner + 1) * span
                        ]
            pooled = pooled * share
            first, partner = pooled[:side], pooled[side:]
            cross = jnp.sum(first * partner, axis=-1, keepdims=True)
            scale_first = lax.rsqrt(jnp.sum(first * first, axis=-1, keepdims=True) + COS_EPS)
            scale_partner = lax.rsqrt(jnp.sum(partner * partner, axis=-1, keepdims=True) + COS_EPS)
            cosine = cross * scale_first * scale_partner
            factor = 2.0 * LOSS_SCALE * (cosine - goal[:, :1])
            both_scales = factor * scale_first * scale_partner
            grad_first = both_scales * partner - (factor * cosine * scale_first * scale_first) * first
            grad_partner = (
                both_scales * first - (factor * cosine * scale_partner * scale_partner) * partner
            )
            grad_home = jnp.concatenate([grad_first, grad_partner], axis=0) * share
            high = grad_home.astype(BF16)
            rest = (grad_home - high.astype(F32)).astype(BF16)
            vec_ref[...] = jnp.zeros_like(vec_ref)
            for number in range(blocks):
                base = slice(number * block, (number + 1) * block)
                grad_out = t_dot(picks[number], high) + t_dot(picks[number], rest)
                normed = acc_scr[base, :]
                resid = norm_backward(grad_out, normed, spread_scr[base, :1], gain_out)
                gres_ref[base, :] = resid
                low = resid.astype(BF16)
                gsl_ref[base, :] = low
                vec_ref[0:1, :] += column_sum(grad_out * normed)
                vec_ref[1:2, :] += column_sum(grad_out)
                vec_ref[2:3, :] += column_sum(low.astype(F32))

    return call(
        kernel,
        "ffn_fwd",
        (steps,),
        (slots, pairing, targets),
        [
            once((rows, width)),
            pl.BlockSpec((width, chunk), lambda j, *_: (0, j)),
            pl.BlockSpec((chunk, width), lambda j, *_: (j, 0)),
            once(table.shape),
            once((batches, 8, span)),
        ],
        [
            pl.BlockSpec((rows, chunk), lambda j, *_: (0, j)),
            pl.BlockSpec((rows, chunk), lambda j, *_: (0, j)),
            once((width, rows)),
            once((slot_count, span, width)),
            once((rows, width)),
            once((rows, width)),
            once((8, width)),
        ],
        [
            shaped((rows, ff), BF16),
            shaped((rows, ff), BF16),
            shaped((width, rows), BF16),
            shaped((slot_count, span, width), BF16),
            shaped((rows, width), F32),
            shaped((rows, width), BF16),
            shaped((8, width), F32),
        ],
        [
            pltpu.VMEM((rows, width), BF16),
            pltpu.VMEM((rows, width), F32),
            pltpu.VMEM((rows, LANES), F32),
        ],
        8 * rows * width * ff,
        40e6,
        (n_attn, w_up, w_down, table, sid),
        38, 0, (2, 5),
    )


def deal(scratch, here_s, outs, z_count, pieces, folds=1):
    send_a, keep_a, send_b, keep_b = outs
    x, y = here_s[2], here_s[3]
    cols = scratch.shape[-1]
    for z in range(z_count):
        for other in range(2):
            at = pl.ds((z * 2 + other) * pieces, pieces)
            for fold in range(folds):
                part = pl.ds(fold * pieces, pieces)
                to = slice(fold * cols, (fold + 1) * cols)
                send_a[at, :, to] = scratch[z, other, 1 - x, 0, part].astype(BF16)
                keep_a[at, :, to] = scratch[z, other, x, 0, part].astype(BF16)
                send_b[at, :, to] = scratch[z, 1 - y, other, 1, part].astype(BF16)
                keep_b[at, :, to] = scratch[z, y, other, 1, part].astype(BF16)


def down_terms(active, grad_second, here, which, got=None):
    rows, ff = active.shape
    width = grad_second.shape[1]
    half = width // 2
    steps = 4
    tall = ff // steps
    pieces = width // 32 // 8
    folds = ff // width

    def give(here_s, act_ref, gs_ref, out_ref):
        out_ref[...] = t_dot(act_ref[...], gs_ref[...]).astype(BF16)

    def own(here_s, act_ref, gs_ref, got_ref, *rest):
        outs, scratch = rest[:4], rest[4]
        term = t_dot(act_ref[...], gs_ref[...]) + got_ref[...].astype(F32)
        scratch[...] = term.reshape(scratch.shape)
        deal(scratch, here_s, outs, 1, pieces, folds)

    in_specs = [
        pl.BlockSpec((rows, tall), lambda i, here_s: (0, i)),
        pl.BlockSpec((rows, half), lambda i, here_s: (0, here_s[which]), pipeline_mode=pl.Buffered(1)),
    ]
    flops = 2 * rows * ff * half
    if got is None:
        return call(
            give, "down_give", (steps,), (here,), in_specs,
            pl.BlockSpec((tall, half), lambda i, *_: (i, 0)),
            shaped((ff, half), BF16), [], flops, 9e6, (active, grad_second), 20, 0, (0,), (1,),
        )
    block = (2 * pieces, 8, folds * half)
    return call(
        own, "down_own", (steps,), (here,),
        in_specs + [pl.BlockSpec((tall, half), lambda i, *_: (i, 0))],
        [pl.BlockSpec(block, lambda i, *_: (i, 0, 0))] * 4,
        [shaped((8 * pieces, 8, folds * half), BF16)] * 4,
        [pltpu.VMEM((1, 2, 2, 2, folds * pieces, 8, half), F32)],
        flops, 11e6, (active, grad_second, got), 24, 1, (0, 2), (1,),
    )


def up_terms(grad_second, slope, hidden_t, w_down, here, which, got=None):
    rows, width = grad_second.shape
    ff = w_down.shape[0]
    half = ff // 2
    chunk = width
    steps = half // chunk
    block = rows // 4
    pieces = width // 32 // 8

    def kernel(here_s, gs_ref, dg_ref, ht_ref, wd_ref, *refs):
        if got is not None:
            got_ref, refs = refs[0], refs[1:]
            outs, refs = refs[:4], refs[4:]
        else:
            out_ref, refs = refs[0], refs[1:]
        gi_ref, bu_ref = refs[:2]
        sums = jnp.zeros((1, chunk), F32)
        for number in range(rows // block):
            base = slice(number * block, (number + 1) * block)
            grad_active = dot_t(gs_ref[base, :], wd_ref[...])
            low = (grad_active * dg_ref[base, :].astype(F32)).astype(BF16)
            gi_ref[base, :] = low
            sums += column_sum(low.astype(F32))
        bu_ref[...] = sums
        term = dot(ht_ref[...], gi_ref[...])
        if got is None:
            out_ref[...] = term.astype(BF16)
        else:
            scratch = refs[2]
            term += got_ref[...].astype(F32)
            scratch[...] = term.reshape(scratch.shape)
            deal(scratch, here_s, outs, 4, pieces)

    def col(i, here_s):
        return here_s[which] * steps + i

    in_specs = [
        once((rows, width)),
        pl.BlockSpec((rows, chunk), lambda i, h: (0, col(i, h))),
        once((width, rows)),
        pl.BlockSpec((chunk, width), lambda i, h: (col(i, h), 0)),
    ]
    args = [grad_second, slope, hidden_t, w_down]
    scratch = []
    if got is None:
        out_specs = [pl.BlockSpec((width, chunk), lambda i, *_: (0, i))]
        out_shape = [shaped((width, half), BF16)]
    else:
        in_specs.append(pl.BlockSpec((width, chunk), lambda i, *_: (0, i)))
        args.append(got)
        out_specs = [pl.BlockSpec((8 * pieces, 8, chunk), lambda i, *_: (0, 0, i))] * 4
        out_shape = [shaped((8 * pieces, 8, half), BF16)] * 4
        scratch.append(pltpu.VMEM((4, 2, 2, 2, pieces, 8, chunk), F32))
    return call(
        kernel, "up_give" if got is None else "up_own", (steps,), (here,), in_specs,
        out_specs
        + [
            pl.BlockSpec((rows, chunk), lambda i, *_: (0, i)),
            pl.BlockSpec((1, chunk), lambda i, *_: (0, i)),
        ],
        out_shape + [shaped((rows, half), BF16), shaped((1, half), F32)],
        scratch, 4 * rows * width * half, 16e6, args, 26, 0 if got is None else 1, (0,) if got is None else (0, 2, 4), (0, 2),
    )


def hidden_gradient(grad_inner, w_up, here, which):
    rows, half = grad_inner.shape
    width = w_up.shape[0]
    block = rows // 2

    def kernel(here_s, gi_ref, wu_ref, out_ref):
        out_ref[...] = dot_t(gi_ref[...], wu_ref[...])

    return call(
        kernel, "hidden_grad", (rows // block,), (here,),
        [
            pl.BlockSpec((block, half), lambda i, h: (i, 0)),
            pl.BlockSpec((width, half), lambda i, h: (0, h[which]), pipeline_mode=pl.Buffered(1)),
        ],
        pl.BlockSpec((block, width), lambda i, h: (i, 0)),
        shaped((rows, width), F32), [], 2 * rows * width * half, 9e6, (grad_inner, w_up), 16, 0, (0,),
    )


def attention_backward(gh, gres, grad_inner, w_up, n_attn, spread, table, w_out, qkv, probs, here, which, span, rows_step):
    rows, width = gh.shape
    half = grad_inner.shape[1]
    pairs = width // LANES
    per_step = rows_step // span

    def kernel(here_s, gh_ref, gres_ref, gi_ref, wu_ref, n_ref, s_ref, tab_ref, wo_ref, qkv_ref, p_ref, gr_ref, gb_ref, gm_ref, vec_ref, ga_scr):
        step = pl.program_id(0)
        low_b, high_b, low_m = head_masks()

        @pl.when(step == 0)
        def _():
            vec_ref[...] = jnp.zeros_like(vec_ref)

        normed = n_ref[...]
        grad_hidden = dot_t(gi_ref[...], wu_ref[...]) + gh_ref[...] + gres_ref[...]
        resid = norm_backward(grad_hidden, normed, s_ref[:, :1], tab_ref[ROW_GA : ROW_GA + 1, :])
        gr_ref[...] = resid
        low = resid.astype(BF16)
        gb_ref[...] = low
        vec_ref[2:3, :] += column_sum(low.astype(F32))
        vec_ref[3:4, :] += column_sum(grad_hidden * normed)
        vec_ref[4:5, :] += column_sum(grad_hidden)
        ga_scr[...] = dot_t(low, wo_ref[...]).astype(BF16)
        for inner in range(per_step):
            base = slice(inner * span, (inner + 1) * span)
            for pair in range(pairs):
                cols = slice(pair * LANES, (pair + 1) * LANES)
                k_cols = slice(width + pair * LANES, width + (pair + 1) * LANES)
                v_cols = slice(2 * width + pair * LANES, 2 * width + (pair + 1) * LANES)
                q, k, v = qkv_ref[base, cols], qkv_ref[base, k_cols], qkv_ref[base, v_cols]
                grad = ga_scr[base, cols]
                grads = jnp.concatenate([grad * low_b, grad * high_b], axis=0)
                both = jnp.concatenate([q * low_b, q * high_b], axis=0)
                weights = p_ref[inner, pair]
                wide = weights.astype(F32)
                grad_probs = dot_t(grads, v)
                balance = jnp.sum(wide * grad_probs, axis=-1, keepdims=True)
                grad_logits = (wide * (grad_probs - balance)).astype(BF16)
                mix = dot(grad_logits, k)
                grad_q = jnp.where(low_m, mix[:span], mix[span:]).astype(BF16) * jnp.bfloat16(0.125)
                grad_v = t_dot(weights, grads).astype(BF16)
                gm_ref[base, cols] = grad_q
                gm_ref[base, k_cols] = t_dot(grad_logits, both).astype(BF16)
                gm_ref[base, v_cols] = grad_v
                vec_ref[0:1, cols] += column_sum(grad_q.astype(F32))
                vec_ref[1:2, cols] += column_sum(grad_v.astype(F32))

    def rows_of(cols):
        return pl.BlockSpec((rows_step, cols), lambda i, h: (i, 0))

    return call(
        kernel,
        "attn_bwd",
        (rows // rows_step,),
        (here,),
        [
            rows_of(width), rows_of(width), rows_of(half),
            pl.BlockSpec((width, half), lambda i, h: (0, h[which]), pipeline_mode=pl.Buffered(1)),
            rows_of(width), rows_of(LANES),
            once(table.shape), once((width, width)), rows_of(3 * width),
            pl.BlockSpec((per_step, pairs, 2 * span, span), lambda i, h: (i, 0, 0, 0)),
        ],
        [rows_of(width), rows_of(width), rows_of(3 * width), full((8, width))],
        [
            shaped((rows, width), F32), shaped((rows, width), BF16),
            shaped((rows, 3 * width), BF16), shaped((8, width), F32),
        ],
        [pltpu.VMEM((rows_step, width), BF16)],
        8 * rows * width * width * 2,
        40e6,
        (gh, gres, grad_inner, w_up, n_attn, spread, table, w_out, qkv, probs),
        24, 0, (1,), (0, 2),
    )


def projection_terms(x, grad_mixed, attended, grad_branch, vectors, here, which, got=None):
    rows, width = x.shape
    part = width // 2
    pieces = width // 32 // 8

    def product(x_ref, gm_ref, att_ref, gb_ref, scr):
        step = pl.program_id(0)

        @pl.when(step < 3)
        def _():
            scr[...] = t_dot(x_ref[...], gm_ref[...])

        @pl.when(step == 3)
        def _():
            scr[...] = t_dot(att_ref[...], gb_ref[...])

    def small(here_s, ffn_ref, attn_ref, sent_ref, kept_ref, store):
        first = here_s[0] == 0
        for step in range(4):

            @pl.when(pl.program_id(0) == step)
            def _():
                side, at = step // 2, slice(step % 2 * part, (step % 2 + 1) * part)
                wide = slice(step * part, (step + 1) * part)
                rows_of = (
                    (ffn_ref[0:1, at], ffn_ref[2:3, at], attn_ref[1:2, at], attn_ref[3:4, at]),
                    (ffn_ref[1:2, at], attn_ref[0:1, at], attn_ref[2:3, at], attn_ref[4:5, at]),
                )[side]
                sent, kept = sent_ref[:, wide], kept_ref[:, wide]
                ups = (jnp.where(first, kept, sent), jnp.where(first, sent, kept))
                store(jnp.concatenate(rows_of + ups + (jnp.zeros((2, part), F32),), axis=0))

    def give(here_s, x_ref, gm_ref, att_ref, gb_ref, ffn_ref, attn_ref, sent_ref, kept_ref, out_ref, scr):
        product(x_ref, gm_ref, att_ref, gb_ref, scr)
        out_ref[:width, :] = scr[...].astype(BF16)

        def store(value):
            out_ref[width:, :] = value.astype(BF16)

        small(here_s, ffn_ref, attn_ref, sent_ref, kept_ref, store)

    def own(
        here_s, x_ref, gm_ref, att_ref, gb_ref, ffn_ref, attn_ref, sent_ref, kept_ref, got_ref,
        send_a, keep_a, send_b, keep_b, scr, cut,
    ):
        product(x_ref, gm_ref, att_ref, gb_ref, scr)
        term = scr[...] + got_ref[:width, :].astype(F32)
        cut[...] = term.reshape(cut.shape)
        deal(cut, here_s, (send_a, keep_a, send_b, keep_b), 4, pieces)

        def store(value):
            extra = (value + got_ref[width:, :].astype(F32)).astype(BF16)
            send_a[8 * pieces] = extra
            keep_a[8 * pieces] = extra

        small(here_s, ffn_ref, attn_ref, sent_ref, kept_ref, store)

    in_specs = [
        once((rows, width)),
        pl.BlockSpec((rows, part), lambda i, h: (0, h[which] * 3 + jnp.minimum(i, 2))),
        once((rows, width)),
        pl.BlockSpec((rows, part), lambda i, h: (0, h[which]), pipeline_mode=pl.Buffered(1)),
    ] + [once(item.shape) for item in vectors]
    args = [x, grad_mixed, attended, grad_branch, *vectors]
    flops = 4 * rows * width * width
    if got is None:
        return call(
            give, "proj_give", (4,), (here,), in_specs,
            pl.BlockSpec((width + 8, part), lambda i, *_: (0, i)),
            shaped((width + 8, 4 * part), BF16),
            [pltpu.VMEM((width, part), F32)], flops, 9e6, args, 20, 0, (0,), (3,),
        )
    return call(
        own, "proj_own", (4,), (here,),
        in_specs + [pl.BlockSpec((width + 8, part), lambda i, *_: (0, i))],
        [
            pl.BlockSpec((8 * pieces + extra, 8, part), lambda i, *_: (0, 0, i))
            for extra in (1, 1, 0, 0)
        ],
        [shaped((8 * pieces + extra, 8, 4 * part), BF16) for extra in (1, 1, 0, 0)],
        [pltpu.VMEM((width, part), F32), pltpu.VMEM((4, 2, 2, 2, pieces, 8, part), F32)],
        flops, 11e6, args + [got], 24, 1, (0, 1, 2, 3), (3,),
    )


def input_gradient(grad_mixed, w_qkv, grad_resid, rows_step):
    rows, width = grad_resid.shape

    def kernel(gm_ref, wq_ref, gr_ref, out_ref):
        out_ref[...] = (dot_t(gm_ref[...], wq_ref[...]) + gr_ref[...]).astype(BF16)

    return call(
        kernel, "input_grad", (rows // rows_step,), (),
        [
            pl.BlockSpec((rows_step, 3 * width), lambda i: (i, 0)),
            once((width, 3 * width)),
            pl.BlockSpec((rows_step, width), lambda i: (i, 0)),
        ],
        pl.BlockSpec((rows_step, width), lambda i: (i, 0)),
        shaped((rows, width), BF16), [], 6 * rows * width * width, 13e6,
        (grad_mixed, w_qkv, grad_resid), 20,
    )


def copied(item, here, block):
    rows, width = item.shape

    def kernel(here_s, in_ref, out_ref):
        out_ref[...] = in_ref[...]

    spec = pl.BlockSpec((block, width), lambda i, *_: (i, 0))
    return call(
        kernel, "copied", (rows // block,), (here,), [spec], spec,
        shaped((rows, width), item.dtype), [], 1, 3e6, (item,), 4,
    )


def small_call(kernel, name, here, args, outs, vmem=12):
    return pl.pallas_call(
        kernel,
        in_specs=[pl.BlockSpec(memory_space=pltpu.SMEM)]
        + [pl.BlockSpec(memory_space=pltpu.VMEM)] * len(args),
        out_specs=[pl.BlockSpec(memory_space=pltpu.VMEM)] * len(outs),
        out_shape=outs,
        compiler_params=pltpu.CompilerParams(vmem_limit_bytes=vmem * MIB),
        cost_estimate=pl.CostEstimate(flops=int(1e6 * COST), bytes_accessed=int(4e6 * COST), transcendentals=0),
        name=name,
    )(here, *args)


def add(left, right):
    return (left.astype(F32) + right.astype(F32)).astype(BF16)


def fold_second(terms, here, pieces, extra):
    cols = terms[0][0].shape[2]
    count = len(terms)

    def kernel(here_s, *refs):
        send_a, left_a, send_b, left_b = refs[4 * count :]
        x, y = here_s[2], here_s[3]
        for term in range(count):
            ka, ga, kb, gb = refs[4 * term : 4 * term + 4]
            for z in range(4):
                at = pl.ds((term * 4 + z) * pieces, pieces)

                def sum_of(keep, got, other):
                    rows = pl.ds(z * 2 * pieces + other * pieces, pieces)
                    return add(keep[rows], got[rows])

                send_a[at] = sum_of(ka, ga, 1 - y)
                left_a[at] = sum_of(ka, ga, y)
                send_b[at] = sum_of(kb, gb, 1 - x)
                left_b[at] = sum_of(kb, gb, x)
        if extra:
            total = add(refs[0][8 * pieces], refs[1][8 * pieces])
            send_a[4 * count * pieces] = total
            left_a[4 * count * pieces] = total

    a_out = shaped((4 * count * pieces + extra, 8, cols), BF16)
    b_out = shaped((4 * count * pieces, 8, cols), BF16)
    args = [item for term in terms for item in term]
    return small_call(kernel, "fold_second", here, args, [a_out, a_out, b_out, b_out])


def fold_third(pairs, here, pieces, extra):
    cols = pairs[0].shape[2]
    count = pairs[2].shape[0] // (4 * pieces)

    def kernel(here_s, *refs):
        ins, (send, left) = refs[:-2], refs[-2:]
        low = here_s[4]
        for high in range(2):
            for term in range(count):
                for ab in range(2):
                    keep, got = ins[2 * ab : 2 * ab + 2]
                    at = pl.ds(((high * count + term) * 2 + ab) * pieces, pieces)
                    for out, pick in ((send, 1 - low), (left, low)):
                        rows = pl.ds((term * 4 + high * 2 + pick) * pieces, pieces)
                        out[at] = add(keep[rows], got[rows])
        if extra:
            total = add(ins[0][4 * count * pieces], ins[1][4 * count * pieces])
            send[4 * count * pieces] = total
            left[4 * count * pieces] = total

    out = shaped((4 * count * pieces + extra, 8, cols), BF16)
    return small_call(kernel, "fold_third", here, pairs, [out, out])


def fold_fourth(keep, got, here, extra):
    cols = keep.shape[2]
    count = (keep.shape[0] - extra) // 2

    def kernel(here_s, keep_ref, got_ref, send, left):
        high = here_s[5]
        for out, pick in ((send, 1 - high), (left, high)):
            rows = pl.ds(pick * count, count)
            out[:count] = add(keep_ref[rows], got_ref[rows])
        if extra:
            total = add(keep_ref[2 * count], got_ref[2 * count])
            send[count] = total
            left[count] = total

    out = shaped((count + extra, 8, cols), BF16)
    return small_call(kernel, "fold_fourth", here, (keep, got), [out, out])


def fold_last(keep, got, here, extra):
    cols = keep.shape[2]
    count = keep.shape[0] - extra

    def kernel(here_s, keep_ref, got_ref, *outs):
        outs[0][...] = add(keep_ref[:count], got_ref[:count])
        if extra:
            outs[1][0] = add(keep_ref[count], got_ref[count])

    outs = [shaped((count, 8, cols), BF16)] + [shaped((1, 8, cols), BF16)] * extra
    return small_call(kernel, "fold_last", here, (keep, got), outs)


def chosen_part(here_s, refs, core, side, at):
    me, gx, gc, gd = [item[at].astype(F32) for item in refs]
    same_core, same_side = here_s[0] == core, here_s[2] == side
    return jnp.where(same_core, jnp.where(same_side, me, gx), jnp.where(same_side, gc, gd))


def feed_blocks(parts, here, pieces, width):
    cols = parts[0].shape[2]
    half = width // 2
    folds = cols // half
    rows = 2 * pieces * 8

    def kernel(here_s, me, gx, gc, gd, down_ref, up_ref):
        refs = (me, gx, gc, gd)
        for core in range(2):
            for side in range(2):
                tall = side * folds * rows
                for ab in range(2):
                    at = pl.ds(ab * pieces, pieces)
                    value = chosen_part(here_s, refs, core, side, at).reshape(rows // 2, cols)
                    for fold in range(folds):
                        start = tall + (ab * folds + fold) * (rows // 2)
                        down_ref[start : start + rows // 2, core * half : (core + 1) * half] = value[
                            :, fold * half : (fold + 1) * half
                        ]
                at = pl.ds(2 * pieces, 2 * pieces)
                value = chosen_part(here_s, refs, core, side, at).reshape(rows, cols)
                up_ref[side * rows : (side + 1) * rows, core * cols : (core + 1) * cols] = value

    outs = [shaped((2 * folds * rows, width), F32), shaped((2 * rows, 2 * cols), F32)]
    return small_call(kernel, "feed_blocks", here, parts, outs, 16)


def projection_blocks(parts, vectors, here, pieces):
    cols = parts[0].shape[2]
    rows = 2 * pieces * 8
    cut = cols // 4 * 3
    width = cols // 2
    small = width // 8
    large = cols // 4

    def kernel(here_s, me, gx, gc, gd, vec_ref, qkv_ref, out_ref, *outs):
        refs = (me, gx, gc, gd)
        for core in range(2):
            for side in range(2):
                value = chosen_part(here_s, refs, core, side, slice(None)).reshape(rows, cols)
                at = slice(side * rows, (side + 1) * rows)
                qkv_ref[at, core * cut : (core + 1) * cut] = value[:, :cut]
                out_ref[at, core * (cols - cut) : (core + 1) * (cols - cut)] = value[:, cut:]
        table = vec_ref[0].astype(F32)
        wide = here_s[6]
        shift = lax.rem(width - wide * small, width)
        left, right = pltpu.roll(table[:, :width], shift, 1), pltpu.roll(table[:, width:], shift, 1)
        for row in range(4):
            outs[2 * row][...] = left[row : row + 1, :small]
            outs[2 * row + 1][...] = right[row : row + 1, :small]
        turned = pltpu.roll(table, lax.rem(cols - lax.rem(wide, 4) * large, cols), 1)
        outs[8][...] = jnp.where(wide < 4, turned[4:5, :large], turned[5:6, :large])

    outs = [shaped((2 * rows, 2 * cut), F32), shaped((2 * rows, 2 * (cols - cut)), F32)]
    outs += [shaped((1, small), F32)] * 8 + [shaped((1, large), F32)]
    return small_call(kernel, "projection_blocks", here, (*parts, vectors), outs, 16)


def after(item, *earlier):
    return lax.optimization_barrier((item, *earlier))[0]


def swap(item, axis, step):
    count = lax.axis_size(axis)
    return lax.ppermute(item, axis, [(index, index ^ step) for index in range(count)])


def quarters(mine):
    across = swap(mine, "narrow", 2)
    return mine, across, swap(mine, "narrow", 1), swap(across, "narrow", 1)


def regroup_rows(sent, bucket, wide_count, batches):
    span, width = sent.shape[1:]
    if wide_count == batches:
        got = lax.all_to_all(sent, "wide", split_axis=0, concat_axis=0, tiled=True)
        return got.reshape(batches * span, width)
    send = jnp.zeros((wide_count, span, width), sent.dtype).at[bucket].set(sent)
    got = lax.all_to_all(send, "wide", split_axis=0, concat_axis=0, tiled=True)
    marks = jnp.zeros((wide_count, 1), jnp.int32).at[bucket].set(1)
    filled = lax.all_to_all(marks, "wide", split_axis=0, concat_axis=0, tiled=True)[:, 0]
    place = jnp.where(filled > 0, jnp.cumsum(filled) - filled, batches)
    chosen = (
        jnp.zeros((batches,), jnp.int32)
        .at[place]
        .set(jnp.arange(wide_count, dtype=jnp.int32), mode="drop")
    )
    return got[chosen].reshape(batches * span, width)


def sum_anywhere(item, wide_count, narrow_count):
    blocks = item.astype(F32).reshape(wide_count, -1)
    extent = blocks.shape[1]
    padded = (extent + narrow_count - 1) // narrow_count * narrow_count
    blocks = jnp.pad(blocks, ((0, 0), (0, padded - extent))).reshape(-1)
    share = lax.psum_scatter(blocks, ("wide", "narrow"), scatter_dimension=0, tiled=True)
    whole = lax.all_gather(share.astype(BF16), "narrow", axis=0, tiled=True).astype(F32)
    return whole[:extent].reshape((item.shape[0] // wide_count,) + item.shape[1:])


def body(
    tokens, bucket, lengths, pairing, targets, w_qkv, bias_q, bias_v, w_out, bias_out,
    gain_attn, shift_attn, w_up, bias_up, w_down, bias_down, gain_ffn, shift_ffn,
):
    wide_count, narrow_count = lax.axis_size("wide"), lax.axis_size("narrow")
    batches = bucket.shape[0]
    rows, width = tokens.shape
    span = rows // batches
    paired = (wide_count, narrow_count) == (8, 4)
    wide, narrow = lax.axis_index("wide"), lax.axis_index("narrow")
    if paired:
        core = narrow % 2
        here = jnp.stack(
            [core, 1 - core, narrow // 2, wide % 2, wide // 2 % 2, wide // 4, wide, narrow]
        ).astype(jnp.int32)
    else:
        here = jnp.arange(8, dtype=jnp.int32)
    table = vector_table(
        [bias_q, bias_v, bias_out, gain_attn, shift_attn, bias_down, gain_ffn, shift_ffn, bias_up], width
    )
    ordered = wide_count == batches
    slots = bucket if ordered else jnp.arange(batches, dtype=jnp.int32)
    pieces = width // 32 // 8

    qkv, probs, attended, n_attn, spread, sid = attention_forward(
        tokens, w_qkv, w_out, table, bucket, lengths, wide_count // batches, span, 2 * span
    )
    active, slope, hidden_t, sent, gres, grad_second, vec_ffn = feed_forward(
        n_attn, w_up, w_down, table, sid, slots, pairing, targets, batches, 2 * span
    )
    ups = (grad_second, slope, hidden_t, w_down)
    heads = (n_attn, spread, table, w_out, qkv, probs)
    down_sent = down_terms(active, grad_second, here, 1)
    if paired:
        encoded = regroup_rows(after(sent, down_sent), bucket, wide_count, batches)
        up_sent, gi_sent, bup_sent = up_terms(*ups, after(here, down_sent), 1)
        down_dealt = down_terms(active, grad_second, after(here, bup_sent), 0, swap(down_sent, "narrow", 1))
        down_a, down_b = swap(down_dealt[0], "narrow", 2), swap(down_dealt[2], "wide", 1)
        gh = hidden_gradient(gi_sent, w_up, after(here, down_dealt[1]), 1)
        *up_dealt, gi_kept, bup_kept = up_terms(
            *ups, after(here, gh), 0, swap(up_sent, "narrow", 1)
        )
        up_a, up_b = swap(up_dealt[0], "narrow", 2), swap(up_dealt[2], "wide", 1)
        gr, gb, gm, vec_attn = attention_backward(
            gh, gres, gi_kept, w_up, *heads, after(here, up_dealt[1]), 0, span, 2 * span
        )
        feed = fold_second(
            [
                (down_dealt[1], down_a, down_dealt[3], down_b),
                (up_dealt[1], up_a, up_dealt[3], up_b),
            ],
            after(here, vec_attn, encoded), pieces, 0,
        )
        feed_a, feed_b = swap(feed[0], "wide", 1), swap(feed[2], "narrow", 2)
        projections = (tokens, gm, attended, gb, (vec_ffn, vec_attn, bup_sent, bup_kept))
        proj_sent = projection_terms(*projections, after(here, feed[1]), 1)
        proj_dealt = projection_terms(
            *projections, after(here, proj_sent), 0, swap(proj_sent, "narrow", 1)
        )
        proj_a, proj_b = swap(proj_dealt[0], "narrow", 2), swap(proj_dealt[2], "wide", 1)
        send, feed = fold_third(
            [feed[1], feed_a, feed[3], feed_b], after(here, proj_dealt[1]), pieces, 0
        )
        feed_got = swap(send, "wide", 2)
        grad_tokens = input_gradient(after(gm, feed), w_qkv, gr, 2 * span)
        send, feed = fold_fourth(feed, feed_got, after(here, grad_tokens), 0)
        feed_got = swap(send, "wide", 4)
        proj_dealt = fold_second(
            [(proj_dealt[1], proj_a, proj_dealt[3], proj_b)], after(here, feed), pieces, 1
        )
        proj_a, proj_b = swap(proj_dealt[0], "wide", 1), swap(proj_dealt[2], "narrow", 2)
        encoded = copied(encoded, after(here, proj_dealt[1]), span)
        send, proj = fold_third(
            [proj_dealt[1], proj_a, proj_dealt[3], proj_b], after(here, encoded), pieces, 1
        )
        proj_got = swap(send, "wide", 2)
        (feed,) = fold_last(feed, feed_got, after(here, proj), 0)
        send, proj = fold_fourth(proj, proj_got, after(here, feed), 1)
        proj_got = swap(send, "wide", 4)
        feed = quarters(after(feed, proj))
        proj, vectors = fold_last(proj, proj_got, here, 1)
        proj = quarters(proj)
        grad_w_down, grad_w_up = feed_blocks(feed, after(here, proj[0]), pieces, width)
        grad_w_qkv, grad_w_out, *small = projection_blocks(proj, vectors, after(here, grad_w_down), pieces)
        small = [item.reshape(-1) for item in small]
    else:
        encoded = regroup_rows(sent, bucket, wide_count, batches)
        down_kept = down_terms(active, grad_second, here, 0)
        up_sent, gi_sent, bup_sent = up_terms(*ups, here, 1)
        up_kept, gi_kept, bup_kept = up_terms(*ups, here, 0)
        gh = hidden_gradient(gi_sent, w_up, here, 1)
        gr, gb, gm, vec_attn = attention_backward(
            gh, gres, gi_kept, w_up, *heads, here, 0, span, 2 * span
        )
        projections = (tokens, gm, attended, gb, (vec_ffn, vec_attn, bup_sent, bup_kept), here)
        grad_tokens = input_gradient(gm, w_qkv, gr, 2 * span)
        proj_sent, proj_kept = projection_terms(*projections, 1), projection_terms(*projections, 0)
        total = partial(sum_anywhere, wide_count=wide_count, narrow_count=narrow_count)
        cut = width // 2 * 3
        grad_w_down = total(jnp.concatenate([down_kept, down_sent], axis=1))
        grad_w_up = total(jnp.concatenate([up_kept, up_sent], axis=1))
        grad_w_qkv = total(jnp.concatenate([proj_kept[:width, :cut], proj_sent[:width, :cut]], axis=1))
        grad_w_out = total(jnp.concatenate([proj_kept[:width, cut:], proj_sent[:width, cut:]], axis=1))
        small = [
            total(item)
            for item in (*vec_ffn[:3], *vec_attn[:5], jnp.concatenate([bup_kept[0], bup_sent[0]]))
        ]
    gain_out, shift_out, b_down, b_q, b_v, b_out, g_attn, s_attn, b_up = small
    return (
        encoded, grad_tokens, grad_w_qkv, b_q, b_v, grad_w_out, b_out, g_attn, s_attn,
        grad_w_up, b_up, grad_w_down, b_down, gain_out, shift_out,
    )


def solution(mesh):
    split = P(("wide", "narrow"))
    in_specs = (
        P(("wide", "narrow"), None), split, split, P(("wide", "narrow"), None), split,
    ) + (P(),) * 13
    out_specs = (
        P(("wide", "narrow"), None), P(("wide", "narrow"), None),
        P("wide", None), P("wide"), P("wide"), P("wide", None), P("wide"), P("wide"), P("wide"),
        P("wide", None), P("wide"), P("wide", None), P("wide"), P("wide"), P("wide"),
    )
    return jax.shard_map(body, mesh=mesh, in_specs=in_specs, out_specs=out_specs, check_vma=False)
```

```python
from functools import partial

import jax
import jax.numpy as jnp
from jax import lax
from jax.experimental import pallas as pl
from jax.experimental.pallas import tpu as pltpu
from jax.sharding import PartitionSpec as P

HDIM = 64
KTOP = 12
NORM_EPS = 1e-12
COS_EPS = 1e-06
MASKED = -1000000000.0
LOSS_SCALE = 1024.0
F32 = jnp.float32
BF16 = jnp.bfloat16
LANES = 128
MIB = 1024 * 1024
LARGE = 100000
COST = 0.05
HALF_ROOT = 0.7071067811865476
BELL_RATE = -0.7213475204444817
BELL_PEAK = -1.3257480647361595
ROW_BQ, ROW_BV, ROW_BO, ROW_GA, ROW_SA, ROW_BD, ROW_GF, ROW_SF, ROW_BU = range(9)


def dot(left, right):
    return jnp.dot(left, right, preferred_element_type=F32)


def dot_t(left, right):
    return lax.dot_general(left, right, (((1,), (1,)), ((), ())), preferred_element_type=F32)


def t_dot(left, right):
    return lax.dot_general(left, right, (((0,), (0,)), ((), ())), preferred_element_type=F32)


def full(shape):
    return pl.BlockSpec(shape, lambda *_: (0,) * len(shape))


def once(shape):
    return pl.BlockSpec(shape, lambda *_: (0,) * len(shape), pipeline_mode=pl.Buffered(1))


def large(item):
    return item.size >= LARGE


def shaped(shape, dtype):
    return jax.ShapeDtypeStruct(shape, dtype)


def call(
    kernel, name, grid, prefetch, in_specs, out_specs, out_shape, scratch, flops, moved, args, vmem=24, free=0, loose=(), near=()
):
    single = not isinstance(out_shape, list)
    shapes = [out_shape] if single else out_shape
    shapes = [
        pltpu.HBM(item.shape, item.dtype) if large(item) and number not in loose else item
        for number, item in enumerate(shapes)
    ]
    out_shape = shapes[0] if single else shapes
    args = [
        pltpu.with_memory_space_constraint(item, pltpu.HBM)
        if large(item) and number < len(args) - free and number not in near
        else item
        for number, item in enumerate(args)
    ]
    return pl.pallas_call(
        kernel,
        grid_spec=pltpu.PrefetchScalarGridSpec(
            num_scalar_prefetch=len(prefetch),
            grid=grid,
            in_specs=in_specs,
            out_specs=out_specs,
            scratch_shapes=scratch,
        ),
        out_shape=out_shape,
        compiler_params=pltpu.CompilerParams(
            dimension_semantics=("arbitrary",) * len(grid), vmem_limit_bytes=vmem * MIB
        ),
        cost_estimate=pl.CostEstimate(flops=int(flops * COST), bytes_accessed=int(moved * COST), transcendentals=0),
        name=name,
    )(*[pltpu.with_memory_space_constraint(item, pltpu.HBM) for item in prefetch], *args)


def norm_forward(values):
    center = values - jnp.mean(values, axis=-1, keepdims=True)
    spread = lax.rsqrt(jnp.mean(center * center, axis=-1, keepdims=True) + NORM_EPS)
    return center * spread, spread


def norm_backward(grad_out, normed, spread, gain):
    scaled = grad_out * gain
    mean_scaled = jnp.mean(scaled, axis=-1, keepdims=True)
    mean_product = jnp.mean(scaled * normed, axis=-1, keepdims=True)
    return spread * (scaled - mean_scaled - normed * mean_product)


def column_sum(values):
    return jnp.sum(values, axis=0, keepdims=True)


def gelu_pair(v):
    phi = 0.5 + 0.5 * lax.erf(v * HALF_ROOT)
    bell = jnp.exp2((v * v) * BELL_RATE + BELL_PEAK)
    return v * phi, phi + v * bell


def head_masks():
    lane = lax.broadcasted_iota(jnp.int32, (1, LANES), 1)
    low = (lane < HDIM).astype(F32)
    return low.astype(BF16), (1.0 - low).astype(BF16), lane < HDIM


def sentence_count(bucket_s, number, group_size):
    kind = bucket_s[number]
    if group_size > 1:
        kind = kind // group_size
    return jnp.maximum(1, lax.shift_right_logical(jnp.int32(KTOP), kind))


def row_sentences(batch, bucket_s, lengths_s, group_size, batches, sent, span):
    start = jnp.int32(0)
    for other in range(batches):
        start += jnp.where(other < batch, sentence_count(bucket_s, other, group_size), 0)
    count = sentence_count(bucket_s, batch, group_size)
    lane = lax.broadcasted_iota(jnp.int32, (8, span), 1)
    row = lax.broadcasted_iota(jnp.int32, (span, span), 0)
    passed_lane = jnp.zeros((8, span), jnp.int32)
    passed_row = jnp.zeros((span, span), jnp.int32)
    finish = jnp.int32(0)
    for number in range(KTOP):
        finish += lengths_s[jnp.minimum(start + number, sent - 1)]
        bound = jnp.where(number < count, finish, span)
        passed_lane += (lane >= bound).astype(jnp.int32)
        passed_row += (row >= bound).astype(jnp.int32)
    sid_lane = jnp.where(passed_lane < count, start + passed_lane, -1)
    sid_row = jnp.where(passed_row < count, start + passed_row, -1)
    return sid_lane, sid_row


def vector_table(vectors, width):
    def kernel(*refs):
        out_ref = refs[-1]
        at = 0
        for ref in refs[:-1]:
            for part in range(ref.shape[0] // width):
                out_ref[at : at + 1, :] = ref[part * width : (part + 1) * width].astype(F32).reshape(1, width)
                at += 1

    rows = sum(item.shape[0] for item in vectors) // width
    return pl.pallas_call(
        kernel,
        grid=(1,),
        in_specs=[full(item.shape) for item in vectors],
        out_specs=full((rows, width)),
        out_shape=shaped((rows, width), F32),
        compiler_params=pltpu.CompilerParams(vmem_limit_bytes=4 * MIB),
        name="vector_table",
    )(*[pltpu.with_memory_space_constraint(item, pltpu.HBM) for item in vectors])


def attention_forward(x, w_qkv, w_out, table, bucket, lengths, group_size, span, rows_step):
    rows, width = x.shape
    batches = rows // span
    pairs = width // LANES
    sent = lengths.shape[0]
    per_step = rows_step // span

    def kernel(bucket_s, lengths_s, x_ref, wq_ref, wo_ref, tab_ref, qkv_ref, p_ref, att_ref, n_ref, s_ref, sid_ref):
        step = pl.program_id(0)
        low_b, high_b, low_m = head_masks()
        x_in = x_ref[...]
        mixed = dot(x_in, wq_ref[:, :width]) + tab_ref[ROW_BQ : ROW_BQ + 1, :]
        qkv_ref[:, :width] = (mixed * 0.125).astype(BF16)
        qkv_ref[:, width : 2 * width] = dot(x_in, wq_ref[:, width : 2 * width]).astype(BF16)
        mixed = dot(x_in, wq_ref[:, 2 * width :]) + tab_ref[ROW_BV : ROW_BV + 1, :]
        qkv_ref[:, 2 * width :] = mixed.astype(BF16)
        eye = lax.broadcasted_iota(jnp.int32, (span, span), 0) == lax.broadcasted_iota(
            jnp.int32, (span, span), 1
        )
        for inner in range(per_step):
            sid_lane, sid_row = row_sentences(
                step * per_step + inner, bucket_s, lengths_s, group_size, batches, sent, span
            )
            sid_ref[inner] = sid_lane
            same = (sid_row == sid_lane[0:1, :]) & (sid_row >= 0)
            bias = jnp.where(same | eye, 0.0, MASKED)
            bias = jnp.concatenate([bias, bias], axis=0)
            base = slice(inner * span, (inner + 1) * span)
            for pair in range(pairs):
                cols = slice(pair * LANES, (pair + 1) * LANES)
                q = qkv_ref[base, cols]
                k = qkv_ref[base, width + pair * LANES : width + (pair + 1) * LANES]
                v = qkv_ref[base, 2 * width + pair * LANES : 2 * width + (pair + 1) * LANES]
                both = jnp.concatenate([q * low_b, q * high_b], axis=0)
                logits = dot_t(both, k) + bias
                raised = jnp.exp(logits - jnp.max(logits, axis=-1, keepdims=True))
                total = jnp.sum(raised, axis=-1, keepdims=True)
                probs = (raised * (1.0 / total)).astype(BF16)
                p_ref[inner, pair] = probs
                mix = dot(probs, v)
                att_ref[base, cols] = jnp.where(low_m, mix[:span], mix[span:]).astype(BF16)
        branch = dot(att_ref[...], wo_ref[...]) + tab_ref[ROW_BO : ROW_BO + 1, :]
        normed, spread = norm_forward(x_in.astype(F32) + branch)
        n_ref[...] = normed
        s_ref[...] = jnp.broadcast_to(spread, (rows_step, LANES))

    return call(
        kernel,
        "attn_fwd",
        (rows // rows_step,),
        (bucket, lengths),
        [
            pl.BlockSpec((rows_step, width), lambda i, *_: (i, 0)),
            once((width, 3 * width)),
            once((width, width)),
            once(table.shape),
        ],
        [
            pl.BlockSpec((rows_step, 3 * width), lambda i, *_: (i, 0)),
            pl.BlockSpec((per_step, pairs, 2 * span, span), lambda i, *_: (i, 0, 0, 0)),
            pl.BlockSpec((rows_step, width), lambda i, *_: (i, 0)),
            pl.BlockSpec((rows_step, width), lambda i, *_: (i, 0)),
            pl.BlockSpec((rows_step, LANES), lambda i, *_: (i, 0)),
            pl.BlockSpec((per_step, 8, span), lambda i, *_: (i, 0, 0)),
        ],
        [
            shaped((rows, 3 * width), BF16),
            shaped((batches, pairs, 2 * span, span), BF16),
            shaped((rows, width), BF16),
            shaped((rows, width), F32),
            shaped((rows, LANES), F32),
            shaped((batches, 8, span), jnp.int32),
        ],
        [],
        8 * rows * width * width * 2,
        30e6,
        (x, w_qkv, w_out, table),
        26,
    )


def feed_forward(n_attn, w_up, w_down, table, sid, slots, pairing, targets, slot_count, block):
    rows, width = n_attn.shape
    ff = w_up.shape[1]
    batches, _, span = sid.shape
    pair_count = targets.shape[0]
    side = -(-pair_count // 8) * 8
    chunk = width
    steps = ff // chunk
    tall = 2 * block
    blocks = rows // block
    per_block = block // span

    def kernel(
        slots_s, pairing_s, targets_s, n_ref, wu_ref, wd_ref, tab_ref, sid_ref,
        act_ref, dg_ref, ht_ref, enc_ref, gres_ref, gsl_ref, vec_ref, low_scr, acc_scr, spread_scr,
    ):
        step = pl.program_id(0)
        gain = tab_ref[ROW_GA : ROW_GA + 1, :]
        shift = tab_ref[ROW_SA : ROW_SA + 1, :]

        @pl.when(step == 0)
        def _():
            hidden = (n_ref[...] * gain + shift).astype(BF16)
            low_scr[...] = hidden
            ht_ref[...] = hidden.T
            acc_scr[...] = jnp.zeros_like(acc_scr)

        for number in range(rows // tall):
            base = slice(number * tall, (number + 1) * tall)
            inner = dot(low_scr[base, :], wu_ref[...]) + tab_ref[pl.ds(ROW_BU + step, 1), :]
            active, slope = gelu_pair(inner)
            active = active.astype(BF16)
            act_ref[base, :] = active
            dg_ref[base, :] = slope.astype(BF16)
            acc_scr[base, :] += dot(active, wd_ref[...])

        @pl.when(step == steps - 1)
        def _():
            gain_out = tab_ref[ROW_GF : ROW_GF + 1, :]
            shift_out = tab_ref[ROW_SF : ROW_SF + 1, :]
            slot = lax.broadcasted_iota(jnp.int32, (2 * side, span), 0)
            wanted = jnp.full((2 * side, span), -2, jnp.int32)
            goal = jnp.zeros((side, LANES), F32)
            goal_slot = lax.broadcasted_iota(jnp.int32, (side, LANES), 0)
            for number in range(pair_count):
                wanted = jnp.where(slot == number, pairing_s[0, 2 * number], wanted)
                wanted = jnp.where(slot == side + number, pairing_s[0, 2 * number + 1], wanted)
                goal = jnp.where(goal_slot == number, targets_s[number], goal)
            members = [
                (sid_ref[number][0:1, :] == wanted).astype(F32) for number in range(batches)
            ]
            sizes = jnp.zeros((2 * side, 1), F32)
            for member in members:
                sizes += jnp.sum(member, axis=-1, keepdims=True)
            share = 1.0 / jnp.maximum(sizes, 1.0)
            picks = [
                jnp.concatenate(members[number * per_block : (number + 1) * per_block], axis=1).astype(BF16)
                for number in range(blocks)
            ]
            ones = jnp.ones((2 * side, LANES), BF16)
            pooled = jnp.zeros((2 * side, width), F32)
            for number in range(blocks):
                base = slice(number * block, (number + 1) * block)
                resid = (
                    n_ref[base, :] * gain + shift + acc_scr[base, :] + tab_ref[ROW_BD : ROW_BD + 1, :]
                )
                normed, spread = norm_forward(resid)
                acc_scr[base, :] = normed
                spread_scr[base, :] = jnp.broadcast_to(spread, (block, LANES))
                out = normed * gain_out + shift_out
                high = out.astype(BF16)
                rest = (out - high.astype(F32)).astype(BF16)
                pooled += dot(picks[number], high) + dot(picks[number], rest)
                valid = t_dot(picks[number], ones)
                for col in range(width // LANES):
                    cols = slice(col * LANES, (col + 1) * LANES)
                    kept = (out[:, cols] * valid).astype(BF16)
                    for inner in range(per_block):
                        enc_ref[slots_s[number * per_block + inner], :, cols] = kept[
                            inner * span : (inner + 1) * span
                        ]
            pooled = pooled * share
            first, partner = pooled[:side], pooled[side:]
            cross = jnp.sum(first * partner, axis=-1, keepdims=True)
            scale_first = lax.rsqrt(jnp.sum(first * first, axis=-1, keepdims=True) + COS_EPS)
            scale_partner = lax.rsqrt(jnp.sum(partner * partner, axis=-1, keepdims=True) + COS_EPS)
            cosine = cross * scale_first * scale_partner
            factor = 2.0 * LOSS_SCALE * (cosine - goal[:, :1])
            both_scales = factor * scale_first * scale_partner
            grad_first = both_scales * partner - (factor * cosine * scale_first * scale_first) * first
            grad_partner = (
                both_scales * first - (factor * cosine * scale_partner * scale_partner) * partner
            )
            grad_home = jnp.concatenate([grad_first, grad_partner], axis=0) * share
            high = grad_home.astype(BF16)
            rest = (grad_home - high.astype(F32)).astype(BF16)
            vec_ref[...] = jnp.zeros_like(vec_ref)
            for number in range(blocks):
                base = slice(number * block, (number + 1) * block)
                grad_out = t_dot(picks[number], high) + t_dot(picks[number], rest)
                normed = acc_scr[base, :]
                resid = norm_backward(grad_out, normed, spread_scr[base, :1], gain_out)
                gres_ref[base, :] = resid
                low = resid.astype(BF16)
                gsl_ref[base, :] = low
                vec_ref[0:1, :] += column_sum(grad_out * normed)
                vec_ref[1:2, :] += column_sum(grad_out)
                vec_ref[2:3, :] += column_sum(low.astype(F32))

    return call(
        kernel,
        "ffn_fwd",
        (steps,),
        (slots, pairing, targets),
        [
            once((rows, width)),
            pl.BlockSpec((width, chunk), lambda j, *_: (0, j)),
            pl.BlockSpec((chunk, width), lambda j, *_: (j, 0)),
            once(table.shape),
            once((batches, 8, span)),
        ],
        [
            pl.BlockSpec((rows, chunk), lambda j, *_: (0, j)),
            pl.BlockSpec((rows, chunk), lambda j, *_: (0, j)),
            once((width, rows)),
            once((slot_count, span, width)),
            once((rows, width)),
            once((rows, width)),
            once((8, width)),
        ],
        [
            shaped((rows, ff), BF16),
            shaped((rows, ff), BF16),
            shaped((width, rows), BF16),
            shaped((slot_count, span, width), BF16),
            shaped((rows, width), F32),
            shaped((rows, width), BF16),
            shaped((8, width), F32),
        ],
        [
            pltpu.VMEM((rows, width), BF16),
            pltpu.VMEM((rows, width), F32),
            pltpu.VMEM((rows, LANES), F32),
        ],
        8 * rows * width * ff,
        40e6,
        (n_attn, w_up, w_down, table, sid),
        38, 0, (2, 5),
    )


def deal(scratch, here_s, outs, z_count, pieces, folds=1):
    send_a, keep_a, send_b, keep_b = outs
    x, y = here_s[2], here_s[3]
    cols = scratch.shape[-1]
    for z in range(z_count):
        for other in range(2):
            at = pl.ds((z * 2 + other) * pieces, pieces)
            for fold in range(folds):
                part = pl.ds(fold * pieces, pieces)
                to = slice(fold * cols, (fold + 1) * cols)
                send_a[at, :, to] = scratch[z, other, 1 - x, 0, part].astype(BF16)
                keep_a[at, :, to] = scratch[z, other, x, 0, part].astype(BF16)
                send_b[at, :, to] = scratch[z, 1 - y, other, 1, part].astype(BF16)
                keep_b[at, :, to] = scratch[z, y, other, 1, part].astype(BF16)


def down_terms(active, grad_second, here, which, got=None):
    rows, ff = active.shape
    width = grad_second.shape[1]
    half = width // 2
    steps = 4
    tall = ff // steps
    pieces = width // 32 // 8
    folds = ff // width

    def give(here_s, act_ref, gs_ref, out_ref):
        out_ref[...] = t_dot(act_ref[...], gs_ref[...]).astype(BF16)

    def own(here_s, act_ref, gs_ref, got_ref, *rest):
        outs, scratch = rest[:4], rest[4]
        term = t_dot(act_ref[...], gs_ref[...]) + got_ref[...].astype(F32)
        scratch[...] = term.reshape(scratch.shape)
        deal(scratch, here_s, outs, 1, pieces, folds)

    in_specs = [
        pl.BlockSpec((rows, tall), lambda i, here_s: (0, i)),
        pl.BlockSpec((rows, half), lambda i, here_s: (0, here_s[which]), pipeline_mode=pl.Buffered(1)),
    ]
    flops = 2 * rows * ff * half
    if got is None:
        return call(
            give, "down_give", (steps,), (here,), in_specs,
            pl.BlockSpec((tall, half), lambda i, *_: (i, 0)),
            shaped((ff, half), BF16), [], flops, 9e6, (active, grad_second), 20, 0, (0,), (1,),
        )
    block = (2 * pieces, 8, folds * half)
    return call(
        own, "down_own", (steps,), (here,),
        in_specs + [pl.BlockSpec((tall, half), lambda i, *_: (i, 0))],
        [pl.BlockSpec(block, lambda i, *_: (i, 0, 0))] * 4,
        [shaped((8 * pieces, 8, folds * half), BF16)] * 4,
        [pltpu.VMEM((1, 2, 2, 2, folds * pieces, 8, half), F32)],
        flops, 11e6, (active, grad_second, got), 24, 1, (0, 2), (1,),
    )


def up_terms(grad_second, slope, hidden_t, w_down, here, which, got=None):
    rows, width = grad_second.shape
    ff = w_down.shape[0]
    half = ff // 2
    chunk = width
    steps = half // chunk
    block = rows // 2
    pieces = width // 32 // 8

    def kernel(here_s, gs_ref, dg_ref, ht_ref, wd_ref, *refs):
        if got is not None:
            got_ref, refs = refs[0], refs[1:]
            outs, refs = refs[:4], refs[4:]
        else:
            out_ref, refs = refs[0], refs[1:]
        gi_ref, bu_ref = refs[:2]
        sums = jnp.zeros((1, chunk), F32)
        for number in range(rows // block):
            base = slice(number * block, (number + 1) * block)
            grad_active = dot_t(gs_ref[base, :], wd_ref[...])
            low = (grad_active * dg_ref[base, :].astype(F32)).astype(BF16)
            gi_ref[base, :] = low
            sums += column_sum(low.astype(F32))
        bu_ref[...] = sums
        term = dot(ht_ref[...], gi_ref[...])
        if got is None:
            out_ref[...] = term.astype(BF16)
        else:
            scratch = refs[2]
            term += got_ref[...].astype(F32)
            scratch[...] = term.reshape(scratch.shape)
            deal(scratch, here_s, outs, 4, pieces)

    def col(i, here_s):
        return here_s[which] * steps + i

    in_specs = [
        once((rows, width)),
        pl.BlockSpec((rows, chunk), lambda i, h: (0, col(i, h))),
        once((width, rows)),
        pl.BlockSpec((chunk, width), lambda i, h: (col(i, h), 0)),
    ]
    args = [grad_second, slope, hidden_t, w_down]
    scratch = []
    if got is None:
        out_specs = [pl.BlockSpec((width, chunk), lambda i, *_: (0, i))]
        out_shape = [shaped((width, half), BF16)]
    else:
        in_specs.append(pl.BlockSpec((width, chunk), lambda i, *_: (0, i)))
        args.append(got)
        out_specs = [pl.BlockSpec((8 * pieces, 8, chunk), lambda i, *_: (0, 0, i))] * 4
        out_shape = [shaped((8 * pieces, 8, half), BF16)] * 4
        scratch.append(pltpu.VMEM((4, 2, 2, 2, pieces, 8, chunk), F32))
    return call(
        kernel, "up_give" if got is None else "up_own", (steps,), (here,), in_specs,
        out_specs
        + [
            pl.BlockSpec((rows, chunk), lambda i, *_: (0, i)),
            pl.BlockSpec((1, chunk), lambda i, *_: (0, i)),
        ],
        out_shape + [shaped((rows, half), BF16), shaped((1, half), F32)],
        scratch, 4 * rows * width * half, 16e6, args, 26, 0 if got is None else 1, (0,) if got is None else (0, 2, 4), (0, 2),
    )


def attention_backward(grads_inner, gres, w_up, n_attn, spread, table, w_out, qkv, probs, here, span, rows_step):
    rows, width = gres.shape
    half = grads_inner[0].shape[1]
    pairs = width // LANES
    per_step = rows_step // span

    def kernel(here_s, gi_ref, other_ref, gres_ref, wu_ref, wu_other_ref, n_ref, s_ref, tab_ref, wo_ref, qkv_ref, p_ref, gr_ref, gb_ref, gm_ref, vec_ref, ga_scr):
        step = pl.program_id(0)
        low_b, high_b, low_m = head_masks()

        @pl.when(step == 0)
        def _():
            vec_ref[...] = jnp.zeros_like(vec_ref)

        normed = n_ref[...]
        grad_hidden = (
            dot_t(gi_ref[...], wu_ref[...]) + dot_t(other_ref[...], wu_other_ref[...]) + gres_ref[...]
        )
        resid = norm_backward(grad_hidden, normed, s_ref[:, :1], tab_ref[ROW_GA : ROW_GA + 1, :])
        gr_ref[...] = resid
        low = resid.astype(BF16)
        gb_ref[...] = low
        vec_ref[2:3, :] += column_sum(low.astype(F32))
        vec_ref[3:4, :] += column_sum(grad_hidden * normed)
        vec_ref[4:5, :] += column_sum(grad_hidden)
        ga_scr[...] = dot_t(low, wo_ref[...]).astype(BF16)
        for inner in range(per_step):
            base = slice(inner * span, (inner + 1) * span)
            for pair in range(pairs):
                cols = slice(pair * LANES, (pair + 1) * LANES)
                k_cols = slice(width + pair * LANES, width + (pair + 1) * LANES)
                v_cols = slice(2 * width + pair * LANES, 2 * width + (pair + 1) * LANES)
                q, k, v = qkv_ref[base, cols], qkv_ref[base, k_cols], qkv_ref[base, v_cols]
                grad = ga_scr[base, cols]
                grads = jnp.concatenate([grad * low_b, grad * high_b], axis=0)
                both = jnp.concatenate([q * low_b, q * high_b], axis=0)
                weights = p_ref[inner, pair]
                wide = weights.astype(F32)
                grad_probs = dot_t(grads, v)
                balance = jnp.sum(wide * grad_probs, axis=-1, keepdims=True)
                grad_logits = (wide * (grad_probs - balance)).astype(BF16)
                mix = dot(grad_logits, k)
                grad_q = jnp.where(low_m, mix[:span], mix[span:]).astype(BF16) * jnp.bfloat16(0.125)
                grad_v = t_dot(weights, grads).astype(BF16)
                gm_ref[base, cols] = grad_q
                gm_ref[base, k_cols] = t_dot(grad_logits, both).astype(BF16)
                gm_ref[base, v_cols] = grad_v
                vec_ref[0:1, cols] += column_sum(grad_q.astype(F32))
                vec_ref[1:2, cols] += column_sum(grad_v.astype(F32))

    def rows_of(cols):
        return pl.BlockSpec((rows_step, cols), lambda i, h: (i, 0))

    return call(
        kernel,
        "attn_bwd",
        (rows // rows_step,),
        (here,),
        [
            rows_of(half), rows_of(half), rows_of(width),
            pl.BlockSpec((width, half), lambda i, h: (0, h[0]), pipeline_mode=pl.Buffered(1)),
            pl.BlockSpec((width, half), lambda i, h: (0, h[1]), pipeline_mode=pl.Buffered(1)),
            rows_of(width), rows_of(LANES),
            once(table.shape), once((width, width)), rows_of(3 * width),
            pl.BlockSpec((per_step, pairs, 2 * span, span), lambda i, h: (i, 0, 0, 0)),
        ],
        [rows_of(width), rows_of(width), rows_of(3 * width), full((8, width))],
        [
            shaped((rows, width), F32), shaped((rows, width), BF16),
            shaped((rows, 3 * width), BF16), shaped((8, width), F32),
        ],
        [pltpu.VMEM((rows_step, width), BF16)],
        8 * rows * width * width * 2,
        40e6,
        (*grads_inner, gres, w_up, w_up, n_attn, spread, table, w_out, qkv, probs),
        40, 0, (1,), (0, 1),
    )


def projection_terms(x, grad_mixed, attended, grad_branch, vectors, here, which, got=None):
    rows, width = x.shape
    part = width // 2
    pieces = width // 32 // 8

    def product(x_ref, gm_ref, att_ref, gb_ref, scr):
        step = pl.program_id(0)

        @pl.when(step < 3)
        def _():
            scr[...] = t_dot(x_ref[...], gm_ref[...])

        @pl.when(step == 3)
        def _():
            scr[...] = t_dot(att_ref[...], gb_ref[...])

    def small(here_s, ffn_ref, attn_ref, sent_ref, kept_ref, store):
        first = here_s[0] == 0
        for step in range(4):

            @pl.when(pl.program_id(0) == step)
            def _():
                side, at = step // 2, slice(step % 2 * part, (step % 2 + 1) * part)
                wide = slice(step * part, (step + 1) * part)
                rows_of = (
                    (ffn_ref[0:1, at], ffn_ref[2:3, at], attn_ref[1:2, at], attn_ref[3:4, at]),
                    (ffn_ref[1:2, at], attn_ref[0:1, at], attn_ref[2:3, at], attn_ref[4:5, at]),
                )[side]
                sent, kept = sent_ref[:, wide], kept_ref[:, wide]
                ups = (jnp.where(first, kept, sent), jnp.where(first, sent, kept))
                store(jnp.concatenate(rows_of + ups + (jnp.zeros((2, part), F32),), axis=0))

    def give(here_s, x_ref, gm_ref, att_ref, gb_ref, ffn_ref, attn_ref, sent_ref, kept_ref, out_ref, scr):
        product(x_ref, gm_ref, att_ref, gb_ref, scr)
        out_ref[:width, :] = scr[...].astype(BF16)

        def store(value):
            out_ref[width:, :] = value.astype(BF16)

        small(here_s, ffn_ref, attn_ref, sent_ref, kept_ref, store)

    def own(
        here_s, x_ref, gm_ref, att_ref, gb_ref, ffn_ref, attn_ref, sent_ref, kept_ref, got_ref,
        send_a, keep_a, send_b, keep_b, scr, cut,
    ):
        product(x_ref, gm_ref, att_ref, gb_ref, scr)
        term = scr[...] + got_ref[:width, :].astype(F32)
        cut[...] = term.reshape(cut.shape)
        deal(cut, here_s, (send_a, keep_a, send_b, keep_b), 4, pieces)

        def store(value):
            extra = (value + got_ref[width:, :].astype(F32)).astype(BF16)
            send_a[8 * pieces] = extra
            keep_a[8 * pieces] = extra

        small(here_s, ffn_ref, attn_ref, sent_ref, kept_ref, store)

    in_specs = [
        once((rows, width)),
        pl.BlockSpec((rows, part), lambda i, h: (0, h[which] * 3 + jnp.minimum(i, 2))),
        once((rows, width)),
        pl.BlockSpec((rows, part), lambda i, h: (0, h[which]), pipeline_mode=pl.Buffered(1)),
    ] + [once(item.shape) for item in vectors]
    args = [x, grad_mixed, attended, grad_branch, *vectors]
    flops = 4 * rows * width * width
    if got is None:
        return call(
            give, "proj_give", (4,), (here,), in_specs,
            pl.BlockSpec((width + 8, part), lambda i, *_: (0, i)),
            shaped((width + 8, 4 * part), BF16),
            [pltpu.VMEM((width, part), F32)], flops, 9e6, args, 20, 0, (0,), (3,),
        )
    return call(
        own, "proj_own", (4,), (here,),
        in_specs + [pl.BlockSpec((width + 8, part), lambda i, *_: (0, i))],
        [
            pl.BlockSpec((8 * pieces + extra, 8, part), lambda i, *_: (0, 0, i))
            for extra in (1, 1, 0, 0)
        ],
        [shaped((8 * pieces + extra, 8, 4 * part), BF16) for extra in (1, 1, 0, 0)],
        [pltpu.VMEM((width, part), F32), pltpu.VMEM((4, 2, 2, 2, pieces, 8, part), F32)],
        flops, 11e6, args + [got], 24, 1, (0, 1, 2, 3), (3,),
    )


def input_gradient(grad_mixed, w_qkv, grad_resid, rows_step):
    rows, width = grad_resid.shape

    def kernel(gm_ref, wq_ref, gr_ref, out_ref):
        out_ref[...] = (dot_t(gm_ref[...], wq_ref[...]) + gr_ref[...]).astype(BF16)

    return call(
        kernel, "input_grad", (rows // rows_step,), (),
        [
            pl.BlockSpec((rows_step, 3 * width), lambda i: (i, 0)),
            once((width, 3 * width)),
            pl.BlockSpec((rows_step, width), lambda i: (i, 0)),
        ],
        pl.BlockSpec((rows_step, width), lambda i: (i, 0)),
        shaped((rows, width), BF16), [], 6 * rows * width * width, 13e6,
        (grad_mixed, w_qkv, grad_resid), 20,
    )


def copied(item, here, block):
    rows, width = item.shape

    def kernel(here_s, in_ref, out_ref):
        out_ref[...] = in_ref[...]

    spec = pl.BlockSpec((block, width), lambda i, *_: (i, 0))
    return call(
        kernel, "copied", (rows // block,), (here,), [spec], spec,
        shaped((rows, width), item.dtype), [], 1, 3e6, (item,), 4,
    )


def small_call(kernel, name, here, args, outs, vmem=12):
    return pl.pallas_call(
        kernel,
        in_specs=[pl.BlockSpec(memory_space=pltpu.SMEM)]
        + [pl.BlockSpec(memory_space=pltpu.VMEM)] * len(args),
        out_specs=[pl.BlockSpec(memory_space=pltpu.VMEM)] * len(outs),
        out_shape=outs,
        compiler_params=pltpu.CompilerParams(vmem_limit_bytes=vmem * MIB),
        cost_estimate=pl.CostEstimate(flops=int(1e6 * COST), bytes_accessed=int(4e6 * COST), transcendentals=0),
        name=name,
    )(here, *args)


def add(left, right):
    return (left.astype(F32) + right.astype(F32)).astype(BF16)


def fold_second(terms, here, pieces, extra):
    cols = terms[0][0].shape[2]
    count = len(terms)

    def kernel(here_s, *refs):
        send_a, left_a, send_b, left_b = refs[4 * count :]
        x, y = here_s[2], here_s[3]
        for term in range(count):
            ka, ga, kb, gb = refs[4 * term : 4 * term + 4]
            for z in range(4):
                at = pl.ds((term * 4 + z) * pieces, pieces)

                def sum_of(keep, got, other):
                    rows = pl.ds(z * 2 * pieces + other * pieces, pieces)
                    return add(keep[rows], got[rows])

                send_a[at] = sum_of(ka, ga, 1 - y)
                left_a[at] = sum_of(ka, ga, y)
                send_b[at] = sum_of(kb, gb, 1 - x)
                left_b[at] = sum_of(kb, gb, x)
        if extra:
            total = add(refs[0][8 * pieces], refs[1][8 * pieces])
            send_a[4 * count * pieces] = total
            left_a[4 * count * pieces] = total

    a_out = shaped((4 * count * pieces + extra, 8, cols), BF16)
    b_out = shaped((4 * count * pieces, 8, cols), BF16)
    args = [item for term in terms for item in term]
    return small_call(kernel, "fold_second", here, args, [a_out, a_out, b_out, b_out])


def fold_third(pairs, here, pieces, extra):
    cols = pairs[0].shape[2]
    count = pairs[2].shape[0] // (4 * pieces)

    def kernel(here_s, *refs):
        ins, (send, left) = refs[:-2], refs[-2:]
        low = here_s[4]
        for high in range(2):
            for term in range(count):
                for ab in range(2):
                    keep, got = ins[2 * ab : 2 * ab + 2]
                    at = pl.ds(((high * count + term) * 2 + ab) * pieces, pieces)
                    for out, pick in ((send, 1 - low), (left, low)):
                        rows = pl.ds((term * 4 + high * 2 + pick) * pieces, pieces)
                        out[at] = add(keep[rows], got[rows])
        if extra:
            total = add(ins[0][4 * count * pieces], ins[1][4 * count * pieces])
            send[4 * count * pieces] = total
            left[4 * count * pieces] = total

    out = shaped((4 * count * pieces + extra, 8, cols), BF16)
    return small_call(kernel, "fold_third", here, pairs, [out, out])


def fold_fourth(keep, got, here, extra):
    cols = keep.shape[2]
    count = (keep.shape[0] - extra) // 2

    def kernel(here_s, keep_ref, got_ref, send, left):
        high = here_s[5]
        for out, pick in ((send, 1 - high), (left, high)):
            rows = pl.ds(pick * count, count)
            out[:count] = add(keep_ref[rows], got_ref[rows])
        if extra:
            total = add(keep_ref[2 * count], got_ref[2 * count])
            send[count] = total
            left[count] = total

    out = shaped((count + extra, 8, cols), BF16)
    return small_call(kernel, "fold_fourth", here, (keep, got), [out, out])


def fold_last(keep, got, here, extra):
    cols = keep.shape[2]
    count = keep.shape[0] - extra

    def kernel(here_s, keep_ref, got_ref, *outs):
        outs[0][...] = add(keep_ref[:count], got_ref[:count])
        if extra:
            outs[1][0] = add(keep_ref[count], got_ref[count])

    outs = [shaped((count, 8, cols), BF16)] + [shaped((1, 8, cols), BF16)] * extra
    return small_call(kernel, "fold_last", here, (keep, got), outs)


def chosen_part(here_s, refs, core, side, at):
    me, gx, gc, gd = [item[at].astype(F32) for item in refs]
    same_core, same_side = here_s[0] == core, here_s[2] == side
    return jnp.where(same_core, jnp.where(same_side, me, gx), jnp.where(same_side, gc, gd))


def feed_blocks(parts, here, pieces, width):
    cols = parts[0].shape[2]
    half = width // 2
    folds = cols // half
    rows = 2 * pieces * 8

    def kernel(here_s, me, gx, gc, gd, down_ref, up_ref):
        refs = (me, gx, gc, gd)
        for core in range(2):
            for side in range(2):
                tall = side * folds * rows
                for ab in range(2):
                    at = pl.ds(ab * pieces, pieces)
                    value = chosen_part(here_s, refs, core, side, at).reshape(rows // 2, cols)
                    for fold in range(folds):
                        start = tall + (ab * folds + fold) * (rows // 2)
                        down_ref[start : start + rows // 2, core * half : (core + 1) * half] = value[
                            :, fold * half : (fold + 1) * half
                        ]
                at = pl.ds(2 * pieces, 2 * pieces)
                value = chosen_part(here_s, refs, core, side, at).reshape(rows, cols)
                up_ref[side * rows : (side + 1) * rows, core * cols : (core + 1) * cols] = value

    outs = [shaped((2 * folds * rows, width), F32), shaped((2 * rows, 2 * cols), F32)]
    return small_call(kernel, "feed_blocks", here, parts, outs, 16)


def projection_blocks(parts, vectors, here, pieces):
    cols = parts[0].shape[2]
    rows = 2 * pieces * 8
    cut = cols // 4 * 3
    width = cols // 2
    small = width // 8
    large = cols // 4

    def kernel(here_s, me, gx, gc, gd, vec_ref, qkv_ref, out_ref, *outs):
        refs = (me, gx, gc, gd)
        for core in range(2):
            for side in range(2):
                value = chosen_part(here_s, refs, core, side, slice(None)).reshape(rows, cols)
                at = slice(side * rows, (side + 1) * rows)
                qkv_ref[at, core * cut : (core + 1) * cut] = value[:, :cut]
                out_ref[at, core * (cols - cut) : (core + 1) * (cols - cut)] = value[:, cut:]
        table = vec_ref[0].astype(F32)
        wide = here_s[6]
        shift = lax.rem(width - wide * small, width)
        left, right = pltpu.roll(table[:, :width], shift, 1), pltpu.roll(table[:, width:], shift, 1)
        for row in range(4):
            outs[2 * row][...] = left[row : row + 1, :small]
            outs[2 * row + 1][...] = right[row : row + 1, :small]
        turned = pltpu.roll(table, lax.rem(cols - lax.rem(wide, 4) * large, cols), 1)
        outs[8][...] = jnp.where(wide < 4, turned[4:5, :large], turned[5:6, :large])

    outs = [shaped((2 * rows, 2 * cut), F32), shaped((2 * rows, 2 * (cols - cut)), F32)]
    outs += [shaped((1, small), F32)] * 8 + [shaped((1, large), F32)]
    return small_call(kernel, "projection_blocks", here, (*parts, vectors), outs, 16)


def after(item, *earlier):
    return lax.optimization_barrier((item, *earlier))[0]


def swap(item, axis, step):
    count = lax.axis_size(axis)
    return lax.ppermute(item, axis, [(index, index ^ step) for index in range(count)])


def quarters(mine):
    across = swap(mine, "narrow", 2)
    return mine, across, swap(mine, "narrow", 1), swap(across, "narrow", 1)


def regroup_rows(sent, bucket, wide_count, batches):
    span, width = sent.shape[1:]
    if wide_count == batches:
        got = lax.all_to_all(sent, "wide", split_axis=0, concat_axis=0, tiled=True)
        return got.reshape(batches * span, width)
    send = jnp.zeros((wide_count, span, width), sent.dtype).at[bucket].set(sent)
    got = lax.all_to_all(send, "wide", split_axis=0, concat_axis=0, tiled=True)
    marks = jnp.zeros((wide_count, 1), jnp.int32).at[bucket].set(1)
    filled = lax.all_to_all(marks, "wide", split_axis=0, concat_axis=0, tiled=True)[:, 0]
    place = jnp.where(filled > 0, jnp.cumsum(filled) - filled, batches)
    chosen = (
        jnp.zeros((batches,), jnp.int32)
        .at[place]
        .set(jnp.arange(wide_count, dtype=jnp.int32), mode="drop")
    )
    return got[chosen].reshape(batches * span, width)


def sum_anywhere(item, wide_count, narrow_count):
    blocks = item.astype(F32).reshape(wide_count, -1)
    extent = blocks.shape[1]
    padded = (extent + narrow_count - 1) // narrow_count * narrow_count
    blocks = jnp.pad(blocks, ((0, 0), (0, padded - extent))).reshape(-1)
    share = lax.psum_scatter(blocks, ("wide", "narrow"), scatter_dimension=0, tiled=True)
    whole = lax.all_gather(share.astype(BF16), "narrow", axis=0, tiled=True).astype(F32)
    return whole[:extent].reshape((item.shape[0] // wide_count,) + item.shape[1:])


def body(
    tokens, bucket, lengths, pairing, targets, w_qkv, bias_q, bias_v, w_out, bias_out,
    gain_attn, shift_attn, w_up, bias_up, w_down, bias_down, gain_ffn, shift_ffn,
):
    wide_count, narrow_count = lax.axis_size("wide"), lax.axis_size("narrow")
    batches = bucket.shape[0]
    rows, width = tokens.shape
    span = rows // batches
    paired = (wide_count, narrow_count) == (8, 4)
    wide, narrow = lax.axis_index("wide"), lax.axis_index("narrow")
    if paired:
        core = narrow % 2
        here = jnp.stack(
            [core, 1 - core, narrow // 2, wide % 2, wide // 2 % 2, wide // 4, wide, narrow]
        ).astype(jnp.int32)
    else:
        here = jnp.arange(8, dtype=jnp.int32)
    table = vector_table(
        [bias_q, bias_v, bias_out, gain_attn, shift_attn, bias_down, gain_ffn, shift_ffn, bias_up], width
    )
    ordered = wide_count == batches
    slots = bucket if ordered else jnp.arange(batches, dtype=jnp.int32)
    pieces = width // 32 // 8

    qkv, probs, attended, n_attn, spread, sid = attention_forward(
        tokens, w_qkv, w_out, table, bucket, lengths, wide_count // batches, span, 4 * span
    )
    active, slope, hidden_t, sent, gres, grad_second, vec_ffn = feed_forward(
        n_attn, w_up, w_down, table, sid, slots, pairing, targets, batches, 2 * span
    )
    ups = (grad_second, slope, hidden_t, w_down)
    heads = (n_attn, spread, table, w_out, qkv, probs)
    down_sent = down_terms(active, grad_second, here, 1)
    if paired:
        encoded = regroup_rows(after(sent, down_sent), bucket, wide_count, batches)
        up_sent, gi_sent, bup_sent = up_terms(*ups, after(here, down_sent), 1)
        down_dealt = down_terms(active, grad_second, after(here, bup_sent), 0, swap(down_sent, "narrow", 1))
        down_a, down_b = swap(down_dealt[0], "narrow", 2), swap(down_dealt[2], "wide", 1)
        *up_dealt, gi_kept, bup_kept = up_terms(
            *ups, after(here, down_dealt[1]), 0, swap(up_sent, "narrow", 1)
        )
        up_a, up_b = swap(up_dealt[0], "narrow", 2), swap(up_dealt[2], "wide", 1)
        gr, gb, gm, vec_attn = attention_backward(
            (gi_kept, gi_sent), gres, w_up, *heads, after(here, up_dealt[1]), span, 4 * span
        )
        feed = fold_second(
            [
                (down_dealt[1], down_a, down_dealt[3], down_b),
                (up_dealt[1], up_a, up_dealt[3], up_b),
            ],
            after(here, vec_attn, encoded), pieces, 0,
        )
        feed_a, feed_b = swap(feed[0], "wide", 1), swap(feed[2], "narrow", 2)
        projections = (tokens, gm, attended, gb, (vec_ffn, vec_attn, bup_sent, bup_kept))
        proj_sent = projection_terms(*projections, after(here, feed[1]), 1)
        proj_dealt = projection_terms(
            *projections, after(here, proj_sent), 0, swap(proj_sent, "narrow", 1)
        )
        proj_a, proj_b = swap(proj_dealt[0], "narrow", 2), swap(proj_dealt[2], "wide", 1)
        send, feed = fold_third(
            [feed[1], feed_a, feed[3], feed_b], after(here, proj_dealt[1]), pieces, 0
        )
        feed_got = swap(send, "wide", 2)
        grad_tokens = input_gradient(after(gm, feed), w_qkv, gr, 4 * span)
        send, feed = fold_fourth(feed, feed_got, after(here, grad_tokens), 0)
        feed_got = swap(send, "wide", 4)
        proj_dealt = fold_second(
            [(proj_dealt[1], proj_a, proj_dealt[3], proj_b)], after(here, feed), pieces, 1
        )
        proj_a, proj_b = swap(proj_dealt[0], "wide", 1), swap(proj_dealt[2], "narrow", 2)
        encoded = copied(encoded, after(here, proj_dealt[1]), span)
        send, proj = fold_third(
            [proj_dealt[1], proj_a, proj_dealt[3], proj_b], after(here, encoded), pieces, 1
        )
        proj_got = swap(send, "wide", 2)
        (feed,) = fold_last(feed, feed_got, after(here, proj), 0)
        send, proj = fold_fourth(proj, proj_got, after(here, feed), 1)
        proj_got = swap(send, "wide", 4)
        feed = quarters(after(feed, proj))
        proj, vectors = fold_last(proj, proj_got, here, 1)
        proj = quarters(proj)
        grad_w_down, grad_w_up = feed_blocks(feed, after(here, proj[0]), pieces, width)
        grad_w_qkv, grad_w_out, *small = projection_blocks(proj, vectors, after(here, grad_w_down), pieces)
        small = [item.reshape(-1) for item in small]
    else:
        encoded = regroup_rows(sent, bucket, wide_count, batches)
        down_kept = down_terms(active, grad_second, here, 0)
        up_sent, gi_sent, bup_sent = up_terms(*ups, here, 1)
        up_kept, gi_kept, bup_kept = up_terms(*ups, here, 0)
        gr, gb, gm, vec_attn = attention_backward(
            (gi_kept, gi_sent), gres, w_up, *heads, here, span, 2 * span
        )
        projections = (tokens, gm, attended, gb, (vec_ffn, vec_attn, bup_sent, bup_kept), here)
        grad_tokens = input_gradient(gm, w_qkv, gr, 2 * span)
        proj_sent, proj_kept = projection_terms(*projections, 1), projection_terms(*projections, 0)
        total = partial(sum_anywhere, wide_count=wide_count, narrow_count=narrow_count)
        cut = width // 2 * 3
        grad_w_down = total(jnp.concatenate([down_kept, down_sent], axis=1))
        grad_w_up = total(jnp.concatenate([up_kept, up_sent], axis=1))
        grad_w_qkv = total(jnp.concatenate([proj_kept[:width, :cut], proj_sent[:width, :cut]], axis=1))
        grad_w_out = total(jnp.concatenate([proj_kept[:width, cut:], proj_sent[:width, cut:]], axis=1))
        small = [
            total(item)
            for item in (*vec_ffn[:3], *vec_attn[:5], jnp.concatenate([bup_kept[0], bup_sent[0]]))
        ]
    gain_out, shift_out, b_down, b_q, b_v, b_out, g_attn, s_attn, b_up = small
    return (
        encoded, grad_tokens, grad_w_qkv, b_q, b_v, grad_w_out, b_out, g_attn, s_attn,
        grad_w_up, b_up, grad_w_down, b_down, gain_out, shift_out,
    )


def solution(mesh):
    split = P(("wide", "narrow"))
    in_specs = (
        P(("wide", "narrow"), None), split, split, P(("wide", "narrow"), None), split,
    ) + (P(),) * 13
    out_specs = (
        P(("wide", "narrow"), None), P(("wide", "narrow"), None),
        P("wide", None), P("wide"), P("wide"), P("wide", None), P("wide"), P("wide"), P("wide"),
        P("wide", None), P("wide"), P("wide", None), P("wide"), P("wide"), P("wide"),
    )
    return jax.shard_map(body, mesh=mesh, in_specs=in_specs, out_specs=out_specs, check_vma=False)
```

```python
from functools import partial

import jax
import jax.numpy as jnp
from jax import lax
from jax.experimental import pallas as pl
from jax.experimental.pallas import tpu as pltpu
from jax.sharding import PartitionSpec as P

HDIM = 64
KTOP = 12
NORM_EPS = 1e-12
COS_EPS = 1e-06
MASKED = -1000000000.0
LOSS_SCALE = 1024.0
F32 = jnp.float32
BF16 = jnp.bfloat16
LANES = 128
MIB = 1024 * 1024
LARGE = 100000
COST = 0.05
HALF_ROOT = 0.7071067811865476
BELL_RATE = -0.7213475204444817
BELL_PEAK = -1.3257480647361595
ROW_BQ, ROW_BV, ROW_BO, ROW_GA, ROW_SA, ROW_BD, ROW_GF, ROW_SF, ROW_BU = range(9)


def dot(left, right):
    return jnp.dot(left, right, preferred_element_type=F32)


def dot_t(left, right):
    return lax.dot_general(left, right, (((1,), (1,)), ((), ())), preferred_element_type=F32)


def t_dot(left, right):
    return lax.dot_general(left, right, (((0,), (0,)), ((), ())), preferred_element_type=F32)


def full(shape):
    return pl.BlockSpec(shape, lambda *_: (0,) * len(shape))


def once(shape):
    return pl.BlockSpec(shape, lambda *_: (0,) * len(shape), pipeline_mode=pl.Buffered(1))


def large(item):
    return item.size >= LARGE


def shaped(shape, dtype):
    return jax.ShapeDtypeStruct(shape, dtype)


def call(
    kernel, name, grid, prefetch, in_specs, out_specs, out_shape, scratch, flops, moved, args, vmem=24, free=0, loose=(), near=()
):
    single = not isinstance(out_shape, list)
    shapes = [out_shape] if single else out_shape
    shapes = [
        pltpu.HBM(item.shape, item.dtype) if large(item) and number not in loose else item
        for number, item in enumerate(shapes)
    ]
    out_shape = shapes[0] if single else shapes
    args = [
        pltpu.with_memory_space_constraint(item, pltpu.HBM)
        if large(item) and number < len(args) - free and number not in near
        else item
        for number, item in enumerate(args)
    ]
    return pl.pallas_call(
        kernel,
        grid_spec=pltpu.PrefetchScalarGridSpec(
            num_scalar_prefetch=len(prefetch),
            grid=grid,
            in_specs=in_specs,
            out_specs=out_specs,
            scratch_shapes=scratch,
        ),
        out_shape=out_shape,
        compiler_params=pltpu.CompilerParams(
            dimension_semantics=("arbitrary",) * len(grid), vmem_limit_bytes=vmem * MIB
        ),
        cost_estimate=pl.CostEstimate(flops=int(flops * COST), bytes_accessed=int(moved * COST), transcendentals=0),
        name=name,
    )(*[pltpu.with_memory_space_constraint(item, pltpu.HBM) for item in prefetch], *args)


def norm_forward(values):
    center = values - jnp.mean(values, axis=-1, keepdims=True)
    spread = lax.rsqrt(jnp.mean(center * center, axis=-1, keepdims=True) + NORM_EPS)
    return center * spread, spread


def norm_backward(grad_out, normed, spread, gain):
    scaled = grad_out * gain
    mean_scaled = jnp.mean(scaled, axis=-1, keepdims=True)
    mean_product = jnp.mean(scaled * normed, axis=-1, keepdims=True)
    return spread * (scaled - mean_scaled - normed * mean_product)


def column_sum(values):
    return jnp.sum(values, axis=0, keepdims=True)


def gelu_pair(v):
    phi = 0.5 + 0.5 * lax.erf(v * HALF_ROOT)
    bell = jnp.exp2((v * v) * BELL_RATE + BELL_PEAK)
    return v * phi, phi + v * bell


def head_masks():
    lane = lax.broadcasted_iota(jnp.int32, (1, LANES), 1)
    low = (lane < HDIM).astype(F32)
    return low.astype(BF16), (1.0 - low).astype(BF16), lane < HDIM


def sentence_count(bucket_s, number, group_size):
    kind = bucket_s[number]
    if group_size > 1:
        kind = kind // group_size
    return jnp.maximum(1, lax.shift_right_logical(jnp.int32(KTOP), kind))


def row_sentences(batch, bucket_s, lengths_s, group_size, batches, sent, span):
    start = jnp.int32(0)
    for other in range(batches):
        start += jnp.where(other < batch, sentence_count(bucket_s, other, group_size), 0)
    count = sentence_count(bucket_s, batch, group_size)
    lane = lax.broadcasted_iota(jnp.int32, (8, span), 1)
    row = lax.broadcasted_iota(jnp.int32, (span, span), 0)
    passed_lane = jnp.zeros((8, span), jnp.int32)
    passed_row = jnp.zeros((span, span), jnp.int32)
    finish = jnp.int32(0)
    for number in range(KTOP):
        finish += lengths_s[jnp.minimum(start + number, sent - 1)]
        bound = jnp.where(number < count, finish, span)
        passed_lane += (lane >= bound).astype(jnp.int32)
        passed_row += (row >= bound).astype(jnp.int32)
    sid_lane = jnp.where(passed_lane < count, start + passed_lane, -1)
    sid_row = jnp.where(passed_row < count, start + passed_row, -1)
    return sid_lane, sid_row


def vector_table(vectors, width):
    def kernel(*refs):
        out_ref = refs[-1]
        at = 0
        for ref in refs[:-1]:
            for part in range(ref.shape[0] // width):
                out_ref[at : at + 1, :] = ref[part * width : (part + 1) * width].astype(F32).reshape(1, width)
                at += 1

    rows = sum(item.shape[0] for item in vectors) // width
    return pl.pallas_call(
        kernel,
        grid=(1,),
        in_specs=[full(item.shape) for item in vectors],
        out_specs=full((rows, width)),
        out_shape=shaped((rows, width), F32),
        compiler_params=pltpu.CompilerParams(vmem_limit_bytes=4 * MIB),
        name="vector_table",
    )(*[pltpu.with_memory_space_constraint(item, pltpu.HBM) for item in vectors])


def attention_forward(x, w_qkv, w_out, table, bucket, lengths, group_size, span, rows_step):
    rows, width = x.shape
    batches = rows // span
    pairs = width // LANES
    sent = lengths.shape[0]
    per_step = rows_step // span

    def kernel(bucket_s, lengths_s, x_ref, wq_ref, wo_ref, tab_ref, qkv_ref, p_ref, att_ref, n_ref, s_ref, sid_ref):
        step = pl.program_id(0)
        low_b, high_b, low_m = head_masks()
        x_in = x_ref[...]
        mixed = dot(x_in, wq_ref[:, :width]) + tab_ref[ROW_BQ : ROW_BQ + 1, :]
        qkv_ref[:, :width] = (mixed * 0.125).astype(BF16)
        qkv_ref[:, width : 2 * width] = dot(x_in, wq_ref[:, width : 2 * width]).astype(BF16)
        mixed = dot(x_in, wq_ref[:, 2 * width :]) + tab_ref[ROW_BV : ROW_BV + 1, :]
        qkv_ref[:, 2 * width :] = mixed.astype(BF16)
        eye = lax.broadcasted_iota(jnp.int32, (span, span), 0) == lax.broadcasted_iota(
            jnp.int32, (span, span), 1
        )
        for inner in range(per_step):
            sid_lane, sid_row = row_sentences(
                step * per_step + inner, bucket_s, lengths_s, group_size, batches, sent, span
            )
            sid_ref[inner] = sid_lane
            same = (sid_row == sid_lane[0:1, :]) & (sid_row >= 0)
            bias = jnp.where(same | eye, 0.0, MASKED)
            bias = jnp.concatenate([bias, bias], axis=0)
            base = slice(inner * span, (inner + 1) * span)
            for pair in range(pairs):
                cols = slice(pair * LANES, (pair + 1) * LANES)
                q = qkv_ref[base, cols]
                k = qkv_ref[base, width + pair * LANES : width + (pair + 1) * LANES]
                v = qkv_ref[base, 2 * width + pair * LANES : 2 * width + (pair + 1) * LANES]
                both = jnp.concatenate([q * low_b, q * high_b], axis=0)
                logits = dot_t(both, k) + bias
                raised = jnp.exp(logits - jnp.max(logits, axis=-1, keepdims=True))
                total = jnp.sum(raised, axis=-1, keepdims=True)
                probs = (raised * (1.0 / total)).astype(BF16)
                p_ref[inner, pair] = probs
                mix = dot(probs, v)
                att_ref[base, cols] = jnp.where(low_m, mix[:span], mix[span:]).astype(BF16)
        branch = dot(att_ref[...], wo_ref[...]) + tab_ref[ROW_BO : ROW_BO + 1, :]
        normed, spread = norm_forward(x_in.astype(F32) + branch)
        n_ref[...] = normed
        s_ref[...] = jnp.broadcast_to(spread, (rows_step, LANES))

    return call(
        kernel,
        "attn_fwd",
        (rows // rows_step,),
        (bucket, lengths),
        [
            pl.BlockSpec((rows_step, width), lambda i, *_: (i, 0)),
            once((width, 3 * width)),
            once((width, width)),
            once(table.shape),
        ],
        [
            pl.BlockSpec((rows_step, 3 * width), lambda i, *_: (i, 0)),
            pl.BlockSpec((per_step, pairs, 2 * span, span), lambda i, *_: (i, 0, 0, 0)),
            pl.BlockSpec((rows_step, width), lambda i, *_: (i, 0)),
            pl.BlockSpec((rows_step, width), lambda i, *_: (i, 0)),
            pl.BlockSpec((rows_step, LANES), lambda i, *_: (i, 0)),
            pl.BlockSpec((per_step, 8, span), lambda i, *_: (i, 0, 0)),
        ],
        [
            shaped((rows, 3 * width), BF16),
            shaped((batches, pairs, 2 * span, span), BF16),
            shaped((rows, width), BF16),
            shaped((rows, width), F32),
            shaped((rows, LANES), F32),
            shaped((batches, 8, span), jnp.int32),
        ],
        [],
        8 * rows * width * width * 2,
        30e6,
        (x, w_qkv, w_out, table),
        26,
    )


def feed_forward(n_attn, w_up, w_down, table, sid, slots, pairing, targets, slot_count, block):
    rows, width = n_attn.shape
    ff = w_up.shape[1]
    batches, _, span = sid.shape
    pair_count = targets.shape[0]
    side = -(-pair_count // 8) * 8
    chunk = width
    steps = ff // chunk
    tall = 2 * block
    blocks = rows // block
    per_block = block // span

    def kernel(
        slots_s, pairing_s, targets_s, n_ref, wu_ref, wd_ref, tab_ref, sid_ref,
        act_ref, dg_ref, ht_ref, enc_ref, gres_ref, gsl_ref, vec_ref, low_scr, acc_scr, spread_scr,
    ):
        step = pl.program_id(0)
        gain = tab_ref[ROW_GA : ROW_GA + 1, :]
        shift = tab_ref[ROW_SA : ROW_SA + 1, :]

        @pl.when(step == 0)
        def _():
            hidden = (n_ref[...] * gain + shift).astype(BF16)
            low_scr[...] = hidden
            ht_ref[...] = hidden.T
            acc_scr[...] = jnp.zeros_like(acc_scr)

        for number in range(rows // tall):
            base = slice(number * tall, (number + 1) * tall)
            inner = dot(low_scr[base, :], wu_ref[...]) + tab_ref[pl.ds(ROW_BU + step, 1), :]
            active, slope = gelu_pair(inner)
            active = active.astype(BF16)
            act_ref[base, :] = active
            dg_ref[base, :] = slope.astype(BF16)
            acc_scr[base, :] += dot(active, wd_ref[...])

        @pl.when(step == steps - 1)
        def _():
            gain_out = tab_ref[ROW_GF : ROW_GF + 1, :]
            shift_out = tab_ref[ROW_SF : ROW_SF + 1, :]
            slot = lax.broadcasted_iota(jnp.int32, (2 * side, span), 0)
            wanted = jnp.full((2 * side, span), -2, jnp.int32)
            goal = jnp.zeros((side, LANES), F32)
            goal_slot = lax.broadcasted_iota(jnp.int32, (side, LANES), 0)
            for number in range(pair_count):
                wanted = jnp.where(slot == number, pairing_s[0, 2 * number], wanted)
                wanted = jnp.where(slot == side + number, pairing_s[0, 2 * number + 1], wanted)
                goal = jnp.where(goal_slot == number, targets_s[number], goal)
            members = [
                (sid_ref[number][0:1, :] == wanted).astype(F32) for number in range(batches)
            ]
            sizes = jnp.zeros((2 * side, 1), F32)
            for member in members:
                sizes += jnp.sum(member, axis=-1, keepdims=True)
            share = 1.0 / jnp.maximum(sizes, 1.0)
            picks = [
                jnp.concatenate(members[number * per_block : (number + 1) * per_block], axis=1).astype(BF16)
                for number in range(blocks)
            ]
            ones = jnp.ones((2 * side, LANES), BF16)
            pooled = jnp.zeros((2 * side, width), F32)
            for number in range(blocks):
                base = slice(number * block, (number + 1) * block)
                resid = (
                    n_ref[base, :] * gain + shift + acc_scr[base, :] + tab_ref[ROW_BD : ROW_BD + 1, :]
                )
                normed, spread = norm_forward(resid)
                acc_scr[base, :] = normed
                spread_scr[base, :] = jnp.broadcast_to(spread, (block, LANES))
                out = normed * gain_out + shift_out
                high = out.astype(BF16)
                rest = (out - high.astype(F32)).astype(BF16)
                pooled += dot(picks[number], high) + dot(picks[number], rest)
                valid = t_dot(picks[number], ones)
                for col in range(width // LANES):
                    cols = slice(col * LANES, (col + 1) * LANES)
                    kept = (out[:, cols] * valid).astype(BF16)
                    for inner in range(per_block):
                        enc_ref[slots_s[number * per_block + inner], :, cols] = kept[
                            inner * span : (inner + 1) * span
                        ]
            pooled = pooled * share
            first, partner = pooled[:side], pooled[side:]
            cross = jnp.sum(first * partner, axis=-1, keepdims=True)
            scale_first = lax.rsqrt(jnp.sum(first * first, axis=-1, keepdims=True) + COS_EPS)
            scale_partner = lax.rsqrt(jnp.sum(partner * partner, axis=-1, keepdims=True) + COS_EPS)
            cosine = cross * scale_first * scale_partner
            factor = 2.0 * LOSS_SCALE * (cosine - goal[:, :1])
            both_scales = factor * scale_first * scale_partner
            grad_first = both_scales * partner - (factor * cosine * scale_first * scale_first) * first
            grad_partner = (
                both_scales * first - (factor * cosine * scale_partner * scale_partner) * partner
            )
            grad_home = jnp.concatenate([grad_first, grad_partner], axis=0) * share
            high = grad_home.astype(BF16)
            rest = (grad_home - high.astype(F32)).astype(BF16)
            vec_ref[...] = jnp.zeros_like(vec_ref)
            for number in range(blocks):
                base = slice(number * block, (number + 1) * block)
                grad_out = t_dot(picks[number], high) + t_dot(picks[number], rest)
                normed = acc_scr[base, :]
                resid = norm_backward(grad_out, normed, spread_scr[base, :1], gain_out)
                gres_ref[base, :] = resid
                low = resid.astype(BF16)
                gsl_ref[base, :] = low
                vec_ref[0:1, :] += column_sum(grad_out * normed)
                vec_ref[1:2, :] += column_sum(grad_out)
                vec_ref[2:3, :] += column_sum(low.astype(F32))

    return call(
        kernel,
        "ffn_fwd",
        (steps,),
        (slots, pairing, targets),
        [
            once((rows, width)),
            pl.BlockSpec((width, chunk), lambda j, *_: (0, j)),
            pl.BlockSpec((chunk, width), lambda j, *_: (j, 0)),
            once(table.shape),
            once((batches, 8, span)),
        ],
        [
            pl.BlockSpec((rows, chunk), lambda j, *_: (0, j)),
            pl.BlockSpec((rows, chunk), lambda j, *_: (0, j)),
            once((width, rows)),
            once((slot_count, span, width)),
            once((rows, width)),
            once((rows, width)),
            once((8, width)),
        ],
        [
            shaped((rows, ff), BF16),
            shaped((rows, ff), BF16),
            shaped((width, rows), BF16),
            shaped((slot_count, span, width), BF16),
            shaped((rows, width), F32),
            shaped((rows, width), BF16),
            shaped((8, width), F32),
        ],
        [
            pltpu.VMEM((rows, width), BF16),
            pltpu.VMEM((rows, width), F32),
            pltpu.VMEM((rows, LANES), F32),
        ],
        8 * rows * width * ff,
        40e6,
        (n_attn, w_up, w_down, table, sid),
        38, 0, (2, 5),
    )


def deal(scratch, here_s, outs, z_count, pieces, folds=1):
    send_a, keep_a, send_b, keep_b = outs
    x, y = here_s[2], here_s[3]
    cols = scratch.shape[-1]
    for z in range(z_count):
        for other in range(2):
            at = pl.ds((z * 2 + other) * pieces, pieces)
            for fold in range(folds):
                part = pl.ds(fold * pieces, pieces)
                to = slice(fold * cols, (fold + 1) * cols)
                send_a[at, :, to] = scratch[z, other, 1 - x, 0, part].astype(BF16)
                keep_a[at, :, to] = scratch[z, other, x, 0, part].astype(BF16)
                send_b[at, :, to] = scratch[z, 1 - y, other, 1, part].astype(BF16)
                keep_b[at, :, to] = scratch[z, y, other, 1, part].astype(BF16)


def down_terms(active, grad_second, here, which, got=None):
    rows, ff = active.shape
    width = grad_second.shape[1]
    half = width // 2
    steps = 4
    tall = ff // steps
    pieces = width // 32 // 8
    folds = ff // width

    def give(here_s, act_ref, gs_ref, out_ref):
        out_ref[...] = t_dot(act_ref[...], gs_ref[...]).astype(BF16)

    def own(here_s, act_ref, gs_ref, got_ref, *rest):
        outs, scratch = rest[:4], rest[4]
        term = t_dot(act_ref[...], gs_ref[...]) + got_ref[...].astype(F32)
        scratch[...] = term.reshape(scratch.shape)
        deal(scratch, here_s, outs, 1, pieces, folds)

    in_specs = [
        pl.BlockSpec((rows, tall), lambda i, here_s: (0, i)),
        pl.BlockSpec((rows, half), lambda i, here_s: (0, here_s[which]), pipeline_mode=pl.Buffered(1)),
    ]
    flops = 2 * rows * ff * half
    if got is None:
        return call(
            give, "down_give", (steps,), (here,), in_specs,
            pl.BlockSpec((tall, half), lambda i, *_: (i, 0)),
            shaped((ff, half), BF16), [], flops, 9e6, (active, grad_second), 20, 0, (0,), (1,),
        )
    block = (2 * pieces, 8, folds * half)
    return call(
        own, "down_own", (steps,), (here,),
        in_specs + [pl.BlockSpec((tall, half), lambda i, *_: (i, 0))],
        [pl.BlockSpec(block, lambda i, *_: (i, 0, 0))] * 4,
        [shaped((8 * pieces, 8, folds * half), BF16)] * 4,
        [pltpu.VMEM((1, 2, 2, 2, folds * pieces, 8, half), F32)],
        flops, 11e6, (active, grad_second, got), 24, 1, (0, 2), (1,),
    )


def up_terms(grad_second, slope, hidden_t, w_down, here, which, got=None):
    rows, width = grad_second.shape
    ff = w_down.shape[0]
    half = ff // 2
    chunk = width
    steps = half // chunk
    block = rows // 2
    pieces = width // 32 // 8

    def kernel(here_s, gs_ref, dg_ref, ht_ref, wd_ref, *refs):
        if got is not None:
            got_ref, refs = refs[0], refs[1:]
            outs, refs = refs[:4], refs[4:]
        else:
            out_ref, refs = refs[0], refs[1:]
        gi_ref, bu_ref = refs[:2]
        sums = jnp.zeros((1, chunk), F32)
        for number in range(rows // block):
            base = slice(number * block, (number + 1) * block)
            grad_active = dot_t(gs_ref[base, :], wd_ref[...])
            low = (grad_active * dg_ref[base, :].astype(F32)).astype(BF16)
            gi_ref[base, :] = low
            sums += column_sum(low.astype(F32))
        bu_ref[...] = sums
        term = dot(ht_ref[...], gi_ref[...])
        if got is None:
            out_ref[...] = term.astype(BF16)
        else:
            scratch = refs[2]
            term += got_ref[...].astype(F32)
            scratch[...] = term.reshape(scratch.shape)
            deal(scratch, here_s, outs, 4, pieces)

    def col(i, here_s):
        return here_s[which] * steps + i

    in_specs = [
        once((rows, width)),
        pl.BlockSpec((rows, chunk), lambda i, h: (0, col(i, h))),
        once((width, rows)),
        pl.BlockSpec((chunk, width), lambda i, h: (col(i, h), 0)),
    ]
    args = [grad_second, slope, hidden_t, w_down]
    scratch = []
    if got is None:
        out_specs = [pl.BlockSpec((width, chunk), lambda i, *_: (0, i))]
        out_shape = [shaped((width, half), BF16)]
    else:
        in_specs.append(pl.BlockSpec((width, chunk), lambda i, *_: (0, i)))
        args.append(got)
        out_specs = [pl.BlockSpec((8 * pieces, 8, chunk), lambda i, *_: (0, 0, i))] * 4
        out_shape = [shaped((8 * pieces, 8, half), BF16)] * 4
        scratch.append(pltpu.VMEM((4, 2, 2, 2, pieces, 8, chunk), F32))
    return call(
        kernel, "up_give" if got is None else "up_own", (steps,), (here,), in_specs,
        out_specs
        + [
            pl.BlockSpec((rows, chunk), lambda i, *_: (0, i)),
            pl.BlockSpec((1, chunk), lambda i, *_: (0, i)),
        ],
        out_shape + [shaped((rows, half), BF16), shaped((1, half), F32)],
        scratch, 4 * rows * width * half, 16e6, args, 26, 0 if got is None else 1, (0,) if got is None else (0, 2, 4), (0, 2),
    )


def attention_backward(grads_inner, gres, w_up, n_attn, spread, table, w_out, qkv, probs, here, span, rows_step):
    rows, width = gres.shape
    half = grads_inner[0].shape[1]
    pairs = width // LANES
    per_step = rows_step // span

    def kernel(here_s, gi_ref, other_ref, gres_ref, wu_ref, wu_other_ref, n_ref, s_ref, tab_ref, wo_ref, qkv_ref, p_ref, gr_ref, gb_ref, gm_ref, vec_ref, ga_scr):
        step = pl.program_id(0)
        low_b, high_b, low_m = head_masks()

        @pl.when(step == 0)
        def _():
            vec_ref[...] = jnp.zeros_like(vec_ref)

        normed = n_ref[...]
        grad_hidden = (
            dot_t(gi_ref[...], wu_ref[...]) + dot_t(other_ref[...], wu_other_ref[...]) + gres_ref[...]
        )
        resid = norm_backward(grad_hidden, normed, s_ref[:, :1], tab_ref[ROW_GA : ROW_GA + 1, :])
        gr_ref[...] = resid
        low = resid.astype(BF16)
        gb_ref[...] = low
        vec_ref[2:3, :] += column_sum(low.astype(F32))
        vec_ref[3:4, :] += column_sum(grad_hidden * normed)
        vec_ref[4:5, :] += column_sum(grad_hidden)
        ga_scr[...] = dot_t(low, wo_ref[...]).astype(BF16)
        for inner in range(per_step):
            base = slice(inner * span, (inner + 1) * span)
            for pair in range(pairs):
                cols = slice(pair * LANES, (pair + 1) * LANES)
                k_cols = slice(width + pair * LANES, width + (pair + 1) * LANES)
                v_cols = slice(2 * width + pair * LANES, 2 * width + (pair + 1) * LANES)
                q, k, v = qkv_ref[base, cols], qkv_ref[base, k_cols], qkv_ref[base, v_cols]
                grad = ga_scr[base, cols]
                grads = jnp.concatenate([grad * low_b, grad * high_b], axis=0)
                both = jnp.concatenate([q * low_b, q * high_b], axis=0)
                weights = p_ref[inner, pair]
                wide = weights.astype(F32)
                grad_probs = dot_t(grads, v)
                balance = jnp.sum(wide * grad_probs, axis=-1, keepdims=True)
                grad_logits = (wide * (grad_probs - balance)).astype(BF16)
                mix = dot(grad_logits, k)
                grad_q = jnp.where(low_m, mix[:span], mix[span:]).astype(BF16) * jnp.bfloat16(0.125)
                grad_v = t_dot(weights, grads).astype(BF16)
                gm_ref[base, cols] = grad_q
                gm_ref[base, k_cols] = t_dot(grad_logits, both).astype(BF16)
                gm_ref[base, v_cols] = grad_v
                vec_ref[0:1, cols] += column_sum(grad_q.astype(F32))
                vec_ref[1:2, cols] += column_sum(grad_v.astype(F32))

    def rows_of(cols):
        return pl.BlockSpec((rows_step, cols), lambda i, h: (i, 0))

    return call(
        kernel,
        "attn_bwd",
        (rows // rows_step,),
        (here,),
        [
            rows_of(half), rows_of(half), rows_of(width),
            pl.BlockSpec((width, half), lambda i, h: (0, h[0]), pipeline_mode=pl.Buffered(1)),
            pl.BlockSpec((width, half), lambda i, h: (0, h[1]), pipeline_mode=pl.Buffered(1)),
            rows_of(width), rows_of(LANES),
            once(table.shape), once((width, width)), rows_of(3 * width),
            pl.BlockSpec((per_step, pairs, 2 * span, span), lambda i, h: (i, 0, 0, 0)),
        ],
        [rows_of(width), rows_of(width), rows_of(3 * width), full((8, width))],
        [
            shaped((rows, width), F32), shaped((rows, width), BF16),
            shaped((rows, 3 * width), BF16), shaped((8, width), F32),
        ],
        [pltpu.VMEM((rows_step, width), BF16)],
        8 * rows * width * width * 2,
        40e6,
        (*grads_inner, gres, w_up, w_up, n_attn, spread, table, w_out, qkv, probs),
        40, 0, (1,), (0, 1, 3, 4, 8),
    )


def projection_terms(x, grad_mixed, attended, grad_branch, vectors, here, which, got=None):
    rows, width = x.shape
    part = width // 2
    pieces = width // 32 // 8

    def product(x_ref, gm_ref, att_ref, gb_ref, scr):
        step = pl.program_id(0)

        @pl.when(step < 3)
        def _():
            scr[...] = t_dot(x_ref[...], gm_ref[...])

        @pl.when(step == 3)
        def _():
            scr[...] = t_dot(att_ref[...], gb_ref[...])

    def small(here_s, ffn_ref, attn_ref, sent_ref, kept_ref, store):
        first = here_s[0] == 0
        for step in range(4):

            @pl.when(pl.program_id(0) == step)
            def _():
                side, at = step // 2, slice(step % 2 * part, (step % 2 + 1) * part)
                wide = slice(step * part, (step + 1) * part)
                rows_of = (
                    (ffn_ref[0:1, at], ffn_ref[2:3, at], attn_ref[1:2, at], attn_ref[3:4, at]),
                    (ffn_ref[1:2, at], attn_ref[0:1, at], attn_ref[2:3, at], attn_ref[4:5, at]),
                )[side]
                sent, kept = sent_ref[:, wide], kept_ref[:, wide]
                ups = (jnp.where(first, kept, sent), jnp.where(first, sent, kept))
                store(jnp.concatenate(rows_of + ups + (jnp.zeros((2, part), F32),), axis=0))

    def give(here_s, x_ref, gm_ref, att_ref, gb_ref, ffn_ref, attn_ref, sent_ref, kept_ref, out_ref, scr):
        product(x_ref, gm_ref, att_ref, gb_ref, scr)
        out_ref[:width, :] = scr[...].astype(BF16)

        def store(value):
            out_ref[width:, :] = value.astype(BF16)

        small(here_s, ffn_ref, attn_ref, sent_ref, kept_ref, store)

    def own(
        here_s, x_ref, gm_ref, att_ref, gb_ref, ffn_ref, attn_ref, sent_ref, kept_ref, got_ref,
        send_a, keep_a, send_b, keep_b, scr, cut,
    ):
        product(x_ref, gm_ref, att_ref, gb_ref, scr)
        term = scr[...] + got_ref[:width, :].astype(F32)
        cut[...] = term.reshape(cut.shape)
        deal(cut, here_s, (send_a, keep_a, send_b, keep_b), 4, pieces)

        def store(value):
            extra = (value + got_ref[width:, :].astype(F32)).astype(BF16)
            send_a[8 * pieces] = extra
            keep_a[8 * pieces] = extra

        small(here_s, ffn_ref, attn_ref, sent_ref, kept_ref, store)

    in_specs = [
        once((rows, width)),
        pl.BlockSpec((rows, part), lambda i, h: (0, h[which] * 3 + jnp.minimum(i, 2))),
        once((rows, width)),
        pl.BlockSpec((rows, part), lambda i, h: (0, h[which]), pipeline_mode=pl.Buffered(1)),
    ] + [once(item.shape) for item in vectors]
    args = [x, grad_mixed, attended, grad_branch, *vectors]
    flops = 4 * rows * width * width
    if got is None:
        return call(
            give, "proj_give", (4,), (here,), in_specs,
            pl.BlockSpec((width + 8, part), lambda i, *_: (0, i)),
            shaped((width + 8, 4 * part), BF16),
            [pltpu.VMEM((width, part), F32)], flops, 9e6, args, 20, 0, (0,), (0, 2, 3),
        )
    return call(
        own, "proj_own", (4,), (here,),
        in_specs + [pl.BlockSpec((width + 8, part), lambda i, *_: (0, i))],
        [
            pl.BlockSpec((8 * pieces + extra, 8, part), lambda i, *_: (0, 0, i))
            for extra in (1, 1, 0, 0)
        ],
        [shaped((8 * pieces + extra, 8, 4 * part), BF16) for extra in (1, 1, 0, 0)],
        [pltpu.VMEM((width, part), F32), pltpu.VMEM((4, 2, 2, 2, pieces, 8, part), F32)],
        flops, 11e6, args + [got], 24, 1, (0, 1, 2, 3), (0, 2, 3),
    )


def input_gradient(grad_mixed, w_qkv, grad_resid, rows_step):
    rows, width = grad_resid.shape

    def kernel(gm_ref, wq_ref, gr_ref, out_ref):
        out_ref[...] = (dot_t(gm_ref[...], wq_ref[...]) + gr_ref[...]).astype(BF16)

    return call(
        kernel, "input_grad", (rows // rows_step,), (),
        [
            pl.BlockSpec((rows_step, 3 * width), lambda i: (i, 0)),
            once((width, 3 * width)),
            pl.BlockSpec((rows_step, width), lambda i: (i, 0)),
        ],
        pl.BlockSpec((rows_step, width), lambda i: (i, 0)),
        shaped((rows, width), BF16), [], 6 * rows * width * width, 13e6,
        (grad_mixed, w_qkv, grad_resid), 20, 0, (), (1,),
    )


def copied(item, here, block):
    rows, width = item.shape

    def kernel(here_s, in_ref, out_ref):
        out_ref[...] = in_ref[...]

    spec = pl.BlockSpec((block, width), lambda i, *_: (i, 0))
    return call(
        kernel, "copied", (rows // block,), (here,), [spec], spec,
        shaped((rows, width), item.dtype), [], 1, 3e6, (item,), 4,
    )


def small_call(kernel, name, here, args, outs, vmem=12):
    return pl.pallas_call(
        kernel,
        in_specs=[pl.BlockSpec(memory_space=pltpu.SMEM)]
        + [pl.BlockSpec(memory_space=pltpu.VMEM)] * len(args),
        out_specs=[pl.BlockSpec(memory_space=pltpu.VMEM)] * len(outs),
        out_shape=outs,
        compiler_params=pltpu.CompilerParams(vmem_limit_bytes=vmem * MIB),
        cost_estimate=pl.CostEstimate(flops=int(1e6 * COST), bytes_accessed=int(4e6 * COST), transcendentals=0),
        name=name,
    )(here, *args)


def add(left, right):
    return (left.astype(F32) + right.astype(F32)).astype(BF16)


def fold_second(terms, here, pieces, extra):
    cols = terms[0][0].shape[2]
    count = len(terms)

    def kernel(here_s, *refs):
        send_a, left_a, send_b, left_b = refs[4 * count :]
        x, y = here_s[2], here_s[3]
        for term in range(count):
            ka, ga, kb, gb = refs[4 * term : 4 * term + 4]
            for z in range(4):
                at = pl.ds((term * 4 + z) * pieces, pieces)

                def sum_of(keep, got, other):
                    rows = pl.ds(z * 2 * pieces + other * pieces, pieces)
                    return add(keep[rows], got[rows])

                send_a[at] = sum_of(ka, ga, 1 - y)
                left_a[at] = sum_of(ka, ga, y)
                send_b[at] = sum_of(kb, gb, 1 - x)
                left_b[at] = sum_of(kb, gb, x)
        if extra:
            total = add(refs[0][8 * pieces], refs[1][8 * pieces])
            send_a[4 * count * pieces] = total
            left_a[4 * count * pieces] = total

    a_out = shaped((4 * count * pieces + extra, 8, cols), BF16)
    b_out = shaped((4 * count * pieces, 8, cols), BF16)
    args = [item for term in terms for item in term]
    return small_call(kernel, "fold_second", here, args, [a_out, a_out, b_out, b_out])


def fold_third(pairs, here, pieces, extra):
    cols = pairs[0].shape[2]
    count = pairs[2].shape[0] // (4 * pieces)

    def kernel(here_s, *refs):
        ins, (send, left) = refs[:-2], refs[-2:]
        low = here_s[4]
        for high in range(2):
            for term in range(count):
                for ab in range(2):
                    keep, got = ins[2 * ab : 2 * ab + 2]
                    at = pl.ds(((high * count + term) * 2 + ab) * pieces, pieces)
                    for out, pick in ((send, 1 - low), (left, low)):
                        rows = pl.ds((term * 4 + high * 2 + pick) * pieces, pieces)
                        out[at] = add(keep[rows], got[rows])
        if extra:
            total = add(ins[0][4 * count * pieces], ins[1][4 * count * pieces])
            send[4 * count * pieces] = total
            left[4 * count * pieces] = total

    out = shaped((4 * count * pieces + extra, 8, cols), BF16)
    return small_call(kernel, "fold_third", here, pairs, [out, out])


def fold_fourth(keep, got, here, extra):
    cols = keep.shape[2]
    count = (keep.shape[0] - extra) // 2

    def kernel(here_s, keep_ref, got_ref, send, left):
        high = here_s[5]
        for out, pick in ((send, 1 - high), (left, high)):
            rows = pl.ds(pick * count, count)
            out[:count] = add(keep_ref[rows], got_ref[rows])
        if extra:
            total = add(keep_ref[2 * count], got_ref[2 * count])
            send[count] = total
            left[count] = total

    out = shaped((count + extra, 8, cols), BF16)
    return small_call(kernel, "fold_fourth", here, (keep, got), [out, out])


def fold_last(keep, got, here, extra):
    cols = keep.shape[2]
    count = keep.shape[0] - extra

    def kernel(here_s, keep_ref, got_ref, *outs):
        outs[0][...] = add(keep_ref[:count], got_ref[:count])
        if extra:
            outs[1][0] = add(keep_ref[count], got_ref[count])

    outs = [shaped((count, 8, cols), BF16)] + [shaped((1, 8, cols), BF16)] * extra
    return small_call(kernel, "fold_last", here, (keep, got), outs)


def chosen_part(here_s, refs, core, side, at):
    me, gx, gc, gd = [item[at].astype(F32) for item in refs]
    same_core, same_side = here_s[0] == core, here_s[2] == side
    return jnp.where(same_core, jnp.where(same_side, me, gx), jnp.where(same_side, gc, gd))


def feed_blocks(parts, here, pieces, width):
    cols = parts[0].shape[2]
    half = width // 2
    folds = cols // half
    rows = 2 * pieces * 8

    def kernel(here_s, me, gx, gc, gd, down_ref, up_ref):
        refs = (me, gx, gc, gd)
        for core in range(2):
            for side in range(2):
                tall = side * folds * rows
                for ab in range(2):
                    at = pl.ds(ab * pieces, pieces)
                    value = chosen_part(here_s, refs, core, side, at).reshape(rows // 2, cols)
                    for fold in range(folds):
                        start = tall + (ab * folds + fold) * (rows // 2)
                        down_ref[start : start + rows // 2, core * half : (core + 1) * half] = value[
                            :, fold * half : (fold + 1) * half
                        ]
                at = pl.ds(2 * pieces, 2 * pieces)
                value = chosen_part(here_s, refs, core, side, at).reshape(rows, cols)
                up_ref[side * rows : (side + 1) * rows, core * cols : (core + 1) * cols] = value

    outs = [shaped((2 * folds * rows, width), F32), shaped((2 * rows, 2 * cols), F32)]
    return small_call(kernel, "feed_blocks", here, parts, outs, 16)


def projection_blocks(parts, vectors, here, pieces):
    cols = parts[0].shape[2]
    rows = 2 * pieces * 8
    cut = cols // 4 * 3
    width = cols // 2
    small = width // 8
    large = cols // 4

    def kernel(here_s, me, gx, gc, gd, vec_ref, qkv_ref, out_ref, *outs):
        refs = (me, gx, gc, gd)
        for core in range(2):
            for side in range(2):
                value = chosen_part(here_s, refs, core, side, slice(None)).reshape(rows, cols)
                at = slice(side * rows, (side + 1) * rows)
                qkv_ref[at, core * cut : (core + 1) * cut] = value[:, :cut]
                out_ref[at, core * (cols - cut) : (core + 1) * (cols - cut)] = value[:, cut:]
        table = vec_ref[0].astype(F32)
        wide = here_s[6]
        shift = lax.rem(width - wide * small, width)
        left, right = pltpu.roll(table[:, :width], shift, 1), pltpu.roll(table[:, width:], shift, 1)
        for row in range(4):
            outs[2 * row][...] = left[row : row + 1, :small]
            outs[2 * row + 1][...] = right[row : row + 1, :small]
        turned = pltpu.roll(table, lax.rem(cols - lax.rem(wide, 4) * large, cols), 1)
        outs[8][...] = jnp.where(wide < 4, turned[4:5, :large], turned[5:6, :large])

    outs = [shaped((2 * rows, 2 * cut), F32), shaped((2 * rows, 2 * (cols - cut)), F32)]
    outs += [shaped((1, small), F32)] * 8 + [shaped((1, large), F32)]
    return small_call(kernel, "projection_blocks", here, (*parts, vectors), outs, 16)


def after(item, *earlier):
    return lax.optimization_barrier((item, *earlier))[0]


def swap(item, axis, step):
    count = lax.axis_size(axis)
    return lax.ppermute(item, axis, [(index, index ^ step) for index in range(count)])


def quarters(mine):
    across = swap(mine, "narrow", 2)
    return mine, across, swap(mine, "narrow", 1), swap(across, "narrow", 1)


def regroup_rows(sent, bucket, wide_count, batches):
    span, width = sent.shape[1:]
    if wide_count == batches:
        got = lax.all_to_all(sent, "wide", split_axis=0, concat_axis=0, tiled=True)
        return got.reshape(batches * span, width)
    send = jnp.zeros((wide_count, span, width), sent.dtype).at[bucket].set(sent)
    got = lax.all_to_all(send, "wide", split_axis=0, concat_axis=0, tiled=True)
    marks = jnp.zeros((wide_count, 1), jnp.int32).at[bucket].set(1)
    filled = lax.all_to_all(marks, "wide", split_axis=0, concat_axis=0, tiled=True)[:, 0]
    place = jnp.where(filled > 0, jnp.cumsum(filled) - filled, batches)
    chosen = (
        jnp.zeros((batches,), jnp.int32)
        .at[place]
        .set(jnp.arange(wide_count, dtype=jnp.int32), mode="drop")
    )
    return got[chosen].reshape(batches * span, width)


def sum_anywhere(item, wide_count, narrow_count):
    blocks = item.astype(F32).reshape(wide_count, -1)
    extent = blocks.shape[1]
    padded = (extent + narrow_count - 1) // narrow_count * narrow_count
    blocks = jnp.pad(blocks, ((0, 0), (0, padded - extent))).reshape(-1)
    share = lax.psum_scatter(blocks, ("wide", "narrow"), scatter_dimension=0, tiled=True)
    whole = lax.all_gather(share.astype(BF16), "narrow", axis=0, tiled=True).astype(F32)
    return whole[:extent].reshape((item.shape[0] // wide_count,) + item.shape[1:])


def body(
    tokens, bucket, lengths, pairing, targets, w_qkv, bias_q, bias_v, w_out, bias_out,
    gain_attn, shift_attn, w_up, bias_up, w_down, bias_down, gain_ffn, shift_ffn,
):
    wide_count, narrow_count = lax.axis_size("wide"), lax.axis_size("narrow")
    batches = bucket.shape[0]
    rows, width = tokens.shape
    span = rows // batches
    paired = (wide_count, narrow_count) == (8, 4)
    wide, narrow = lax.axis_index("wide"), lax.axis_index("narrow")
    if paired:
        core = narrow % 2
        here = jnp.stack(
            [core, 1 - core, narrow // 2, wide % 2, wide // 2 % 2, wide // 4, wide, narrow]
        ).astype(jnp.int32)
    else:
        here = jnp.arange(8, dtype=jnp.int32)
    table = vector_table(
        [bias_q, bias_v, bias_out, gain_attn, shift_attn, bias_down, gain_ffn, shift_ffn, bias_up], width
    )
    ordered = wide_count == batches
    slots = bucket if ordered else jnp.arange(batches, dtype=jnp.int32)
    pieces = width // 32 // 8

    qkv, probs, attended, n_attn, spread, sid = attention_forward(
        tokens, w_qkv, w_out, table, bucket, lengths, wide_count // batches, span, 2 * span
    )
    active, slope, hidden_t, sent, gres, grad_second, vec_ffn = feed_forward(
        n_attn, w_up, w_down, table, sid, slots, pairing, targets, batches, 2 * span
    )
    ups = (grad_second, slope, hidden_t, w_down)
    heads = (n_attn, spread, table, w_out, qkv, probs)
    down_sent = down_terms(active, grad_second, here, 1)
    if paired:
        encoded = regroup_rows(after(sent, down_sent), bucket, wide_count, batches)
        up_sent, gi_sent, bup_sent = up_terms(*ups, after(here, down_sent), 1)
        down_dealt = down_terms(active, grad_second, after(here, bup_sent), 0, swap(down_sent, "narrow", 1))
        down_a, down_b = swap(down_dealt[0], "narrow", 2), swap(down_dealt[2], "wide", 1)
        *up_dealt, gi_kept, bup_kept = up_terms(
            *ups, after(here, down_dealt[1]), 0, swap(up_sent, "narrow", 1)
        )
        up_a, up_b = swap(up_dealt[0], "narrow", 2), swap(up_dealt[2], "wide", 1)
        gr, gb, gm, vec_attn = attention_backward(
            (gi_kept, gi_sent), gres, w_up, *heads, after(here, up_dealt[1]), span, 4 * span
        )
        feed = fold_second(
            [
                (down_dealt[1], down_a, down_dealt[3], down_b),
                (up_dealt[1], up_a, up_dealt[3], up_b),
            ],
            after(here, vec_attn, encoded), pieces, 0,
        )
        feed_a, feed_b = swap(feed[0], "wide", 1), swap(feed[2], "narrow", 2)
        projections = (tokens, gm, attended, gb, (vec_ffn, vec_attn, bup_sent, bup_kept))
        proj_sent = projection_terms(*projections, after(here, feed[1]), 1)
        proj_dealt = projection_terms(
            *projections, after(here, proj_sent), 0, swap(proj_sent, "narrow", 1)
        )
        proj_a, proj_b = swap(proj_dealt[0], "narrow", 2), swap(proj_dealt[2], "wide", 1)
        send, feed = fold_third(
            [feed[1], feed_a, feed[3], feed_b], after(here, proj_dealt[1]), pieces, 0
        )
        feed_got = swap(send, "wide", 2)
        grad_tokens = input_gradient(after(gm, feed), w_qkv, gr, 4 * span)
        send, feed = fold_fourth(feed, feed_got, after(here, grad_tokens), 0)
        feed_got = swap(send, "wide", 4)
        proj_dealt = fold_second(
            [(proj_dealt[1], proj_a, proj_dealt[3], proj_b)], after(here, feed), pieces, 1
        )
        proj_a, proj_b = swap(proj_dealt[0], "wide", 1), swap(proj_dealt[2], "narrow", 2)
        encoded = copied(encoded, after(here, proj_dealt[1]), span)
        send, proj = fold_third(
            [proj_dealt[1], proj_a, proj_dealt[3], proj_b], after(here, encoded), pieces, 1
        )
        proj_got = swap(send, "wide", 2)
        (feed,) = fold_last(feed, feed_got, after(here, proj), 0)
        send, proj = fold_fourth(proj, proj_got, after(here, feed), 1)
        proj_got = swap(send, "wide", 4)
        feed = quarters(after(feed, proj))
        proj, vectors = fold_last(proj, proj_got, here, 1)
        proj = quarters(proj)
        grad_w_down, grad_w_up = feed_blocks(feed, after(here, proj[0]), pieces, width)
        grad_w_qkv, grad_w_out, *small = projection_blocks(proj, vectors, after(here, grad_w_down), pieces)
        small = [item.reshape(-1) for item in small]
    else:
        encoded = regroup_rows(sent, bucket, wide_count, batches)
        down_kept = down_terms(active, grad_second, here, 0)
        up_sent, gi_sent, bup_sent = up_terms(*ups, here, 1)
        up_kept, gi_kept, bup_kept = up_terms(*ups, here, 0)
        gr, gb, gm, vec_attn = attention_backward(
            (gi_kept, gi_sent), gres, w_up, *heads, here, span, 2 * span
        )
        projections = (tokens, gm, attended, gb, (vec_ffn, vec_attn, bup_sent, bup_kept), here)
        grad_tokens = input_gradient(gm, w_qkv, gr, 2 * span)
        proj_sent, proj_kept = projection_terms(*projections, 1), projection_terms(*projections, 0)
        total = partial(sum_anywhere, wide_count=wide_count, narrow_count=narrow_count)
        cut = width // 2 * 3
        grad_w_down = total(jnp.concatenate([down_kept, down_sent], axis=1))
        grad_w_up = total(jnp.concatenate([up_kept, up_sent], axis=1))
        grad_w_qkv = total(jnp.concatenate([proj_kept[:width, :cut], proj_sent[:width, :cut]], axis=1))
        grad_w_out = total(jnp.concatenate([proj_kept[:width, cut:], proj_sent[:width, cut:]], axis=1))
        small = [
            total(item)
            for item in (*vec_ffn[:3], *vec_attn[:5], jnp.concatenate([bup_kept[0], bup_sent[0]]))
        ]
    gain_out, shift_out, b_down, b_q, b_v, b_out, g_attn, s_attn, b_up = small
    return (
        encoded, grad_tokens, grad_w_qkv, b_q, b_v, grad_w_out, b_out, g_attn, s_attn,
        grad_w_up, b_up, grad_w_down, b_down, gain_out, shift_out,
    )


def solution(mesh):
    split = P(("wide", "narrow"))
    in_specs = (
        P(("wide", "narrow"), None), split, split, P(("wide", "narrow"), None), split,
    ) + (P(),) * 13
    out_specs = (
        P(("wide", "narrow"), None), P(("wide", "narrow"), None),
        P("wide", None), P("wide"), P("wide"), P("wide", None), P("wide"), P("wide"), P("wide"),
        P("wide", None), P("wide"), P("wide", None), P("wide"), P("wide"), P("wide"),
    )
    return jax.shard_map(body, mesh=mesh, in_specs=in_specs, out_specs=out_specs, check_vma=False)
```

```python
from functools import partial

import jax
import jax.numpy as jnp
from jax import lax
from jax.experimental import pallas as pl
from jax.experimental.pallas import tpu as pltpu
from jax.sharding import PartitionSpec as P

HDIM = 64
KTOP = 12
NORM_EPS = 1e-12
COS_EPS = 1e-06
MASKED = -1000000000.0
LOSS_SCALE = 1024.0
F32 = jnp.float32
BF16 = jnp.bfloat16
LANES = 128
MIB = 1024 * 1024
LARGE = 100000
COST = 0.05
HALF_ROOT = 0.7071067811865476
BELL_RATE = -0.7213475204444817
BELL_PEAK = -1.3257480647361595
ROW_BQ, ROW_BV, ROW_BO, ROW_GA, ROW_SA, ROW_BD, ROW_GF, ROW_SF, ROW_BU = range(9)


def dot(left, right):
    return jnp.dot(left, right, preferred_element_type=F32)


def dot_t(left, right):
    return lax.dot_general(left, right, (((1,), (1,)), ((), ())), preferred_element_type=F32)


def t_dot(left, right):
    return lax.dot_general(left, right, (((0,), (0,)), ((), ())), preferred_element_type=F32)


def full(shape):
    return pl.BlockSpec(shape, lambda *_: (0,) * len(shape))


def once(shape):
    return pl.BlockSpec(shape, lambda *_: (0,) * len(shape), pipeline_mode=pl.Buffered(1))


def large(item):
    return item.size >= LARGE


def shaped(shape, dtype):
    return jax.ShapeDtypeStruct(shape, dtype)


def call(
    kernel, name, grid, prefetch, in_specs, out_specs, out_shape, scratch, flops, moved, args, vmem=24, free=0, loose=(), near=()
):
    single = not isinstance(out_shape, list)
    shapes = [out_shape] if single else out_shape
    shapes = [
        pltpu.HBM(item.shape, item.dtype) if large(item) and number not in loose else item
        for number, item in enumerate(shapes)
    ]
    out_shape = shapes[0] if single else shapes
    args = [
        pltpu.with_memory_space_constraint(item, pltpu.HBM)
        if large(item) and number < len(args) - free and number not in near
        else item
        for number, item in enumerate(args)
    ]
    return pl.pallas_call(
        kernel,
        grid_spec=pltpu.PrefetchScalarGridSpec(
            num_scalar_prefetch=len(prefetch),
            grid=grid,
            in_specs=in_specs,
            out_specs=out_specs,
            scratch_shapes=scratch,
        ),
        out_shape=out_shape,
        compiler_params=pltpu.CompilerParams(
            dimension_semantics=("arbitrary",) * len(grid), vmem_limit_bytes=vmem * MIB
        ),
        cost_estimate=pl.CostEstimate(flops=int(flops * COST), bytes_accessed=int(moved * COST), transcendentals=0),
        name=name,
    )(*[pltpu.with_memory_space_constraint(item, pltpu.HBM) for item in prefetch], *args)


def norm_forward(values):
    center = values - jnp.mean(values, axis=-1, keepdims=True)
    spread = lax.rsqrt(jnp.mean(center * center, axis=-1, keepdims=True) + NORM_EPS)
    return center * spread, spread


def norm_backward(grad_out, normed, spread, gain):
    scaled = grad_out * gain
    mean_scaled = jnp.mean(scaled, axis=-1, keepdims=True)
    mean_product = jnp.mean(scaled * normed, axis=-1, keepdims=True)
    return spread * (scaled - mean_scaled - normed * mean_product)


def column_sum(values):
    return jnp.sum(values, axis=0, keepdims=True)


def gelu_pair(v):
    phi = 0.5 + 0.5 * lax.erf(v * HALF_ROOT)
    bell = jnp.exp2((v * v) * BELL_RATE + BELL_PEAK)
    return v * phi, phi + v * bell


def head_masks():
    lane = lax.broadcasted_iota(jnp.int32, (1, LANES), 1)
    low = (lane < HDIM).astype(F32)
    return low.astype(BF16), (1.0 - low).astype(BF16), lane < HDIM


def sentence_count(bucket_s, number, group_size):
    kind = bucket_s[number]
    if group_size > 1:
        kind = kind // group_size
    return jnp.maximum(1, lax.shift_right_logical(jnp.int32(KTOP), kind))


def row_sentences(batch, bucket_s, lengths_s, group_size, batches, sent, span):
    start = jnp.int32(0)
    for other in range(batches):
        start += jnp.where(other < batch, sentence_count(bucket_s, other, group_size), 0)
    count = sentence_count(bucket_s, batch, group_size)
    lane = lax.broadcasted_iota(jnp.int32, (8, span), 1)
    row = lax.broadcasted_iota(jnp.int32, (span, span), 0)
    passed_lane = jnp.zeros((8, span), jnp.int32)
    passed_row = jnp.zeros((span, span), jnp.int32)
    finish = jnp.int32(0)
    for number in range(KTOP):
        finish += lengths_s[jnp.minimum(start + number, sent - 1)]
        bound = jnp.where(number < count, finish, span)
        passed_lane += (lane >= bound).astype(jnp.int32)
        passed_row += (row >= bound).astype(jnp.int32)
    sid_lane = jnp.where(passed_lane < count, start + passed_lane, -1)
    sid_row = jnp.where(passed_row < count, start + passed_row, -1)
    return sid_lane, sid_row


def vector_table(vectors, width):
    def kernel(*refs):
        out_ref = refs[-1]
        at = 0
        for ref in refs[:-1]:
            for part in range(ref.shape[0] // width):
                out_ref[at : at + 1, :] = ref[part * width : (part + 1) * width].astype(F32).reshape(1, width)
                at += 1

    rows = sum(item.shape[0] for item in vectors) // width
    return pl.pallas_call(
        kernel,
        grid=(1,),
        in_specs=[full(item.shape) for item in vectors],
        out_specs=full((rows, width)),
        out_shape=shaped((rows, width), F32),
        compiler_params=pltpu.CompilerParams(vmem_limit_bytes=4 * MIB),
        name="vector_table",
    )(*[pltpu.with_memory_space_constraint(item, pltpu.HBM) for item in vectors])


def attention_forward(x, w_qkv, w_out, table, bucket, lengths, group_size, span, rows_step):
    rows, width = x.shape
    batches = rows // span
    pairs = width // LANES
    sent = lengths.shape[0]
    per_step = rows_step // span

    def kernel(bucket_s, lengths_s, x_ref, wq_ref, wo_ref, tab_ref, qkv_ref, p_ref, att_ref, n_ref, s_ref, sid_ref):
        step = pl.program_id(0)
        low_b, high_b, low_m = head_masks()
        x_in = x_ref[...]
        mixed = dot(x_in, wq_ref[:, :width]) + tab_ref[ROW_BQ : ROW_BQ + 1, :]
        qkv_ref[:, :width] = (mixed * 0.125).astype(BF16)
        qkv_ref[:, width : 2 * width] = dot(x_in, wq_ref[:, width : 2 * width]).astype(BF16)
        mixed = dot(x_in, wq_ref[:, 2 * width :]) + tab_ref[ROW_BV : ROW_BV + 1, :]
        qkv_ref[:, 2 * width :] = mixed.astype(BF16)
        eye = lax.broadcasted_iota(jnp.int32, (span, span), 0) == lax.broadcasted_iota(
            jnp.int32, (span, span), 1
        )
        for inner in range(per_step):
            sid_lane, sid_row = row_sentences(
                step * per_step + inner, bucket_s, lengths_s, group_size, batches, sent, span
            )
            sid_ref[inner] = sid_lane
            same = (sid_row == sid_lane[0:1, :]) & (sid_row >= 0)
            bias = jnp.where(same | eye, 0.0, MASKED)
            bias = jnp.concatenate([bias, bias], axis=0)
            base = slice(inner * span, (inner + 1) * span)
            for pair in range(pairs):
                cols = slice(pair * LANES, (pair + 1) * LANES)
                q = qkv_ref[base, cols]
                k = qkv_ref[base, width + pair * LANES : width + (pair + 1) * LANES]
                v = qkv_ref[base, 2 * width + pair * LANES : 2 * width + (pair + 1) * LANES]
                both = jnp.concatenate([q * low_b, q * high_b], axis=0)
                logits = dot_t(both, k) + bias
                raised = jnp.exp(logits - jnp.max(logits, axis=-1, keepdims=True))
                total = jnp.sum(raised, axis=-1, keepdims=True)
                probs = (raised * (1.0 / total)).astype(BF16)
                p_ref[inner, pair] = probs
                mix = dot(probs, v)
                att_ref[base, cols] = jnp.where(low_m, mix[:span], mix[span:]).astype(BF16)
        branch = dot(att_ref[...], wo_ref[...]) + tab_ref[ROW_BO : ROW_BO + 1, :]
        normed, spread = norm_forward(x_in.astype(F32) + branch)
        n_ref[...] = normed
        s_ref[...] = jnp.broadcast_to(spread, (rows_step, LANES))

    return call(
        kernel,
        "attn_fwd",
        (rows // rows_step,),
        (bucket, lengths),
        [
            pl.BlockSpec((rows_step, width), lambda i, *_: (i, 0)),
            once((width, 3 * width)),
            once((width, width)),
            once(table.shape),
        ],
        [
            pl.BlockSpec((rows_step, 3 * width), lambda i, *_: (i, 0)),
            pl.BlockSpec((per_step, pairs, 2 * span, span), lambda i, *_: (i, 0, 0, 0)),
            pl.BlockSpec((rows_step, width), lambda i, *_: (i, 0)),
            pl.BlockSpec((rows_step, width), lambda i, *_: (i, 0)),
            pl.BlockSpec((rows_step, LANES), lambda i, *_: (i, 0)),
            pl.BlockSpec((per_step, 8, span), lambda i, *_: (i, 0, 0)),
        ],
        [
            shaped((rows, 3 * width), BF16),
            shaped((batches, pairs, 2 * span, span), BF16),
            shaped((rows, width), BF16),
            shaped((rows, width), F32),
            shaped((rows, LANES), F32),
            shaped((batches, 8, span), jnp.int32),
        ],
        [],
        8 * rows * width * width * 2,
        30e6,
        (x, w_qkv, w_out, table),
        26,
    )


def feed_forward(n_attn, w_up, w_down, table, sid, slots, pairing, targets, slot_count, block):
    rows, width = n_attn.shape
    ff = w_up.shape[1]
    batches, _, span = sid.shape
    pair_count = targets.shape[0]
    side = -(-pair_count // 8) * 8
    chunk = width
    steps = ff // chunk
    tall = 2 * block
    blocks = rows // block
    per_block = block // span

    def kernel(
        slots_s, pairing_s, targets_s, n_ref, wu_ref, wd_ref, tab_ref, sid_ref,
        act_ref, dg_ref, ht_ref, enc_ref, gres_ref, gsl_ref, vec_ref, low_scr, acc_scr, spread_scr,
    ):
        step = pl.program_id(0)
        gain = tab_ref[ROW_GA : ROW_GA + 1, :]
        shift = tab_ref[ROW_SA : ROW_SA + 1, :]

        @pl.when(step == 0)
        def _():
            hidden = (n_ref[...] * gain + shift).astype(BF16)
            low_scr[...] = hidden
            ht_ref[...] = hidden.T
            acc_scr[...] = jnp.zeros_like(acc_scr)

        for number in range(rows // tall):
            base = slice(number * tall, (number + 1) * tall)
            inner = dot(low_scr[base, :], wu_ref[...]) + tab_ref[pl.ds(ROW_BU + step, 1), :]
            active, slope = gelu_pair(inner)
            active = active.astype(BF16)
            act_ref[base, :] = active
            dg_ref[base, :] = slope.astype(BF16)
            acc_scr[base, :] += dot(active, wd_ref[...])

        @pl.when(step == steps - 1)
        def _():
            gain_out = tab_ref[ROW_GF : ROW_GF + 1, :]
            shift_out = tab_ref[ROW_SF : ROW_SF + 1, :]
            slot = lax.broadcasted_iota(jnp.int32, (2 * side, span), 0)
            wanted = jnp.full((2 * side, span), -2, jnp.int32)
            goal = jnp.zeros((side, LANES), F32)
            goal_slot = lax.broadcasted_iota(jnp.int32, (side, LANES), 0)
            for number in range(pair_count):
                wanted = jnp.where(slot == number, pairing_s[0, 2 * number], wanted)
                wanted = jnp.where(slot == side + number, pairing_s[0, 2 * number + 1], wanted)
                goal = jnp.where(goal_slot == number, targets_s[number], goal)
            members = [
                (sid_ref[number][0:1, :] == wanted).astype(F32) for number in range(batches)
            ]
            sizes = jnp.zeros((2 * side, 1), F32)
            for member in members:
                sizes += jnp.sum(member, axis=-1, keepdims=True)
            share = 1.0 / jnp.maximum(sizes, 1.0)
            picks = [
                jnp.concatenate(members[number * per_block : (number + 1) * per_block], axis=1).astype(BF16)
                for number in range(blocks)
            ]
            ones = jnp.ones((2 * side, LANES), BF16)
            pooled = jnp.zeros((2 * side, width), F32)
            for number in range(blocks):
                base = slice(number * block, (number + 1) * block)
                resid = (
                    n_ref[base, :] * gain + shift + acc_scr[base, :] + tab_ref[ROW_BD : ROW_BD + 1, :]
                )
                normed, spread = norm_forward(resid)
                acc_scr[base, :] = normed
                spread_scr[base, :] = jnp.broadcast_to(spread, (block, LANES))
                out = normed * gain_out + shift_out
                high = out.astype(BF16)
                rest = (out - high.astype(F32)).astype(BF16)
                pooled += dot(picks[number], high) + dot(picks[number], rest)
                valid = t_dot(picks[number], ones)
                for col in range(width // LANES):
                    cols = slice(col * LANES, (col + 1) * LANES)
                    kept = (out[:, cols] * valid).astype(BF16)
                    for inner in range(per_block):
                        enc_ref[slots_s[number * per_block + inner], :, cols] = kept[
                            inner * span : (inner + 1) * span
                        ]
            pooled = pooled * share
            first, partner = pooled[:side], pooled[side:]
            cross = jnp.sum(first * partner, axis=-1, keepdims=True)
            scale_first = lax.rsqrt(jnp.sum(first * first, axis=-1, keepdims=True) + COS_EPS)
            scale_partner = lax.rsqrt(jnp.sum(partner * partner, axis=-1, keepdims=True) + COS_EPS)
            cosine = cross * scale_first * scale_partner
            factor = 2.0 * LOSS_SCALE * (cosine - goal[:, :1])
            both_scales = factor * scale_first * scale_partner
            grad_first = both_scales * partner - (factor * cosine * scale_first * scale_first) * first
            grad_partner = (
                both_scales * first - (factor * cosine * scale_partner * scale_partner) * partner
            )
            grad_home = jnp.concatenate([grad_first, grad_partner], axis=0) * share
            high = grad_home.astype(BF16)
            rest = (grad_home - high.astype(F32)).astype(BF16)
            vec_ref[...] = jnp.zeros_like(vec_ref)
            for number in range(blocks):
                base = slice(number * block, (number + 1) * block)
                grad_out = t_dot(picks[number], high) + t_dot(picks[number], rest)
                normed = acc_scr[base, :]
                resid = norm_backward(grad_out, normed, spread_scr[base, :1], gain_out)
                gres_ref[base, :] = resid
                low = resid.astype(BF16)
                gsl_ref[base, :] = low
                vec_ref[0:1, :] += column_sum(grad_out * normed)
                vec_ref[1:2, :] += column_sum(grad_out)
                vec_ref[2:3, :] += column_sum(low.astype(F32))

    return call(
        kernel,
        "ffn_fwd",
        (steps,),
        (slots, pairing, targets),
        [
            once((rows, width)),
            pl.BlockSpec((width, chunk), lambda j, *_: (0, j)),
            pl.BlockSpec((chunk, width), lambda j, *_: (j, 0)),
            once(table.shape),
            once((batches, 8, span)),
        ],
        [
            pl.BlockSpec((rows, chunk), lambda j, *_: (0, j)),
            pl.BlockSpec((rows, chunk), lambda j, *_: (0, j)),
            once((width, rows)),
            once((slot_count, span, width)),
            once((rows, width)),
            once((rows, width)),
            once((8, width)),
        ],
        [
            shaped((rows, ff), BF16),
            shaped((rows, ff), BF16),
            shaped((width, rows), BF16),
            shaped((slot_count, span, width), BF16),
            shaped((rows, width), F32),
            shaped((rows, width), BF16),
            shaped((8, width), F32),
        ],
        [
            pltpu.VMEM((rows, width), BF16),
            pltpu.VMEM((rows, width), F32),
            pltpu.VMEM((rows, LANES), F32),
        ],
        8 * rows * width * ff,
        40e6,
        (n_attn, w_up, w_down, table, sid),
        38, 0, (2, 5), (2,),
    )


def deal(scratch, here_s, outs, z_count, pieces, folds=1):
    send_a, keep_a, send_b, keep_b = outs
    x, y = here_s[2], here_s[3]
    cols = scratch.shape[-1]
    for z in range(z_count):
        for other in range(2):
            at = pl.ds((z * 2 + other) * pieces, pieces)
            for fold in range(folds):
                part = pl.ds(fold * pieces, pieces)
                to = slice(fold * cols, (fold + 1) * cols)
                send_a[at, :, to] = scratch[z, other, 1 - x, 0, part].astype(BF16)
                keep_a[at, :, to] = scratch[z, other, x, 0, part].astype(BF16)
                send_b[at, :, to] = scratch[z, 1 - y, other, 1, part].astype(BF16)
                keep_b[at, :, to] = scratch[z, y, other, 1, part].astype(BF16)


def down_terms(active, grad_second, here, which, got=None):
    rows, ff = active.shape
    width = grad_second.shape[1]
    half = width // 2
    steps = 4
    tall = ff // steps
    pieces = width // 32 // 8
    folds = ff // width

    def give(here_s, act_ref, gs_ref, out_ref):
        out_ref[...] = t_dot(act_ref[...], gs_ref[...]).astype(BF16)

    def own(here_s, act_ref, gs_ref, got_ref, *rest):
        outs, scratch = rest[:4], rest[4]
        term = t_dot(act_ref[...], gs_ref[...]) + got_ref[...].astype(F32)
        scratch[...] = term.reshape(scratch.shape)
        deal(scratch, here_s, outs, 1, pieces, folds)

    in_specs = [
        pl.BlockSpec((rows, tall), lambda i, here_s: (0, i)),
        pl.BlockSpec((rows, half), lambda i, here_s: (0, here_s[which]), pipeline_mode=pl.Buffered(1)),
    ]
    flops = 2 * rows * ff * half
    if got is None:
        return call(
            give, "down_give", (steps,), (here,), in_specs,
            pl.BlockSpec((tall, half), lambda i, *_: (i, 0)),
            shaped((ff, half), BF16), [], flops, 9e6, (active, grad_second), 20, 0, (0,), (1,),
        )
    block = (2 * pieces, 8, folds * half)
    return call(
        own, "down_own", (steps,), (here,),
        in_specs + [pl.BlockSpec((tall, half), lambda i, *_: (i, 0))],
        [pl.BlockSpec(block, lambda i, *_: (i, 0, 0))] * 4,
        [shaped((8 * pieces, 8, folds * half), BF16)] * 4,
        [pltpu.VMEM((1, 2, 2, 2, folds * pieces, 8, half), F32)],
        flops, 11e6, (active, grad_second, got), 24, 1, (0, 2), (1,),
    )


def up_terms(grad_second, slope, hidden_t, w_down, here, which, got=None):
    rows, width = grad_second.shape
    ff = w_down.shape[0]
    half = ff // 2
    chunk = width
    steps = half // chunk
    block = rows // 2
    pieces = width // 32 // 8

    def kernel(here_s, gs_ref, dg_ref, ht_ref, wd_ref, *refs):
        if got is not None:
            got_ref, refs = refs[0], refs[1:]
            outs, refs = refs[:4], refs[4:]
        else:
            out_ref, refs = refs[0], refs[1:]
        gi_ref, bu_ref = refs[:2]
        sums = jnp.zeros((1, chunk), F32)
        for number in range(rows // block):
            base = slice(number * block, (number + 1) * block)
            grad_active = dot_t(gs_ref[base, :], wd_ref[...])
            low = (grad_active * dg_ref[base, :].astype(F32)).astype(BF16)
            gi_ref[base, :] = low
            sums += column_sum(low.astype(F32))
        bu_ref[...] = sums
        term = dot(ht_ref[...], gi_ref[...])
        if got is None:
            out_ref[...] = term.astype(BF16)
        else:
            scratch = refs[2]
            term += got_ref[...].astype(F32)
            scratch[...] = term.reshape(scratch.shape)
            deal(scratch, here_s, outs, 4, pieces)

    def col(i, here_s):
        return here_s[which] * steps + i

    in_specs = [
        once((rows, width)),
        pl.BlockSpec((rows, chunk), lambda i, h: (0, col(i, h))),
        once((width, rows)),
        pl.BlockSpec((chunk, width), lambda i, h: (col(i, h), 0)),
    ]
    args = [grad_second, slope, hidden_t, w_down]
    scratch = []
    if got is None:
        out_specs = [pl.BlockSpec((width, chunk), lambda i, *_: (0, i))]
        out_shape = [shaped((width, half), BF16)]
    else:
        in_specs.append(pl.BlockSpec((width, chunk), lambda i, *_: (0, i)))
        args.append(got)
        out_specs = [pl.BlockSpec((8 * pieces, 8, chunk), lambda i, *_: (0, 0, i))] * 4
        out_shape = [shaped((8 * pieces, 8, half), BF16)] * 4
        scratch.append(pltpu.VMEM((4, 2, 2, 2, pieces, 8, chunk), F32))
    return call(
        kernel, "up_give" if got is None else "up_own", (steps,), (here,), in_specs,
        out_specs
        + [
            pl.BlockSpec((rows, chunk), lambda i, *_: (0, i)),
            pl.BlockSpec((1, chunk), lambda i, *_: (0, i)),
        ],
        out_shape + [shaped((rows, half), BF16), shaped((1, half), F32)],
        scratch, 4 * rows * width * half, 16e6, args, 26, 0 if got is None else 1, (0,) if got is None else (0, 2, 4), (0, 2, 3),
    )


def attention_backward(grads_inner, gres, w_up, n_attn, spread, table, w_out, qkv, probs, here, span, rows_step):
    rows, width = gres.shape
    half = grads_inner[0].shape[1]
    pairs = width // LANES
    per_step = rows_step // span

    def kernel(here_s, gi_ref, other_ref, gres_ref, wu_ref, wu_other_ref, n_ref, s_ref, tab_ref, wo_ref, qkv_ref, p_ref, gr_ref, gb_ref, gm_ref, vec_ref, ga_scr):
        step = pl.program_id(0)
        low_b, high_b, low_m = head_masks()

        @pl.when(step == 0)
        def _():
            vec_ref[...] = jnp.zeros_like(vec_ref)

        normed = n_ref[...]
        grad_hidden = (
            dot_t(gi_ref[...], wu_ref[...]) + dot_t(other_ref[...], wu_other_ref[...]) + gres_ref[...]
        )
        resid = norm_backward(grad_hidden, normed, s_ref[:, :1], tab_ref[ROW_GA : ROW_GA + 1, :])
        gr_ref[...] = resid
        low = resid.astype(BF16)
        gb_ref[...] = low
        vec_ref[2:3, :] += column_sum(low.astype(F32))
        vec_ref[3:4, :] += column_sum(grad_hidden * normed)
        vec_ref[4:5, :] += column_sum(grad_hidden)
        ga_scr[...] = dot_t(low, wo_ref[...]).astype(BF16)
        for inner in range(per_step):
            base = slice(inner * span, (inner + 1) * span)
            for pair in range(pairs):
                cols = slice(pair * LANES, (pair + 1) * LANES)
                k_cols = slice(width + pair * LANES, width + (pair + 1) * LANES)
                v_cols = slice(2 * width + pair * LANES, 2 * width + (pair + 1) * LANES)
                q, k, v = qkv_ref[base, cols], qkv_ref[base, k_cols], qkv_ref[base, v_cols]
                grad = ga_scr[base, cols]
                grads = jnp.concatenate([grad * low_b, grad * high_b], axis=0)
                both = jnp.concatenate([q * low_b, q * high_b], axis=0)
                weights = p_ref[inner, pair]
                wide = weights.astype(F32)
                grad_probs = dot_t(grads, v)
                balance = jnp.sum(wide * grad_probs, axis=-1, keepdims=True)
                grad_logits = (wide * (grad_probs - balance)).astype(BF16)
                mix = dot(grad_logits, k)
                grad_q = jnp.where(low_m, mix[:span], mix[span:]).astype(BF16) * jnp.bfloat16(0.125)
                grad_v = t_dot(weights, grads).astype(BF16)
                gm_ref[base, cols] = grad_q
                gm_ref[base, k_cols] = t_dot(grad_logits, both).astype(BF16)
                gm_ref[base, v_cols] = grad_v
                vec_ref[0:1, cols] += column_sum(grad_q.astype(F32))
                vec_ref[1:2, cols] += column_sum(grad_v.astype(F32))

    def rows_of(cols):
        return pl.BlockSpec((rows_step, cols), lambda i, h: (i, 0))

    return call(
        kernel,
        "attn_bwd",
        (rows // rows_step,),
        (here,),
        [
            rows_of(half), rows_of(half), rows_of(width),
            pl.BlockSpec((width, half), lambda i, h: (0, h[0]), pipeline_mode=pl.Buffered(1)),
            pl.BlockSpec((width, half), lambda i, h: (0, h[1]), pipeline_mode=pl.Buffered(1)),
            rows_of(width), rows_of(LANES),
            once(table.shape), once((width, width)), rows_of(3 * width),
            pl.BlockSpec((per_step, pairs, 2 * span, span), lambda i, h: (i, 0, 0, 0)),
        ],
        [rows_of(width), rows_of(width), rows_of(3 * width), full((8, width))],
        [
            shaped((rows, width), F32), shaped((rows, width), BF16),
            shaped((rows, 3 * width), BF16), shaped((8, width), F32),
        ],
        [pltpu.VMEM((rows_step, width), BF16)],
        8 * rows * width * width * 2,
        40e6,
        (*grads_inner, gres, w_up, w_up, n_attn, spread, table, w_out, qkv, probs),
        40, 0, (1,), (0, 1, 3, 4, 8),
    )


def projection_terms(x, grad_mixed, attended, grad_branch, vectors, here, which, got=None):
    rows, width = x.shape
    part = width // 2
    pieces = width // 32 // 8

    def product(x_ref, gm_ref, att_ref, gb_ref, scr):
        step = pl.program_id(0)

        @pl.when(step < 3)
        def _():
            scr[...] = t_dot(x_ref[...], gm_ref[...])

        @pl.when(step == 3)
        def _():
            scr[...] = t_dot(att_ref[...], gb_ref[...])

    def small(here_s, ffn_ref, attn_ref, sent_ref, kept_ref, store):
        first = here_s[0] == 0
        for step in range(4):

            @pl.when(pl.program_id(0) == step)
            def _():
                side, at = step // 2, slice(step % 2 * part, (step % 2 + 1) * part)
                wide = slice(step * part, (step + 1) * part)
                rows_of = (
                    (ffn_ref[0:1, at], ffn_ref[2:3, at], attn_ref[1:2, at], attn_ref[3:4, at]),
                    (ffn_ref[1:2, at], attn_ref[0:1, at], attn_ref[2:3, at], attn_ref[4:5, at]),
                )[side]
                sent, kept = sent_ref[:, wide], kept_ref[:, wide]
                ups = (jnp.where(first, kept, sent), jnp.where(first, sent, kept))
                store(jnp.concatenate(rows_of + ups + (jnp.zeros((2, part), F32),), axis=0))

    def give(here_s, x_ref, gm_ref, att_ref, gb_ref, ffn_ref, attn_ref, sent_ref, kept_ref, out_ref, scr):
        product(x_ref, gm_ref, att_ref, gb_ref, scr)
        out_ref[:width, :] = scr[...].astype(BF16)

        def store(value):
            out_ref[width:, :] = value.astype(BF16)

        small(here_s, ffn_ref, attn_ref, sent_ref, kept_ref, store)

    def own(
        here_s, x_ref, gm_ref, att_ref, gb_ref, ffn_ref, attn_ref, sent_ref, kept_ref, got_ref,
        send_a, keep_a, send_b, keep_b, scr, cut,
    ):
        product(x_ref, gm_ref, att_ref, gb_ref, scr)
        term = scr[...] + got_ref[:width, :].astype(F32)
        cut[...] = term.reshape(cut.shape)
        deal(cut, here_s, (send_a, keep_a, send_b, keep_b), 4, pieces)

        def store(value):
            extra = (value + got_ref[width:, :].astype(F32)).astype(BF16)
            send_a[8 * pieces] = extra
            keep_a[8 * pieces] = extra

        small(here_s, ffn_ref, attn_ref, sent_ref, kept_ref, store)

    in_specs = [
        once((rows, width)),
        pl.BlockSpec((rows, part), lambda i, h: (0, h[which] * 3 + jnp.minimum(i, 2))),
        once((rows, width)),
        pl.BlockSpec((rows, part), lambda i, h: (0, h[which]), pipeline_mode=pl.Buffered(1)),
    ] + [once(item.shape) for item in vectors]
    args = [x, grad_mixed, attended, grad_branch, *vectors]
    flops = 4 * rows * width * width
    if got is None:
        return call(
            give, "proj_give", (4,), (here,), in_specs,
            pl.BlockSpec((width + 8, part), lambda i, *_: (0, i)),
            shaped((width + 8, 4 * part), BF16),
            [pltpu.VMEM((width, part), F32)], flops, 9e6, args, 20, 0, (0,), (0, 2, 3),
        )
    return call(
        own, "proj_own", (4,), (here,),
        in_specs + [pl.BlockSpec((width + 8, part), lambda i, *_: (0, i))],
        [
            pl.BlockSpec((8 * pieces + extra, 8, part), lambda i, *_: (0, 0, i))
            for extra in (1, 1, 0, 0)
        ],
        [shaped((8 * pieces + extra, 8, 4 * part), BF16) for extra in (1, 1, 0, 0)],
        [pltpu.VMEM((width, part), F32), pltpu.VMEM((4, 2, 2, 2, pieces, 8, part), F32)],
        flops, 11e6, args + [got], 24, 1, (0, 1, 2, 3), (0, 2, 3),
    )


def input_gradient(grad_mixed, w_qkv, grad_resid, rows_step):
    rows, width = grad_resid.shape

    def kernel(gm_ref, wq_ref, gr_ref, out_ref):
        out_ref[...] = (dot_t(gm_ref[...], wq_ref[...]) + gr_ref[...]).astype(BF16)

    return call(
        kernel, "input_grad", (rows // rows_step,), (),
        [
            pl.BlockSpec((rows_step, 3 * width), lambda i: (i, 0)),
            once((width, 3 * width)),
            pl.BlockSpec((rows_step, width), lambda i: (i, 0)),
        ],
        pl.BlockSpec((rows_step, width), lambda i: (i, 0)),
        shaped((rows, width), BF16), [], 6 * rows * width * width, 13e6,
        (grad_mixed, w_qkv, grad_resid), 20, 0, (), (1,),
    )


def copied(item, here, block):
    rows, width = item.shape

    def kernel(here_s, in_ref, out_ref):
        out_ref[...] = in_ref[...]

    spec = pl.BlockSpec((block, width), lambda i, *_: (i, 0))
    return call(
        kernel, "copied", (rows // block,), (here,), [spec], spec,
        shaped((rows, width), item.dtype), [], 1, 3e6, (item,), 4,
    )


def small_call(kernel, name, here, args, outs, vmem=12):
    return pl.pallas_call(
        kernel,
        in_specs=[pl.BlockSpec(memory_space=pltpu.SMEM)]
        + [pl.BlockSpec(memory_space=pltpu.VMEM)] * len(args),
        out_specs=[pl.BlockSpec(memory_space=pltpu.VMEM)] * len(outs),
        out_shape=outs,
        compiler_params=pltpu.CompilerParams(vmem_limit_bytes=vmem * MIB),
        cost_estimate=pl.CostEstimate(flops=int(1e6 * COST), bytes_accessed=int(4e6 * COST), transcendentals=0),
        name=name,
    )(here, *args)


def add(left, right):
    return (left.astype(F32) + right.astype(F32)).astype(BF16)


def fold_second(terms, here, pieces, extra):
    cols = terms[0][0].shape[2]
    count = len(terms)

    def kernel(here_s, *refs):
        send_a, left_a, send_b, left_b = refs[4 * count :]
        x, y = here_s[2], here_s[3]
        for term in range(count):
            ka, ga, kb, gb = refs[4 * term : 4 * term + 4]
            for z in range(4):
                at = pl.ds((term * 4 + z) * pieces, pieces)

                def sum_of(keep, got, other):
                    rows = pl.ds(z * 2 * pieces + other * pieces, pieces)
                    return add(keep[rows], got[rows])

                send_a[at] = sum_of(ka, ga, 1 - y)
                left_a[at] = sum_of(ka, ga, y)
                send_b[at] = sum_of(kb, gb, 1 - x)
                left_b[at] = sum_of(kb, gb, x)
        if extra:
            total = add(refs[0][8 * pieces], refs[1][8 * pieces])
            send_a[4 * count * pieces] = total
            left_a[4 * count * pieces] = total

    a_out = shaped((4 * count * pieces + extra, 8, cols), BF16)
    b_out = shaped((4 * count * pieces, 8, cols), BF16)
    args = [item for term in terms for item in term]
    return small_call(kernel, "fold_second", here, args, [a_out, a_out, b_out, b_out])


def fold_third(pairs, here, pieces, extra):
    cols = pairs[0].shape[2]
    count = pairs[2].shape[0] // (4 * pieces)

    def kernel(here_s, *refs):
        ins, (send, left) = refs[:-2], refs[-2:]
        low = here_s[4]
        for high in range(2):
            for term in range(count):
                for ab in range(2):
                    keep, got = ins[2 * ab : 2 * ab + 2]
                    at = pl.ds(((high * count + term) * 2 + ab) * pieces, pieces)
                    for out, pick in ((send, 1 - low), (left, low)):
                        rows = pl.ds((term * 4 + high * 2 + pick) * pieces, pieces)
                        out[at] = add(keep[rows], got[rows])
        if extra:
            total = add(ins[0][4 * count * pieces], ins[1][4 * count * pieces])
            send[4 * count * pieces] = total
            left[4 * count * pieces] = total

    out = shaped((4 * count * pieces + extra, 8, cols), BF16)
    return small_call(kernel, "fold_third", here, pairs, [out, out])


def fold_fourth(keep, got, here, extra):
    cols = keep.shape[2]
    count = (keep.shape[0] - extra) // 2

    def kernel(here_s, keep_ref, got_ref, send, left):
        high = here_s[5]
        for out, pick in ((send, 1 - high), (left, high)):
            rows = pl.ds(pick * count, count)
            out[:count] = add(keep_ref[rows], got_ref[rows])
        if extra:
            total = add(keep_ref[2 * count], got_ref[2 * count])
            send[count] = total
            left[count] = total

    out = shaped((count + extra, 8, cols), BF16)
    return small_call(kernel, "fold_fourth", here, (keep, got), [out, out])


def fold_last(keep, got, here, extra):
    cols = keep.shape[2]
    count = keep.shape[0] - extra

    def kernel(here_s, keep_ref, got_ref, *outs):
        outs[0][...] = add(keep_ref[:count], got_ref[:count])
        if extra:
            outs[1][0] = add(keep_ref[count], got_ref[count])

    outs = [shaped((count, 8, cols), BF16)] + [shaped((1, 8, cols), BF16)] * extra
    return small_call(kernel, "fold_last", here, (keep, got), outs)


def chosen_part(here_s, refs, core, side, at):
    me, gx, gc, gd = [item[at].astype(F32) for item in refs]
    same_core, same_side = here_s[0] == core, here_s[2] == side
    return jnp.where(same_core, jnp.where(same_side, me, gx), jnp.where(same_side, gc, gd))


def feed_blocks(parts, here, pieces, width):
    cols = parts[0].shape[2]
    half = width // 2
    folds = cols // half
    rows = 2 * pieces * 8

    def kernel(here_s, me, gx, gc, gd, down_ref, up_ref):
        refs = (me, gx, gc, gd)
        for core in range(2):
            for side in range(2):
                tall = side * folds * rows
                for ab in range(2):
                    at = pl.ds(ab * pieces, pieces)
                    value = chosen_part(here_s, refs, core, side, at).reshape(rows // 2, cols)
                    for fold in range(folds):
                        start = tall + (ab * folds + fold) * (rows // 2)
                        down_ref[start : start + rows // 2, core * half : (core + 1) * half] = value[
                            :, fold * half : (fold + 1) * half
                        ]
                at = pl.ds(2 * pieces, 2 * pieces)
                value = chosen_part(here_s, refs, core, side, at).reshape(rows, cols)
                up_ref[side * rows : (side + 1) * rows, core * cols : (core + 1) * cols] = value

    outs = [shaped((2 * folds * rows, width), F32), shaped((2 * rows, 2 * cols), F32)]
    return small_call(kernel, "feed_blocks", here, parts, outs, 16)


def projection_blocks(parts, vectors, here, pieces):
    cols = parts[0].shape[2]
    rows = 2 * pieces * 8
    cut = cols // 4 * 3
    width = cols // 2
    small = width // 8
    large = cols // 4

    def kernel(here_s, me, gx, gc, gd, vec_ref, qkv_ref, out_ref, *outs):
        refs = (me, gx, gc, gd)
        for core in range(2):
            for side in range(2):
                value = chosen_part(here_s, refs, core, side, slice(None)).reshape(rows, cols)
                at = slice(side * rows, (side + 1) * rows)
                qkv_ref[at, core * cut : (core + 1) * cut] = value[:, :cut]
                out_ref[at, core * (cols - cut) : (core + 1) * (cols - cut)] = value[:, cut:]
        table = vec_ref[0].astype(F32)
        wide = here_s[6]
        shift = lax.rem(width - wide * small, width)
        left, right = pltpu.roll(table[:, :width], shift, 1), pltpu.roll(table[:, width:], shift, 1)
        for row in range(4):
            outs[2 * row][...] = left[row : row + 1, :small]
            outs[2 * row + 1][...] = right[row : row + 1, :small]
        turned = pltpu.roll(table, lax.rem(cols - lax.rem(wide, 4) * large, cols), 1)
        outs[8][...] = jnp.where(wide < 4, turned[4:5, :large], turned[5:6, :large])

    outs = [shaped((2 * rows, 2 * cut), F32), shaped((2 * rows, 2 * (cols - cut)), F32)]
    outs += [shaped((1, small), F32)] * 8 + [shaped((1, large), F32)]
    return small_call(kernel, "projection_blocks", here, (*parts, vectors), outs, 16)


def after(item, *earlier):
    return lax.optimization_barrier((item, *earlier))[0]


def swap(item, axis, step):
    count = lax.axis_size(axis)
    return lax.ppermute(item, axis, [(index, index ^ step) for index in range(count)])


def quarters(mine):
    across = swap(mine, "narrow", 2)
    return mine, across, swap(mine, "narrow", 1), swap(across, "narrow", 1)


def regroup_rows(sent, bucket, wide_count, batches):
    span, width = sent.shape[1:]
    if wide_count == batches:
        got = lax.all_to_all(sent, "wide", split_axis=0, concat_axis=0, tiled=True)
        return got.reshape(batches * span, width)
    send = jnp.zeros((wide_count, span, width), sent.dtype).at[bucket].set(sent)
    got = lax.all_to_all(send, "wide", split_axis=0, concat_axis=0, tiled=True)
    marks = jnp.zeros((wide_count, 1), jnp.int32).at[bucket].set(1)
    filled = lax.all_to_all(marks, "wide", split_axis=0, concat_axis=0, tiled=True)[:, 0]
    place = jnp.where(filled > 0, jnp.cumsum(filled) - filled, batches)
    chosen = (
        jnp.zeros((batches,), jnp.int32)
        .at[place]
        .set(jnp.arange(wide_count, dtype=jnp.int32), mode="drop")
    )
    return got[chosen].reshape(batches * span, width)


def sum_anywhere(item, wide_count, narrow_count):
    blocks = item.astype(F32).reshape(wide_count, -1)
    extent = blocks.shape[1]
    padded = (extent + narrow_count - 1) // narrow_count * narrow_count
    blocks = jnp.pad(blocks, ((0, 0), (0, padded - extent))).reshape(-1)
    share = lax.psum_scatter(blocks, ("wide", "narrow"), scatter_dimension=0, tiled=True)
    whole = lax.all_gather(share.astype(BF16), "narrow", axis=0, tiled=True).astype(F32)
    return whole[:extent].reshape((item.shape[0] // wide_count,) + item.shape[1:])


def body(
    tokens, bucket, lengths, pairing, targets, w_qkv, bias_q, bias_v, w_out, bias_out,
    gain_attn, shift_attn, w_up, bias_up, w_down, bias_down, gain_ffn, shift_ffn,
):
    wide_count, narrow_count = lax.axis_size("wide"), lax.axis_size("narrow")
    batches = bucket.shape[0]
    rows, width = tokens.shape
    span = rows // batches
    paired = (wide_count, narrow_count) == (8, 4)
    wide, narrow = lax.axis_index("wide"), lax.axis_index("narrow")
    if paired:
        core = narrow % 2
        here = jnp.stack(
            [core, 1 - core, narrow // 2, wide % 2, wide // 2 % 2, wide // 4, wide, narrow]
        ).astype(jnp.int32)
    else:
        here = jnp.arange(8, dtype=jnp.int32)
    table = vector_table(
        [bias_q, bias_v, bias_out, gain_attn, shift_attn, bias_down, gain_ffn, shift_ffn, bias_up], width
    )
    ordered = wide_count == batches
    slots = bucket if ordered else jnp.arange(batches, dtype=jnp.int32)
    pieces = width // 32 // 8

    qkv, probs, attended, n_attn, spread, sid = attention_forward(
        tokens, w_qkv, w_out, table, bucket, lengths, wide_count // batches, span, 2 * span
    )
    active, slope, hidden_t, sent, gres, grad_second, vec_ffn = feed_forward(
        n_attn, w_up, w_down, table, sid, slots, pairing, targets, batches, 2 * span
    )
    ups = (grad_second, slope, hidden_t, w_down)
    heads = (n_attn, spread, table, w_out, qkv, probs)
    down_sent = down_terms(active, grad_second, here, 1)
    if paired:
        encoded = regroup_rows(after(sent, down_sent), bucket, wide_count, batches)
        up_sent, gi_sent, bup_sent = up_terms(*ups, after(here, down_sent), 1)
        down_dealt = down_terms(active, grad_second, after(here, bup_sent), 0, swap(down_sent, "narrow", 1))
        down_a, down_b = swap(down_dealt[0], "narrow", 2), swap(down_dealt[2], "wide", 1)
        *up_dealt, gi_kept, bup_kept = up_terms(
            *ups, after(here, down_dealt[1]), 0, swap(up_sent, "narrow", 1)
        )
        up_a, up_b = swap(up_dealt[0], "narrow", 2), swap(up_dealt[2], "wide", 1)
        gr, gb, gm, vec_attn = attention_backward(
            (gi_kept, gi_sent), gres, w_up, *heads, after(here, up_dealt[1]), span, 4 * span
        )
        feed = fold_second(
            [
                (down_dealt[1], down_a, down_dealt[3], down_b),
                (up_dealt[1], up_a, up_dealt[3], up_b),
            ],
            after(here, vec_attn, encoded), pieces, 0,
        )
        feed_a, feed_b = swap(feed[0], "wide", 1), swap(feed[2], "narrow", 2)
        projections = (tokens, gm, attended, gb, (vec_ffn, vec_attn, bup_sent, bup_kept))
        proj_sent = projection_terms(*projections, after(here, feed[1]), 1)
        proj_dealt = projection_terms(
            *projections, after(here, proj_sent), 0, swap(proj_sent, "narrow", 1)
        )
        proj_a, proj_b = swap(proj_dealt[0], "narrow", 2), swap(proj_dealt[2], "wide", 1)
        send, feed = fold_third(
            [feed[1], feed_a, feed[3], feed_b], after(here, proj_dealt[1]), pieces, 0
        )
        feed_got = swap(send, "wide", 2)
        grad_tokens = input_gradient(after(gm, feed), w_qkv, gr, 4 * span)
        send, feed = fold_fourth(feed, feed_got, after(here, grad_tokens), 0)
        feed_got = swap(send, "wide", 4)
        proj_dealt = fold_second(
            [(proj_dealt[1], proj_a, proj_dealt[3], proj_b)], after(here, feed), pieces, 1
        )
        proj_a, proj_b = swap(proj_dealt[0], "wide", 1), swap(proj_dealt[2], "narrow", 2)
        encoded = copied(encoded, after(here, proj_dealt[1]), span)
        send, proj = fold_third(
            [proj_dealt[1], proj_a, proj_dealt[3], proj_b], after(here, encoded), pieces, 1
        )
        proj_got = swap(send, "wide", 2)
        (feed,) = fold_last(feed, feed_got, after(here, proj), 0)
        send, proj = fold_fourth(proj, proj_got, after(here, feed), 1)
        proj_got = swap(send, "wide", 4)
        feed = quarters(after(feed, proj))
        proj, vectors = fold_last(proj, proj_got, here, 1)
        proj = quarters(proj)
        grad_w_down, grad_w_up = feed_blocks(feed, after(here, proj[0]), pieces, width)
        grad_w_qkv, grad_w_out, *small = projection_blocks(proj, vectors, after(here, grad_w_down), pieces)
        small = [item.reshape(-1) for item in small]
    else:
        encoded = regroup_rows(sent, bucket, wide_count, batches)
        down_kept = down_terms(active, grad_second, here, 0)
        up_sent, gi_sent, bup_sent = up_terms(*ups, here, 1)
        up_kept, gi_kept, bup_kept = up_terms(*ups, here, 0)
        gr, gb, gm, vec_attn = attention_backward(
            (gi_kept, gi_sent), gres, w_up, *heads, here, span, 2 * span
        )
        projections = (tokens, gm, attended, gb, (vec_ffn, vec_attn, bup_sent, bup_kept), here)
        grad_tokens = input_gradient(gm, w_qkv, gr, 2 * span)
        proj_sent, proj_kept = projection_terms(*projections, 1), projection_terms(*projections, 0)
        total = partial(sum_anywhere, wide_count=wide_count, narrow_count=narrow_count)
        cut = width // 2 * 3
        grad_w_down = total(jnp.concatenate([down_kept, down_sent], axis=1))
        grad_w_up = total(jnp.concatenate([up_kept, up_sent], axis=1))
        grad_w_qkv = total(jnp.concatenate([proj_kept[:width, :cut], proj_sent[:width, :cut]], axis=1))
        grad_w_out = total(jnp.concatenate([proj_kept[:width, cut:], proj_sent[:width, cut:]], axis=1))
        small = [
            total(item)
            for item in (*vec_ffn[:3], *vec_attn[:5], jnp.concatenate([bup_kept[0], bup_sent[0]]))
        ]
    gain_out, shift_out, b_down, b_q, b_v, b_out, g_attn, s_attn, b_up = small
    return (
        encoded, grad_tokens, grad_w_qkv, b_q, b_v, grad_w_out, b_out, g_attn, s_attn,
        grad_w_up, b_up, grad_w_down, b_down, gain_out, shift_out,
    )


def solution(mesh):
    split = P(("wide", "narrow"))
    in_specs = (
        P(("wide", "narrow"), None), split, split, P(("wide", "narrow"), None), split,
    ) + (P(),) * 13
    out_specs = (
        P(("wide", "narrow"), None), P(("wide", "narrow"), None),
        P("wide", None), P("wide"), P("wide"), P("wide", None), P("wide"), P("wide"), P("wide"),
        P("wide", None), P("wide"), P("wide", None), P("wide"), P("wide"), P("wide"),
    )
    return jax.shard_map(body, mesh=mesh, in_specs=in_specs, out_specs=out_specs, check_vma=False)
```
